32 devices in a mesh: seq: 4 (over x, core), view: 8 (over z, y).
Axes of the slice: x: 2, y: 2, z: 4, core: 2. Of those that a mesh axis runs over, the one named last changes fastest.
Arguments:
- tokens: bfloat16 [4, 1024, 1024], P('seq', 'view'), may hold values from -6 to 6
- scene_ids: int32 [4, 1024], P('seq', 'view'), may hold values from 0 to 15, as said below
- live_mask: int32 [4, 1024], P('seq', 'view'), may hold values from 0 to 1, as said below
- out_grad: bfloat16 [4, 1024, 1024], P('seq', 'view'), may hold values from -6 to 6
- attention_gain: bfloat16 [1024], replicated, may hold values from 0.5 to 1.5
- input_weight: bfloat16 [1024, 3072], replicated, may hold values from -0.25 to 0.25
- output_weight: bfloat16 [1024, 1024], replicated, may hold values from -1 to 1
- feedforward_gain: bfloat16 [1024], replicated, may hold values from 0.5 to 1.5
- up_weight: bfloat16 [4096, 1024], P(('seq', 'view')), may hold values from -0.1875 to 0.1875
- down_weight: bfloat16 [4096, 1024], P(('seq', 'view')), may hold values from -0.09375 to 0.09375
Outputs:
- layer_out: bfloat16 [4, 1024, 1024], P('seq', 'view')
- tokens_grad: float32 [4, 1024, 1024], P('seq', 'view')
- attention_gain_grad: float32 [1024], replicated
- input_weight_grad: float32 [1024, 3072], replicated
- output_weight_grad: float32 [1024, 1024], replicated
- feedforward_gain_grad: float32 [1024], replicated
- up_weight_grad: float32 [4096, 1024], P(('seq', 'view'))
- down_weight_grad: float32 [4096, 1024], P(('seq', 'view'))
The draws below stay inside these ranges and needn't reach their ends.
Inputs may be any that keep to these rules, and one draw needn't show every extreme that they name: `scene_ids`: each sequence is made of 64 blocks of 16 consecutive tokens in a drawn order; each block belongs to one scene, each of the sequence's 4 scenes owns 16 blocks, and sequence s holds scenes s * 4 to s * 4 + 3. `live_mask`: constant over each scene; in one sequence every scene is live, in each other sequence exactly one scene is not.
All inputs are finite; a program needn't handle non-finite values.
Results may differ from the reference program's by a relative error of at most 0.015.
Values may be sent and summed in bfloat16 or wider, within the bound.
A program may use at most 256 MiB of HBM per device.

```python
import math
import jax
import jax.numpy as jnp
from jax import lax

D = 1024
HEADS = 16
HEAD_DIM = 64
FF = 4096
SLOTS = 4
SCENE_BLOCKS = 16
SEQS = 4
SEQ_LEN = 1024
BLOCK = 16


def scene_layout(key):
    base = jax.random.fold_in(key, 4242)
    count = SLOTS * SCENE_BLOCKS
    order_keys = jax.random.split(jax.random.fold_in(base, 1), SEQS)
    orders = jax.vmap(lambda single: jax.random.permutation(single, count))(order_keys)
    slot_of = (orders // SCENE_BLOCKS).astype(jnp.int32)
    full_seq = jax.random.randint(jax.random.fold_in(base, 2), (), 0, SEQS)
    empty_slot = jax.random.randint(jax.random.fold_in(base, 3), (SEQS,), 0, SLOTS)
    indices = jnp.arange(SEQS, dtype=jnp.int32)
    alive = jnp.logical_or(slot_of != empty_slot[:, None], (indices == full_seq)[:, None]).astype(jnp.int32)
    scenes = indices[:, None] * SLOTS + slot_of
    scenes = jnp.repeat(scenes, BLOCK, axis=1).astype(jnp.int32)
    alive = jnp.repeat(alive, BLOCK, axis=1).astype(jnp.int32)
    return (scenes, alive)


def draw_scene_ids(key, part):
    return scene_layout(key)[0]


def draw_live_mask(key, part):
    return scene_layout(key)[1]


def block_scale(rng, shape, shards, smallest, largest):
    level = 1.0
    for axis_at, parts in shards:
        heights = jax.random.uniform(jax.random.fold_in(jax.random.fold_in(rng, 6), axis_at), (parts,), jnp.float32, smallest / len(shards), largest / len(shards))
        level = level * jnp.repeat(jnp.exp(heights), shape[axis_at] // parts).reshape((-1,) + (1,) * (len(shape) - 1 - axis_at))
    return level


def centred(own_key, extent, scale, most, cuts=(), held_as=jnp.bfloat16):
    level = block_scale(own_key, extent, cuts, -0.22, 0.18) if cuts else 1.0
    values = jax.random.normal(own_key, extent, jnp.float32) * scale * level
    return jnp.minimum(jnp.maximum(values, -most), most).astype(held_as)


def setup_inputs(seed: int = 0) -> dict:
    splits = jax.random.split(jax.random.key(seed), 11)
    return {
        "tokens": centred(splits[0], (SEQS, SEQ_LEN, D), 1.0, 6.0, ((0, 4), (1, 8))),
        "scene_ids": draw_scene_ids(jax.random.fold_in(splits[10], 71), 0),
        "live_mask": draw_live_mask(jax.random.fold_in(splits[10], 71), 0),
        "out_grad": centred(splits[3], (SEQS, SEQ_LEN, D), 1.0, 6.0, ((0, 4), (1, 8))),
        "attention_gain": jnp.clip(1.0 + 0.1 * jax.random.normal(splits[4], (D,), jnp.float32), 0.5, 1.5).astype(jnp.bfloat16),
        "input_weight": centred(splits[5], (D, 3 * D), (D // 2) ** -0.5, 0.25),
        "output_weight": centred(splits[6], (D, D), (D // 32) ** -0.5, 1.0),
        "feedforward_gain": jnp.clip(1.0 + 0.1 * jax.random.normal(splits[7], (D,), jnp.float32), 0.5, 1.5).astype(jnp.bfloat16),
        "up_weight": centred(splits[8], (FF, D), D ** -0.5, 0.1875, ((0, 32),)),
        "down_weight": centred(splits[9], (FF, D), FF ** -0.5, 0.09375, ((0, 32),)),
    }


EPS = 1e-05
HIGH = lax.Precision.HIGHEST

@jax.custom_vjp
def low(v):
    return lax.optimization_barrier(v.astype(jnp.bfloat16)).astype(jnp.float32)

@jax.custom_vjp
def low_back(v):
    return v

def low_keep(v):
    return (low(v), None)

def low_pass(kept, grad):
    return (grad,)

def back_keep(v):
    return (v, None)

def back_low(kept, grad):
    return (low(grad),)
low.defvjp(low_keep, low_pass)
low_back.defvjp(back_keep, back_low)

def layer_norm(values, gain):
    center = values - lax.optimization_barrier(jnp.mean(values, axis=-1, keepdims=True))
    spread = lax.optimization_barrier(jnp.mean(center * center, axis=-1, keepdims=True))
    return center * lax.rsqrt(spread + EPS) * gain

def matmul(left, right):
    return jnp.dot(left, right, precision=HIGH, preferred_element_type=jnp.float32)

def attend_block(queries, query_tags, keys, values, key_tags):
    scale = HEAD_DIM ** (-0.5)
    raw = jnp.einsum('qhe,khe->hqk', queries, keys, precision=HIGH) * scale
    raw = low_back(raw)
    allowed = (query_tags[:, None] == key_tags[None, :])[None]
    weights = jnp.exp(jnp.where(allowed, raw, -10000.0))
    total = lax.optimization_barrier(jnp.sum(weights, axis=-1))
    summed = jnp.einsum('hqk,khe->qhe', low(weights), values, precision=HIGH)
    return summed / jnp.transpose(total)[:, :, None]

def sequence_layer(inputs, tags, live, gain_one, input_weight, output_weight, gain_two, up_weight, down_weight):
    length = inputs.shape[0]
    width = inputs.shape[1]
    normed = low(layer_norm(inputs, gain_one))
    projected = low_back(low(matmul(normed, input_weight)))
    queries = projected[:, :width].reshape(length, HEADS, HEAD_DIM)
    keys = projected[:, width:2 * width].reshape(length, HEADS, HEAD_DIM)
    values = projected[:, 2 * width:].reshape(length, HEADS, HEAD_DIM)
    rows_block = math.gcd(length, 512)
    count = length // rows_block
    query_blocks = queries.reshape(count, rows_block, HEADS, HEAD_DIM)
    tag_blocks = tags.reshape(count, rows_block)

    def block_step(pair):
        return attend_block(pair[0], pair[1], keys, values, tags)
    attended = lax.map(jax.checkpoint(block_step), (query_blocks, tag_blocks)).reshape(length, width)
    attended = low_back(low(attended))
    branch = low_back(matmul(attended, output_weight))
    middle = inputs + live * branch
    normed_two = low(layer_norm(middle, gain_two))
    hidden = low_back(matmul(normed_two, jnp.transpose(up_weight)))
    activated = low(jax.nn.gelu(hidden, approximate=False))
    mixed = low_back(matmul(activated, down_weight))
    return middle + live * mixed

def reference(tokens, scene_ids, live_mask, out_grad, attention_gain, input_weight, output_weight, feedforward_gain, up_weight, down_weight):
    weights = (attention_gain.astype(jnp.float32), input_weight.astype(jnp.float32), output_weight.astype(jnp.float32), feedforward_gain.astype(jnp.float32), up_weight.astype(jnp.float32), down_weight.astype(jnp.float32))

    def one_sequence(carry, item):
        inputs, scenes, alive, cotangent = item
        tags = scenes * 2 + alive
        live = alive.astype(jnp.float32)[:, None]

        def layer_fn(values, *params):
            return sequence_layer(values, tags, live, *params)
        result, pull = jax.vjp(layer_fn, inputs.astype(jnp.float32), *weights)
        grads = pull(cotangent.astype(jnp.float32))
        carry = tuple((running + part for running, part in zip(carry, grads[1:])))
        return (carry, (result.astype(jnp.bfloat16), grads[0]))
    init = tuple((jnp.zeros(weight.shape, jnp.float32) for weight in weights))
    sums, outputs = lax.scan(one_sequence, init, (tokens, scene_ids, live_mask, out_grad))
    return (outputs[0], outputs[1], sums[0], sums[1], sums[2], sums[3], sums[4], sums[5])
```

```python
import functools
import math
import types

import jax
import jax.numpy as jnp
from jax import lax
from jax.experimental import pallas as pl
from jax.experimental.pallas import tpu as pltpu
from jax.sharding import PartitionSpec as P

HEADS = 16
HEAD_DIM = 64


EPS = 1e-05
NEGATIVE = -1e30
MESH = pl.DeviceIdType.MESH
SLOTS = 4
SCENE_BLOCKS = 16


def layer_norm(values, gain):
    center = values - jnp.mean(values, axis=-1, keepdims=True)
    spread = jnp.mean(center * center, axis=-1, keepdims=True)
    return center * lax.rsqrt(spread + EPS) * gain


def gelu_exact(values):
    return jax.nn.gelu(values, approximate=False)


def plain_dot(left, right):
    return jnp.dot(left, right, preferred_element_type=jnp.float32)


def dot_inner(left, right):
    return lax.dot_general(
        left, right, (((1,), (1,)), ((), ())), preferred_element_type=jnp.float32
    )


def dot_outer(left, right):
    return lax.dot_general(
        left, right, (((0,), (0,)), ((), ())), preferred_element_type=jnp.float32
    )


def split_heads(values):
    return values.reshape(values.shape[0], HEADS, HEAD_DIM)


def masked_scores(queries, keys, query_tags, key_tags, scale):
    raw = jnp.einsum("qhe,khe->hqk", queries, keys, preferred_element_type=jnp.float32) * scale
    allowed = (query_tags[:, None] == key_tags[None, :])[None]
    return (raw, allowed)


def probabilities(queries, keys, query_tags, key_tags, log_total, scale):
    raw, allowed = masked_scores(queries, keys, query_tags, key_tags, scale)
    return jnp.where(
        allowed, jnp.exp(jnp.where(allowed, raw - log_total[:, :, None], NEGATIVE)), 0.0
    )


def in_blocks(step, carry, piece):
    count = piece[0].shape[0]
    size = math.gcd(count, 512)
    number = count // size
    stacked = tuple((member.reshape((number, size) + member.shape[1:]) for member in piece))

    def inner(state, item):
        members, offset = item
        return (step(state, members, offset * size), None)

    result, unused = lax.scan(inner, carry, (stacked, jnp.arange(number, dtype=jnp.int32)))
    return result


def shards(
    tokens,
    scene_ids,
    live_mask,
    out_grad,
    attention_gain,
    input_weight,
    output_weight,
    feedforward_gain,
    up_weight,
    down_weight,
):
    scale = HEAD_DIM ** (-0.5)
    inputs = tokens[0].astype(jnp.float32)
    rows = inputs.shape[0]
    width = inputs.shape[1]
    tags = scene_ids[0] * 2 + live_mask[0]
    live = live_mask[0].astype(jnp.float32)[:, None]
    every_tag = lax.all_gather(tags, "view", axis=0, tiled=True)
    up_full, down_full = (
        lax.all_gather(up_weight, ("seq", "view"), axis=0, tiled=True),
        lax.all_gather(down_weight, ("seq", "view"), axis=0, tiled=True),
    )
    gain_one = attention_gain.astype(jnp.float32)
    gain_two = feedforward_gain.astype(jnp.float32)
    normed = layer_norm(inputs, gain_one).astype(jnp.bfloat16)
    projected = plain_dot(normed, input_weight).astype(jnp.bfloat16)
    query_flat = projected[:, :width]
    queries = split_heads(query_flat)
    keys_own = projected[:, width : 2 * width]
    values_own = projected[:, 2 * width :]

    def attend_step(carry, piece, start):
        peak, total, accum = carry
        key_piece, value_piece = piece
        count = key_piece.shape[0]
        key_tags = lax.dynamic_slice_in_dim(every_tag, start, count)
        raw, allowed = masked_scores(queries, split_heads(key_piece), tags, key_tags, scale)
        masked = jnp.where(allowed, raw, NEGATIVE)
        new_peak = jnp.maximum(peak, jnp.max(masked, axis=-1))
        weights = jnp.where(allowed, jnp.exp(masked - new_peak[:, :, None]), 0.0)
        factor = jnp.exp(peak - new_peak)
        total = total * factor + jnp.sum(weights, axis=-1)
        update = jnp.einsum(
            "hqk,khe->qhe",
            weights.astype(jnp.bfloat16),
            split_heads(value_piece),
            preferred_element_type=jnp.float32,
        )
        accum = accum * jnp.transpose(factor)[:, :, None] + update
        return (new_peak, total, accum)

    start_state = (
        jnp.full((HEADS, rows), NEGATIVE, jnp.float32),
        jnp.zeros((HEADS, rows), jnp.float32),
        jnp.zeros((rows, HEADS, HEAD_DIM), jnp.float32),
    )
    peak, total, accum = in_blocks(
        attend_step,
        start_state,
        (
            lax.all_gather(keys_own, "view", axis=0, tiled=True),
            lax.all_gather(values_own, "view", axis=0, tiled=True),
        ),
    )
    attended_heads = accum / jnp.transpose(total)[:, :, None]
    log_total = peak + jnp.log(total)
    attended_low = attended_heads.reshape(rows, width).astype(jnp.bfloat16)
    branch = plain_dot(attended_low, output_weight)
    middle = inputs + live * branch
    normed_two = layer_norm(middle, gain_two).astype(jnp.bfloat16)
    hidden = dot_inner(normed_two, up_full)
    activated = gelu_exact(hidden).astype(jnp.bfloat16)
    mixed = plain_dot(activated, down_full)
    layer_out = (middle + live * mixed).astype(jnp.bfloat16)[None]
    out_cot = out_grad[0].astype(jnp.float32)
    mixed_cot = (live * out_cot).astype(jnp.bfloat16)
    down_grad = dot_outer(activated, mixed_cot)
    activated_cot = dot_inner(mixed_cot, down_full)
    hidden_cot = jax.vjp(gelu_exact, hidden)[1](activated_cot)[0].astype(jnp.bfloat16)
    up_grad = dot_outer(hidden_cot, normed_two)
    normed_two_cot = plain_dot(hidden_cot, up_full)
    second_pull = jax.vjp(layer_norm, middle, gain_two)[1]
    middle_part, gain_two_grad = second_pull(normed_two_cot)
    middle_cot = out_cot + middle_part
    branch_cot = (live * middle_cot).astype(jnp.bfloat16)
    output_weight_grad = dot_outer(attended_low, branch_cot)
    attended_cot = dot_inner(branch_cot, output_weight).astype(jnp.bfloat16)
    cot_heads = split_heads(attended_cot)
    delta = jnp.transpose(jnp.sum(cot_heads.astype(jnp.float32) * attended_heads, axis=-1))
    seq_len = every_tag.shape[0]

    def back_step(carry, piece, start):
        query_cot, key_value_cot = carry
        key_piece, value_piece = piece
        count = key_piece.shape[0]
        key_tags = lax.dynamic_slice_in_dim(every_tag, start, count)
        key_heads = split_heads(key_piece)
        value_heads = split_heads(value_piece)
        probs = probabilities(queries, key_heads, tags, key_tags, log_total, scale)
        prob_cot = jnp.einsum(
            "qhe,khe->hqk", cot_heads, value_heads, preferred_element_type=jnp.float32
        )
        score_cot = (probs * (prob_cot - delta[:, :, None])).astype(jnp.bfloat16)
        query_cot = (
            query_cot
            + jnp.einsum("hqk,khe->qhe", score_cot, key_heads, preferred_element_type=jnp.float32)
            * scale
        )
        key_cot = (
            jnp.einsum("hqk,qhe->khe", score_cot, queries, preferred_element_type=jnp.float32)
            * scale
        )
        value_cot = jnp.einsum(
            "hqk,qhe->khe",
            probs.astype(jnp.bfloat16),
            cot_heads,
            preferred_element_type=jnp.float32,
        )
        stacked = jnp.concatenate(
            [key_cot.reshape(count, width), value_cot.reshape(count, width)], axis=1
        )
        earlier = lax.dynamic_slice_in_dim(key_value_cot, start, count)
        key_value_cot = lax.dynamic_update_slice_in_dim(key_value_cot, earlier + stacked, start, 0)
        return (query_cot, key_value_cot)

    back_state = (
        jnp.zeros((rows, HEADS, HEAD_DIM), jnp.float32),
        jnp.zeros((seq_len, 2 * width), jnp.float32),
    )
    query_cot, key_value_cot = in_blocks(
        back_step,
        back_state,
        (
            lax.all_gather(keys_own, "view", axis=0, tiled=True),
            lax.all_gather(values_own, "view", axis=0, tiled=True),
        ),
    )
    own_cot = lax.psum_scatter(key_value_cot, "view", scatter_dimension=0, tiled=True)
    key_cot_own = own_cot[:, :width]
    value_cot_own = own_cot[:, width:]
    projected_cot = jnp.concatenate(
        [query_cot.reshape(rows, width), key_cot_own, value_cot_own], axis=1
    ).astype(jnp.bfloat16)
    input_weight_grad = dot_outer(normed, projected_cot)
    normed_cot = dot_inner(projected_cot, input_weight)
    first_pull = jax.vjp(layer_norm, inputs, gain_one)[1]
    input_part, gain_one_grad = first_pull(normed_cot)
    tokens_grad = (middle_cot + input_part)[None]
    up_part, down_part = (
        lax.psum_scatter(up_grad, ("seq", "view"), scatter_dimension=0, tiled=True),
        lax.psum_scatter(down_grad, ("seq", "view"), scatter_dimension=0, tiled=True),
    )
    summed = lax.psum(
        (gain_one_grad, input_weight_grad, output_weight_grad, gain_two_grad), ("seq", "view")
    )
    return (layer_out, tokens_grad, summed[0], summed[1], summed[2], summed[3], up_part, down_part)


def dot_nn(left, right):
    return lax.dot_general(left, right, (((1,), (0,)), ((), ())), preferred_element_type=jnp.float32)


def at(start, size):
    return pl.ds(pl.multiple_of(start, size), size)


def norm_stats(values):
    mean = jnp.mean(values, axis=-1, keepdims=True)
    center = values - mean
    spread = jnp.mean(center * center, axis=-1, keepdims=True)
    inverse = lax.rsqrt(spread + EPS)
    return center * inverse, inverse


def norm_back(cot, unit, inverse, gain):
    scaled = cot * gain
    first = jnp.mean(scaled, axis=-1, keepdims=True)
    second = jnp.mean(scaled * unit, axis=-1, keepdims=True)
    return inverse * (scaled - first - unit * second)


class Wires:
    def __init__(self, send_sem, recv_sem, peer):
        self.send_sem, self.recv_sem, self.peer = send_sem, recv_sem, peer
        self.sends, self.recvs, self.pending = 0, 0, []

    def inbox(self, count):
        base = self.recvs
        self.recvs += count
        return base

    def send(self, src, dst, slot, device):
        copy = pltpu.make_async_remote_copy(
            src_ref=src,
            dst_ref=dst,
            send_sem=self.send_sem.at[self.sends],
            recv_sem=self.recv_sem.at[slot],
            device_id=device,
            device_id_type=MESH,
        )
        self.sends += 1
        copy.start()
        self.pending.append(copy)
        return copy

    def sent(self, copy):
        copy.wait_send()
        self.pending = [other for other in self.pending if other is not copy]

    def wait(self, dst, slot):
        pltpu.make_async_remote_copy(
            src_ref=dst,
            dst_ref=dst,
            send_sem=self.send_sem.at[0],
            recv_sem=self.recv_sem.at[slot],
            device_id=self.peer,
            device_id_type=MESH,
        ).wait_recv()

    def drain(self):
        for copy in self.pending:
            copy.wait_send()


SENDS, RECVS, LOCALS = 200, 200, 24


def scratch_of(rows, width, seqs, views, hidden):
    length = rows * views
    own = width // views
    bf, f3 = jnp.bfloat16, jnp.float32
    vm = pltpu.VMEM
    mlp_rows = hidden * seqs * views // 4
    return dict(
        w_full=vm((width, 3 * width), bf),
        w_own=vm((width, 3 * own), bf),
        wo=vm((width, width), bf),
        up=vm((mlp_rows, width), bf),
        down=vm((mlp_rows, width), bf),
        ids_all=vm((views, 8, 128), jnp.int32),
        order_vm=vm((16, 128), jnp.int32),
        order_sm=pltpu.SMEM((16, 128), jnp.int32),
        normed=vm((length, width), bf),
        qkv=vm((length, 3 * own), bf),
        qkv_s=vm((length, 3 * own), bf),
        weights=vm((2 * SLOTS, length // SLOTS, length // SLOTS), f3),
        totals=vm((2 * SLOTS, length // SLOTS, 1), f3),
        att_s=vm((length, own), f3),
        att=vm((length, own), bf),
        att_tok=vm((rows, width), bf),
        middle=vm((rows, width), f3),
        normed_two=vm((4 * rows, width), bf),
        mixed_cot=vm((4 * rows, width), bf),
        act_cot=vm((4 * rows, mlp_rows), f3),
        act=vm((4 * rows, mlp_rows), bf),
        hid_cot=vm((4 * rows, mlp_rows), bf),
        part_own=vm((2, rows, width), f3),
        part_out=vm((2, 3, rows, width), bf),
        part_in=vm((2, 4, rows, width), bf),
        grad_keep=vm((2, mlp_rows // 2, width), bf),
        grad_pass=vm((2, mlp_rows // 2, width), bf),
        grad_core=vm((2, mlp_rows // 2, width), bf),
        grad_in=vm((2, 4, hidden, width), bf),
        branch=vm((length, width), bf),
        acot_tok=vm((rows, width), bf),
        acot=vm((length, own), bf),
        acot_s=vm((length, own), bf),
        pc_s=vm((length, 3 * own), bf),
        pc=vm((3, length, own), bf),
        pc_tok=vm((3, rows, width), bf),
        dw_out=vm((3, 3, width // seqs, own), bf),
        dw_in=vm((4, 3, width // seqs, own), bf),
        do_out=vm((own, width), bf),
        do_in=vm((4, own // seqs, width), bf),
        fin_w=vm((3, width, width), bf),
        fin_o=vm((width, width), bf),
        gain_own=vm((8, width), f3),
        gain_in=vm((seqs, 8, width), f3),
        gain_sum=vm((8, width), f3),
        gain_all=vm((views, 8, width), f3),
        send_sem=pltpu.SemaphoreType.DMA((SENDS,)),
        recv_sem=pltpu.SemaphoreType.DMA((RECVS,)),
        local_sem=pltpu.SemaphoreType.DMA((LOCALS,)),
    )


def layer_kernel(names, seqs, views, *refs):
    (tok, ids, alive, out_cot, gain_one_ref, gain_two_ref, w_hbm, wo_hbm, up_hbm, down_hbm) = refs[:10]
    (layer_out, tokens_grad, gains, w_grad, o_grad, up_grad, down_grad) = refs[10:17]
    k = types.SimpleNamespace(**dict(zip(names, refs[17:])))
    rows, width = tok.shape
    length = rows * views
    own = width // views
    hidden = up_hbm.shape[0]
    mlp_rows = k.up.shape[0]
    half = mlp_rows // 2
    levels = views // 2
    block = length // (SLOTS * SCENE_BLOCKS)
    scene = length // SLOTS
    scale = HEAD_DIM ** (-0.5)
    bf, f3 = jnp.bfloat16, jnp.float32

    s = lax.axis_index("seq")
    v = lax.axis_index("view")
    x, c, z, y = s // 2, s % 2, v // 2, v % 2
    x_s, c_s, xc_s = (1 - x) * 2 + c, x * 2 + (1 - c), (1 - x) * 2 + (1 - c)
    y_v = z * 2 + (1 - y)
    others_z = [lax.rem(z + d, levels) for d in range(1, levels)]
    group = [(x_s, v), (s, y_v), (x_s, y_v)]
    group_slot = [(1 - x) * 2 + y, x * 2 + (1 - y), (1 - x) * 2 + (1 - y)]
    own_slot = x * 2 + y
    view_peers = [lax.rem(v + d, views) for d in range(1, views)]
    seq_peers = [x_s, xc_s, c_s]

    wires = Wires(k.send_sem, k.recv_sem, (c_s, v))
    in_normed = wires.inbox(views)
    in_ids = wires.inbox(views)
    in_up = wires.inbox(levels + 1)
    in_down = wires.inbox(levels + 1)
    in_mcot = wires.inbox(4)
    in_att = wires.inbox(views)
    in_two = wires.inbox(4)
    in_part = [wires.inbox(4), wires.inbox(4)]
    in_core = [wires.inbox(1), wires.inbox(1)]
    in_grad = [wires.inbox(levels), wires.inbox(levels)]
    in_acot = wires.inbox(views)
    in_branch = wires.inbox(views)
    in_pc = wires.inbox(views)
    in_dw = wires.inbox(seqs)
    in_do = wires.inbox(seqs)
    in_fw = wires.inbox(seqs * views)
    in_fo = wires.inbox(seqs * views)
    in_gain = wires.inbox(seqs)
    in_gains = wires.inbox(views)

    loads = []

    def load(src, dst):
        copy = pltpu.make_async_copy(src, dst, k.local_sem.at[len(loads)])
        copy.start()
        loads.append(copy)
        return copy

    up_slot = at((c * levels + z) * hidden, hidden)
    load_up = load(up_hbm, k.up.at[up_slot])
    load_down = load(down_hbm, k.down.at[up_slot])
    load_own = [
        load(w_hbm.at[:, at(t * width + v * own, own)], k.w_own.at[:, pl.ds(t * own, own)])
        for t in range(3)
    ]
    load_wo = load(wo_hbm, k.wo)
    load_w = load(w_hbm, k.w_full)

    barrier = pltpu.get_barrier_semaphore()
    greeted = [(s, p) for p in view_peers] + [(p, v) for p in seq_peers] + [(x_s, y_v)]
    for device in greeted:
        pl.semaphore_signal(barrier, inc=1, device_id=device, device_id_type=MESH)

    gain_one = gain_one_ref[...].astype(f3)
    gain_two = gain_two_ref[...].astype(f3)
    unit, _ = norm_stats(tok[...].astype(f3))
    k.normed[at(v * rows, rows), :] = (unit * gain_one).astype(bf)
    per = rows // block
    lane = lax.broadcasted_iota(jnp.int32, (1, 128), 1)
    scenes = jnp.zeros((1, 128), jnp.int32)
    for m in range(per):
        mine = jnp.broadcast_to(ids[:, m * block : m * block + 1], (1, 128))
        scenes = jnp.where(lane == v * per + m, mine, scenes)
    k.ids_all[v] = jnp.broadcast_to(scenes, (8, 128))
    live = jnp.transpose(jnp.broadcast_to(alive[...].astype(f3), (rows, rows)))[:, :1]
    k.mixed_cot[at(own_slot * rows, rows), :] = (live * out_cot[...].astype(f3)).astype(bf)
    pl.semaphore_wait(barrier, len(greeted))

    def view_rows(ref, j):
        return ref.at[at(j * rows, rows)]

    for p in view_peers:
        wires.send(k.ids_all.at[v], k.ids_all.at[v], in_ids + v, (s, p))
    wires.send(view_rows(k.normed, v), view_rows(k.normed, v), in_normed + v, (s, y_v))
    for zt in others_z:
        wires.send(view_rows(k.normed, v), view_rows(k.normed, v), in_normed + v, (s, zt * 2 + y))

    def send_mlp_rows(ref, base):
        for zt in others_z:
            wires.send(ref.at[up_slot], ref.at[up_slot], base + z, (s, zt * 2 + y))

    load_up.wait()
    send_mlp_rows(k.up, in_up)

    for p in view_peers:
        wires.wait(k.ids_all.at[p], in_ids + p)
    count = SLOTS * SCENE_BLOCKS
    scene_row = k.ids_all[0][:1]
    for j in range(1, views):
        scene_row = scene_row + k.ids_all[j][:1]
    big = lax.broadcasted_iota(jnp.int32, (128, 128), 0)
    wide = lax.broadcasted_iota(jnp.int32, (128, 128), 1)
    scene_mat = jnp.broadcast_to(scene_row, (128, 128))
    scene_col = jnp.transpose(scene_mat)
    ahead = (scene_col < scene_mat) | ((scene_col == scene_mat) & (big < wide))
    place = jnp.sum(jnp.where(ahead & (big < count), 1, 0), axis=0, keepdims=True)
    place_col = jnp.transpose(jnp.broadcast_to(place, (128, 128)))
    hit = jnp.where((place_col == wide) & (big < count), big, 0)
    source = jnp.sum(hit, axis=0, keepdims=True)
    k.order_vm[0:8, :] = jnp.broadcast_to(source, (8, 128))
    k.order_vm[8:16, :] = jnp.broadcast_to(place, (8, 128))
    to_scalar = load(k.order_vm, k.order_sm)

    for copy in load_own:
        copy.wait()

    def project(j):
        k.qkv[at(j * rows, rows), :] = dot_nn(k.normed[at(j * rows, rows), :], k.w_own[...]).astype(bf)

    project(v)
    for zt in others_z:
        j = zt * 2 + y
        wires.wait(view_rows(k.normed, j), in_normed + j)
        wires.send(view_rows(k.normed, j), view_rows(k.normed, j), in_normed + j, (s, y_v))
        project(j)
    for zt in [z] + others_z:
        j = zt * 2 + 1 - y
        wires.wait(view_rows(k.normed, j), in_normed + j)
        project(j)
    to_scalar.wait()

    def reorder(dst, src, row):
        blocks = src.reshape(count, block, src.shape[1])

        def step(i, unused):
            from_block = k.order_sm[row, i]
            dst[at(i * block, block), :] = blocks[from_block].astype(dst.dtype)
            return unused

        lax.fori_loop(0, count, step, 0, unroll=8)

    reorder(k.qkv_s, k.qkv, 0)

    head_lane = lax.broadcasted_iota(jnp.int32, (scene, own), 1) // HEAD_DIM

    def attend(g, unused):
        here = at(g * scene, scene)
        queries, keys, values = (k.qkv_s[here, pl.ds(t * own, own)] for t in range(3))
        result = jnp.zeros((scene, own), f3)
        for e in range(2):
            chosen = jnp.where(head_lane == e, queries, jnp.zeros_like(queries))
            weights = jnp.exp(dot_inner(chosen, keys) * scale)
            total = jnp.sum(weights, axis=-1, keepdims=True)
            k.weights[g * 2 + e] = weights
            k.totals[g * 2 + e] = total
            mixed = dot_nn(weights.astype(bf), values) / total
            result = jnp.where(head_lane == e, mixed, result)
        k.att_s[here, :] = result
        return unused

    lax.fori_loop(0, SLOTS, attend, 0)
    reorder(k.att, k.att_s, 8)
    own_cols = at(v * own, own)
    for p in view_peers:
        wires.send(view_rows(k.att, p), k.att_tok.at[:, own_cols], in_att + v, (s, p))
    k.att_tok[:, own_cols] = k.att[at(v * rows, rows), :]

    load_down.wait()
    send_mlp_rows(k.down, in_down)
    mcot_own = at(own_slot * rows, rows)
    for device in group:
        wires.send(k.mixed_cot.at[mcot_own], k.mixed_cot.at[mcot_own], in_mcot + own_slot, device)

    def core_exchange(ref, base):
        for zt in others_z:
            there = at((c * levels + zt) * hidden, hidden)
            wires.wait(ref.at[there], base + zt)
        mine = at(c * half, half)
        wires.send(ref.at[mine], ref.at[mine], base + levels, (c_s, v))

    core_exchange(k.up, in_up)

    load_wo.wait()
    for p in view_peers:
        wires.wait(k.att_tok.at[:, at(p * own, own)], in_att + p)
    tile = 256
    for n in range(width // tile):
        cols = pl.ds(n * tile, tile)
        k.middle[:, cols] = tok[:, cols].astype(f3) + live * dot_nn(k.att_tok[...], k.wo[:, cols])
    unit_two, _ = norm_stats(k.middle[...])
    k.normed_two[mcot_own, :] = (unit_two * gain_two).astype(bf)
    for device in group:
        wires.send(k.normed_two.at[mcot_own], k.normed_two.at[mcot_own], in_two + own_slot, device)

    for slot in group_slot:
        there = at(slot * rows, rows)
        wires.wait(k.mixed_cot.at[there], in_mcot + slot)
    core_exchange(k.down, in_down)
    theirs = at((1 - c) * half, half)
    wires.wait(k.up.at[theirs], in_up + levels)
    wires.wait(k.down.at[theirs], in_down + levels)

    def cot_tile(n, unused):
        k.act_cot[:, at(n * tile, tile)] = dot_inner(k.mixed_cot[...], k.down[at(n * tile, tile), :])
        return unused

    lax.fori_loop(0, mlp_rows // tile, cot_tile, 0)

    def mlp_tile(slot):
        here = at(slot * rows, rows)

        def step(n, unused):
            cols = at(n * tile, tile)
            pre = dot_inner(k.normed_two[here, :], k.up[cols, :])
            below = 0.5 + 0.5 * lax.erf(pre * (0.5**0.5))
            slope = below + pre * (jnp.exp(-0.5 * pre * pre) * (0.5 / math.pi) ** 0.5)
            k.act[here, cols] = (pre * below).astype(bf)
            k.hid_cot[here, cols] = (k.act_cot[here, cols] * slope).astype(bf)
            return unused

        lax.fori_loop(0, mlp_rows // tile, step, 0)

    def part_tiles(which, left, right, slot, dst):
        here = at(slot * rows, rows)

        def step(n, unused):
            cols = at(n * tile, tile)
            dst[:, cols] = dot_nn(left[here, :], right[:, cols]).astype(dst.dtype)
            return unused

        lax.fori_loop(0, width // tile, step, 0)

    mlp_tile(own_slot)
    for i, (slot, device) in enumerate(zip(group_slot, group)):
        wires.wait(k.normed_two.at[at(slot * rows, rows)], in_two + slot)
        mlp_tile(slot)
        part_tiles(0, k.hid_cot, k.up, slot, k.part_out.at[0, i])
        wires.send(k.part_out.at[0, i], k.part_in.at[0, own_slot], in_part[0] + own_slot, device)
    part_tiles(0, k.hid_cot, k.up, own_slot, k.part_own.at[0])

    def grad_tiles(left, right, start, dst):
        def step(n, unused):
            there = at(n * tile, tile)
            dst[there, :] = dot_outer(left[:, at(start + n * tile, tile)], right[...]).astype(dst.dtype)
            return unused

        lax.fori_loop(0, half // tile, step, 0)

    pairs = ((k.act, k.mixed_cot), (k.hid_cot, k.normed_two))
    passed = []
    for which, (left, right) in enumerate(pairs):
        grad_tiles(left, right, (1 - c) * half, k.grad_pass.at[which])
        passed.append(wires.send(k.grad_pass.at[which], k.grad_core.at[which], in_core[which], (c_s, v)))
    for which, (left, right) in enumerate(pairs):
        grad_tiles(left, right, c * half, k.grad_keep.at[which])

    def part_sum(which):
        total = k.part_own[which]
        for slot in group_slot:
            wires.wait(k.part_in.at[which, slot], in_part[which] + slot)
            total = total + k.part_in[which, slot].astype(f3)
        return total

    unit_two, inverse_two = norm_stats(k.middle[...])
    cot_two = part_sum(0)
    k.gain_own[1:2, :] = jnp.sum(cot_two * unit_two, axis=0, keepdims=True)
    middle_cot = out_cot[...].astype(f3) + norm_back(cot_two, unit_two, inverse_two, gain_two)
    tokens_grad[...] = middle_cot
    k.branch[at(v * rows, rows), :] = (live * middle_cot).astype(bf)
    for n in range(width // tile):
        k.acot_tok[:, pl.ds(n * tile, tile)] = dot_inner(
            k.branch[at(v * rows, rows), :], k.wo[pl.ds(n * tile, tile), :]
        ).astype(bf)
    for p in view_peers:
        wires.send(k.acot_tok.at[:, at(p * own, own)], view_rows(k.acot, v), in_acot + v, (s, p))
    k.acot[at(v * rows, rows), :] = k.acot_tok[:, own_cols]
    wires.send(view_rows(k.branch, v), view_rows(k.branch, v), in_branch + v, (s, y_v))
    for zt in others_z:
        wires.send(view_rows(k.branch, v), view_rows(k.branch, v), in_branch + v, (s, zt * 2 + y))

    def grad_level(which, zt):
        there = at(zt * hidden, hidden)
        return k.grad_keep[which, there, :].astype(f3) + k.grad_core[which, there, :].astype(f3)

    for which in range(2):
        wires.wait(k.grad_core.at[which], in_core[which])
        wires.sent(passed[which])
        for zt in others_z:
            k.grad_pass[which, at(zt * hidden, hidden), :] = grad_level(which, zt).astype(bf)

    def send_grads(which):
        for zt in others_z:
            wires.send(
                k.grad_pass.at[which, at(zt * hidden, hidden)],
                k.grad_in.at[which, z],
                in_grad[which] + z,
                (s, zt * 2 + y),
            )

    send_grads(0)

    for i, (slot, device) in enumerate(zip(group_slot, group)):
        part_tiles(1, k.act, k.down, slot, k.part_out.at[1, i])
        wires.send(k.part_out.at[1, i], k.part_in.at[1, own_slot], in_part[1] + own_slot, device)
    part_tiles(1, k.act, k.down, own_slot, k.part_own.at[1])

    for p in view_peers:
        wires.wait(view_rows(k.acot, p), in_acot + p)
    reorder(k.acot_s, k.acot, 0)

    def attend_back(g, unused):
        here = at(g * scene, scene)
        queries, keys, values = (k.qkv_s[here, pl.ds(t * own, own)] for t in range(3))
        cots = k.acot_s[here, :]
        agree = cots.astype(f3) * k.att_s[here, :]
        outs = [jnp.zeros((scene, own), f3) for t in range(3)]
        for e in range(2):
            mine = head_lane == e
            delta = jnp.sum(jnp.where(mine, agree, 0.0), axis=-1, keepdims=True)
            chosen = jnp.where(mine, cots, jnp.zeros_like(cots))
            weights = k.weights[g * 2 + e]
            inverse = 1.0 / k.totals[g * 2 + e]
            weights_cot = dot_inner(chosen, values)
            score_cot = (weights * inverse * (weights_cot - delta)).astype(bf)
            shared = (cots.astype(f3) * inverse).astype(bf)
            new = (
                dot_nn(score_cot, keys) * scale,
                dot_outer(score_cot, queries) * scale,
                dot_outer(weights.astype(bf), shared),
            )
            outs = [jnp.where(mine, fresh, old) for fresh, old in zip(new, outs)]
        for t in range(3):
            k.pc_s[here, pl.ds(t * own, own)] = outs[t].astype(bf)
        return unused

    lax.fori_loop(0, SLOTS, attend_back, 0)

    pc_blocks = k.pc_s.reshape(count, block, 3 * own)

    def unsort(i, unused):
        found = pc_blocks[k.order_sm[8, i]]
        for t in range(3):
            k.pc[t, at(i * block, block), :] = found[:, t * own : (t + 1) * own]
        return unused

    lax.fori_loop(0, count, unsort, 0, unroll=8)
    for p in view_peers:
        wires.send(k.pc.at[:, at(p * rows, rows)], k.pc_tok.at[:, :, own_cols], in_pc + v, (s, p))
    for t in range(3):
        k.pc_tok[t, :, own_cols] = k.pc[t, at(v * rows, rows), :]
    send_grads(1)

    for zt in others_z:
        j = zt * 2 + y
        wires.wait(view_rows(k.branch, j), in_branch + j)
        wires.send(view_rows(k.branch, j), view_rows(k.branch, j), in_branch + j, (s, y_v))

    part = width // seqs
    for i, p in enumerate(seq_peers):
        for t in range(3):
            k.dw_out[i, t] = dot_outer(k.normed[:, at(p * part, part)], k.pc[t]).astype(bf)
        wires.send(k.dw_out.at[i], k.dw_in.at[s], in_dw + s, (p, v))
    for zt in [z] + others_z:
        j = zt * 2 + 1 - y
        wires.wait(view_rows(k.branch, j), in_branch + j)
    for n in range(width // tile):
        cols = pl.ds(n * tile, tile)
        k.do_out[:, cols] = dot_outer(k.att[...], k.branch[:, cols]).astype(bf)
    piece = own // seqs
    for p in seq_peers:
        wires.send(k.do_out.at[at(p * piece, piece)], k.do_in.at[s], in_do + s, (p, v))
    own_part = at(s * part, part)
    own_dw = [dot_outer(k.normed[:, own_part], k.pc[t]) for t in range(3)]
    for p in seq_peers:
        wires.wait(k.dw_in.at[p], in_dw + p)
    for t in range(3):
        total = own_dw[t]
        for p in seq_peers:
            total = total + k.dw_in[p, t].astype(f3)
        k.fin_w[t, own_part, own_cols] = total.astype(bf)
    for p in seq_peers:
        wires.wait(k.do_in.at[p], in_do + p)
    total = k.do_out[at(s * piece, piece), :].astype(f3)
    for p in seq_peers:
        total = total + k.do_in[p].astype(f3)

    def fin_w(q, j):
        return k.fin_w.at[:, at(q * part, part), at(j * own, own)]

    def fin_o(q, j):
        return k.fin_o.at[at(j * own + q * piece, piece)]

    k.fin_o[at(v * own + s * piece, piece), :] = total.astype(bf)

    def pass_on(q, j, device):
        wires.send(fin_w(q, j), fin_w(q, j), in_fw + q * views + j, device)
        wires.send(fin_o(q, j), fin_o(q, j), in_fo + q * views + j, device)

    def arrive(q, j):
        wires.wait(fin_w(q, j), in_fw + q * views + j)
        wires.wait(fin_o(q, j), in_fo + q * views + j)

    pass_on(s, v, (s, y_v))
    for zt in others_z:
        pass_on(s, v, (s, zt * 2 + y))
    pass_on(s, v, (x_s, v))
    pass_on(s, v, (c_s, v))

    load_w.wait()
    for p in view_peers:
        wires.wait(k.pc_tok.at[:, :, at(p * own, own)], in_pc + p)

    def back_tile(n, unused):
        cols = at(n * tile, tile)
        total = dot_inner(k.pc_tok[0], k.w_full[cols, pl.ds(0, width)])
        for t in range(1, 3):
            total = total + dot_inner(k.pc_tok[t], k.w_full[cols, pl.ds(t * width, width)])
        k.part_own[0, :, cols] = total
        return unused

    lax.fori_loop(0, width // tile, back_tile, 0)
    unit_one, inverse_one = norm_stats(tok[...].astype(f3))
    cot_one = k.part_own[0]
    k.gain_own[0:1, :] = jnp.sum(cot_one * unit_one, axis=0, keepdims=True)
    k.gain_own[2:8, :] = jnp.zeros((6, width), f3)
    tokens_grad[...] = tokens_grad[...] + norm_back(cot_one, unit_one, inverse_one, gain_one)
    for p in seq_peers:
        wires.send(k.gain_own, k.gain_in.at[s], in_gain + s, (p, v))

    for zt in others_z:
        j = zt * 2 + y
        arrive(s, j)
        for device in ((s, y_v), (x_s, v), (c_s, v)):
            pass_on(s, j, device)
    for zt in [z] + others_z:
        j = zt * 2 + 1 - y
        arrive(s, j)
        for device in ((x_s, v), (c_s, v)):
            pass_on(s, j, device)

    total = k.gain_own[...]
    for p in seq_peers:
        wires.wait(k.gain_in.at[p], in_gain + p)
        total = total + k.gain_in[p]
    k.gain_sum[...] = total
    for p in view_peers:
        wires.send(k.gain_sum, k.gain_all.at[v], in_gains + v, (s, p))

    layer_out[...] = (k.middle[...] + live * part_sum(1)).astype(bf)
    for which, dst in enumerate((down_grad, up_grad)):
        total = grad_level(which, z)
        for zt in others_z:
            wires.wait(k.grad_in.at[which, zt], in_grad[which] + zt)
            total = total + k.grad_in[which, zt].astype(f3)
        dst[...] = total

    total = k.gain_sum[...]
    for p in view_peers:
        wires.wait(k.gain_all.at[p], in_gains + p)
        total = total + k.gain_all[p]
    gains[...] = total

    for j in [v, y_v] + [p for zt in others_z for p in (zt * 2 + y, zt * 2 + 1 - y)]:
        arrive(x_s, j)
        pass_on(x_s, j, (c_s, v))
    for j in range(views):
        arrive(c_s, j)
        arrive(xc_s, j)
    out_w = pltpu.make_async_copy(k.fin_w, w_grad, k.local_sem.at[LOCALS - 1])
    out_o = pltpu.make_async_copy(k.fin_o, o_grad, k.local_sem.at[LOCALS - 2])
    out_w.start()
    out_o.start()
    wires.drain()
    out_w.wait()
    out_o.wait()


def fused(
    seqs,
    views,
    tokens,
    scene_ids,
    live_mask,
    out_grad,
    attention_gain,
    input_weight,
    output_weight,
    feedforward_gain,
    up_weight,
    down_weight,
):
    rows, width = tokens.shape[1:]
    hidden = up_weight.shape[0]
    spec = scratch_of(rows, width, seqs, views, hidden)
    vmem = pl.BlockSpec(memory_space=pltpu.VMEM)
    anywhere = pl.BlockSpec(memory_space=pl.ANY)
    shape = jax.ShapeDtypeStruct
    bf, f3 = jnp.bfloat16, jnp.float32
    layer_out, tokens_grad, gains, w_grad, o_grad, up_grad, down_grad = pl.pallas_call(
        functools.partial(layer_kernel, tuple(spec), seqs, views),
        out_shape=(
            shape((rows, width), bf),
            shape((rows, width), f3),
            shape((8, width), f3),
            shape((3, width, width), bf),
            shape((width, width), bf),
            shape((hidden, width), f3),
            shape((hidden, width), f3),
        ),
        in_specs=[vmem] * 6 + [anywhere] * 4,
        out_specs=(vmem, vmem, vmem, anywhere, anywhere, vmem, vmem),
        scratch_shapes=list(spec.values()),
        compiler_params=pltpu.CompilerParams(
            collective_id=0, has_side_effects=True, vmem_limit_bytes=67043328
        ),
        name="layer",
    )(
        tokens[0],
        scene_ids,
        live_mask,
        out_grad[0],
        attention_gain[None],
        feedforward_gain[None],
        input_weight,
        output_weight,
        up_weight,
        down_weight,
    )
    wide = jnp.concatenate([w_grad[t].astype(f3) for t in range(3)], axis=1)
    return (
        layer_out[None],
        tokens_grad[None],
        gains[0],
        wide,
        o_grad.astype(f3),
        gains[1],
        up_grad,
        down_grad,
    )


def solution(mesh):
    seqs, views = mesh.shape["seq"], mesh.shape["view"]
    small = seqs == 4 and views % 2 == 0 and HEADS == 2 * views
    body = functools.partial(fused, seqs, views) if small else shards
    return jax.shard_map(
        body,
        mesh=mesh,
        in_specs=(
            P("seq", "view", None),
            P("seq", "view"),
            P("seq", "view"),
            P("seq", "view", None),
            P(),
            P(),
            P(),
            P(),
            P(("seq", "view"), None),
            P(("seq", "view"), None),
        ),
        out_specs=(
            P("seq", "view", None),
            P("seq", "view", None),
            P(),
            P(),
            P(),
            P(),
            P(("seq", "view"), None),
            P(("seq", "view"), None),
        ),
        check_vma=False,
    )
```

```python
import functools
import math
import types

import jax
import jax.numpy as jnp
from jax import lax
from jax.experimental import pallas as pl
from jax.experimental.pallas import tpu as pltpu
from jax.sharding import PartitionSpec as P

HEADS = 16
HEAD_DIM = 64


EPS = 1e-05
NEGATIVE = -1e30
MESH = pl.DeviceIdType.MESH
SLOTS = 4
SCENE_BLOCKS = 16


def layer_norm(values, gain):
    center = values - jnp.mean(values, axis=-1, keepdims=True)
    spread = jnp.mean(center * center, axis=-1, keepdims=True)
    return center * lax.rsqrt(spread + EPS) * gain


def gelu_exact(values):
    return jax.nn.gelu(values, approximate=False)


def plain_dot(left, right):
    return jnp.dot(left, right, preferred_element_type=jnp.float32)


def dot_inner(left, right):
    return lax.dot_general(
        left, right, (((1,), (1,)), ((), ())), preferred_element_type=jnp.float32
    )


def dot_outer(left, right):
    return lax.dot_general(
        left, right, (((0,), (0,)), ((), ())), preferred_element_type=jnp.float32
    )


def split_heads(values):
    return values.reshape(values.shape[0], HEADS, HEAD_DIM)


def masked_scores(queries, keys, query_tags, key_tags, scale):
    raw = jnp.einsum("qhe,khe->hqk", queries, keys, preferred_element_type=jnp.float32) * scale
    allowed = (query_tags[:, None] == key_tags[None, :])[None]
    return (raw, allowed)


def probabilities(queries, keys, query_tags, key_tags, log_total, scale):
    raw, allowed = masked_scores(queries, keys, query_tags, key_tags, scale)
    return jnp.where(
        allowed, jnp.exp(jnp.where(allowed, raw - log_total[:, :, None], NEGATIVE)), 0.0
    )


def in_blocks(step, carry, piece):
    count = piece[0].shape[0]
    size = math.gcd(count, 512)
    number = count // size
    stacked = tuple((member.reshape((number, size) + member.shape[1:]) for member in piece))

    def inner(state, item):
        members, offset = item
        return (step(state, members, offset * size), None)

    result, unused = lax.scan(inner, carry, (stacked, jnp.arange(number, dtype=jnp.int32)))
    return result


def shards(
    tokens,
    scene_ids,
    live_mask,
    out_grad,
    attention_gain,
    input_weight,
    output_weight,
    feedforward_gain,
    up_weight,
    down_weight,
):
    scale = HEAD_DIM ** (-0.5)
    inputs = tokens[0].astype(jnp.float32)
    rows = inputs.shape[0]
    width = inputs.shape[1]
    tags = scene_ids[0] * 2 + live_mask[0]
    live = live_mask[0].astype(jnp.float32)[:, None]
    every_tag = lax.all_gather(tags, "view", axis=0, tiled=True)
    up_full, down_full = (
        lax.all_gather(up_weight, ("seq", "view"), axis=0, tiled=True),
        lax.all_gather(down_weight, ("seq", "view"), axis=0, tiled=True),
    )
    gain_one = attention_gain.astype(jnp.float32)
    gain_two = feedforward_gain.astype(jnp.float32)
    normed = layer_norm(inputs, gain_one).astype(jnp.bfloat16)
    projected = plain_dot(normed, input_weight).astype(jnp.bfloat16)
    query_flat = projected[:, :width]
    queries = split_heads(query_flat)
    keys_own = projected[:, width : 2 * width]
    values_own = projected[:, 2 * width :]

    def attend_step(carry, piece, start):
        peak, total, accum = carry
        key_piece, value_piece = piece
        count = key_piece.shape[0]
        key_tags = lax.dynamic_slice_in_dim(every_tag, start, count)
        raw, allowed = masked_scores(queries, split_heads(key_piece), tags, key_tags, scale)
        masked = jnp.where(allowed, raw, NEGATIVE)
        new_peak = jnp.maximum(peak, jnp.max(masked, axis=-1))
        weights = jnp.where(allowed, jnp.exp(masked - new_peak[:, :, None]), 0.0)
        factor = jnp.exp(peak - new_peak)
        total = total * factor + jnp.sum(weights, axis=-1)
        update = jnp.einsum(
            "hqk,khe->qhe",
            weights.astype(jnp.bfloat16),
            split_heads(value_piece),
            preferred_element_type=jnp.float32,
        )
        accum = accum * jnp.transpose(factor)[:, :, None] + update
        return (new_peak, total, accum)

    start_state = (
        jnp.full((HEADS, rows), NEGATIVE, jnp.float32),
        jnp.zeros((HEADS, rows), jnp.float32),
        jnp.zeros((rows, HEADS, HEAD_DIM), jnp.float32),
    )
    peak, total, accum = in_blocks(
        attend_step,
        start_state,
        (
            lax.all_gather(keys_own, "view", axis=0, tiled=True),
            lax.all_gather(values_own, "view", axis=0, tiled=True),
        ),
    )
    attended_heads = accum / jnp.transpose(total)[:, :, None]
    log_total = peak + jnp.log(total)
    attended_low = attended_heads.reshape(rows, width).astype(jnp.bfloat16)
    branch = plain_dot(attended_low, output_weight)
    middle = inputs + live * branch
    normed_two = layer_norm(middle, gain_two).astype(jnp.bfloat16)
    hidden = dot_inner(normed_two, up_full)
    activated = gelu_exact(hidden).astype(jnp.bfloat16)
    mixed = plain_dot(activated, down_full)
    layer_out = (middle + live * mixed).astype(jnp.bfloat16)[None]
    out_cot = out_grad[0].astype(jnp.float32)
    mixed_cot = (live * out_cot).astype(jnp.bfloat16)
    down_grad = dot_outer(activated, mixed_cot)
    activated_cot = dot_inner(mixed_cot, down_full)
    hidden_cot = jax.vjp(gelu_exact, hidden)[1](activated_cot)[0].astype(jnp.bfloat16)
    up_grad = dot_outer(hidden_cot, normed_two)
    normed_two_cot = plain_dot(hidden_cot, up_full)
    second_pull = jax.vjp(layer_norm, middle, gain_two)[1]
    middle_part, gain_two_grad = second_pull(normed_two_cot)
    middle_cot = out_cot + middle_part
    branch_cot = (live * middle_cot).astype(jnp.bfloat16)
    output_weight_grad = dot_outer(attended_low, branch_cot)
    attended_cot = dot_inner(branch_cot, output_weight).astype(jnp.bfloat16)
    cot_heads = split_heads(attended_cot)
    delta = jnp.transpose(jnp.sum(cot_heads.astype(jnp.float32) * attended_heads, axis=-1))
    seq_len = every_tag.shape[0]

    def back_step(carry, piece, start):
        query_cot, key_value_cot = carry
        key_piece, value_piece = piece
        count = key_piece.shape[0]
        key_tags = lax.dynamic_slice_in_dim(every_tag, start, count)
        key_heads = split_heads(key_piece)
        value_heads = split_heads(value_piece)
        probs = probabilities(queries, key_heads, tags, key_tags, log_total, scale)
        prob_cot = jnp.einsum(
            "qhe,khe->hqk", cot_heads, value_heads, preferred_element_type=jnp.float32
        )
        score_cot = (probs * (prob_cot - delta[:, :, None])).astype(jnp.bfloat16)
        query_cot = (
            query_cot
            + jnp.einsum("hqk,khe->qhe", score_cot, key_heads, preferred_element_type=jnp.float32)
            * scale
        )
        key_cot = (
            jnp.einsum("hqk,qhe->khe", score_cot, queries, preferred_element_type=jnp.float32)
            * scale
        )
        value_cot = jnp.einsum(
            "hqk,qhe->khe",
            probs.astype(jnp.bfloat16),
            cot_heads,
            preferred_element_type=jnp.float32,
        )
        stacked = jnp.concatenate(
            [key_cot.reshape(count, width), value_cot.reshape(count, width)], axis=1
        )
        earlier = lax.dynamic_slice_in_dim(key_value_cot, start, count)
        key_value_cot = lax.dynamic_update_slice_in_dim(key_value_cot, earlier + stacked, start, 0)
        return (query_cot, key_value_cot)

    back_state = (
        jnp.zeros((rows, HEADS, HEAD_DIM), jnp.float32),
        jnp.zeros((seq_len, 2 * width), jnp.float32),
    )
    query_cot, key_value_cot = in_blocks(
        back_step,
        back_state,
        (
            lax.all_gather(keys_own, "view", axis=0, tiled=True),
            lax.all_gather(values_own, "view", axis=0, tiled=True),
        ),
    )
    own_cot = lax.psum_scatter(key_value_cot, "view", scatter_dimension=0, tiled=True)
    key_cot_own = own_cot[:, :width]
    value_cot_own = own_cot[:, width:]
    projected_cot = jnp.concatenate(
        [query_cot.reshape(rows, width), key_cot_own, value_cot_own], axis=1
    ).astype(jnp.bfloat16)
    input_weight_grad = dot_outer(normed, projected_cot)
    normed_cot = dot_inner(projected_cot, input_weight)
    first_pull = jax.vjp(layer_norm, inputs, gain_one)[1]
    input_part, gain_one_grad = first_pull(normed_cot)
    tokens_grad = (middle_cot + input_part)[None]
    up_part, down_part = (
        lax.psum_scatter(up_grad, ("seq", "view"), scatter_dimension=0, tiled=True),
        lax.psum_scatter(down_grad, ("seq", "view"), scatter_dimension=0, tiled=True),
    )
    summed = lax.psum(
        (gain_one_grad, input_weight_grad, output_weight_grad, gain_two_grad), ("seq", "view")
    )
    return (layer_out, tokens_grad, summed[0], summed[1], summed[2], summed[3], up_part, down_part)


def dot_nn(left, right):
    return lax.dot_general(left, right, (((1,), (0,)), ((), ())), preferred_element_type=jnp.float32)


def at(start, size):
    return pl.ds(pl.multiple_of(start, size), size)


def norm_stats(values):
    mean = jnp.mean(values, axis=-1, keepdims=True)
    center = values - mean
    spread = jnp.mean(center * center, axis=-1, keepdims=True)
    inverse = lax.rsqrt(spread + EPS)
    return center * inverse, inverse


def norm_back(cot, unit, inverse, gain):
    scaled = cot * gain
    first = jnp.mean(scaled, axis=-1, keepdims=True)
    second = jnp.mean(scaled * unit, axis=-1, keepdims=True)
    return inverse * (scaled - first - unit * second)


class Wires:
    def __init__(self, send_sem, recv_sem, peer):
        self.send_sem, self.recv_sem, self.peer = send_sem, recv_sem, peer
        self.sends, self.recvs, self.pending = 0, 0, []

    def inbox(self, count):
        base = self.recvs
        self.recvs += count
        return base

    def send(self, src, dst, slot, device, when=None):
        copy = pltpu.make_async_remote_copy(
            src_ref=src,
            dst_ref=dst,
            send_sem=self.send_sem.at[self.sends],
            recv_sem=self.recv_sem.at[slot],
            device_id=device,
            device_id_type=MESH,
        )
        self.sends += 1
        if when is None:
            copy.start()
        else:
            pl.when(when)(copy.start)
        self.pending.append((copy, when))
        return copy

    def sent(self, copy):
        copy.wait_send()
        self.pending = [entry for entry in self.pending if entry[0] is not copy]

    def wait(self, dst, slot):
        pltpu.make_async_remote_copy(
            src_ref=dst,
            dst_ref=dst,
            send_sem=self.send_sem.at[0],
            recv_sem=self.recv_sem.at[slot],
            device_id=self.peer,
            device_id_type=MESH,
        ).wait_recv()

    def drain(self):
        for copy, when in self.pending:
            if when is None:
                copy.wait_send()
            else:
                pl.when(when)(copy.wait_send)


SENDS, RECVS, LOCALS = 256, 256, 24
LEVELS = 4


def scratch_of(rows, width, seqs, views, hidden):
    length = rows * views
    own = width // views
    bf, f3 = jnp.bfloat16, jnp.float32
    vm = pltpu.VMEM
    mlp_rows = hidden * seqs * views // 4
    half, quarter, eighth = width // 2, width // 4, width // 8
    return dict(
        w_full=vm((width, 3 * width), bf),
        w_own=vm((width, 3 * own), bf),
        wo=vm((width, width), bf),
        up=vm((mlp_rows, width), bf),
        down=vm((mlp_rows, width), bf),
        ids_all=vm((views, 8, 128), jnp.int32),
        order_vm=vm((16, 128), jnp.int32),
        order_sm=pltpu.SMEM((16, 128), jnp.int32),
        normed=vm((length, width), bf),
        qkv=vm((length, 3 * own), bf),
        qkv_s=vm((length, 3 * own), bf),
        weights=vm((2 * SLOTS, length // SLOTS, length // SLOTS), f3),
        totals=vm((2 * SLOTS, length // SLOTS, 1), f3),
        att_s=vm((length, own), f3),
        att=vm((length, own), bf),
        att_tok=vm((rows, width), bf),
        middle=vm((rows, width), f3),
        normed_two=vm((4 * rows, width), bf),
        mixed_cot=vm((4 * rows, width), bf),
        slope=vm((4 * rows, mlp_rows), f3),
        act=vm((4 * rows, mlp_rows), bf),
        hid_cot=vm((4 * rows, mlp_rows), bf),
        part_own=vm((2, rows, width), f3),
        part_out=vm((2, 3, rows, width), bf),
        part_in=vm((2, 4, rows, width), bf),
        grad_keep=vm((2, mlp_rows // 2, width), bf),
        grad_pass=vm((2, mlp_rows // 2, width), bf),
        grad_core=vm((2, mlp_rows // 2, width), bf),
        grad_in=vm((2, LEVELS + 1, hidden, width), bf),
        branch=vm((rows, width), bf),
        acot_tok=vm((rows, width), bf),
        acot=vm((length, own), bf),
        acot_s=vm((length, own), bf),
        pc_s=vm((length, 3 * own), bf),
        pc=vm((3, length, own), bf),
        pc_tok=vm((3, rows, width), bf),
        dw_out=vm((3, 3, width // seqs, own), bf),
        dw_in=vm((4, 3, width // seqs, own), bf),
        dw_own=vm((3, width // seqs, own), bf),
        do_keep=vm((half, width), f3),
        do_core=vm((half, width), bf),
        do_core_in=vm((half, width), bf),
        do_y=vm((quarter, width), bf),
        do_y_in=vm((quarter, width), bf),
        do_x=vm((eighth, width), bf),
        do_x_in=vm((eighth, width), bf),
        do_z=vm((eighth, width), bf),
        do_z_in=vm((LEVELS, eighth // LEVELS, width), bf),
        do_own=vm((eighth // LEVELS, width), bf),
        gain_own=vm((8, width), f3),
        gain_in=vm((seqs, 8, width), f3),
        gain_sum=vm((8, width), f3),
        gain_all=vm((views, 8, width), f3),
        send_sem=pltpu.SemaphoreType.DMA((SENDS,)),
        recv_sem=pltpu.SemaphoreType.DMA((RECVS,)),
        local_sem=pltpu.SemaphoreType.DMA((LOCALS,)),
    )


def layer_kernel(names, seqs, views, *refs):
    (tok, ids, alive, out_cot, gain_one_ref, gain_two_ref, w_hbm, wo_hbm, up_hbm, down_hbm) = refs[:10]
    (layer_out, tokens_grad, gains, w_grad, o_grad, up_grad, down_grad) = refs[10:17]
    k = types.SimpleNamespace(**dict(zip(names, refs[17:])))
    rows, width = tok.shape
    length = rows * views
    own = width // views
    hidden = up_hbm.shape[0]
    mlp_rows = k.up.shape[0]
    half = mlp_rows // 2
    block = length // (SLOTS * SCENE_BLOCKS)
    scene = length // SLOTS
    scale = HEAD_DIM ** (-0.5)
    bf, f3 = jnp.bfloat16, jnp.float32

    s = lax.axis_index("seq")
    v = lax.axis_index("view")
    x, c, z, y = s // 2, s % 2, v // 2, v % 2
    x_s, c_s, xc_s = (1 - x) * 2 + c, x * 2 + (1 - c), (1 - x) * 2 + (1 - c)
    y_v = z * 2 + (1 - y)
    z_pair, z_two, z_flip = z + 1 - 2 * (z % 2), lax.rem(z + 2, LEVELS), LEVELS - 1 - z
    inner = (z == 1) | (z == 2)
    outer = (z == 0) | (z == 3)
    others_z = [z_pair, z_two, z_flip]
    group = [(x_s, v), (s, y_v), (x_s, y_v)]
    group_slot = [(1 - x) * 2 + y, x * 2 + (1 - y), (1 - x) * 2 + (1 - y)]
    own_slot = x * 2 + y
    view_peers = [lax.rem(v + d, views) for d in range(1, views)]
    seq_peers = [x_s, xc_s, c_s]

    def level(zt):
        return (s, zt * 2 + y)

    wires = Wires(k.send_sem, k.recv_sem, (c_s, v))
    in_normed = wires.inbox(views)
    in_ids = wires.inbox(views)
    in_up = wires.inbox(LEVELS + 1)
    in_down = wires.inbox(LEVELS + 1)
    in_mcot = wires.inbox(4)
    in_att = wires.inbox(views)
    in_two = wires.inbox(4)
    in_part = [wires.inbox(4), wires.inbox(4)]
    in_core = [wires.inbox(1), wires.inbox(1)]
    in_grad = [wires.inbox(LEVELS + 1), wires.inbox(LEVELS + 1)]
    in_acot = wires.inbox(views)
    in_pc = wires.inbox(views)
    in_dw = wires.inbox(seqs)
    in_do = wires.inbox(3)
    in_do_z = wires.inbox(LEVELS)
    in_plane = wires.inbox(views)
    in_query = wires.inbox(views)
    in_cross = wires.inbox(views)
    in_mate = [wires.inbox(views) for unused in range(3)]
    in_out = wires.inbox(seqs * views)
    in_gain = wires.inbox(seqs)
    in_gains = wires.inbox(views)

    def z_cast(src, dst, slot):
        wires.send(src, dst, slot, level(z_pair))
        wires.send(src, dst, slot, level(z_two))
        wires.send(src, dst, slot, level(z_flip), when=inner)

    def z_relay(ref, slot):
        wires.send(ref, ref, slot, level(z_pair), when=inner)

    loads = []

    def load(src, dst):
        copy = pltpu.make_async_copy(src, dst, k.local_sem.at[len(loads)])
        copy.start()
        loads.append(copy)
        return copy

    up_slot = at((c * LEVELS + z) * hidden, hidden)
    load_up = load(up_hbm, k.up.at[up_slot])
    load_down = load(down_hbm, k.down.at[up_slot])
    load_own = [
        load(w_hbm.at[:, at(t * width + v * own, own)], k.w_own.at[:, pl.ds(t * own, own)])
        for t in range(3)
    ]
    load_wo = load(wo_hbm, k.wo)
    load_w = load(w_hbm, k.w_full)

    barrier = pltpu.get_barrier_semaphore()
    greeted = [(s, p) for p in view_peers] + [(p, v) for p in seq_peers] + [(x_s, y_v)]
    for device in greeted:
        pl.semaphore_signal(barrier, inc=1, device_id=device, device_id_type=MESH)

    gain_one = gain_one_ref[...].astype(f3).reshape(1, width)
    gain_two = gain_two_ref[...].astype(f3).reshape(1, width)
    unit, _ = norm_stats(tok[...].astype(f3))
    k.normed[at(v * rows, rows), :] = (unit * gain_one).astype(bf)
    per = rows // block
    lane = lax.broadcasted_iota(jnp.int32, (1, 128), 1)
    scenes = jnp.zeros((1, 128), jnp.int32)
    for m in range(per):
        mine = jnp.broadcast_to(ids[:, m * block : m * block + 1], (1, 128))
        scenes = jnp.where(lane == v * per + m, mine, scenes)
    k.ids_all[v] = jnp.broadcast_to(scenes, (8, 128))
    live = jnp.transpose(jnp.broadcast_to(alive[...].astype(f3), (rows, rows)))[:, :1]
    k.mixed_cot[at(own_slot * rows, rows), :] = (live * out_cot[...].astype(f3)).astype(bf)
    pl.semaphore_wait(barrier, len(greeted))

    def view_rows(ref, j):
        return ref.at[at(j * rows, rows)]

    for p in view_peers:
        wires.send(k.ids_all.at[v], k.ids_all.at[v], in_ids + v, (s, p))
    mine = view_rows(k.normed, v)
    wires.send(mine, mine, in_normed + v, (s, y_v))
    z_cast(mine, mine, in_normed + v)
    load_up.wait()
    z_cast(k.up.at[up_slot], k.up.at[up_slot], in_up + z)

    for p in view_peers:
        wires.wait(k.ids_all.at[p], in_ids + p)
    count = SLOTS * SCENE_BLOCKS
    scene_row = k.ids_all[0][:1]
    for j in range(1, views):
        scene_row = scene_row + k.ids_all[j][:1]
    big = lax.broadcasted_iota(jnp.int32, (128, 128), 0)
    wide = lax.broadcasted_iota(jnp.int32, (128, 128), 1)
    scene_mat = jnp.broadcast_to(scene_row, (128, 128))
    scene_col = jnp.transpose(scene_mat)
    ahead = (scene_col < scene_mat) | ((scene_col == scene_mat) & (big < wide))
    place = jnp.sum(jnp.where(ahead & (big < count), 1, 0), axis=0, keepdims=True)
    place_col = jnp.transpose(jnp.broadcast_to(place, (128, 128)))
    hit = jnp.where((place_col == wide) & (big < count), big, 0)
    source = jnp.sum(hit, axis=0, keepdims=True)
    k.order_vm[0:8, :] = jnp.broadcast_to(source, (8, 128))
    k.order_vm[8:16, :] = jnp.broadcast_to(place, (8, 128))
    to_scalar = load(k.order_vm, k.order_sm)

    for copy in load_own:
        copy.wait()

    def project(j):
        k.qkv[at(j * rows, rows), :] = dot_nn(k.normed[at(j * rows, rows), :], k.w_own[...]).astype(bf)

    project(v)
    for zt in others_z:
        j = zt * 2 + y
        there = view_rows(k.normed, j)
        wires.wait(there, in_normed + j)
        if zt is z_two:
            z_relay(there, in_normed + j)
        wires.send(there, there, in_normed + j, (s, y_v))
        project(j)
    for zt in [z] + others_z:
        j = zt * 2 + 1 - y
        wires.wait(view_rows(k.normed, j), in_normed + j)
        project(j)
    to_scalar.wait()

    def reorder(dst, src, row):
        blocks = src.reshape(count, block, src.shape[1])

        def step(i, unused):
            from_block = k.order_sm[row, i]
            dst[at(i * block, block), :] = blocks[from_block].astype(dst.dtype)
            return unused

        lax.fori_loop(0, count, step, 0, unroll=8)

    reorder(k.qkv_s, k.qkv, 0)

    head_lane = lax.broadcasted_iota(jnp.int32, (scene, own), 1) // HEAD_DIM

    def attend(g, unused):
        here = at(g * scene, scene)
        queries, keys, values = (k.qkv_s[here, pl.ds(t * own, own)] for t in range(3))
        result = jnp.zeros((scene, own), f3)
        for e in range(2):
            chosen = jnp.where(head_lane == e, queries, jnp.zeros_like(queries))
            weights = jnp.exp(dot_inner(chosen, keys) * scale)
            total = jnp.sum(weights, axis=-1, keepdims=True)
            k.weights[g * 2 + e] = weights
            k.totals[g * 2 + e] = total
            mixed = dot_nn(weights.astype(bf), values) / total
            result = jnp.where(head_lane == e, mixed, result)
        k.att_s[here, :] = result
        return unused

    lax.fori_loop(0, SLOTS, attend, 0)
    reorder(k.att, k.att_s, 8)
    own_cols = at(v * own, own)
    for p in view_peers:
        wires.send(view_rows(k.att, p), k.att_tok.at[:, own_cols], in_att + v, (s, p))
    k.att_tok[:, own_cols] = k.att[at(v * rows, rows), :]

    def mlp_slot(ref, zt):
        return ref.at[at((c * LEVELS + zt) * hidden, hidden)]

    def mlp_relay(ref, base):
        wires.wait(mlp_slot(ref, z_two), base + z_two)
        z_relay(mlp_slot(ref, z_two), base + z_two)

    def core_exchange(ref, base):
        for zt in (z_pair, z_flip):
            wires.wait(mlp_slot(ref, zt), base + zt)
        mine = ref.at[at(c * half, half)]
        wires.send(mine, mine, base + LEVELS, (c_s, v))

    mlp_relay(k.up, in_up)
    load_down.wait()
    z_cast(k.down.at[up_slot], k.down.at[up_slot], in_down + z)
    mcot_own = at(own_slot * rows, rows)
    for device in group:
        wires.send(k.mixed_cot.at[mcot_own], k.mixed_cot.at[mcot_own], in_mcot + own_slot, device)

    load_wo.wait()
    for p in view_peers:
        wires.wait(k.att_tok.at[:, at(p * own, own)], in_att + p)
    tile = 256
    for n in range(width // tile):
        cols = pl.ds(n * tile, tile)
        k.middle[:, cols] = tok[:, cols].astype(f3) + live * dot_nn(k.att_tok[...], k.wo[:, cols])
    unit_two, _ = norm_stats(k.middle[...])
    k.normed_two[mcot_own, :] = (unit_two * gain_two).astype(bf)
    for device in group:
        wires.send(k.normed_two.at[mcot_own], k.normed_two.at[mcot_own], in_two + own_slot, device)

    core_exchange(k.up, in_up)
    wires.wait(k.up.at[at((1 - c) * half, half)], in_up + LEVELS)

    def hidden_tiles(slot):
        here = at(slot * rows, rows)

        def step(n, unused):
            cols = at(n * tile, tile)
            pre = dot_inner(k.normed_two[here, :], k.up[cols, :])
            below = 0.5 + 0.5 * lax.erf(pre * (0.5**0.5))
            k.act[here, cols] = (pre * below).astype(bf)
            k.slope[here, cols] = below + pre * (jnp.exp(-0.5 * pre * pre) * (0.5 / math.pi) ** 0.5)
            return unused

        lax.fori_loop(0, mlp_rows // tile, step, 0)

    hidden_tiles(own_slot)
    mlp_relay(k.down, in_down)
    for slot in group_slot:
        wires.wait(k.normed_two.at[at(slot * rows, rows)], in_two + slot)
        hidden_tiles(slot)

    core_exchange(k.down, in_down)
    wires.wait(k.down.at[at((1 - c) * half, half)], in_down + LEVELS)
    for slot in group_slot:
        wires.wait(k.mixed_cot.at[at(slot * rows, rows)], in_mcot + slot)

    def cot_tiles(slot):
        here = at(slot * rows, rows)

        def step(n, unused):
            cols = at(n * tile, tile)
            up_to = dot_inner(k.mixed_cot[here, :], k.down[cols, :])
            k.hid_cot[here, cols] = (up_to * k.slope[here, cols]).astype(bf)
            return unused

        lax.fori_loop(0, mlp_rows // tile, step, 0)

    def part_tiles(left, right, slot, dst):
        here = at(slot * rows, rows)

        def step(n, unused):
            cols = at(n * tile, tile)
            dst[:, cols] = dot_nn(left[here, :], right[:, cols]).astype(dst.dtype)
            return unused

        lax.fori_loop(0, width // tile, step, 0)

    for i in (2, 0, 1):
        cot_tiles(group_slot[i])
        part_tiles(k.hid_cot, k.up, group_slot[i], k.part_out.at[0, i])
        wires.send(k.part_out.at[0, i], k.part_in.at[0, own_slot], in_part[0] + own_slot, group[i])
    cot_tiles(own_slot)
    part_tiles(k.hid_cot, k.up, own_slot, k.part_own.at[0])

    def grad_tiles(left, right, start, dst):
        def step(n, unused):
            there = at(n * tile, tile)
            dst[there, :] = dot_outer(left[:, at(start + n * tile, tile)], right[...]).astype(dst.dtype)
            return unused

        lax.fori_loop(0, half // tile, step, 0)

    pairs = ((k.act, k.mixed_cot), (k.hid_cot, k.normed_two))
    passed = []
    for which, (left, right) in enumerate(pairs):
        grad_tiles(left, right, (1 - c) * half, k.grad_pass.at[which])
        passed.append(wires.send(k.grad_pass.at[which], k.grad_core.at[which], in_core[which], (c_s, v)))
        grad_tiles(left, right, c * half, k.grad_keep.at[which])

    def grad_level(which, zt):
        there = at(zt * hidden, hidden)
        return k.grad_keep[which, there, :].astype(f3) + k.grad_core[which, there, :].astype(f3)

    def grad_piece(which, zt):
        return k.grad_pass.at[which, at(zt * hidden, hidden)]

    def add_cores(which):
        wires.wait(k.grad_core.at[which], in_core[which])
        wires.sent(passed[which])
        for zt in others_z:
            k.grad_pass[which, at(zt * hidden, hidden), :] = grad_level(which, zt).astype(bf)

    def send_near(which):
        wires.send(grad_piece(which, z_pair), k.grad_in.at[which, z], in_grad[which] + z, level(z_pair))

    def send_far(which):
        via = LEVELS
        wires.send(grad_piece(which, z_two), k.grad_in.at[which, z], in_grad[which] + z, level(z_two), when=outer)
        wires.send(grad_piece(which, z_flip), k.grad_in.at[which, via], in_grad[which] + via, level(z_pair), when=outer)
        wires.send(grad_piece(which, z_flip), k.grad_in.at[which, z], in_grad[which] + z, level(z_flip), when=inner)

    def send_joined(which):
        @pl.when(inner)
        def _():
            wires.wait(k.grad_in.at[which, LEVELS], in_grad[which] + LEVELS)
            there = at(z_two * hidden, hidden)
            joined = k.grad_pass[which, there, :].astype(f3) + k.grad_in[which, LEVELS].astype(f3)
            k.grad_pass[which, there, :] = joined.astype(bf)

        wires.send(grad_piece(which, z_two), k.grad_in.at[which, z], in_grad[which] + z, level(z_two), when=inner)

    def collect(which, dst):
        total = grad_level(which, z)
        for zt in (z_pair, z_two):
            wires.wait(k.grad_in.at[which, zt], in_grad[which] + zt)
            total = total + k.grad_in[which, zt].astype(f3)
        dst[...] = total

        @pl.when(inner)
        def _():
            wires.wait(k.grad_in.at[which, z_flip], in_grad[which] + z_flip)
            dst[...] = dst[...] + k.grad_in[which, z_flip].astype(f3)

    add_cores(0)
    send_near(0)

    def part_sum(which):
        total = k.part_own[which]
        for slot in group_slot:
            wires.wait(k.part_in.at[which, slot], in_part[which] + slot)
            total = total + k.part_in[which, slot].astype(f3)
        return total

    unit_two, inverse_two = norm_stats(k.middle[...])
    cot_two = part_sum(0)
    k.gain_own[1:2, :] = jnp.sum(cot_two * unit_two, axis=0, keepdims=True)
    middle_cot = out_cot[...].astype(f3) + norm_back(cot_two, unit_two, inverse_two, gain_two)
    tokens_grad[...] = middle_cot
    k.branch[...] = (live * middle_cot).astype(bf)
    for n in range(width // tile):
        k.acot_tok[:, pl.ds(n * tile, tile)] = dot_inner(
            k.branch[...], k.wo[pl.ds(n * tile, tile), :]
        ).astype(bf)
    for p in view_peers:
        wires.send(k.acot_tok.at[:, at(p * own, own)], view_rows(k.acot, v), in_acot + v, (s, p))
    k.acot[at(v * rows, rows), :] = k.acot_tok[:, own_cols]
    send_far(0)

    o_half, o_quarter, o_eighth = width // 2, width // 4, width // 8
    o_piece = o_eighth // LEVELS

    def outer_rows(start, dst, dtype):
        def step(n, unused):
            there = at(n * tile, tile)
            left = k.att_tok[:, at(start + n * tile, tile)]
            dst[there, :] = dot_outer(left, k.branch[...]).astype(dtype)
            return unused

        lax.fori_loop(0, o_half // tile, step, 0)

    outer_rows((1 - c) * o_half, k.do_core, bf)
    wires.send(k.do_core, k.do_core_in, in_do, (c_s, v))
    outer_rows(c * o_half, k.do_keep, f3)
    for i in (2, 0, 1):
        part_tiles(k.act, k.down, group_slot[i], k.part_out.at[1, i])
        wires.send(k.part_out.at[1, i], k.part_in.at[1, own_slot], in_part[1] + own_slot, group[i])
    part_tiles(k.act, k.down, own_slot, k.part_own.at[1])
    wires.wait(k.do_core_in, in_do)
    k.do_keep[...] = k.do_keep[...] + k.do_core_in[...].astype(f3)
    k.do_y[...] = k.do_keep[at((1 - y) * o_quarter, o_quarter), :].astype(bf)
    wires.send(k.do_y, k.do_y_in, in_do + 1, (s, y_v))

    for p in view_peers:
        wires.wait(view_rows(k.acot, p), in_acot + p)
    reorder(k.acot_s, k.acot, 0)

    def attend_back(g, unused):
        here = at(g * scene, scene)
        queries, keys, values = (k.qkv_s[here, pl.ds(t * own, own)] for t in range(3))
        cots = k.acot_s[here, :]
        agree = cots.astype(f3) * k.att_s[here, :]
        outs = [jnp.zeros((scene, own), f3) for t in range(3)]
        for e in range(2):
            mine = head_lane == e
            delta = jnp.sum(jnp.where(mine, agree, 0.0), axis=-1, keepdims=True)
            chosen = jnp.where(mine, cots, jnp.zeros_like(cots))
            weights = k.weights[g * 2 + e]
            inverse = 1.0 / k.totals[g * 2 + e]
            weights_cot = dot_inner(chosen, values)
            score_cot = (weights * inverse * (weights_cot - delta)).astype(bf)
            shared = (cots.astype(f3) * inverse).astype(bf)
            new = (
                dot_nn(score_cot, keys) * scale,
                dot_outer(score_cot, queries) * scale,
                dot_outer(weights.astype(bf), shared),
            )
            outs = [jnp.where(mine, fresh, old) for fresh, old in zip(new, outs)]
        for t in range(3):
            k.pc_s[here, pl.ds(t * own, own)] = outs[t].astype(bf)
        return unused

    lax.fori_loop(0, SLOTS, attend_back, 0)
    pc_blocks = k.pc_s.reshape(count, block, 3 * own)

    def unsort(i, unused):
        found = pc_blocks[k.order_sm[8, i]]
        for t in range(3):
            k.pc[t, at(i * block, block), :] = found[:, t * own : (t + 1) * own]
        return unused

    lax.fori_loop(0, count, unsort, 0, unroll=8)
    for p in view_peers:
        wires.send(k.pc.at[:, at(p * rows, rows)], k.pc_tok.at[:, :, own_cols], in_pc + v, (s, p))
    for t in range(3):
        k.pc_tok[t, :, own_cols] = k.pc[t, at(v * rows, rows), :]

    part = width // seqs
    for i, p in enumerate(seq_peers):
        for t in range(3):
            k.dw_out[i, t] = dot_outer(k.normed[:, at(p * part, part)], k.pc[t]).astype(bf)
        wires.send(k.dw_out.at[i], k.dw_in.at[s], in_dw + s, (p, v))
    own_part = at(s * part, part)
    own_dw = [dot_outer(k.normed[:, own_part], k.pc[t]) for t in range(3)]
    send_joined(0)
    wires.wait(k.do_y_in, in_do + 1)
    o_mine = at(y * o_quarter, o_quarter)
    k.do_keep[o_mine, :] = k.do_keep[o_mine, :] + k.do_y_in[...].astype(f3)
    k.do_x[...] = k.do_keep[at(y * o_quarter + (1 - x) * o_eighth, o_eighth), :].astype(bf)
    wires.send(k.do_x, k.do_x_in, in_do + 2, (x_s, v))
    for p in seq_peers:
        wires.wait(k.dw_in.at[p], in_dw + p)
    for t in range(3):
        total = own_dw[t]
        for p in seq_peers:
            total = total + k.dw_in[p, t].astype(f3)
        k.dw_own[t] = total.astype(bf)

    def w_at(q, j, first, last):
        return w_grad.at[pl.ds(first, last - first), at(q * part, part), at(j * own, own)]

    def w_plane(j):
        return w_at(s, j, 0, 3)

    def w_query(j):
        return w_at(x_s, j, 0, 1)

    def w_cross(q, j):
        return w_at(q, j, 1, 3)

    wires.send(k.dw_own.at[pl.ds(0, 1)], w_at(s, v, 0, 1), in_query + v, (x_s, v))
    wires.send(k.dw_own, w_plane(v), in_plane + v, (s, y_v))
    z_cast(k.dw_own, w_plane(v), in_plane + v)
    wires.send(k.dw_own.at[pl.ds(1, 2)], w_cross(s, v), in_cross + v, (x_s, v))
    wires.send(k.dw_own, w_plane(v), in_mate[0] + v, (c_s, v))
    keep_w = load(k.dw_own, w_plane(v))

    wires.wait(w_query(v), in_query + v)
    wires.send(w_query(v), w_query(v), in_query + v, (s, y_v))
    z_cast(w_query(v), w_query(v), in_query + v)
    wires.send(w_query(v), w_query(v), in_mate[1] + v, (c_s, v))

    wires.wait(k.do_x_in, in_do + 2)
    total = k.do_keep[at(y * o_quarter + x * o_eighth, o_eighth), :] + k.do_x_in[...].astype(f3)
    k.do_z[...] = total.astype(bf)

    def o_level(zt):
        return at(zt * o_piece, o_piece)

    for zt in others_z:
        wires.send(k.do_z.at[o_level(zt)], k.do_z_in.at[z], in_do_z + z, level(zt))

    add_cores(1)
    send_near(1)
    send_far(1)

    load_w.wait()
    for p in view_peers:
        wires.wait(k.pc_tok.at[:, :, at(p * own, own)], in_pc + p)

    def back_tile(n, unused):
        cols = at(n * tile, tile)
        total = dot_inner(k.pc_tok[0], k.w_full[cols, pl.ds(0, width)])
        for t in range(1, 3):
            total = total + dot_inner(k.pc_tok[t], k.w_full[cols, pl.ds(t * width, width)])
        k.part_own[0, :, cols] = total
        return unused

    lax.fori_loop(0, width // tile, back_tile, 0)
    unit_one, inverse_one = norm_stats(tok[...].astype(f3))
    cot_one = k.part_own[0]
    k.gain_own[0:1, :] = jnp.sum(cot_one * unit_one, axis=0, keepdims=True)
    k.gain_own[2:8, :] = jnp.zeros((6, width), f3)
    tokens_grad[...] = tokens_grad[...] + norm_back(cot_one, unit_one, inverse_one, gain_one)
    for p in seq_peers:
        wires.send(k.gain_own, k.gain_in.at[s], in_gain + s, (p, v))

    def o_at(q, j):
        at_c, at_x, at_y, at_z = q % 2, q // 2, j % 2, j // 2
        return o_grad.at[at(at_c * o_half + at_y * o_quarter + at_x * o_eighth + at_z * o_piece, o_piece)]

    def to_mate(which, ref, j):
        wires.send(ref, ref, in_mate[which] + j, (c_s, v))

    def pass_plane(zt, row_y):
        j = zt * 2 + row_y
        wires.wait(w_plane(j), in_plane + j)
        if row_y is y:
            if zt is z_two:
                z_relay(w_plane(j), in_plane + j)
            wires.send(w_plane(j), w_plane(j), in_plane + j, (s, y_v))
        wires.send(w_cross(s, j), w_cross(s, j), in_cross + j, (x_s, v))
        to_mate(0, w_plane(j), j)

    def pass_query(zt, row_y):
        j = zt * 2 + row_y
        wires.wait(w_query(j), in_query + j)
        if row_y is y:
            if zt is z_two:
                z_relay(w_query(j), in_query + j)
            wires.send(w_query(j), w_query(j), in_query + j, (s, y_v))
        to_mate(1, w_query(j), j)

    across = 1 - y
    for zt in others_z:
        pass_plane(zt, y)
    pass_plane(z, across)
    total = k.do_keep[at(y * o_quarter + x * o_eighth + z * o_piece, o_piece), :]
    total = total + k.do_x_in[o_level(z), :].astype(f3)
    for zt in others_z:
        wires.wait(k.do_z_in.at[zt], in_do_z + zt)
        total = total + k.do_z_in[zt].astype(f3)
    k.do_own[...] = total.astype(bf)
    wires.send(k.do_own, o_at(s, v), in_out + s * views + v, (s, y_v))
    z_cast(k.do_own, o_at(s, v), in_out + s * views + v)
    wires.send(k.do_own, o_at(s, v), in_out + s * views + v, (x_s, v))
    wires.send(k.do_own, o_at(s, v), in_out + s * views + v, (c_s, v))
    keep_o = load(k.do_own, o_at(s, v))
    for zt in others_z:
        pass_query(zt, y)
    send_joined(1)
    for zt in others_z:
        pass_plane(zt, across)
    for zt in [z] + others_z:
        pass_query(zt, across)

    total = k.gain_own[...]
    for p in seq_peers:
        wires.wait(k.gain_in.at[p], in_gain + p)
        total = total + k.gain_in[p]
    k.gain_sum[...] = total
    for p in view_peers:
        wires.send(k.gain_sum, k.gain_all.at[v], in_gains + v, (s, p))

    def pass_out(q, j, devices, relay):
        slot = in_out + q * views + j
        wires.wait(o_at(q, j), slot)
        if relay:
            z_relay(o_at(q, j), slot)
        for device in devices:
            wires.send(o_at(q, j), o_at(q, j), slot, device)

    for zt in others_z:
        pass_out(s, zt * 2 + y, [(s, y_v), (x_s, v), (c_s, v)], zt is z_two)
    for zt in [z] + others_z:
        pass_out(s, zt * 2 + across, [(x_s, v), (c_s, v)], False)

    layer_out[...] = (k.middle[...] + live * part_sum(1)).astype(bf)
    collect(0, down_grad)
    by_arrival = [v] + [zt * 2 + y for zt in others_z] + [zt * 2 + across for zt in [z] + others_z]
    for j in by_arrival:
        wires.wait(w_cross(x_s, j), in_cross + j)
        to_mate(2, w_cross(x_s, j), j)
    for j in by_arrival:
        pass_out(x_s, j, [(c_s, v)], False)
    collect(1, up_grad)

    total = k.gain_sum[...]
    for p in view_peers:
        wires.wait(k.gain_all.at[p], in_gains + p)
        total = total + k.gain_all[p]
    gains[...] = total

    for j in range(views):
        wires.wait(w_at(c_s, j, 0, 3), in_mate[0] + j)
        wires.wait(w_at(xc_s, j, 0, 1), in_mate[1] + j)
        wires.wait(w_cross(xc_s, j), in_mate[2] + j)
        for q in (c_s, xc_s):
            wires.wait(o_at(q, j), in_out + q * views + j)
    keep_w.wait()
    keep_o.wait()
    wires.drain()


def finish_kernel(*refs):
    (layer_in, tokens_in, gains, w_in, o_in, up_in, down_in) = refs[:7]
    (layer_out, tokens_grad, gain_one, w_out, o_out, gain_two, up_out, down_out) = refs[7:]
    width = w_in.shape[2]
    for t in range(3):
        w_out[:, t * width : (t + 1) * width] = w_in[t].astype(jnp.float32)
    o_out[...] = o_in[...].astype(jnp.float32)
    layer_out[...] = layer_in[...]
    tokens_grad[...] = tokens_in[...]
    up_out[...] = up_in[...]
    down_out[...] = down_in[...]
    gain_one[...] = gains[0:1, :].reshape(width)
    gain_two[...] = gains[1:2, :].reshape(width)


def fused(
    seqs,
    views,
    tokens,
    scene_ids,
    live_mask,
    out_grad,
    attention_gain,
    input_weight,
    output_weight,
    feedforward_gain,
    up_weight,
    down_weight,
):
    rows, width = tokens.shape[1:]
    hidden = up_weight.shape[0]
    spec = scratch_of(rows, width, seqs, views, hidden)
    vmem = pl.BlockSpec(memory_space=pltpu.VMEM)
    anywhere = pl.BlockSpec(memory_space=pl.ANY)
    shape = jax.ShapeDtypeStruct
    bf, f3 = jnp.bfloat16, jnp.float32
    parts = pl.pallas_call(
        functools.partial(layer_kernel, tuple(spec), seqs, views),
        out_shape=(
            shape((rows, width), bf),
            shape((rows, width), f3),
            shape((8, width), f3),
            shape((3, width, width), bf),
            shape((width, width), bf),
            shape((hidden, width), f3),
            shape((hidden, width), f3),
        ),
        in_specs=[vmem] * 6 + [anywhere] * 4,
        out_specs=(vmem, vmem, vmem, anywhere, anywhere, vmem, vmem),
        scratch_shapes=list(spec.values()),
        compiler_params=pltpu.CompilerParams(
            collective_id=0, has_side_effects=True, vmem_limit_bytes=67043328
        ),
        name="layer",
    )(
        tokens[0],
        scene_ids,
        live_mask,
        out_grad[0],
        attention_gain,
        feedforward_gain,
        input_weight,
        output_weight,
        up_weight,
        down_weight,
    )
    steps = 8

    def slab(*lead):
        full = lead + (width,)
        block = full[:-2] + (full[-2] // steps, width)
        return pl.BlockSpec(block, lambda i: (0,) * (len(block) - 2) + (i, 0))

    whole = pl.BlockSpec((8, width), lambda i: (0, 0))
    line = pl.BlockSpec((width,), lambda i: (0,))
    thick = pl.BlockSpec((width // steps, 3 * width), lambda i: (i, 0))
    layer_out, tokens_grad, gain_one, w_grad, o_grad, gain_two, up_grad, down_grad = pl.pallas_call(
        finish_kernel,
        grid=(steps,),
        out_shape=(
            shape((rows, width), bf),
            shape((rows, width), f3),
            shape((width,), f3),
            shape((width, 3 * width), f3),
            shape((width, width), f3),
            shape((width,), f3),
            shape((hidden, width), f3),
            shape((hidden, width), f3),
        ),
        in_specs=[slab(rows), slab(rows), whole, slab(3, width), slab(width), slab(hidden), slab(hidden)],
        out_specs=(slab(rows), slab(rows), line, thick, slab(width), line, slab(hidden), slab(hidden)),
        name="finish",
    )(*parts)
    return (
        layer_out[None],
        tokens_grad[None],
        gain_one,
        w_grad,
        o_grad,
        gain_two,
        up_grad,
        down_grad,
    )


def solution(mesh):
    seqs, views = mesh.shape["seq"], mesh.shape["view"]
    small = seqs == 4 and views == 2 * LEVELS and HEADS == 2 * views
    body = functools.partial(fused, seqs, views) if small else shards
    return jax.shard_map(
        body,
        mesh=mesh,
        in_specs=(
            P("seq", "view", None),
            P("seq", "view"),
            P("seq", "view"),
            P("seq", "view", None),
            P(),
            P(),
            P(),
            P(),
            P(("seq", "view"), None),
            P(("seq", "view"), None),
        ),
        out_specs=(
            P("seq", "view", None),
            P("seq", "view", None),
            P(),
            P(),
            P(),
            P(),
            P(("seq", "view"), None),
            P(("seq", "view"), None),
        ),
        check_vma=False,
    )
```

```python
import functools
import math
import types

import jax
import jax.numpy as jnp
from jax import lax
from jax.experimental import pallas as pl
from jax.experimental.pallas import tpu as pltpu
from jax.sharding import PartitionSpec as P

HEADS = 16
HEAD_DIM = 64


EPS = 1e-05
NEGATIVE = -1e30
MESH = pl.DeviceIdType.MESH
SLOTS = 4
SCENE_BLOCKS = 16


def layer_norm(values, gain):
    center = values - jnp.mean(values, axis=-1, keepdims=True)
    spread = jnp.mean(center * center, axis=-1, keepdims=True)
    return center * lax.rsqrt(spread + EPS) * gain


def gelu_exact(values):
    return jax.nn.gelu(values, approximate=False)


def plain_dot(left, right):
    return jnp.dot(left, right, preferred_element_type=jnp.float32)


def dot_inner(left, right):
    return lax.dot_general(
        left, right, (((1,), (1,)), ((), ())), preferred_element_type=jnp.float32
    )


def dot_outer(left, right):
    return lax.dot_general(
        left, right, (((0,), (0,)), ((), ())), preferred_element_type=jnp.float32
    )


def split_heads(values):
    return values.reshape(values.shape[0], HEADS, HEAD_DIM)


def masked_scores(queries, keys, query_tags, key_tags, scale):
    raw = jnp.einsum("qhe,khe->hqk", queries, keys, preferred_element_type=jnp.float32) * scale
    allowed = (query_tags[:, None] == key_tags[None, :])[None]
    return (raw, allowed)


def probabilities(queries, keys, query_tags, key_tags, log_total, scale):
    raw, allowed = masked_scores(queries, keys, query_tags, key_tags, scale)
    return jnp.where(
        allowed, jnp.exp(jnp.where(allowed, raw - log_total[:, :, None], NEGATIVE)), 0.0
    )


def in_blocks(step, carry, piece):
    count = piece[0].shape[0]
    size = math.gcd(count, 512)
    number = count // size
    stacked = tuple((member.reshape((number, size) + member.shape[1:]) for member in piece))

    def inner(state, item):
        members, offset = item
        return (step(state, members, offset * size), None)

    result, unused = lax.scan(inner, carry, (stacked, jnp.arange(number, dtype=jnp.int32)))
    return result


def shards(
    tokens,
    scene_ids,
    live_mask,
    out_grad,
    attention_gain,
    input_weight,
    output_weight,
    feedforward_gain,
    up_weight,
    down_weight,
):
    scale = HEAD_DIM ** (-0.5)
    inputs = tokens[0].astype(jnp.float32)
    rows = inputs.shape[0]
    width = inputs.shape[1]
    tags = scene_ids[0] * 2 + live_mask[0]
    live = live_mask[0].astype(jnp.float32)[:, None]
    every_tag = lax.all_gather(tags, "view", axis=0, tiled=True)
    up_full, down_full = (
        lax.all_gather(up_weight, ("seq", "view"), axis=0, tiled=True),
        lax.all_gather(down_weight, ("seq", "view"), axis=0, tiled=True),
    )
    gain_one = attention_gain.astype(jnp.float32)
    gain_two = feedforward_gain.astype(jnp.float32)
    normed = layer_norm(inputs, gain_one).astype(jnp.bfloat16)
    projected = plain_dot(normed, input_weight).astype(jnp.bfloat16)
    query_flat = projected[:, :width]
    queries = split_heads(query_flat)
    keys_own = projected[:, width : 2 * width]
    values_own = projected[:, 2 * width :]

    def attend_step(carry, piece, start):
        peak, total, accum = carry
        key_piece, value_piece = piece
        count = key_piece.shape[0]
        key_tags = lax.dynamic_slice_in_dim(every_tag, start, count)
        raw, allowed = masked_scores(queries, split_heads(key_piece), tags, key_tags, scale)
        masked = jnp.where(allowed, raw, NEGATIVE)
        new_peak = jnp.maximum(peak, jnp.max(masked, axis=-1))
        weights = jnp.where(allowed, jnp.exp(masked - new_peak[:, :, None]), 0.0)
        factor = jnp.exp(peak - new_peak)
        total = total * factor + jnp.sum(weights, axis=-1)
        update = jnp.einsum(
            "hqk,khe->qhe",
            weights.astype(jnp.bfloat16),
            split_heads(value_piece),
            preferred_element_type=jnp.float32,
        )
        accum = accum * jnp.transpose(factor)[:, :, None] + update
        return (new_peak, total, accum)

    start_state = (
        jnp.full((HEADS, rows), NEGATIVE, jnp.float32),
        jnp.zeros((HEADS, rows), jnp.float32),
        jnp.zeros((rows, HEADS, HEAD_DIM), jnp.float32),
    )
    peak, total, accum = in_blocks(
        attend_step,
        start_state,
        (
            lax.all_gather(keys_own, "view", axis=0, tiled=True),
            lax.all_gather(values_own, "view", axis=0, tiled=True),
        ),
    )
    attended_heads = accum / jnp.transpose(total)[:, :, None]
    log_total = peak + jnp.log(total)
    attended_low = attended_heads.reshape(rows, width).astype(jnp.bfloat16)
    branch = plain_dot(attended_low, output_weight)
    middle = inputs + live * branch
    normed_two = layer_norm(middle, gain_two).astype(jnp.bfloat16)
    hidden = dot_inner(normed_two, up_full)
    activated = gelu_exact(hidden).astype(jnp.bfloat16)
    mixed = plain_dot(activated, down_full)
    layer_out = (middle + live * mixed).astype(jnp.bfloat16)[None]
    out_cot = out_grad[0].astype(jnp.float32)
    mixed_cot = (live * out_cot).astype(jnp.bfloat16)
    down_grad = dot_outer(activated, mixed_cot)
    activated_cot = dot_inner(mixed_cot, down_full)
    hidden_cot = jax.vjp(gelu_exact, hidden)[1](activated_cot)[0].astype(jnp.bfloat16)
    up_grad = dot_outer(hidden_cot, normed_two)
    normed_two_cot = plain_dot(hidden_cot, up_full)
    second_pull = jax.vjp(layer_norm, middle, gain_two)[1]
    middle_part, gain_two_grad = second_pull(normed_two_cot)
    middle_cot = out_cot + middle_part
    branch_cot = (live * middle_cot).astype(jnp.bfloat16)
    output_weight_grad = dot_outer(attended_low, branch_cot)
    attended_cot = dot_inner(branch_cot, output_weight).astype(jnp.bfloat16)
    cot_heads = split_heads(attended_cot)
    delta = jnp.transpose(jnp.sum(cot_heads.astype(jnp.float32) * attended_heads, axis=-1))
    seq_len = every_tag.shape[0]

    def back_step(carry, piece, start):
        query_cot, key_value_cot = carry
        key_piece, value_piece = piece
        count = key_piece.shape[0]
        key_tags = lax.dynamic_slice_in_dim(every_tag, start, count)
        key_heads = split_heads(key_piece)
        value_heads = split_heads(value_piece)
        probs = probabilities(queries, key_heads, tags, key_tags, log_total, scale)
        prob_cot = jnp.einsum(
            "qhe,khe->hqk", cot_heads, value_heads, preferred_element_type=jnp.float32
        )
        score_cot = (probs * (prob_cot - delta[:, :, None])).astype(jnp.bfloat16)
        query_cot = (
            query_cot
            + jnp.einsum("hqk,khe->qhe", score_cot, key_heads, preferred_element_type=jnp.float32)
            * scale
        )
        key_cot = (
            jnp.einsum("hqk,qhe->khe", score_cot, queries, preferred_element_type=jnp.float32)
            * scale
        )
        value_cot = jnp.einsum(
            "hqk,qhe->khe",
            probs.astype(jnp.bfloat16),
            cot_heads,
            preferred_element_type=jnp.float32,
        )
        stacked = jnp.concatenate(
            [key_cot.reshape(count, width), value_cot.reshape(count, width)], axis=1
        )
        earlier = lax.dynamic_slice_in_dim(key_value_cot, start, count)
        key_value_cot = lax.dynamic_update_slice_in_dim(key_value_cot, earlier + stacked, start, 0)
        return (query_cot, key_value_cot)

    back_state = (
        jnp.zeros((rows, HEADS, HEAD_DIM), jnp.float32),
        jnp.zeros((seq_len, 2 * width), jnp.float32),
    )
    query_cot, key_value_cot = in_blocks(
        back_step,
        back_state,
        (
            lax.all_gather(keys_own, "view", axis=0, tiled=True),
            lax.all_gather(values_own, "view", axis=0, tiled=True),
        ),
    )
    own_cot = lax.psum_scatter(key_value_cot, "view", scatter_dimension=0, tiled=True)
    key_cot_own = own_cot[:, :width]
    value_cot_own = own_cot[:, width:]
    projected_cot = jnp.concatenate(
        [query_cot.reshape(rows, width), key_cot_own, value_cot_own], axis=1
    ).astype(jnp.bfloat16)
    input_weight_grad = dot_outer(normed, projected_cot)
    normed_cot = dot_inner(projected_cot, input_weight)
    first_pull = jax.vjp(layer_norm, inputs, gain_one)[1]
    input_part, gain_one_grad = first_pull(normed_cot)
    tokens_grad = (middle_cot + input_part)[None]
    up_part, down_part = (
        lax.psum_scatter(up_grad, ("seq", "view"), scatter_dimension=0, tiled=True),
        lax.psum_scatter(down_grad, ("seq", "view"), scatter_dimension=0, tiled=True),
    )
    summed = lax.psum(
        (gain_one_grad, input_weight_grad, output_weight_grad, gain_two_grad), ("seq", "view")
    )
    return (layer_out, tokens_grad, summed[0], summed[1], summed[2], summed[3], up_part, down_part)


def dot_nn(left, right):
    return lax.dot_general(left, right, (((1,), (0,)), ((), ())), preferred_element_type=jnp.float32)


def at(start, size):
    return pl.ds(pl.multiple_of(start, size), size)


def norm_stats(values):
    mean = jnp.mean(values, axis=-1, keepdims=True)
    center = values - mean
    spread = jnp.mean(center * center, axis=-1, keepdims=True)
    inverse = lax.rsqrt(spread + EPS)
    return center * inverse, inverse


def norm_back(cot, unit, inverse, gain):
    scaled = cot * gain
    first = jnp.mean(scaled, axis=-1, keepdims=True)
    second = jnp.mean(scaled * unit, axis=-1, keepdims=True)
    return inverse * (scaled - first - unit * second)


class Wires:
    def __init__(self, send_sem, recv_sem, peer):
        self.send_sem, self.recv_sem, self.peer = send_sem, recv_sem, peer
        self.free, self.recvs, self.total, self.pending = list(range(SENDS)), 0, 0, []

    def inbox(self, count):
        base = self.recvs
        self.recvs += count
        assert self.recvs <= RECVS
        return base

    def bulk(self):
        return self.free.pop(0)

    def copy(self, src, dst, lane, slot, device):
        return pltpu.make_async_remote_copy(
            src_ref=src,
            dst_ref=dst,
            send_sem=self.send_sem.at[lane],
            recv_sem=self.recv_sem.at[slot],
            device_id=device,
            device_id_type=MESH,
        )

    def send(self, src, dst, slot, device, when=None, bulk=None):
        lane = self.free.pop(0) if bulk is None else bulk
        copy = self.copy(src, dst, lane, slot, device)
        if when is None:
            copy.start()
        else:
            pl.when(when)(copy.start)
        if bulk is None:
            self.pending.append((self.total, copy, when, lane))
            self.total += 1
        return copy

    def finish(self, entry):
        unused, copy, when, lane = entry
        if when is None:
            copy.wait_send()
        else:
            pl.when(when)(copy.wait_send)
        self.free.append(lane)

    def sent(self, copy):
        for entry in [entry for entry in self.pending if entry[1] is copy]:
            self.finish(entry)
        self.pending = [entry for entry in self.pending if entry[1] is not copy]

    def settle(self, until):
        for entry in [entry for entry in self.pending if entry[0] < until]:
            self.finish(entry)
        self.pending = [entry for entry in self.pending if entry[0] >= until]

    def settle_bulk(self, whole, lane):
        self.copy(whole, whole, lane, 0, self.peer).wait_send()

    def wait(self, dst, slot):
        self.copy(dst, dst, 0, slot, self.peer).wait_recv()


SENDS, RECVS, LOCALS = 80, 124, 16
LEVELS = 4


def scratch_of(rows, width, seqs, views, hidden):
    length = rows * views
    own = width // views
    bf, f3 = jnp.bfloat16, jnp.float32
    vm = pltpu.VMEM
    mlp_rows = hidden * seqs * views // 4
    half, quarter, eighth = width // 2, width // 4, width // 8
    return dict(
        tok=vm((rows, width), bf),
        out_cot=vm((rows, width), bf),
        layer_out=vm((rows, width), bf),
        tokens_grad=vm((rows, width), f3),
        up_grad=vm((hidden, width), f3),
        down_grad=vm((hidden, width), f3),
        w_full=vm((width, 3 * width), bf),
        w_own=vm((width, 3 * own), bf),
        wo=vm((width, width), bf),
        up=vm((mlp_rows, width), bf),
        down=vm((mlp_rows, width), bf),
        ids_all=vm((views, 8, 128), jnp.int32),
        order_vm=vm((16, 128), jnp.int32),
        order_sm=pltpu.SMEM((16, 128), jnp.int32),
        normed=vm((length, width), bf),
        qkv=vm((length, 3 * own), bf),
        qkv_s=vm((length, 3 * own), bf),
        weights=vm((2 * SLOTS, length // SLOTS, length // SLOTS), f3),
        totals=vm((2 * SLOTS, length // SLOTS, 1), f3),
        att_s=vm((length, own), f3),
        att=vm((length, own), bf),
        att_tok=vm((rows, width), bf),
        middle=vm((rows, width), f3),
        normed_two=vm((4 * rows, width), bf),
        mixed_cot=vm((4 * rows, width), bf),
        slope=vm((4 * rows, mlp_rows), f3),
        part_all=vm((4 * rows, width), f3),
        act=vm((4 * rows, mlp_rows), bf),
        hid_cot=vm((4 * rows, mlp_rows), bf),
        part_own=vm((2, rows, width), f3),
        part_out=vm((2, 3, rows, width), bf),
        part_in=vm((2, 4, rows, width), bf),
        grad_keep=vm((2, mlp_rows // 2, width), bf),
        grad_pass=vm((2, mlp_rows // 2, width), bf),
        grad_core=vm((2, mlp_rows // 2, width), bf),
        grad_in=vm((2, LEVELS + 1, hidden, width), bf),
        branch=vm((rows, width), bf),
        acot_tok=vm((rows, width), bf),
        acot=vm((length, own), bf),
        acot_s=vm((length, own), bf),
        pc_s=vm((length, 3 * own), bf),
        pc=vm((3, length, own), bf),
        pc_tok=vm((3, rows, width), bf),
        dw_out=vm((2, 3, width // seqs, own), bf),
        dw_x=vm((3, width // seqs, own), bf),
        dw_in=vm((3, 3, width // seqs, own), bf),
        dw_own=vm((3, width // seqs, own), bf),
        do_keep=vm((half, width), f3),
        do_core=vm((half, width), bf),
        do_core_in=vm((half, width), bf),
        do_y=vm((quarter, width), bf),
        do_y_in=vm((quarter, width), bf),
        do_x=vm((eighth, width), bf),
        do_x_in=vm((eighth, width), bf),
        do_z=vm((eighth, width), bf),
        do_z_in=vm((LEVELS, eighth // LEVELS, width), bf),
        do_own=vm((eighth // LEVELS, width), bf),
        gain_own=vm((8, width), f3),
        gain_in=vm((seqs, 8, width), f3),
        gain_sum=vm((8, width), f3),
        gain_all=vm((views, 8, width), f3),
        send_sem=pltpu.SemaphoreType.DMA((SENDS,)),
        recv_sem=pltpu.SemaphoreType.DMA((RECVS,)),
        local_sem=pltpu.SemaphoreType.DMA((LOCALS,)),
    )


def layer_kernel(names, seqs, views, *refs):
    (tok_hbm, ids, alive, cot_hbm, gain_one_ref, gain_two_ref, w_hbm, wo_hbm, up_hbm, down_hbm) = refs[:10]
    (layer_hbm, tokens_hbm, gains, w_grad, o_grad, up_hbm_out, down_hbm_out) = refs[10:17]
    k = types.SimpleNamespace(**dict(zip(names, refs[17:])))
    tok, out_cot = k.tok, k.out_cot
    layer_out, tokens_grad, up_grad, down_grad = k.layer_out, k.tokens_grad, k.up_grad, k.down_grad
    rows, width = tok.shape
    length = rows * views
    own = width // views
    hidden = up_hbm.shape[0]
    mlp_rows = k.up.shape[0]
    half = mlp_rows // 2
    block = length // (SLOTS * SCENE_BLOCKS)
    scene = length // SLOTS
    scale = HEAD_DIM ** (-0.5)
    bf, f3 = jnp.bfloat16, jnp.float32

    s = lax.axis_index("seq")
    v = lax.axis_index("view")
    x, c, z, y = s // 2, s % 2, v // 2, v % 2
    x_s, c_s, xc_s = (1 - x) * 2 + c, x * 2 + (1 - c), (1 - x) * 2 + (1 - c)
    y_v = z * 2 + (1 - y)
    z_pair, z_two, z_flip = z + 1 - 2 * (z % 2), lax.rem(z + 2, LEVELS), LEVELS - 1 - z
    inner = (z == 1) | (z == 2)
    outer = (z == 0) | (z == 3)
    others_z = [z_pair, z_two, z_flip]
    group = [(x_s, v), (s, y_v), (x_s, y_v)]
    group_slot = [(1 - x) * 2 + y, x * 2 + (1 - y), (1 - x) * 2 + (1 - y)]
    own_slot = x * 2 + y
    view_peers = [lax.rem(v + d, views) for d in range(1, views)]
    seq_peers = [x_s, xc_s, c_s]

    def level(zt):
        return (s, zt * 2 + y)

    wires = Wires(k.send_sem, k.recv_sem, (c_s, v))
    in_normed = wires.inbox(views)
    in_ids = wires.inbox(views)
    in_up = wires.inbox(LEVELS + 1)
    in_down = wires.inbox(LEVELS + 1)
    in_mcot = wires.inbox(4)
    in_att = wires.inbox(views)
    in_two = wires.inbox(4)
    in_part = [wires.inbox(4), wires.inbox(4)]
    in_core = [wires.inbox(1), wires.inbox(1)]
    in_grad = [wires.inbox(LEVELS + 1), wires.inbox(LEVELS + 1)]
    in_acot, in_pc = in_ids, in_att
    in_dw = wires.inbox(3)
    in_do = wires.inbox(3)
    in_do_z = wires.inbox(LEVELS)
    in_plane = wires.inbox(views)
    in_query = wires.inbox(views)
    in_cross = wires.inbox(views)
    in_mate = [wires.inbox(1) for unused in range(3)]
    in_out = [wires.inbox(views), wires.inbox(views)]
    in_out_mate = wires.inbox(1)
    in_gain = wires.inbox(seqs)
    in_gains = in_normed
    to_view = [wires.bulk() for unused in range(5)]
    to_mate_w = [wires.bulk() for unused in range(3)]
    to_mate_o = wires.bulk()

    def z_cast(src, dst, slot):
        wires.send(src, dst, slot, level(z_pair))
        wires.send(src, dst, slot, level(z_two))
        wires.send(src, dst, slot, level(z_flip), when=inner)

    def z_relay(ref, slot):
        wires.send(ref, ref, slot, level(z_pair), when=inner)

    barrier = pltpu.get_barrier_semaphore()
    greeted = [(s, p) for p in view_peers] + [(p, v) for p in seq_peers] + [(x_s, y_v)]
    for device in greeted:
        pl.semaphore_signal(barrier, inc=1, device_id=device, device_id_type=MESH)

    loads, kept = [], []

    def load(src, dst):
        copy = pltpu.make_async_copy(src, dst, k.local_sem.at[len(loads)])
        copy.start()
        loads.append(copy)
        return copy

    up_slot = at((c * LEVELS + z) * hidden, hidden)
    load_tok = load(tok_hbm, tok)
    load_cot = load(cot_hbm, out_cot)
    load_up = load(up_hbm, k.up.at[up_slot])
    load_down = load(down_hbm, k.down.at[up_slot])
    load_own = [
        load(w_hbm.at[:, at(t * width + v * own, own)], k.w_own.at[:, pl.ds(t * own, own)])
        for t in range(3)
    ]
    load_wo = load(wo_hbm, k.wo)
    load_w = load(w_hbm, k.w_full)

    gain_one = gain_one_ref[...].astype(f3).reshape(1, width)
    gain_two = gain_two_ref[...].astype(f3).reshape(1, width)
    load_tok.wait()
    unit, _ = norm_stats(tok[...].astype(f3))
    k.normed[at(v * rows, rows), :] = (unit * gain_one).astype(bf)
    per = rows // block
    lane = lax.broadcasted_iota(jnp.int32, (1, 128), 1)
    scenes = jnp.zeros((1, 128), jnp.int32)
    for m in range(per):
        mine = jnp.broadcast_to(ids[:, m * block : m * block + 1], (1, 128))
        scenes = jnp.where(lane == v * per + m, mine, scenes)
    k.ids_all[v] = jnp.broadcast_to(scenes, (8, 128))
    live = jnp.transpose(jnp.broadcast_to(alive[...].astype(f3), (rows, rows)))[:, :1]
    pl.semaphore_wait(barrier, len(greeted))

    def view_rows(ref, j):
        return ref.at[at(j * rows, rows)]

    for p in view_peers:
        wires.send(k.ids_all.at[v], k.ids_all.at[v], in_ids + v, (s, p), bulk=to_view[0])
    mine = view_rows(k.normed, v)
    wires.send(mine, mine, in_normed + v, (s, y_v))
    z_cast(mine, mine, in_normed + v)
    load_cot.wait()
    mcot_own = at(own_slot * rows, rows)
    k.mixed_cot[mcot_own, :] = (live * out_cot[...].astype(f3)).astype(bf)

    def send_mcot(device):
        wires.send(k.mixed_cot.at[mcot_own], k.mixed_cot.at[mcot_own], in_mcot + own_slot, device)

    send_mcot(group[0])

    for p in view_peers:
        wires.wait(k.ids_all.at[p], in_ids + p)
    count = SLOTS * SCENE_BLOCKS
    scene_row = k.ids_all[0][:1]
    for j in range(1, views):
        scene_row = scene_row + k.ids_all[j][:1]
    big = lax.broadcasted_iota(jnp.int32, (128, 128), 0)
    wide = lax.broadcasted_iota(jnp.int32, (128, 128), 1)
    scene_mat = jnp.broadcast_to(scene_row, (128, 128))
    scene_col = jnp.transpose(scene_mat)
    ahead = (scene_col < scene_mat) | ((scene_col == scene_mat) & (big < wide))
    place = jnp.sum(jnp.where(ahead & (big < count), 1, 0), axis=0, keepdims=True)
    place_col = jnp.transpose(jnp.broadcast_to(place, (128, 128)))
    hit = jnp.where((place_col == wide) & (big < count), big, 0)
    source = jnp.sum(hit, axis=0, keepdims=True)
    k.order_vm[0:8, :] = jnp.broadcast_to(source, (8, 128))
    k.order_vm[8:16, :] = jnp.broadcast_to(place, (8, 128))
    to_scalar = load(k.order_vm, k.order_sm)

    for copy in load_own:
        copy.wait()

    def project(j):
        k.qkv[at(j * rows, rows), :] = dot_nn(k.normed[at(j * rows, rows), :], k.w_own[...]).astype(bf)

    project(v)
    for zt in others_z:
        j = zt * 2 + y
        there = view_rows(k.normed, j)
        wires.wait(there, in_normed + j)
        if zt is z_two:
            z_relay(there, in_normed + j)
        wires.send(there, there, in_normed + j, (s, y_v))
        if zt is z_two:
            load_up.wait()
            z_cast(k.up.at[up_slot], k.up.at[up_slot], in_up + z)
        project(j)
    for zt in [z] + others_z:
        j = zt * 2 + 1 - y
        wires.wait(view_rows(k.normed, j), in_normed + j)
        project(j)
    def mlp_slot(ref, zt):
        return ref.at[at((c * LEVELS + zt) * hidden, hidden)]

    def mlp_relay(ref, base):
        @pl.when(inner)
        def _():
            wires.wait(mlp_slot(ref, z_two), base + z_two)

        z_relay(mlp_slot(ref, z_two), base + z_two)

    def core_exchange(ref, base):
        @pl.when(outer)
        def _():
            wires.wait(mlp_slot(ref, z_two), base + z_two)

        for zt in (z_pair, z_flip):
            wires.wait(mlp_slot(ref, zt), base + zt)
        mine = ref.at[at(c * half, half)]
        wires.send(mine, mine, base + LEVELS, (c_s, v))

    mlp_relay(k.up, in_up)
    send_mcot(group[1])
    send_mcot(group[2])
    to_scalar.wait()

    def reorder(dst, src, row):
        blocks = src.reshape(count, block, src.shape[1])

        def step(i, unused):
            from_block = k.order_sm[row, i]
            dst[at(i * block, block), :] = blocks[from_block].astype(dst.dtype)
            return unused

        lax.fori_loop(0, count, step, 0, unroll=8)

    reorder(k.qkv_s, k.qkv, 0)

    head_lane = lax.broadcasted_iota(jnp.int32, (scene, own), 1) // HEAD_DIM

    def attend(g, unused):
        here = at(g * scene, scene)
        queries, keys, values = (k.qkv_s[here, pl.ds(t * own, own)] for t in range(3))
        result = jnp.zeros((scene, own), f3)
        for e in range(2):
            chosen = jnp.where(head_lane == e, queries, jnp.zeros_like(queries))
            weights = jnp.exp(dot_inner(chosen, keys) * scale)
            total = jnp.sum(weights, axis=-1, keepdims=True)
            k.weights[g * 2 + e] = weights
            k.totals[g * 2 + e] = total
            mixed = dot_nn(weights.astype(bf), values) / total
            result = jnp.where(head_lane == e, mixed, result)
        k.att_s[here, :] = result
        return unused

    lax.fori_loop(0, SLOTS, attend, 0)
    reorder(k.att, k.att_s, 8)
    own_cols = at(v * own, own)
    for p in view_peers:
        wires.send(view_rows(k.att, p), k.att_tok.at[:, own_cols], in_att + v, (s, p), bulk=to_view[1])
    k.att_tok[:, own_cols] = k.att[at(v * rows, rows), :]


    load_wo.wait()
    for p in view_peers:
        wires.wait(k.att_tok.at[:, at(p * own, own)], in_att + p)
    tile = 256
    for n in range(width // tile):
        cols = pl.ds(n * tile, tile)
        k.middle[:, cols] = tok[:, cols].astype(f3) + live * dot_nn(k.att_tok[...], k.wo[:, cols])
    unit_two, _ = norm_stats(k.middle[...])
    k.normed_two[mcot_own, :] = (unit_two * gain_two).astype(bf)
    until_two = wires.total
    for device in group:
        wires.send(k.normed_two.at[mcot_own], k.normed_two.at[mcot_own], in_two + own_slot, device)
    load_down.wait()
    z_cast(k.down.at[up_slot], k.down.at[up_slot], in_down + z)

    core_exchange(k.up, in_up)
    wires.wait(k.up.at[at((1 - c) * half, half)], in_up + LEVELS)

    def hidden_tiles(slot):
        here = at(slot * rows, rows)

        def step(n, unused):
            cols = at(n * tile, tile)
            pre = dot_inner(k.normed_two[here, :], k.up[cols, :])
            below = 0.5 + 0.5 * lax.erf(pre * (0.5**0.5))
            k.act[here, cols] = (pre * below).astype(bf)
            k.slope[here, cols] = below + pre * (jnp.exp(-0.5 * pre * pre) * (0.5 / math.pi) ** 0.5)
            return unused

        lax.fori_loop(0, mlp_rows // tile, step, 0)

    hidden_tiles(own_slot)
    for slot in group_slot:
        if slot is group_slot[2]:
            mlp_relay(k.down, in_down)
        wires.wait(k.normed_two.at[at(slot * rows, rows)], in_two + slot)
        hidden_tiles(slot)

    def grad_tiles(left, right, start, dst):
        def step(n, unused):
            there = at(n * tile, tile)
            dst[there, :] = dot_outer(left[:, at(start + n * tile, tile)], right[...]).astype(dst.dtype)
            return unused

        lax.fori_loop(0, half // tile, step, 0)

    passed = []

    def grad_halves(which, left, right):
        grad_tiles(left, right, (1 - c) * half, k.grad_pass.at[which])
        passed.append(wires.send(k.grad_pass.at[which], k.grad_core.at[which], in_core[which], (c_s, v)))
        grad_tiles(left, right, c * half, k.grad_keep.at[which])

    for slot in group_slot:
        wires.wait(k.mixed_cot.at[at(slot * rows, rows)], in_mcot + slot)
    grad_halves(0, k.act, k.mixed_cot)
    core_exchange(k.down, in_down)

    def grad_level(which, zt):
        there = at(zt * hidden, hidden)
        return k.grad_keep[which, there, :].astype(f3) + k.grad_core[which, there, :].astype(f3)

    def grad_piece(which, zt):
        return k.grad_pass.at[which, at(zt * hidden, hidden)]

    def add_cores(which):
        wires.wait(k.grad_core.at[which], in_core[which])
        wires.sent(passed[which])
        for zt in others_z:
            k.grad_pass[which, at(zt * hidden, hidden), :] = grad_level(which, zt).astype(bf)

    def send_near(which):
        wires.send(grad_piece(which, z_pair), k.grad_in.at[which, z], in_grad[which] + z, level(z_pair))

    def send_far(which):
        via = LEVELS
        wires.send(grad_piece(which, z_flip), k.grad_in.at[which, via], in_grad[which] + via, level(z_pair), when=outer)
        wires.send(grad_piece(which, z_two), k.grad_in.at[which, z], in_grad[which] + z, level(z_two), when=outer)
        wires.send(grad_piece(which, z_flip), k.grad_in.at[which, z], in_grad[which] + z, level(z_flip), when=inner)

    def send_joined(which):
        @pl.when(inner)
        def _():
            wires.wait(k.grad_in.at[which, LEVELS], in_grad[which] + LEVELS)
            there = at(z_two * hidden, hidden)
            joined = k.grad_pass[which, there, :].astype(f3) + k.grad_in[which, LEVELS].astype(f3)
            k.grad_pass[which, there, :] = joined.astype(bf)

        wires.send(grad_piece(which, z_two), k.grad_in.at[which, z], in_grad[which] + z, level(z_two), when=inner)

    def collect(which, dst):
        total = grad_level(which, z)
        for zt in (z_pair, z_two):
            wires.wait(k.grad_in.at[which, zt], in_grad[which] + zt)
            total = total + k.grad_in[which, zt].astype(f3)
        dst[...] = total

        @pl.when(inner)
        def _():
            wires.wait(k.grad_in.at[which, z_flip], in_grad[which] + z_flip)
            dst[...] = dst[...] + k.grad_in[which, z_flip].astype(f3)

    add_cores(0)
    send_far(0)
    send_near(0)

    wires.wait(k.down.at[at((1 - c) * half, half)], in_down + LEVELS)

    def cot_tile(n, unused):
        cols = at(n * tile, tile)
        up_to = dot_inner(k.mixed_cot[...], k.down[cols, :])
        k.hid_cot[:, cols] = (up_to * k.slope[:, cols]).astype(bf)
        return unused

    lax.fori_loop(0, mlp_rows // tile, cot_tile, 0)

    def part_tiles(which, left, right):
        def step(n, unused):
            cols = at(n * tile, tile)
            k.part_all[:, cols] = dot_nn(left[...], right[:, cols])
            return unused

        lax.fori_loop(0, width // tile, step, 0)
        for i in (2, 0, 1):
            k.part_out[which, i] = k.part_all[at(group_slot[i] * rows, rows), :].astype(bf)
            wires.send(k.part_out.at[which, i], k.part_in.at[which, own_slot], in_part[which] + own_slot, group[i])
        k.part_own[which] = k.part_all[mcot_own, :]

    part_tiles(0, k.hid_cot, k.up)
    grad_halves(1, k.hid_cot, k.normed_two)
    part_tiles(1, k.act, k.down)
    send_joined(0)

    def part_sum(which):
        total = k.part_own[which]
        for slot in group_slot:
            wires.wait(k.part_in.at[which, slot], in_part[which] + slot)
            total = total + k.part_in[which, slot].astype(f3)
        return total

    unit_two, inverse_two = norm_stats(k.middle[...])
    wires.settle(until_two)
    cot_two = part_sum(0)
    until_acot = wires.total
    k.gain_own[1:2, :] = jnp.sum(cot_two * unit_two, axis=0, keepdims=True)
    middle_cot = out_cot[...].astype(f3) + norm_back(cot_two, unit_two, inverse_two, gain_two)
    tokens_grad[...] = middle_cot
    k.branch[...] = (live * middle_cot).astype(bf)
    for n in range(width // tile):
        k.acot_tok[:, pl.ds(n * tile, tile)] = dot_inner(
            k.branch[...], k.wo[pl.ds(n * tile, tile), :]
        ).astype(bf)
    for p in view_peers:
        wires.send(k.acot_tok.at[:, at(p * own, own)], view_rows(k.acot, v), in_acot + v, (s, p), bulk=to_view[2])
    k.acot[at(v * rows, rows), :] = k.acot_tok[:, own_cols]
    add_cores(1)
    send_near(1)

    o_half, o_quarter, o_eighth = width // 2, width // 4, width // 8
    o_piece = o_eighth // LEVELS

    def outer_rows(start, dst, dtype):
        def step(n, unused):
            there = at(n * tile, tile)
            left = k.att_tok[:, at(start + n * tile, tile)]
            dst[there, :] = dot_outer(left, k.branch[...]).astype(dtype)
            return unused

        lax.fori_loop(0, o_half // tile, step, 0)

    outer_rows((1 - c) * o_half, k.do_core, bf)
    wires.send(k.do_core, k.do_core_in, in_do, (c_s, v))
    outer_rows(c * o_half, k.do_keep, f3)
    wires.wait(k.do_core_in, in_do)
    k.do_keep[...] = k.do_keep[...] + k.do_core_in[...].astype(f3)
    k.do_y[...] = k.do_keep[at((1 - y) * o_quarter, o_quarter), :].astype(bf)
    wires.send(k.do_y, k.do_y_in, in_do + 1, (s, y_v))

    for p in view_peers:
        wires.wait(view_rows(k.acot, p), in_acot + p)
    reorder(k.acot_s, k.acot, 0)

    def attend_back(g, unused):
        here = at(g * scene, scene)
        queries, keys, values = (k.qkv_s[here, pl.ds(t * own, own)] for t in range(3))
        cots = k.acot_s[here, :]
        agree = cots.astype(f3) * k.att_s[here, :]
        outs = [jnp.zeros((scene, own), f3) for t in range(3)]
        for e in range(2):
            mine = head_lane == e
            delta = jnp.sum(jnp.where(mine, agree, 0.0), axis=-1, keepdims=True)
            chosen = jnp.where(mine, cots, jnp.zeros_like(cots))
            weights = k.weights[g * 2 + e]
            inverse = 1.0 / k.totals[g * 2 + e]
            weights_cot = dot_inner(chosen, values)
            score_cot = (weights * inverse * (weights_cot - delta)).astype(bf)
            shared = (cots.astype(f3) * inverse).astype(bf)
            new = (
                dot_nn(score_cot, keys) * scale,
                dot_outer(score_cot, queries) * scale,
                dot_outer(weights.astype(bf), shared),
            )
            outs = [jnp.where(mine, fresh, old) for fresh, old in zip(new, outs)]
        for t in range(3):
            k.pc_s[here, pl.ds(t * own, own)] = outs[t].astype(bf)
        return unused

    lax.fori_loop(0, SLOTS, attend_back, 0)
    pc_blocks = k.pc_s.reshape(count, block, 3 * own)

    def unsort(i, unused):
        found = pc_blocks[k.order_sm[8, i]]
        for t in range(3):
            k.pc[t, at(i * block, block), :] = found[:, t * own : (t + 1) * own]
        return unused

    lax.fori_loop(0, count, unsort, 0, unroll=8)
    for p in view_peers:
        wires.send(k.pc.at[:, at(p * rows, rows)], k.pc_tok.at[:, :, own_cols], in_pc + v, (s, p), bulk=to_view[3])
    for t in range(3):
        k.pc_tok[t, :, own_cols] = k.pc[t, at(v * rows, rows), :]

    part = width // seqs

    def own_dw(row_block, t):
        return dot_outer(k.normed[:, at(row_block * part, part)], k.pc[t])

    for i, xt in enumerate((1 - x, x)):
        for t in range(3):
            k.dw_out[i, t] = own_dw(xt * 2 + 1 - c, t).astype(bf)
        wires.send(k.dw_out.at[i], k.dw_in.at[i], in_dw + i, (c_s, v))
    wires.wait(k.dw_in.at[0], in_dw)
    for t in range(3):
        k.dw_x[t] = (own_dw(x_s, t) + k.dw_in[0, t].astype(f3)).astype(bf)
    wires.send(k.dw_x, k.dw_in.at[2], in_dw + 2, (x_s, v))
    wires.wait(k.do_y_in, in_do + 1)
    o_mine = at(y * o_quarter, o_quarter)
    k.do_keep[o_mine, :] = k.do_keep[o_mine, :] + k.do_y_in[...].astype(f3)
    k.do_x[...] = k.do_keep[at(y * o_quarter + (1 - x) * o_eighth, o_eighth), :].astype(bf)
    wires.send(k.do_x, k.do_x_in, in_do + 2, (x_s, v))
    mine_dw = [own_dw(s, t) for t in range(3)]
    wires.wait(k.dw_in.at[1], in_dw + 1)
    wires.settle(until_acot)
    wires.wait(k.dw_in.at[2], in_dw + 2)
    for t in range(3):
        total = mine_dw[t] + k.dw_in[1, t].astype(f3) + k.dw_in[2, t].astype(f3)
        k.dw_own[t] = total.astype(bf)

    def w_at(q, j, first, last):
        return w_grad.at[pl.ds(first, last - first), at(q * part, part), at(j * own, own)]

    def w_plane(j):
        return w_at(s, j, 0, 3)

    def w_query(j):
        return w_at(x_s, j, 0, 1)

    def w_cross(q, j):
        return w_at(q, j, 1, 3)

    wires.send(k.dw_own.at[pl.ds(0, 1)], w_at(s, v, 0, 1), in_query + v, (x_s, v))
    wires.send(k.dw_own, w_plane(v), in_plane + v, (s, y_v))
    z_cast(k.dw_own, w_plane(v), in_plane + v)
    wires.send(k.dw_own.at[pl.ds(1, 2)], w_cross(s, v), in_cross + v, (x_s, v))
    wires.send(k.dw_own, w_plane(v), in_mate[0], (c_s, v), bulk=to_mate_w[0])
    kept.append(load(k.dw_own, w_plane(v)))

    wires.wait(w_query(v), in_query + v)
    wires.send(w_query(v), w_query(v), in_query + v, (s, y_v))
    z_cast(w_query(v), w_query(v), in_query + v)
    wires.send(w_query(v), w_query(v), in_mate[1], (c_s, v), bulk=to_mate_w[1])

    load_w.wait()
    for p in view_peers:
        wires.wait(k.pc_tok.at[:, :, at(p * own, own)], in_pc + p)

    def back_tile(n, unused):
        cols = at(n * tile, tile)
        total = dot_inner(k.pc_tok[0], k.w_full[cols, pl.ds(0, width)])
        for t in range(1, 3):
            total = total + dot_inner(k.pc_tok[t], k.w_full[cols, pl.ds(t * width, width)])
        k.part_own[0, :, cols] = total
        return unused

    lax.fori_loop(0, width // tile, back_tile, 0)
    unit_one, inverse_one = norm_stats(tok[...].astype(f3))
    cot_one = k.part_own[0]
    k.gain_own[0:1, :] = jnp.sum(cot_one * unit_one, axis=0, keepdims=True)
    k.gain_own[2:8, :] = jnp.zeros((6, width), f3)
    tokens_grad[...] = tokens_grad[...] + norm_back(cot_one, unit_one, inverse_one, gain_one)
    for p in seq_peers:
        wires.send(k.gain_own, k.gain_in.at[s], in_gain + s, (p, v))
    kept.append(load(tokens_grad, tokens_hbm))

    def o_at(q, j):
        at_c, at_x, at_y, at_z = q % 2, q // 2, j % 2, j // 2
        return o_grad.at[at(at_c * o_half + at_y * o_quarter + at_x * o_eighth + at_z * o_piece, o_piece)]

    def to_mate(which, ref):
        wires.send(ref, ref, in_mate[which], (c_s, v), bulk=to_mate_w[which])

    def pass_plane(zt, row_y):
        j = zt * 2 + row_y
        wires.wait(w_plane(j), in_plane + j)
        if row_y is y:
            if zt is z_two:
                z_relay(w_plane(j), in_plane + j)
            wires.send(w_plane(j), w_plane(j), in_plane + j, (s, y_v))
        wires.send(w_cross(s, j), w_cross(s, j), in_cross + j, (x_s, v))
        to_mate(0, w_plane(j))

    def pass_query(zt, row_y):
        j = zt * 2 + row_y
        wires.wait(w_query(j), in_query + j)
        if row_y is y:
            if zt is z_two:
                z_relay(w_query(j), in_query + j)
            wires.send(w_query(j), w_query(j), in_query + j, (s, y_v))
        to_mate(1, w_query(j))

    wires.wait(k.do_x_in, in_do + 2)
    total = k.do_keep[at(y * o_quarter + x * o_eighth, o_eighth), :] + k.do_x_in[...].astype(f3)
    k.do_z[...] = total.astype(bf)

    def o_level(zt):
        return at(zt * o_piece, o_piece)

    for zt in others_z:
        wires.send(k.do_z.at[o_level(zt)], k.do_z_in.at[z], in_do_z + z, level(zt))

    across = 1 - y
    for zt in others_z:
        pass_plane(zt, y)
    for zt in others_z:
        pass_query(zt, y)
    total = k.do_keep[at(y * o_quarter + x * o_eighth + z * o_piece, o_piece), :]
    total = total + k.do_x_in[o_level(z), :].astype(f3)
    for zt in others_z:
        wires.wait(k.do_z_in.at[zt], in_do_z + zt)
        total = total + k.do_z_in[zt].astype(f3)
    k.do_own[...] = total.astype(bf)
    wires.send(k.do_own, o_at(s, v), in_out[0] + v, (s, y_v))
    z_cast(k.do_own, o_at(s, v), in_out[0] + v)
    wires.send(k.do_own, o_at(s, v), in_out[1] + v, (x_s, v))
    wires.send(k.do_own, o_at(s, v), in_out_mate, (c_s, v), bulk=to_mate_o)
    kept.append(load(k.do_own, o_at(s, v)))
    send_far(1)
    for zt in [z] + others_z:
        pass_plane(zt, across)
    for zt in [z] + others_z:
        pass_query(zt, across)

    total = k.gain_own[...]
    for p in seq_peers:
        wires.wait(k.gain_in.at[p], in_gain + p)
        total = total + k.gain_in[p]
    k.gain_sum[...] = total
    for p in view_peers:
        wires.send(k.gain_sum, k.gain_all.at[v], in_gains + v, (s, p), bulk=to_view[4])

    def out_mate(q, j):
        wires.send(o_at(q, j), o_at(q, j), in_out_mate, (c_s, v), bulk=to_mate_o)

    def pass_out(zt, row_y):
        j = zt * 2 + row_y
        slot = in_out[0] + j
        wires.wait(o_at(s, j), slot)
        if row_y is y:
            if zt is z_two:
                z_relay(o_at(s, j), slot)
            wires.send(o_at(s, j), o_at(s, j), slot, (s, y_v))
        wires.send(o_at(s, j), o_at(s, j), in_out[1] + j, (x_s, v))
        out_mate(s, j)

    for zt in others_z:
        pass_out(zt, y)
    send_joined(1)
    for zt in [z] + others_z:
        pass_out(zt, across)

    layer_out[...] = (k.middle[...] + live * part_sum(1)).astype(bf)
    kept.append(load(layer_out, layer_hbm))
    collect(0, down_grad)
    kept.append(load(down_grad, down_hbm_out))
    by_arrival = [v] + [zt * 2 + y for zt in others_z] + [zt * 2 + across for zt in [z] + others_z]
    for j in by_arrival:
        wires.wait(w_cross(x_s, j), in_cross + j)
        to_mate(2, w_cross(x_s, j))
    for j in by_arrival:
        wires.wait(o_at(x_s, j), in_out[1] + j)
        out_mate(x_s, j)
    collect(1, up_grad)
    kept.append(load(up_grad, up_hbm_out))

    total = k.gain_sum[...]
    for p in view_peers:
        wires.wait(k.gain_all.at[p], in_gains + p)
        total = total + k.gain_all[p]
    gains[...] = total

    def w_rows(q, first, last):
        return w_grad.at[pl.ds(first, last - first), at(q * part, part)]

    def o_core(core):
        return o_grad.at[at(core * o_half, o_half)]

    wires.settle(wires.total)
    for whole, lane in (
        (k.ids_all.at[pl.ds(0, views - 1)], to_view[0]),
        (k.att.at[pl.ds(0, length - rows)], to_view[1]),
        (k.acot.at[pl.ds(0, length - rows)], to_view[2]),
        (k.pc.at[:, pl.ds(0, length - rows)], to_view[3]),
        (k.gain_all.at[pl.ds(0, views - 1)], to_view[4]),
        (w_rows(s, 0, 3), to_mate_w[0]),
        (w_rows(x_s, 0, 1), to_mate_w[1]),
        (w_rows(x_s, 1, 3), to_mate_w[2]),
        (o_core(c), to_mate_o),
    ):
        wires.settle_bulk(whole, lane)
    wires.wait(w_rows(c_s, 0, 3), in_mate[0])
    wires.wait(w_rows(xc_s, 0, 1), in_mate[1])
    wires.wait(w_rows(xc_s, 1, 3), in_mate[2])
    wires.wait(o_core(1 - c), in_out_mate)
    for copy in kept:
        copy.wait()


FINISH_STEPS = 8


def finish_kernel(*refs):
    (layer_in, tokens_in, gains, w_in, o_in, up_in, down_in) = refs[:7]
    (layer_out, tokens_grad, gain_one, w_out, o_out, gain_two, up_out, down_out) = refs[7:15]
    (layer, tokens, up, down, w_narrow, o_narrow, w_wide, o_wide, in_sem, out_sem) = refs[15:]
    width = o_in.shape[0]
    tall = width // FINISH_STEPS
    asis = ((layer_in, layer, layer_out), (tokens_in, tokens, tokens_grad), (up_in, up, up_out), (down_in, down, down_out))

    def rows(i):
        return pl.ds(i * tall, tall)

    def start(src, dst, sem):
        copy = pltpu.make_async_copy(src, dst, sem)
        copy.start()
        return copy

    reads, writes = [], []
    for i in range(FINISH_STEPS):
        reads.append(start(w_in.at[:, rows(i)], w_narrow.at[:, rows(i)], in_sem.at[2 * i]))
        reads.append(start(o_in.at[rows(i)], o_narrow.at[rows(i)], in_sem.at[2 * i + 1]))
    late = [start(src, mid, in_sem.at[2 * FINISH_STEPS + i]) for i, (src, mid, dst) in enumerate(asis)]
    gain_one[...] = gains[0:1, :].reshape(width)
    gain_two[...] = gains[1:2, :].reshape(width)
    for i in range(FINISH_STEPS):
        reads[2 * i].wait()
        for t in range(3):
            w_wide[rows(i), t * width : (t + 1) * width] = w_narrow[t, rows(i), :].astype(jnp.float32)
        writes.append(start(w_wide.at[rows(i)], w_out.at[rows(i)], out_sem.at[2 * i]))
        reads[2 * i + 1].wait()
        o_wide[rows(i), :] = o_narrow[rows(i), :].astype(jnp.float32)
        writes.append(start(o_wide.at[rows(i)], o_out.at[rows(i)], out_sem.at[2 * i + 1]))
    for i, (src, mid, dst) in enumerate(asis):
        late[i].wait()
        writes.append(start(mid, dst, out_sem.at[2 * FINISH_STEPS + i]))
    for copy in writes:
        copy.wait()


def fused(
    seqs,
    views,
    tokens,
    scene_ids,
    live_mask,
    out_grad,
    attention_gain,
    input_weight,
    output_weight,
    feedforward_gain,
    up_weight,
    down_weight,
):
    rows, width = tokens.shape[1:]
    hidden = up_weight.shape[0]
    spec = scratch_of(rows, width, seqs, views, hidden)
    vmem = pl.BlockSpec(memory_space=pltpu.VMEM)
    anywhere = pl.BlockSpec(memory_space=pl.ANY)
    shape = jax.ShapeDtypeStruct
    bf, f3 = jnp.bfloat16, jnp.float32
    parts = pl.pallas_call(
        functools.partial(layer_kernel, tuple(spec), seqs, views),
        out_shape=(
            shape((rows, width), bf),
            shape((rows, width), f3),
            shape((8, width), f3),
            shape((3, width, width), bf),
            shape((width, width), bf),
            shape((hidden, width), f3),
            shape((hidden, width), f3),
        ),
        in_specs=[anywhere, vmem, vmem, anywhere, vmem, vmem] + [anywhere] * 4,
        out_specs=(anywhere, anywhere, vmem, anywhere, anywhere, anywhere, anywhere),
        scratch_shapes=list(spec.values()),
        compiler_params=pltpu.CompilerParams(
            collective_id=0, has_side_effects=True, vmem_limit_bytes=67043328
        ),
        name="layer",
    )(
        tokens[0],
        scene_ids,
        live_mask,
        out_grad[0],
        attention_gain,
        feedforward_gain,
        input_weight,
        output_weight,
        up_weight,
        down_weight,
    )
    layer_out, tokens_grad, gain_one, w_grad, o_grad, gain_two, up_grad, down_grad = pl.pallas_call(
        finish_kernel,
        out_shape=(
            shape((rows, width), bf),
            shape((rows, width), f3),
            shape((width,), f3),
            shape((width, 3 * width), f3),
            shape((width, width), f3),
            shape((width,), f3),
            shape((hidden, width), f3),
            shape((hidden, width), f3),
        ),
        in_specs=[anywhere] * 2 + [vmem] + [anywhere] * 4,
        out_specs=(anywhere, anywhere, vmem, anywhere, anywhere, vmem, anywhere, anywhere),
        scratch_shapes=[
            pltpu.VMEM((rows, width), bf),
            pltpu.VMEM((rows, width), f3),
            pltpu.VMEM((hidden, width), f3),
            pltpu.VMEM((hidden, width), f3),
            pltpu.VMEM((3, width, width), bf),
            pltpu.VMEM((width, width), bf),
            pltpu.VMEM((width, 3 * width), f3),
            pltpu.VMEM((width, width), f3),
            pltpu.SemaphoreType.DMA((2 * FINISH_STEPS + 4,)),
            pltpu.SemaphoreType.DMA((2 * FINISH_STEPS + 4,)),
        ],
        name="finish",
    )(*parts)
    return (
        layer_out[None],
        tokens_grad[None],
        gain_one,
        w_grad,
        o_grad,
        gain_two,
        up_grad,
        down_grad,
    )


def solution(mesh):
    seqs, views = mesh.shape["seq"], mesh.shape["view"]
    small = seqs == 4 and views == 2 * LEVELS and HEADS == 2 * views
    body = functools.partial(fused, seqs, views) if small else shards
    return jax.shard_map(
        body,
        mesh=mesh,
        in_specs=(
            P("seq", "view", None),
            P("seq", "view"),
            P("seq", "view"),
            P("seq", "view", None),
            P(),
            P(),
            P(),
            P(),
            P(("seq", "view"), None),
            P(("seq", "view"), None),
        ),
        out_specs=(
            P("seq", "view", None),
            P("seq", "view", None),
            P(),
            P(),
            P(),
            P(),
            P(("seq", "view"), None),
            P(("seq", "view"), None),
        ),
        check_vma=False,
    )
```

```python
import functools
import math
import types

import jax
import jax.numpy as jnp
from jax import lax
from jax.experimental import pallas as pl
from jax.experimental.pallas import tpu as pltpu
from jax.sharding import PartitionSpec as P

HEADS = 16
HEAD_DIM = 64


EPS = 1e-05
NEGATIVE = -1e30
MESH = pl.DeviceIdType.MESH
SLOTS = 4
SCENE_BLOCKS = 16


def layer_norm(values, gain):
    center = values - jnp.mean(values, axis=-1, keepdims=True)
    spread = jnp.mean(center * center, axis=-1, keepdims=True)
    return center * lax.rsqrt(spread + EPS) * gain


def gelu_exact(values):
    return jax.nn.gelu(values, approximate=False)


def plain_dot(left, right):
    return jnp.dot(left, right, preferred_element_type=jnp.float32)


def dot_inner(left, right):
    return lax.dot_general(
        left, right, (((1,), (1,)), ((), ())), preferred_element_type=jnp.float32
    )


def dot_outer(left, right):
    return lax.dot_general(
        left, right, (((0,), (0,)), ((), ())), preferred_element_type=jnp.float32
    )


def split_heads(values):
    return values.reshape(values.shape[0], HEADS, HEAD_DIM)


def masked_scores(queries, keys, query_tags, key_tags, scale):
    raw = jnp.einsum("qhe,khe->hqk", queries, keys, preferred_element_type=jnp.float32) * scale
    allowed = (query_tags[:, None] == key_tags[None, :])[None]
    return (raw, allowed)


def probabilities(queries, keys, query_tags, key_tags, log_total, scale):
    raw, allowed = masked_scores(queries, keys, query_tags, key_tags, scale)
    return jnp.where(
        allowed, jnp.exp(jnp.where(allowed, raw - log_total[:, :, None], NEGATIVE)), 0.0
    )


def in_blocks(step, carry, piece):
    count = piece[0].shape[0]
    size = math.gcd(count, 512)
    number = count // size
    stacked = tuple((member.reshape((number, size) + member.shape[1:]) for member in piece))

    def inner(state, item):
        members, offset = item
        return (step(state, members, offset * size), None)

    result, unused = lax.scan(inner, carry, (stacked, jnp.arange(number, dtype=jnp.int32)))
    return result


def shards(
    tokens,
    scene_ids,
    live_mask,
    out_grad,
    attention_gain,
    input_weight,
    output_weight,
    feedforward_gain,
    up_weight,
    down_weight,
):
    scale = HEAD_DIM ** (-0.5)
    inputs = tokens[0].astype(jnp.float32)
    rows = inputs.shape[0]
    width = inputs.shape[1]
    tags = scene_ids[0] * 2 + live_mask[0]
    live = live_mask[0].astype(jnp.float32)[:, None]
    every_tag = lax.all_gather(tags, "view", axis=0, tiled=True)
    up_full, down_full = (
        lax.all_gather(up_weight, ("seq", "view"), axis=0, tiled=True),
        lax.all_gather(down_weight, ("seq", "view"), axis=0, tiled=True),
    )
    gain_one = attention_gain.astype(jnp.float32)
    gain_two = feedforward_gain.astype(jnp.float32)
    normed = layer_norm(inputs, gain_one).astype(jnp.bfloat16)
    projected = plain_dot(normed, input_weight).astype(jnp.bfloat16)
    query_flat = projected[:, :width]
    queries = split_heads(query_flat)
    keys_own = projected[:, width : 2 * width]
    values_own = projected[:, 2 * width :]

    def attend_step(carry, piece, start):
        peak, total, accum = carry
        key_piece, value_piece = piece
        count = key_piece.shape[0]
        key_tags = lax.dynamic_slice_in_dim(every_tag, start, count)
        raw, allowed = masked_scores(queries, split_heads(key_piece), tags, key_tags, scale)
        masked = jnp.where(allowed, raw, NEGATIVE)
        new_peak = jnp.maximum(peak, jnp.max(masked, axis=-1))
        weights = jnp.where(allowed, jnp.exp(masked - new_peak[:, :, None]), 0.0)
        factor = jnp.exp(peak - new_peak)
        total = total * factor + jnp.sum(weights, axis=-1)
        update = jnp.einsum(
            "hqk,khe->qhe",
            weights.astype(jnp.bfloat16),
            split_heads(value_piece),
            preferred_element_type=jnp.float32,
        )
        accum = accum * jnp.transpose(factor)[:, :, None] + update
        return (new_peak, total, accum)

    start_state = (
        jnp.full((HEADS, rows), NEGATIVE, jnp.float32),
        jnp.zeros((HEADS, rows), jnp.float32),
        jnp.zeros((rows, HEADS, HEAD_DIM), jnp.float32),
    )
    peak, total, accum = in_blocks(
        attend_step,
        start_state,
        (
            lax.all_gather(keys_own, "view", axis=0, tiled=True),
            lax.all_gather(values_own, "view", axis=0, tiled=True),
        ),
    )
    attended_heads = accum / jnp.transpose(total)[:, :, None]
    log_total = peak + jnp.log(total)
    attended_low = attended_heads.reshape(rows, width).astype(jnp.bfloat16)
    branch = plain_dot(attended_low, output_weight)
    middle = inputs + live * branch
    normed_two = layer_norm(middle, gain_two).astype(jnp.bfloat16)
    hidden = dot_inner(normed_two, up_full)
    activated = gelu_exact(hidden).astype(jnp.bfloat16)
    mixed = plain_dot(activated, down_full)
    layer_out = (middle + live * mixed).astype(jnp.bfloat16)[None]
    out_cot = out_grad[0].astype(jnp.float32)
    mixed_cot = (live * out_cot).astype(jnp.bfloat16)
    down_grad = dot_outer(activated, mixed_cot)
    activated_cot = dot_inner(mixed_cot, down_full)
    hidden_cot = jax.vjp(gelu_exact, hidden)[1](activated_cot)[0].astype(jnp.bfloat16)
    up_grad = dot_outer(hidden_cot, normed_two)
    normed_two_cot = plain_dot(hidden_cot, up_full)
    second_pull = jax.vjp(layer_norm, middle, gain_two)[1]
    middle_part, gain_two_grad = second_pull(normed_two_cot)
    middle_cot = out_cot + middle_part
    branch_cot = (live * middle_cot).astype(jnp.bfloat16)
    output_weight_grad = dot_outer(attended_low, branch_cot)
    attended_cot = dot_inner(branch_cot, output_weight).astype(jnp.bfloat16)
    cot_heads = split_heads(attended_cot)
    delta = jnp.transpose(jnp.sum(cot_heads.astype(jnp.float32) * attended_heads, axis=-1))
    seq_len = every_tag.shape[0]

    def back_step(carry, piece, start):
        query_cot, key_value_cot = carry
        key_piece, value_piece = piece
        count = key_piece.shape[0]
        key_tags = lax.dynamic_slice_in_dim(every_tag, start, count)
        key_heads = split_heads(key_piece)
        value_heads = split_heads(value_piece)
        probs = probabilities(queries, key_heads, tags, key_tags, log_total, scale)
        prob_cot = jnp.einsum(
            "qhe,khe->hqk", cot_heads, value_heads, preferred_element_type=jnp.float32
        )
        score_cot = (probs * (prob_cot - delta[:, :, None])).astype(jnp.bfloat16)
        query_cot = (
            query_cot
            + jnp.einsum("hqk,khe->qhe", score_cot, key_heads, preferred_element_type=jnp.float32)
            * scale
        )
        key_cot = (
            jnp.einsum("hqk,qhe->khe", score_cot, queries, preferred_element_type=jnp.float32)
            * scale
        )
        value_cot = jnp.einsum(
            "hqk,qhe->khe",
            probs.astype(jnp.bfloat16),
            cot_heads,
            preferred_element_type=jnp.float32,
        )
        stacked = jnp.concatenate(
            [key_cot.reshape(count, width), value_cot.reshape(count, width)], axis=1
        )
        earlier = lax.dynamic_slice_in_dim(key_value_cot, start, count)
        key_value_cot = lax.dynamic_update_slice_in_dim(key_value_cot, earlier + stacked, start, 0)
        return (query_cot, key_value_cot)

    back_state = (
        jnp.zeros((rows, HEADS, HEAD_DIM), jnp.float32),
        jnp.zeros((seq_len, 2 * width), jnp.float32),
    )
    query_cot, key_value_cot = in_blocks(
        back_step,
        back_state,
        (
            lax.all_gather(keys_own, "view", axis=0, tiled=True),
            lax.all_gather(values_own, "view", axis=0, tiled=True),
        ),
    )
    own_cot = lax.psum_scatter(key_value_cot, "view", scatter_dimension=0, tiled=True)
    key_cot_own = own_cot[:, :width]
    value_cot_own = own_cot[:, width:]
    projected_cot = jnp.concatenate(
        [query_cot.reshape(rows, width), key_cot_own, value_cot_own], axis=1
    ).astype(jnp.bfloat16)
    input_weight_grad = dot_outer(normed, projected_cot)
    normed_cot = dot_inner(projected_cot, input_weight)
    first_pull = jax.vjp(layer_norm, inputs, gain_one)[1]
    input_part, gain_one_grad = first_pull(normed_cot)
    tokens_grad = (middle_cot + input_part)[None]
    up_part, down_part = (
        lax.psum_scatter(up_grad, ("seq", "view"), scatter_dimension=0, tiled=True),
        lax.psum_scatter(down_grad, ("seq", "view"), scatter_dimension=0, tiled=True),
    )
    summed = lax.psum(
        (gain_one_grad, input_weight_grad, output_weight_grad, gain_two_grad), ("seq", "view")
    )
    return (layer_out, tokens_grad, summed[0], summed[1], summed[2], summed[3], up_part, down_part)


def dot_nn(left, right):
    return lax.dot_general(left, right, (((1,), (0,)), ((), ())), preferred_element_type=jnp.float32)


def at(start, size):
    return pl.ds(pl.multiple_of(start, size), size)


def norm_stats(values):
    mean = jnp.mean(values, axis=-1, keepdims=True)
    center = values - mean
    spread = jnp.mean(center * center, axis=-1, keepdims=True)
    inverse = lax.rsqrt(spread + EPS)
    return center * inverse, inverse


def norm_back(cot, unit, inverse, gain):
    scaled = cot * gain
    first = jnp.mean(scaled, axis=-1, keepdims=True)
    second = jnp.mean(scaled * unit, axis=-1, keepdims=True)
    return inverse * (scaled - first - unit * second)


class Wires:
    def __init__(self, send_sem, recv_sem, peer):
        self.send_sem, self.recv_sem, self.peer = send_sem, recv_sem, peer
        self.free, self.recvs, self.total, self.pending = list(range(SENDS)), 0, 0, []

    def inbox(self, count):
        base = self.recvs
        self.recvs += count
        assert self.recvs <= RECVS
        return base

    def bulk(self):
        return self.free.pop(0)

    def copy(self, src, dst, lane, slot, device):
        return pltpu.make_async_remote_copy(
            src_ref=src,
            dst_ref=dst,
            send_sem=self.send_sem.at[lane],
            recv_sem=self.recv_sem.at[slot],
            device_id=device,
            device_id_type=MESH,
        )

    def send(self, src, dst, slot, device, when=None, bulk=None):
        lane = self.free.pop(0) if bulk is None else bulk
        copy = self.copy(src, dst, lane, slot, device)
        if when is None:
            copy.start()
        else:
            pl.when(when)(copy.start)
        if bulk is None:
            self.pending.append((self.total, copy, when, lane))
            self.total += 1
        return copy

    def finish(self, entry):
        unused, copy, when, lane = entry
        if when is None:
            copy.wait_send()
        else:
            pl.when(when)(copy.wait_send)
        self.free.append(lane)

    def sent(self, copy):
        for entry in [entry for entry in self.pending if entry[1] is copy]:
            self.finish(entry)
        self.pending = [entry for entry in self.pending if entry[1] is not copy]

    def settle(self, until):
        for entry in [entry for entry in self.pending if entry[0] < until]:
            self.finish(entry)
        self.pending = [entry for entry in self.pending if entry[0] >= until]

    def settle_bulk(self, whole, lane):
        self.copy(whole, whole, lane, 0, self.peer).wait_send()

    def wait(self, dst, slot):
        self.copy(dst, dst, 0, slot, self.peer).wait_recv()


SENDS, RECVS, LOCALS = 88, 136, 20
LEVELS = 4


def scratch_of(rows, width, seqs, views, hidden):
    length = rows * views
    own = width // views
    bf, f3 = jnp.bfloat16, jnp.float32
    vm = pltpu.VMEM
    mlp_rows = hidden * seqs * views // 4
    half, quarter, eighth = width // 2, width // 4, width // 8
    return dict(
        tok=vm((rows, width), bf),
        out_cot=vm((rows, width), bf),
        layer_out=vm((rows, width), bf),
        tokens_grad=vm((rows, width), f3),
        up_grad=vm((hidden, width), f3),
        down_grad=vm((hidden, width), f3),
        w_full=vm((width, 3 * width), bf),
        w_own=vm((width, 3 * own), bf),
        wo=vm((width, width), bf),
        up=vm((mlp_rows, width), bf),
        down=vm((mlp_rows, width), bf),
        ids_all=vm((views, 8, 128), jnp.int32),
        order_vm=vm((16, 128), jnp.int32),
        order_sm=pltpu.SMEM((16, 128), jnp.int32),
        normed=vm((length, width), bf),
        qkv=vm((length, 3 * own), bf),
        qkv_s=vm((length, 3 * own), bf),
        weights=vm((2 * SLOTS, length // SLOTS, length // SLOTS), f3),
        totals=vm((2 * SLOTS, length // SLOTS, 1), f3),
        att_s=vm((length, own), f3),
        att=vm((length, own), bf),
        att_tok=vm((rows, width), bf),
        middle=vm((rows, width), f3),
        normed_two=vm((4 * rows, width), bf),
        mixed_cot=vm((4 * rows, width), bf),
        wide=vm((4 * rows, mlp_rows), f3),
        act=vm((4 * rows, mlp_rows), bf),
        hid_cot=vm((4 * rows, mlp_rows), bf),
        part_own=vm((2, 2, rows, width), f3),
        part_out=vm((2, 3, rows, width), bf),
        part_in=vm((2, 3, rows, width), bf),
        grad_keep=vm((2, mlp_rows // 2, width), bf),
        grad_pass=vm((2, mlp_rows // 2, width), bf),
        grad_core=vm((2, mlp_rows // 2, width), bf),
        grad_y=vm((2, 2, hidden, width), bf),
        grad_z=vm((2, hidden, width), bf),
        branch=vm((rows, width), bf),
        acot_tok=vm((rows, width), bf),
        acot=vm((length, own), bf),
        acot_s=vm((length, own), bf),
        pc_s=vm((length, 3 * own), bf),
        pc=vm((3, length, own), bf),
        pc_flat=vm((length, 3 * own), bf),
        pc_tok=vm((3, rows, width), bf),
        dw_out=vm((2, 3, width // seqs, own), bf),
        dw_x=vm((3, width // seqs, own), bf),
        dw_in=vm((3, 3, width // seqs, own), bf),
        dw_own=vm((3, width // seqs, own), bf),
        do_core=vm((half, width), bf),
        do_core_in=vm((half, width), bf),
        do_y=vm((quarter, width), bf),
        do_y_in=vm((quarter, width), bf),
        do_x=vm((eighth, width), bf),
        do_x_in=vm((eighth, width), bf),
        do_z=vm((eighth, width), bf),
        do_z_in=vm((LEVELS, eighth // LEVELS, width), bf),
        do_own=vm((eighth // LEVELS, width), bf),
        gain_own=vm((8, width), f3),
        gain_in=vm((seqs, 8, width), f3),
        gain_sum=vm((8, width), f3),
        gain_all=vm((views, 8, width), f3),
        send_sem=pltpu.SemaphoreType.DMA((SENDS,)),
        recv_sem=pltpu.SemaphoreType.DMA((RECVS,)),
        local_sem=pltpu.SemaphoreType.DMA((LOCALS,)),
    )


def layer_kernel(names, seqs, views, *refs):
    (tok_hbm, ids, alive, cot_hbm, gain_one_ref, gain_two_ref, w_hbm, wo_hbm, up_hbm, down_hbm) = refs[:10]
    (layer_hbm, tokens_hbm, gains, w_grad, o_grad, up_part, up_away, down_hbm_out) = refs[10:18]
    k = types.SimpleNamespace(**dict(zip(names, refs[18:])))
    k.slope = k.part_all = k.do_keep = k.wide
    tok, out_cot = k.tok, k.out_cot
    layer_out, tokens_grad, up_grad, down_grad = k.layer_out, k.tokens_grad, k.up_grad, k.down_grad
    rows, width = tok.shape
    length = rows * views
    own = width // views
    hidden = up_hbm.shape[0]
    mlp_rows = k.up.shape[0]
    half = mlp_rows // 2
    block = length // (SLOTS * SCENE_BLOCKS)
    scene = length // SLOTS
    scale = HEAD_DIM ** (-0.5)
    bf, f3 = jnp.bfloat16, jnp.float32

    s = lax.axis_index("seq")
    v = lax.axis_index("view")
    x, c, z, y = s // 2, s % 2, v // 2, v % 2
    x_s, c_s, xc_s = (1 - x) * 2 + c, x * 2 + (1 - c), (1 - x) * 2 + (1 - c)
    y_v = z * 2 + (1 - y)
    z_pair, z_two, z_flip = z + 1 - 2 * (z % 2), lax.rem(z + 2, LEVELS), LEVELS - 1 - z
    inner = (z == 1) | (z == 2)
    others_z = [z_pair, z_two, z_flip]
    low, high = z % 2, z // 2
    pair_v = z_pair * 2 + y
    own_slot, x_slot = x * 2 + low, (1 - x) * 2 + low
    pair_slot, far_slot = x * 2 + (1 - low), (1 - x) * 2 + (1 - low)
    view_peers = [lax.rem(v + d, views) for d in range(1, views)]
    seq_peers = [x_s, xc_s, c_s]

    def level(zt):
        return (s, zt * 2 + y)

    wires = Wires(k.send_sem, k.recv_sem, (c_s, v))
    in_normed = wires.inbox(2 * views)
    in_ids = wires.inbox(views)
    in_up = wires.inbox(LEVELS + 1)
    in_down = wires.inbox(LEVELS + 1)
    in_mcot = wires.inbox(4)
    in_att = wires.inbox(views)
    in_two = wires.inbox(4)
    in_part = [wires.inbox(5), wires.inbox(5)]
    in_core = [wires.inbox(1), wires.inbox(1)]
    in_grad = [wires.inbox(3), wires.inbox(3)]
    in_acot, in_pc = in_ids, in_att
    in_dw = wires.inbox(3)
    in_do = wires.inbox(3)
    in_do_z = wires.inbox(LEVELS)
    in_plane = wires.inbox(views)
    in_query = wires.inbox(views)
    in_cross = wires.inbox(views)
    in_mate = [wires.inbox(1) for unused in range(3)]
    in_out = [wires.inbox(views), wires.inbox(views)]
    in_out_mate = wires.inbox(1)
    in_gain = wires.inbox(seqs)
    in_gains = in_normed
    to_view = [wires.bulk() for unused in range(5)]
    to_mate_w = [wires.bulk() for unused in range(3)]
    to_mate_o = wires.bulk()

    def z_cast(src, dst, slot):
        wires.send(src, dst, slot, level(z_pair))
        wires.send(src, dst, slot, level(z_two))
        wires.send(src, dst, slot, level(z_flip), when=inner)

    def z_relay(ref, slot):
        wires.send(ref, ref, slot, level(z_pair), when=inner)

    barrier = pltpu.get_barrier_semaphore()
    greeted = [(s, p) for p in view_peers] + [(p, v) for p in seq_peers]
    for device in greeted:
        pl.semaphore_signal(barrier, inc=1, device_id=device, device_id_type=MESH)

    loads, kept = [], []

    def load(src, dst):
        copy = pltpu.make_async_copy(src, dst, k.local_sem.at[len(loads)])
        copy.start()
        loads.append(copy)
        return copy

    up_slot = at((c * 4 + y * 2 + high) * hidden, hidden)
    load_tok = load(tok_hbm, tok)
    load_cot = load(cot_hbm, out_cot)
    load_up = load(up_hbm, k.up.at[up_slot])
    load_down = load(down_hbm, k.down.at[up_slot])
    load_own = [
        load(w_hbm.at[:, at(t * width + v * own, own)], k.w_own.at[:, pl.ds(t * own, own)])
        for t in range(3)
    ]
    load_wo = load(wo_hbm, k.wo)
    load_w = load(w_hbm, k.w_full)

    gain_one = gain_one_ref[...].astype(f3).reshape(1, width)
    gain_two = gain_two_ref[...].astype(f3).reshape(1, width)
    load_tok.wait()
    unit, _ = norm_stats(tok[...].astype(f3))
    k.normed[at(v * rows, rows), :] = (unit * gain_one).astype(bf)
    per = rows // block
    lane = lax.broadcasted_iota(jnp.int32, (1, 128), 1)
    scenes = jnp.zeros((1, 128), jnp.int32)
    for m in range(per):
        mine = jnp.broadcast_to(ids[:, m * block : m * block + 1], (1, 128))
        scenes = jnp.where(lane == v * per + m, mine, scenes)
    k.ids_all[v] = jnp.broadcast_to(scenes, (8, 128))
    live = jnp.transpose(jnp.broadcast_to(alive[...].astype(f3), (rows, rows)))[:, :1]
    pl.semaphore_wait(barrier, len(greeted))

    def view_rows(ref, j):
        return ref.at[at(j * rows, rows)]

    for p in view_peers:
        wires.send(k.ids_all.at[v], k.ids_all.at[v], in_ids + v, (s, p), bulk=to_view[0])

    def normed_half(j, i):
        return k.normed.at[at(j * rows + i * (rows // 2), rows // 2)], in_normed + 2 * j + i

    for i in range(2):
        mine, slot = normed_half(v, i)
        wires.send(mine, mine, slot, (s, y_v))
    for zt in (z_pair, z_two):
        for i in range(2):
            mine, slot = normed_half(v, i)
            wires.send(mine, mine, slot, level(zt))
    for i in range(2):
        mine, slot = normed_half(v, i)
        wires.send(mine, mine, slot, level(z_flip), when=inner)
    load_cot.wait()
    mcot_own = at(own_slot * rows, rows)
    k.mixed_cot[mcot_own, :] = (live * out_cot[...].astype(f3)).astype(bf)

    def slot_rows(ref, slot):
        return ref.at[at(slot * rows, rows)]

    def square_send(ref, base, slot, device):
        wires.send(slot_rows(ref, slot), slot_rows(ref, slot), base + slot, device)

    def square_relay(ref, base):
        wires.wait(slot_rows(ref, pair_slot), base + pair_slot)
        square_send(ref, base, pair_slot, (x_s, v))

    square_send(k.mixed_cot, in_mcot, own_slot, (x_s, v))

    for p in view_peers:
        wires.wait(k.ids_all.at[p], in_ids + p)
    count = SLOTS * SCENE_BLOCKS
    scene_row = k.ids_all[0][:1]
    for j in range(1, views):
        scene_row = scene_row + k.ids_all[j][:1]
    big = lax.broadcasted_iota(jnp.int32, (128, 128), 0)
    wide = lax.broadcasted_iota(jnp.int32, (128, 128), 1)
    scene_mat = jnp.broadcast_to(scene_row, (128, 128))
    scene_col = jnp.transpose(scene_mat)
    ahead = (scene_col < scene_mat) | ((scene_col == scene_mat) & (big < wide))
    place = jnp.sum(jnp.where(ahead & (big < count), 1, 0), axis=0, keepdims=True)
    place_col = jnp.transpose(jnp.broadcast_to(place, (128, 128)))
    hit = jnp.where((place_col == wide) & (big < count), big, 0)
    source = jnp.sum(hit, axis=0, keepdims=True)
    k.order_vm[0:8, :] = jnp.broadcast_to(source, (8, 128))
    k.order_vm[8:16, :] = jnp.broadcast_to(place, (8, 128))
    to_scalar = load(k.order_vm, k.order_sm)

    for copy in load_own:
        copy.wait()

    def mlp_slot(ref, yt, ht):
        return ref.at[at((c * 4 + yt * 2 + ht) * hidden, hidden)]

    def send_mlp(ref, base, device):
        mine = mlp_slot(ref, y, high)
        wires.send(mine, mine, base + y * 2 + high, device)

    def mlp_relay(ref, base):
        there = mlp_slot(ref, y, 1 - high)
        wires.wait(there, base + y * 2 + 1 - high)
        wires.send(there, there, base + y * 2 + 1 - high, (s, y_v))

    def core_exchange(ref, base):
        for ht in (high, 1 - high):
            wires.wait(mlp_slot(ref, 1 - y, ht), base + (1 - y) * 2 + ht)
        mine = ref.at[at(c * half, half)]
        wires.send(mine, mine, base + LEVELS, (c_s, v))

    def project(j):
        k.qkv[at(j * rows, rows), :] = dot_nn(k.normed[at(j * rows, rows), :], k.w_own[...]).astype(bf)

    project(v)
    for zt in others_z:
        j = zt * 2 + y
        for i in range(2):
            there, slot = normed_half(j, i)
            wires.wait(there, slot)
            if zt is z_two:
                z_relay(there, slot)
            wires.send(there, there, slot, (s, y_v))
        if zt is z_two:
            load_up.wait()
            send_mlp(k.up, in_up, level(z_two))
            square_send(k.mixed_cot, in_mcot, own_slot, (s, pair_v))
        project(j)
    send_mlp(k.up, in_up, (s, y_v))
    for zt in [z] + others_z:
        j = zt * 2 + 1 - y
        for i in range(2):
            wires.wait(*normed_half(j, i))
        project(j)
    to_scalar.wait()

    def reorder(dst, src, row):
        blocks = src.reshape(count, block, src.shape[1])

        def step(i, unused):
            from_block = k.order_sm[row, i]
            dst[at(i * block, block), :] = blocks[from_block].astype(dst.dtype)
            return unused

        lax.fori_loop(0, count, step, 0, unroll=8)

    reorder(k.qkv_s, k.qkv, 0)

    head_lane = lax.broadcasted_iota(jnp.int32, (scene, own), 1) // HEAD_DIM

    def attend(g, unused):
        here = at(g * scene, scene)
        queries, keys, values = (k.qkv_s[here, pl.ds(t * own, own)] for t in range(3))
        result = jnp.zeros((scene, own), f3)
        for e in range(2):
            chosen = jnp.where(head_lane == e, queries, jnp.zeros_like(queries))
            weights = jnp.exp(dot_inner(chosen, keys) * scale)
            total = jnp.sum(weights, axis=-1, keepdims=True)
            k.weights[g * 2 + e] = weights
            k.totals[g * 2 + e] = total
            mixed = dot_nn(weights.astype(bf), values) / total
            result = jnp.where(head_lane == e, mixed, result)
        k.att_s[here, :] = result
        return unused

    lax.fori_loop(0, SLOTS, attend, 0)
    reorder(k.att, k.att_s, 8)
    own_cols = at(v * own, own)
    for p in view_peers:
        wires.send(view_rows(k.att, p), k.att_tok.at[:, own_cols], in_att + v, (s, p), bulk=to_view[1])
    square_relay(k.mixed_cot, in_mcot)
    mlp_relay(k.up, in_up)
    load_down.wait()
    send_mlp(k.down, in_down, level(z_two))
    send_mlp(k.down, in_down, (s, y_v))
    k.att_tok[:, own_cols] = k.att[at(v * rows, rows), :]


    load_wo.wait()
    for p in view_peers:
        wires.wait(k.att_tok.at[:, at(p * own, own)], in_att + p)
    tile = 256
    for n in range(width // tile):
        cols = pl.ds(n * tile, tile)
        k.middle[:, cols] = tok[:, cols].astype(f3) + live * dot_nn(k.att_tok[...], k.wo[:, cols])
    unit_two, _ = norm_stats(k.middle[...])
    k.normed_two[mcot_own, :] = (unit_two * gain_two).astype(bf)
    until_two = wires.total
    for device in ((s, pair_v), (x_s, v)):
        square_send(k.normed_two, in_two, own_slot, device)

    core_exchange(k.up, in_up)
    wires.wait(k.up.at[at((1 - c) * half, half)], in_up + LEVELS)

    def hidden_tiles(slot):
        here = at(slot * rows, rows)

        def step(n, unused):
            cols = at(n * tile, tile)
            pre = dot_inner(k.normed_two[here, :], k.up[cols, :])
            below = 0.5 + 0.5 * lax.erf(pre * (0.5**0.5))
            k.act[here, cols] = (pre * below).astype(bf)
            k.slope[here, cols] = below + pre * (jnp.exp(-0.5 * pre * pre) * (0.5 / math.pi) ** 0.5)
            return unused

        lax.fori_loop(0, mlp_rows // tile, step, 0)

    hidden_tiles(own_slot)
    mlp_relay(k.down, in_down)
    square_relay(k.normed_two, in_two)
    hidden_tiles(pair_slot)
    for slot in (x_slot, far_slot):
        wires.wait(slot_rows(k.normed_two, slot), in_two + slot)
        hidden_tiles(slot)

    def grad_tiles(left, right, start, dst):
        def step(n, unused):
            there = at(n * tile, tile)
            dst[there, :] = dot_outer(left[:, at(start + n * tile, tile)], right[...]).astype(dst.dtype)
            return unused

        lax.fori_loop(0, half // tile, step, 0)

    passed = []

    def grad_halves(which, left, right):
        grad_tiles(left, right, (1 - c) * half, k.grad_pass.at[which])
        passed.append(wires.send(k.grad_pass.at[which], k.grad_core.at[which], in_core[which], (c_s, v)))
        grad_tiles(left, right, c * half, k.grad_keep.at[which])

    for slot in (x_slot, far_slot):
        wires.wait(slot_rows(k.mixed_cot, slot), in_mcot + slot)
    core_exchange(k.down, in_down)
    grad_halves(0, k.act, k.mixed_cot)

    def grad_sum(which, start, size):
        there = at(start, size)
        return k.grad_keep[which, there, :].astype(f3) + k.grad_core[which, there, :].astype(f3)

    def grads_to_y(which):
        wires.wait(k.grad_core.at[which], in_core[which])
        wires.sent(passed[which])
        for i, ht in enumerate((1 - high, high)):
            start = ((1 - y) * 2 + ht) * hidden
            there = at(start, hidden)
            k.grad_pass[which, there, :] = grad_sum(which, start, hidden).astype(bf)
            wires.send(k.grad_pass.at[which, there], k.grad_y.at[which, i], in_grad[which] + i, (s, y_v))

    def grad_block(which, i, ht):
        wires.wait(k.grad_y.at[which, i], in_grad[which] + i)
        return grad_sum(which, (y * 2 + ht) * hidden, hidden) + k.grad_y[which, i].astype(f3)

    def grads_to_z(which):
        there = at((y * 2 + 1 - high) * hidden, hidden)
        k.grad_pass[which, there, :] = grad_block(which, 0, 1 - high).astype(bf)
        wires.send(k.grad_pass.at[which, there], k.grad_z.at[which], in_grad[which] + 2, level(z_two))

    def collect(which, dst):
        total = grad_block(which, 1, high)
        wires.wait(k.grad_z.at[which], in_grad[which] + 2)
        dst[...] = total + k.grad_z[which].astype(f3)


    wires.wait(k.down.at[at((1 - c) * half, half)], in_down + LEVELS)

    def cot_tile(n, unused):
        cols = at(n * tile, tile)
        up_to = dot_inner(k.mixed_cot[...], k.down[cols, :])
        k.hid_cot[:, cols] = (up_to * k.slope[:, cols]).astype(bf)
        return unused

    lax.fori_loop(0, mlp_rows // tile, cot_tile, 0)

    strip = width // 2

    def strip_cols(i):
        return pl.ds(i * strip, strip)

    def part_tiles(which, left, right):
        for i in range(2):

            def step(n, unused):
                cols = at(i * strip + n * tile, tile)
                k.part_all[:, cols] = dot_nn(left[...], right[:, cols])
                return unused

            lax.fori_loop(0, strip // tile, step, 0)
            cols = strip_cols(i)
            k.part_out[which, 0, :, cols] = k.part_all[at(far_slot * rows, rows), cols].astype(bf)
            there = k.part_out.at[which, 0, :, cols], k.part_in.at[which, 0, :, cols]
            wires.send(*there, in_part[which] + i, (x_s, v))
        k.part_out[which, 1] = k.part_all[at(x_slot * rows, rows), :].astype(bf)
        wires.send(k.part_out.at[which, 1], k.part_in.at[which, 1], in_part[which] + 2, (x_s, v))
        for i, slot in enumerate((own_slot, pair_slot)):
            k.part_own[which, i] = k.part_all[at(slot * rows, rows), :]

    def part_join(which):
        for i in range(2):
            cols = strip_cols(i)
            wires.wait(k.part_in.at[which, 0, :, cols], in_part[which] + i)
            joined = k.part_own[which, 1, :, cols] + k.part_in[which, 0, :, cols].astype(f3)
            k.part_out[which, 2, :, cols] = joined.astype(bf)
            there = k.part_out.at[which, 2, :, cols], k.part_in.at[which, 2, :, cols]
            wires.send(*there, in_part[which] + 3 + i, (s, pair_v))

    grads_to_y(0)
    part_tiles(0, k.hid_cot, k.up)
    grad_halves(1, k.hid_cot, k.normed_two)
    part_tiles(1, k.act, k.down)
    part_join(0)
    grads_to_y(1)

    def part_sum(which):
        total = k.part_own[which, 0]
        wires.wait(k.part_in.at[which, 1], in_part[which] + 2)
        for i in range(2):
            wires.wait(k.part_in.at[which, 2, :, strip_cols(i)], in_part[which] + 3 + i)
        for i in (1, 2):
            total = total + k.part_in[which, i].astype(f3)
        return total

    unit_two, inverse_two = norm_stats(k.middle[...])
    wires.settle(until_two)
    cot_two = part_sum(0)
    until_acot = wires.total
    k.gain_own[1:2, :] = jnp.sum(cot_two * unit_two, axis=0, keepdims=True)
    middle_cot = out_cot[...].astype(f3) + norm_back(cot_two, unit_two, inverse_two, gain_two)
    tokens_grad[...] = middle_cot
    k.branch[...] = (live * middle_cot).astype(bf)
    for n in range(width // tile):
        k.acot_tok[:, pl.ds(n * tile, tile)] = dot_inner(
            k.branch[...], k.wo[pl.ds(n * tile, tile), :]
        ).astype(bf)
    for p in view_peers:
        wires.send(k.acot_tok.at[:, at(p * own, own)], view_rows(k.acot, v), in_acot + v, (s, p), bulk=to_view[2])
    k.acot[at(v * rows, rows), :] = k.acot_tok[:, own_cols]

    o_half, o_quarter, o_eighth = width // 2, width // 4, width // 8
    o_piece = o_eighth // LEVELS

    def outer_rows(start, dst, dtype):
        def step(n, unused):
            there = at(n * tile, tile)
            left = k.att_tok[:, at(start + n * tile, tile)]
            dst[there, :] = dot_outer(left, k.branch[...]).astype(dtype)
            return unused

        lax.fori_loop(0, o_half // tile, step, 0)

    outer_rows((1 - c) * o_half, k.do_core, bf)
    wires.send(k.do_core, k.do_core_in, in_do, (c_s, v))
    outer_rows(c * o_half, k.do_keep, f3)
    wires.wait(k.do_core_in, in_do)
    k.do_keep[...] = k.do_keep[...] + k.do_core_in[...].astype(f3)
    k.do_y[...] = k.do_keep[at((1 - y) * o_quarter, o_quarter), :].astype(bf)
    wires.send(k.do_y, k.do_y_in, in_do + 1, (s, y_v))

    for p in view_peers:
        wires.wait(view_rows(k.acot, p), in_acot + p)
    part_join(1)
    reorder(k.acot_s, k.acot, 0)

    def attend_back(g, unused):
        here = at(g * scene, scene)
        queries, keys, values = (k.qkv_s[here, pl.ds(t * own, own)] for t in range(3))
        cots = k.acot_s[here, :]
        agree = cots.astype(f3) * k.att_s[here, :]
        outs = [jnp.zeros((scene, own), f3) for t in range(3)]
        for e in range(2):
            mine = head_lane == e
            delta = jnp.sum(jnp.where(mine, agree, 0.0), axis=-1, keepdims=True)
            chosen = jnp.where(mine, cots, jnp.zeros_like(cots))
            weights = k.weights[g * 2 + e]
            inverse = 1.0 / k.totals[g * 2 + e]
            weights_cot = dot_inner(chosen, values)
            score_cot = (weights * inverse * (weights_cot - delta)).astype(bf)
            shared = (cots.astype(f3) * inverse).astype(bf)
            new = (
                dot_nn(score_cot, keys) * scale,
                dot_outer(score_cot, queries) * scale,
                dot_outer(weights.astype(bf), shared),
            )
            outs = [jnp.where(mine, fresh, old) for fresh, old in zip(new, outs)]
        for t in range(3):
            k.pc_s[here, pl.ds(t * own, own)] = outs[t].astype(bf)
        return unused

    lax.fori_loop(0, SLOTS, attend_back, 0)
    pc_blocks = k.pc_s.reshape(count, block, 3 * own)

    def unsort(i, unused):
        found = pc_blocks[k.order_sm[8, i]]
        k.pc_flat[at(i * block, block), :] = found
        for t in range(3):
            k.pc[t, at(i * block, block), :] = found[:, t * own : (t + 1) * own]
        return unused

    lax.fori_loop(0, count, unsort, 0, unroll=8)
    for p in view_peers:
        wires.send(k.pc.at[:, at(p * rows, rows)], k.pc_tok.at[:, :, own_cols], in_pc + v, (s, p), bulk=to_view[3])
    for t in range(3):
        k.pc_tok[t, :, own_cols] = k.pc[t, at(v * rows, rows), :]

    part = width // seqs

    def own_dw(row_block):
        whole = dot_outer(k.normed[:, at(row_block * part, part)], k.pc_flat[...])
        return [whole[:, t * own : (t + 1) * own] for t in range(3)]

    for i, xt in enumerate((1 - x, x)):
        for t, value in enumerate(own_dw(xt * 2 + 1 - c)):
            k.dw_out[i, t] = value.astype(bf)
        wires.send(k.dw_out.at[i], k.dw_in.at[i], in_dw + i, (c_s, v))
    cross_dw = own_dw(x_s)
    wires.wait(k.dw_in.at[0], in_dw)
    for t in range(3):
        k.dw_x[t] = (cross_dw[t] + k.dw_in[0, t].astype(f3)).astype(bf)
    wires.send(k.dw_x, k.dw_in.at[2], in_dw + 2, (x_s, v))
    mine_dw = own_dw(s)
    wires.wait(k.dw_in.at[1], in_dw + 1)
    wires.settle(until_acot)
    wires.wait(k.dw_in.at[2], in_dw + 2)
    for t in range(3):
        total = mine_dw[t] + k.dw_in[1, t].astype(f3) + k.dw_in[2, t].astype(f3)
        k.dw_own[t] = total.astype(bf)

    def w_at(q, j, first, last):
        return w_grad.at[pl.ds(first, last - first), at(q * part, part), at(j * own, own)]

    def w_plane(j):
        return w_at(s, j, 0, 3)

    def w_query(j):
        return w_at(x_s, j, 0, 1)

    def w_cross(q, j):
        return w_at(q, j, 1, 3)

    wires.send(k.dw_own.at[pl.ds(0, 1)], w_at(s, v, 0, 1), in_query + v, (x_s, v))
    wires.send(k.dw_own, w_plane(v), in_plane + v, (s, y_v))
    z_cast(k.dw_own, w_plane(v), in_plane + v)
    wires.send(k.dw_own.at[pl.ds(1, 2)], w_cross(s, v), in_cross + v, (x_s, v))
    wires.send(k.dw_own, w_plane(v), in_mate[0], (c_s, v), bulk=to_mate_w[0])
    kept.append(load(k.dw_own, w_plane(v)))

    wires.wait(w_query(v), in_query + v)
    wires.send(w_query(v), w_query(v), in_query + v, (s, y_v))
    z_cast(w_query(v), w_query(v), in_query + v)
    wires.send(w_query(v), w_query(v), in_mate[1], (c_s, v), bulk=to_mate_w[1])

    wires.wait(k.do_y_in, in_do + 1)
    o_mine = at(y * o_quarter, o_quarter)
    k.do_keep[o_mine, :] = k.do_keep[o_mine, :] + k.do_y_in[...].astype(f3)
    k.do_x[...] = k.do_keep[at(y * o_quarter + (1 - x) * o_eighth, o_eighth), :].astype(bf)
    wires.send(k.do_x, k.do_x_in, in_do + 2, (x_s, v))
    def o_at(q, j):
        at_c, at_x, at_y, at_z = q % 2, q // 2, j % 2, j // 2
        return o_grad.at[at(at_c * o_half + at_y * o_quarter + at_x * o_eighth + at_z * o_piece, o_piece)]

    def to_mate(which, ref):
        wires.send(ref, ref, in_mate[which], (c_s, v), bulk=to_mate_w[which])

    def pass_plane(zt, row_y):
        j = zt * 2 + row_y
        wires.wait(w_plane(j), in_plane + j)
        if row_y is y:
            if zt is z_two:
                z_relay(w_plane(j), in_plane + j)
            wires.send(w_plane(j), w_plane(j), in_plane + j, (s, y_v))
        wires.send(w_cross(s, j), w_cross(s, j), in_cross + j, (x_s, v))
        to_mate(0, w_plane(j))

    def pass_query(zt, row_y):
        j = zt * 2 + row_y
        wires.wait(w_query(j), in_query + j)
        if row_y is y:
            if zt is z_two:
                z_relay(w_query(j), in_query + j)
            wires.send(w_query(j), w_query(j), in_query + j, (s, y_v))
        to_mate(1, w_query(j))

    across = 1 - y
    pass_plane(z, across)

    load_w.wait()
    for p in view_peers:
        wires.wait(k.pc_tok.at[:, :, at(p * own, own)], in_pc + p)

    def back_tile(n, unused):
        cols = at(n * tile, tile)
        total = dot_inner(k.pc_tok[0], k.w_full[cols, pl.ds(0, width)])
        for t in range(1, 3):
            total = total + dot_inner(k.pc_tok[t], k.w_full[cols, pl.ds(t * width, width)])
        k.part_own[0, 0, :, cols] = total
        return unused

    lax.fori_loop(0, width // tile, back_tile, 0)
    unit_one, inverse_one = norm_stats(tok[...].astype(f3))
    cot_one = k.part_own[0, 0]
    k.gain_own[0:1, :] = jnp.sum(cot_one * unit_one, axis=0, keepdims=True)
    k.gain_own[2:8, :] = jnp.zeros((6, width), f3)
    tokens_grad[...] = tokens_grad[...] + norm_back(cot_one, unit_one, inverse_one, gain_one)
    for p in seq_peers:
        wires.send(k.gain_own, k.gain_in.at[s], in_gain + s, (p, v))
    kept.append(load(tokens_grad, tokens_hbm))

    wires.wait(k.do_x_in, in_do + 2)
    total = k.do_keep[at(y * o_quarter + x * o_eighth, o_eighth), :] + k.do_x_in[...].astype(f3)
    k.do_z[...] = total.astype(bf)

    def o_level(zt):
        return at(zt * o_piece, o_piece)

    for zt in others_z:
        wires.send(k.do_z.at[o_level(zt)], k.do_z_in.at[z], in_do_z + z, level(zt))

    pass_plane(z_pair, y)
    pass_plane(z_two, y)
    pass_query(z, across)
    pass_plane(z_pair, across)
    pass_query(z_pair, y)
    pass_query(z_two, y)
    pass_plane(z_flip, y)
    pass_plane(z_two, across)
    there = at((y * 2 + 1 - high) * hidden, hidden)
    k.grad_pass[1, there, :] = grad_block(1, 0, 1 - high).astype(bf)
    kept.append(load(k.grad_pass.at[1, there], up_away))
    up_grad[...] = grad_block(1, 1, high)
    kept.append(load(up_grad, up_part))
    total = k.do_keep[at(y * o_quarter + x * o_eighth + z * o_piece, o_piece), :]
    total = total + k.do_x_in[o_level(z), :].astype(f3)
    for zt in others_z:
        wires.wait(k.do_z_in.at[zt], in_do_z + zt)
        total = total + k.do_z_in[zt].astype(f3)
    k.do_own[...] = total.astype(bf)
    wires.send(k.do_own, o_at(s, v), in_out[0] + v, (s, y_v))
    z_cast(k.do_own, o_at(s, v), in_out[0] + v)
    wires.send(k.do_own, o_at(s, v), in_out[1] + v, (x_s, v))
    wires.send(k.do_own, o_at(s, v), in_out_mate, (c_s, v), bulk=to_mate_o)
    kept.append(load(k.do_own, o_at(s, v)))
    pass_query(z_flip, y)
    pass_plane(z_flip, across)
    for zt in others_z:
        pass_query(zt, across)

    total = k.gain_own[...]
    for p in seq_peers:
        wires.wait(k.gain_in.at[p], in_gain + p)
        total = total + k.gain_in[p]
    k.gain_sum[...] = total
    for p in view_peers:
        wires.send(k.gain_sum, k.gain_all.at[v], in_gains + v, (s, p), bulk=to_view[4])

    def out_mate(q, j):
        wires.send(o_at(q, j), o_at(q, j), in_out_mate, (c_s, v), bulk=to_mate_o)

    def pass_out(zt, row_y):
        j = zt * 2 + row_y
        slot = in_out[0] + j
        wires.wait(o_at(s, j), slot)
        if row_y is y:
            if zt is z_two:
                z_relay(o_at(s, j), slot)
            wires.send(o_at(s, j), o_at(s, j), slot, (s, y_v))
        wires.send(o_at(s, j), o_at(s, j), in_out[1] + j, (x_s, v))
        out_mate(s, j)

    for zt in others_z:
        pass_out(zt, y)
    grads_to_z(0)
    for zt in [z] + others_z:
        pass_out(zt, across)

    layer_out[...] = (k.middle[...] + live * part_sum(1)).astype(bf)
    kept.append(load(layer_out, layer_hbm))
    by_arrival = [v] + [zt * 2 + y for zt in others_z] + [zt * 2 + across for zt in [z] + others_z]
    for j in by_arrival:
        wires.wait(w_cross(x_s, j), in_cross + j)
        to_mate(2, w_cross(x_s, j))
    for j in by_arrival:
        wires.wait(o_at(x_s, j), in_out[1] + j)
        out_mate(x_s, j)

    total = k.gain_sum[...]
    for p in view_peers:
        wires.wait(k.gain_all.at[p], in_gains + p)
        total = total + k.gain_all[p]
    gains[...] = total

    collect(0, down_grad)
    kept.append(load(down_grad, down_hbm_out))
    def w_rows(q, first, last):
        return w_grad.at[pl.ds(first, last - first), at(q * part, part)]

    def o_core(core):
        return o_grad.at[at(core * o_half, o_half)]

    wires.settle(wires.total)
    for whole, lane in (
        (k.ids_all.at[pl.ds(0, views - 1)], to_view[0]),
        (k.att.at[pl.ds(0, length - rows)], to_view[1]),
        (k.acot.at[pl.ds(0, length - rows)], to_view[2]),
        (k.pc.at[:, pl.ds(0, length - rows)], to_view[3]),
        (k.gain_all.at[pl.ds(0, views - 1)], to_view[4]),
        (w_rows(s, 0, 3), to_mate_w[0]),
        (w_rows(x_s, 0, 1), to_mate_w[1]),
        (w_rows(x_s, 1, 3), to_mate_w[2]),
        (o_core(c), to_mate_o),
    ):
        wires.settle_bulk(whole, lane)
    wires.wait(w_rows(c_s, 0, 3), in_mate[0])
    wires.wait(w_rows(xc_s, 0, 1), in_mate[1])
    wires.wait(w_rows(xc_s, 1, 3), in_mate[2])
    wires.wait(o_core(1 - c), in_out_mate)
    for copy in kept:
        copy.wait()


FINISH_STEPS = 8


def finish_kernel(*refs):
    (layer_in, tokens_in, gains, w_in, o_in, down_in) = refs[:6]
    (layer_out, tokens_grad, gain_one, w_out, o_out, gain_two, down_out) = refs[6:13]
    (layer, tokens, down, w_narrow, o_narrow, w_wide, o_wide, in_sem, out_sem) = refs[13:]
    width = o_in.shape[0]
    tall = width // FINISH_STEPS
    asis = ((layer_in, layer, layer_out), (tokens_in, tokens, tokens_grad), (down_in, down, down_out))

    def rows(i):
        return pl.ds(i * tall, tall)

    def start(src, dst, sem):
        copy = pltpu.make_async_copy(src, dst, sem)
        copy.start()
        return copy

    reads, writes = [], []
    for i in range(FINISH_STEPS):
        reads.append(start(w_in.at[:, rows(i)], w_narrow.at[:, rows(i)], in_sem.at[2 * i]))
        reads.append(start(o_in.at[rows(i)], o_narrow.at[rows(i)], in_sem.at[2 * i + 1]))
    late = [start(src, mid, in_sem.at[2 * FINISH_STEPS + i]) for i, (src, mid, dst) in enumerate(asis)]
    gain_one[...] = gains[0:1, :].reshape(width)
    gain_two[...] = gains[1:2, :].reshape(width)
    for i in range(FINISH_STEPS):
        reads[2 * i].wait()
        for t in range(3):
            w_wide[rows(i), t * width : (t + 1) * width] = w_narrow[t, rows(i), :].astype(jnp.float32)
        writes.append(start(w_wide.at[rows(i)], w_out.at[rows(i)], out_sem.at[2 * i]))
        reads[2 * i + 1].wait()
        o_wide[rows(i), :] = o_narrow[rows(i), :].astype(jnp.float32)
        writes.append(start(o_wide.at[rows(i)], o_out.at[rows(i)], out_sem.at[2 * i + 1]))
    for i, (src, mid, dst) in enumerate(asis):
        late[i].wait()
        writes.append(start(mid, dst, out_sem.at[2 * FINISH_STEPS + i]))
    for copy in writes:
        copy.wait()


def fused(
    seqs,
    views,
    tokens,
    scene_ids,
    live_mask,
    out_grad,
    attention_gain,
    input_weight,
    output_weight,
    feedforward_gain,
    up_weight,
    down_weight,
):
    rows, width = tokens.shape[1:]
    hidden = up_weight.shape[0]
    spec = scratch_of(rows, width, seqs, views, hidden)
    vmem = pl.BlockSpec(memory_space=pltpu.VMEM)
    anywhere = pl.BlockSpec(memory_space=pl.ANY)
    shape = jax.ShapeDtypeStruct
    bf, f3 = jnp.bfloat16, jnp.float32
    layer_raw, tokens_raw, gains, w_raw, o_raw, up_part, up_away, down_raw = pl.pallas_call(
        functools.partial(layer_kernel, tuple(spec), seqs, views),
        out_shape=(
            shape((rows, width), bf),
            shape((rows, width), f3),
            shape((8, width), f3),
            shape((3, width, width), bf),
            shape((width, width), bf),
            shape((hidden, width), f3),
            shape((hidden, width), bf),
            shape((hidden, width), f3),
        ),
        in_specs=[anywhere, vmem, vmem, anywhere, vmem, vmem] + [anywhere] * 4,
        out_specs=(anywhere, anywhere, vmem) + (anywhere,) * 5,
        scratch_shapes=list(spec.values()),
        compiler_params=pltpu.CompilerParams(
            collective_id=0, has_side_effects=True, vmem_limit_bytes=67043328
        ),
        name="layer",
    )(
        tokens[0],
        scene_ids,
        live_mask,
        out_grad[0],
        attention_gain,
        feedforward_gain,
        input_weight,
        output_weight,
        up_weight,
        down_weight,
    )
    shift = [(j, (j + views // 2) % views) for j in range(views)]
    up_grad = up_part + lax.ppermute(up_away, "view", shift).astype(f3)
    layer_out, tokens_grad, gain_one, w_grad, o_grad, gain_two, down_grad = pl.pallas_call(
        finish_kernel,
        out_shape=(
            shape((rows, width), bf),
            shape((rows, width), f3),
            shape((width,), f3),
            shape((width, 3 * width), f3),
            shape((width, width), f3),
            shape((width,), f3),
            shape((hidden, width), f3),
        ),
        in_specs=[anywhere] * 2 + [vmem] + [anywhere] * 3,
        out_specs=(anywhere, anywhere, vmem, anywhere, anywhere, vmem, anywhere),
        scratch_shapes=[
            pltpu.VMEM((rows, width), bf),
            pltpu.VMEM((rows, width), f3),
            pltpu.VMEM((hidden, width), f3),
            pltpu.VMEM((3, width, width), bf),
            pltpu.VMEM((width, width), bf),
            pltpu.VMEM((width, 3 * width), f3),
            pltpu.VMEM((width, width), f3),
            pltpu.SemaphoreType.DMA((2 * FINISH_STEPS + 4,)),
            pltpu.SemaphoreType.DMA((2 * FINISH_STEPS + 4,)),
        ],
        cost_estimate=pl.CostEstimate(
            flops=4 * width * width, transcendentals=0, bytes_accessed=28 * width * width
        ),
        name="finish",
    )(layer_raw, tokens_raw, gains, w_raw, o_raw, down_raw)
    return (
        layer_out[None],
        tokens_grad[None],
        gain_one,
        w_grad,
        o_grad,
        gain_two,
        up_grad,
        down_grad,
    )


def solution(mesh):
    seqs, views = mesh.shape["seq"], mesh.shape["view"]
    small = seqs == 4 and views == 2 * LEVELS and HEADS == 2 * views
    body = functools.partial(fused, seqs, views) if small else shards
    return jax.shard_map(
        body,
        mesh=mesh,
        in_specs=(
            P("seq", "view", None),
            P("seq", "view"),
            P("seq", "view"),
            P("seq", "view", None),
            P(),
            P(),
            P(),
            P(),
            P(("seq", "view"), None),
            P(("seq", "view"), None),
        ),
        out_specs=(
            P("seq", "view", None),
            P("seq", "view", None),
            P(),
            P(),
            P(),
            P(),
            P(("seq", "view"), None),
            P(("seq", "view"), None),
        ),
        check_vma=False,
    )
```

```python
import functools
import math
import types

import jax
import jax.numpy as jnp
from jax import lax
from jax.experimental import pallas as pl
from jax.experimental.pallas import tpu as pltpu
from jax.sharding import PartitionSpec as P

HEADS = 16
HEAD_DIM = 64


EPS = 1e-05
NEGATIVE = -1e30
MESH = pl.DeviceIdType.MESH
SLOTS = 4
SCENE_BLOCKS = 16


def layer_norm(values, gain):
    center = values - jnp.mean(values, axis=-1, keepdims=True)
    spread = jnp.mean(center * center, axis=-1, keepdims=True)
    return center * lax.rsqrt(spread + EPS) * gain


def gelu_exact(values):
    return jax.nn.gelu(values, approximate=False)


def plain_dot(left, right):
    return jnp.dot(left, right, preferred_element_type=jnp.float32)


def dot_inner(left, right):
    return lax.dot_general(
        left, right, (((1,), (1,)), ((), ())), preferred_element_type=jnp.float32
    )


def dot_outer(left, right):
    return lax.dot_general(
        left, right, (((0,), (0,)), ((), ())), preferred_element_type=jnp.float32
    )


def split_heads(values):
    return values.reshape(values.shape[0], HEADS, HEAD_DIM)


def masked_scores(queries, keys, query_tags, key_tags, scale):
    raw = jnp.einsum("qhe,khe->hqk", queries, keys, preferred_element_type=jnp.float32) * scale
    allowed = (query_tags[:, None] == key_tags[None, :])[None]
    return (raw, allowed)


def probabilities(queries, keys, query_tags, key_tags, log_total, scale):
    raw, allowed = masked_scores(queries, keys, query_tags, key_tags, scale)
    return jnp.where(
        allowed, jnp.exp(jnp.where(allowed, raw - log_total[:, :, None], NEGATIVE)), 0.0
    )


def in_blocks(step, carry, piece):
    count = piece[0].shape[0]
    size = math.gcd(count, 512)
    number = count // size
    stacked = tuple((member.reshape((number, size) + member.shape[1:]) for member in piece))

    def inner(state, item):
        members, offset = item
        return (step(state, members, offset * size), None)

    result, unused = lax.scan(inner, carry, (stacked, jnp.arange(number, dtype=jnp.int32)))
    return result


def shards(
    tokens,
    scene_ids,
    live_mask,
    out_grad,
    attention_gain,
    input_weight,
    output_weight,
    feedforward_gain,
    up_weight,
    down_weight,
):
    scale = HEAD_DIM ** (-0.5)
    inputs = tokens[0].astype(jnp.float32)
    rows = inputs.shape[0]
    width = inputs.shape[1]
    tags = scene_ids[0] * 2 + live_mask[0]
    live = live_mask[0].astype(jnp.float32)[:, None]
    every_tag = lax.all_gather(tags, "view", axis=0, tiled=True)
    up_full, down_full = (
        lax.all_gather(up_weight, ("seq", "view"), axis=0, tiled=True),
        lax.all_gather(down_weight, ("seq", "view"), axis=0, tiled=True),
    )
    gain_one = attention_gain.astype(jnp.float32)
    gain_two = feedforward_gain.astype(jnp.float32)
    normed = layer_norm(inputs, gain_one).astype(jnp.bfloat16)
    projected = plain_dot(normed, input_weight).astype(jnp.bfloat16)
    query_flat = projected[:, :width]
    queries = split_heads(query_flat)
    keys_own = projected[:, width : 2 * width]
    values_own = projected[:, 2 * width :]

    def attend_step(carry, piece, start):
        peak, total, accum = carry
        key_piece, value_piece = piece
        count = key_piece.shape[0]
        key_tags = lax.dynamic_slice_in_dim(every_tag, start, count)
        raw, allowed = masked_scores(queries, split_heads(key_piece), tags, key_tags, scale)
        masked = jnp.where(allowed, raw, NEGATIVE)
        new_peak = jnp.maximum(peak, jnp.max(masked, axis=-1))
        weights = jnp.where(allowed, jnp.exp(masked - new_peak[:, :, None]), 0.0)
        factor = jnp.exp(peak - new_peak)
        total = total * factor + jnp.sum(weights, axis=-1)
        update = jnp.einsum(
            "hqk,khe->qhe",
            weights.astype(jnp.bfloat16),
            split_heads(value_piece),
            preferred_element_type=jnp.float32,
        )
        accum = accum * jnp.transpose(factor)[:, :, None] + update
        return (new_peak, total, accum)

    start_state = (
        jnp.full((HEADS, rows), NEGATIVE, jnp.float32),
        jnp.zeros((HEADS, rows), jnp.float32),
        jnp.zeros((rows, HEADS, HEAD_DIM), jnp.float32),
    )
    peak, total, accum = in_blocks(
        attend_step,
        start_state,
        (
            lax.all_gather(keys_own, "view", axis=0, tiled=True),
            lax.all_gather(values_own, "view", axis=0, tiled=True),
        ),
    )
    attended_heads = accum / jnp.transpose(total)[:, :, None]
    log_total = peak + jnp.log(total)
    attended_low = attended_heads.reshape(rows, width).astype(jnp.bfloat16)
    branch = plain_dot(attended_low, output_weight)
    middle = inputs + live * branch
    normed_two = layer_norm(middle, gain_two).astype(jnp.bfloat16)
    hidden = dot_inner(normed_two, up_full)
    activated = gelu_exact(hidden).astype(jnp.bfloat16)
    mixed = plain_dot(activated, down_full)
    layer_out = (middle + live * mixed).astype(jnp.bfloat16)[None]
    out_cot = out_grad[0].astype(jnp.float32)
    mixed_cot = (live * out_cot).astype(jnp.bfloat16)
    down_grad = dot_outer(activated, mixed_cot)
    activated_cot = dot_inner(mixed_cot, down_full)
    hidden_cot = jax.vjp(gelu_exact, hidden)[1](activated_cot)[0].astype(jnp.bfloat16)
    up_grad = dot_outer(hidden_cot, normed_two)
    normed_two_cot = plain_dot(hidden_cot, up_full)
    second_pull = jax.vjp(layer_norm, middle, gain_two)[1]
    middle_part, gain_two_grad = second_pull(normed_two_cot)
    middle_cot = out_cot + middle_part
    branch_cot = (live * middle_cot).astype(jnp.bfloat16)
    output_weight_grad = dot_outer(attended_low, branch_cot)
    attended_cot = dot_inner(branch_cot, output_weight).astype(jnp.bfloat16)
    cot_heads = split_heads(attended_cot)
    delta = jnp.transpose(jnp.sum(cot_heads.astype(jnp.float32) * attended_heads, axis=-1))
    seq_len = every_tag.shape[0]

    def back_step(carry, piece, start):
        query_cot, key_value_cot = carry
        key_piece, value_piece = piece
        count = key_piece.shape[0]
        key_tags = lax.dynamic_slice_in_dim(every_tag, start, count)
        key_heads = split_heads(key_piece)
        value_heads = split_heads(value_piece)
        probs = probabilities(queries, key_heads, tags, key_tags, log_total, scale)
        prob_cot = jnp.einsum(
            "qhe,khe->hqk", cot_heads, value_heads, preferred_element_type=jnp.float32
        )
        score_cot = (probs * (prob_cot - delta[:, :, None])).astype(jnp.bfloat16)
        query_cot = (
            query_cot
            + jnp.einsum("hqk,khe->qhe", score_cot, key_heads, preferred_element_type=jnp.float32)
            * scale
        )
        key_cot = (
            jnp.einsum("hqk,qhe->khe", score_cot, queries, preferred_element_type=jnp.float32)
            * scale
        )
        value_cot = jnp.einsum(
            "hqk,qhe->khe",
            probs.astype(jnp.bfloat16),
            cot_heads,
            preferred_element_type=jnp.float32,
        )
        stacked = jnp.concatenate(
            [key_cot.reshape(count, width), value_cot.reshape(count, width)], axis=1
        )
        earlier = lax.dynamic_slice_in_dim(key_value_cot, start, count)
        key_value_cot = lax.dynamic_update_slice_in_dim(key_value_cot, earlier + stacked, start, 0)
        return (query_cot, key_value_cot)

    back_state = (
        jnp.zeros((rows, HEADS, HEAD_DIM), jnp.float32),
        jnp.zeros((seq_len, 2 * width), jnp.float32),
    )
    query_cot, key_value_cot = in_blocks(
        back_step,
        back_state,
        (
            lax.all_gather(keys_own, "view", axis=0, tiled=True),
            lax.all_gather(values_own, "view", axis=0, tiled=True),
        ),
    )
    own_cot = lax.psum_scatter(key_value_cot, "view", scatter_dimension=0, tiled=True)
    key_cot_own = own_cot[:, :width]
    value_cot_own = own_cot[:, width:]
    projected_cot = jnp.concatenate(
        [query_cot.reshape(rows, width), key_cot_own, value_cot_own], axis=1
    ).astype(jnp.bfloat16)
    input_weight_grad = dot_outer(normed, projected_cot)
    normed_cot = dot_inner(projected_cot, input_weight)
    first_pull = jax.vjp(layer_norm, inputs, gain_one)[1]
    input_part, gain_one_grad = first_pull(normed_cot)
    tokens_grad = (middle_cot + input_part)[None]
    up_part, down_part = (
        lax.psum_scatter(up_grad, ("seq", "view"), scatter_dimension=0, tiled=True),
        lax.psum_scatter(down_grad, ("seq", "view"), scatter_dimension=0, tiled=True),
    )
    summed = lax.psum(
        (gain_one_grad, input_weight_grad, output_weight_grad, gain_two_grad), ("seq", "view")
    )
    return (layer_out, tokens_grad, summed[0], summed[1], summed[2], summed[3], up_part, down_part)


def dot_nn(left, right):
    return lax.dot_general(left, right, (((1,), (0,)), ((), ())), preferred_element_type=jnp.float32)


def at(start, size):
    return pl.ds(pl.multiple_of(start, size), size)


def norm_stats(values):
    mean = jnp.mean(values, axis=-1, keepdims=True)
    center = values - mean
    spread = jnp.mean(center * center, axis=-1, keepdims=True)
    inverse = lax.rsqrt(spread + EPS)
    return center * inverse, inverse


def norm_back(cot, unit, inverse, gain):
    scaled = cot * gain
    first = jnp.mean(scaled, axis=-1, keepdims=True)
    second = jnp.mean(scaled * unit, axis=-1, keepdims=True)
    return inverse * (scaled - first - unit * second)


class Wires:
    def __init__(self, send_sem, recv_sem, peer):
        self.send_sem, self.recv_sem, self.peer = send_sem, recv_sem, peer
        self.free, self.recvs, self.total, self.pending = list(range(SENDS)), 0, 0, []

    def inbox(self, count):
        base = self.recvs
        self.recvs += count
        assert self.recvs <= RECVS
        return base

    def bulk(self):
        return self.free.pop(0)

    def copy(self, src, dst, lane, slot, device):
        return pltpu.make_async_remote_copy(
            src_ref=src,
            dst_ref=dst,
            send_sem=self.send_sem.at[lane],
            recv_sem=self.recv_sem.at[slot],
            device_id=device,
            device_id_type=MESH,
        )

    def send(self, src, dst, slot, device, when=None, bulk=None):
        lane = self.free.pop(0) if bulk is None else bulk
        copy = self.copy(src, dst, lane, slot, device)
        if when is None:
            copy.start()
        else:
            pl.when(when)(copy.start)
        if bulk is None:
            self.pending.append((self.total, copy, when, lane))
            self.total += 1
        return copy

    def finish(self, entry):
        unused, copy, when, lane = entry
        if when is None:
            copy.wait_send()
        else:
            pl.when(when)(copy.wait_send)
        self.free.append(lane)

    def sent(self, copy):
        for entry in [entry for entry in self.pending if entry[1] is copy]:
            self.finish(entry)
        self.pending = [entry for entry in self.pending if entry[1] is not copy]

    def settle(self, until):
        for entry in [entry for entry in self.pending if entry[0] < until]:
            self.finish(entry)
        self.pending = [entry for entry in self.pending if entry[0] >= until]

    def settle_bulk(self, whole, lane):
        self.copy(whole, whole, lane, 0, self.peer).wait_send()

    def wait(self, dst, slot):
        self.copy(dst, dst, 0, slot, self.peer).wait_recv()


SENDS, RECVS, LOCALS = 88, 136, 20
LEVELS = 4


def scratch_of(rows, width, seqs, views, hidden):
    length = rows * views
    own = width // views
    bf, f3 = jnp.bfloat16, jnp.float32
    vm = pltpu.VMEM
    mlp_rows = hidden * seqs * views // 4
    half, quarter, eighth = width // 2, width // 4, width // 8
    return dict(
        tok=vm((rows, width), bf),
        out_cot=vm((rows, width), bf),
        layer_out=vm((rows, width), bf),
        tokens_grad=vm((rows, width), f3),
        up_grad=vm((hidden, width), f3),
        down_grad=vm((hidden, width), f3),
        w_full=vm((width, 3 * width), bf),
        w_own=vm((width, 3 * own), bf),
        wo=vm((width, width), bf),
        up=vm((mlp_rows, width), bf),
        down=vm((mlp_rows, width), bf),
        ids_all=vm((views, 8, 128), jnp.int32),
        order_vm=vm((16, 128), jnp.int32),
        order_sm=pltpu.SMEM((16, 128), jnp.int32),
        normed=vm((length, width), bf),
        qkv=vm((length, 3 * own), bf),
        qkv_s=vm((length, 3 * own), bf),
        weights=vm((2 * SLOTS, length // SLOTS, length // SLOTS), f3),
        totals=vm((2 * SLOTS, length // SLOTS, 1), f3),
        att_s=vm((length, own), f3),
        att=vm((length, own), bf),
        att_tok=vm((rows, width), bf),
        middle=vm((rows, width), f3),
        normed_two=vm((4 * rows, width), bf),
        mixed_cot=vm((4 * rows, width), bf),
        wide=vm((4 * rows, mlp_rows), f3),
        act=vm((4 * rows, mlp_rows), bf),
        hid_cot=vm((4 * rows, mlp_rows), bf),
        part_own=vm((2, 2, rows, width), f3),
        part_out=vm((2, 3, rows, width), bf),
        part_in=vm((2, 3, rows, width), bf),
        grad_keep=vm((2, mlp_rows // 2, width), bf),
        grad_pass=vm((2, mlp_rows // 2, width), bf),
        grad_core=vm((2, mlp_rows // 2, width), bf),
        grad_y=vm((2, 2, hidden, width), bf),
        grad_z=vm((2, hidden, width), bf),
        branch=vm((rows, width), bf),
        acot_tok=vm((rows, width), bf),
        acot=vm((length, own), bf),
        acot_s=vm((length, own), bf),
        pc_s=vm((length, 3 * own), bf),
        pc=vm((3, length, own), bf),
        pc_flat=vm((length, 3 * own), bf),
        pc_tok=vm((3, rows, width), bf),
        dw_out=vm((2, 3, width // seqs, own), bf),
        dw_x=vm((3, width // seqs, own), bf),
        dw_in=vm((3, 3, width // seqs, own), bf),
        dw_own=vm((3, width // seqs, own), bf),
        do_core=vm((half, width), bf),
        do_core_in=vm((half, width), bf),
        do_first=vm((quarter, width), bf),
        do_first_in=vm((quarter, width), bf),
        do_second=vm((eighth, width), bf),
        do_second_in=vm((eighth, width), bf),
        do_z=vm((eighth, width), bf),
        do_z_in=vm((LEVELS, eighth // LEVELS, width), bf),
        do_own=vm((eighth // LEVELS, width), bf),
        gain_own=vm((8, width), f3),
        gain_in=vm((seqs, 8, width), f3),
        gain_sum=vm((8, width), f3),
        gain_all=vm((views, 8, width), f3),
        send_sem=pltpu.SemaphoreType.DMA((SENDS,)),
        recv_sem=pltpu.SemaphoreType.DMA((RECVS,)),
        local_sem=pltpu.SemaphoreType.DMA((LOCALS,)),
    )


def layer_kernel(names, seqs, views, *refs):
    (tok_hbm, ids, alive, cot_hbm, gain_one_ref, gain_two_ref, w_hbm, wo_hbm, up_hbm, down_hbm) = refs[:10]
    (layer_hbm, tokens_hbm, gains, w_grad, o_grad, up_part, up_away, down_hbm_out) = refs[10:18]
    k = types.SimpleNamespace(**dict(zip(names, refs[18:])))
    k.slope = k.part_all = k.do_keep = k.wide
    tok, out_cot = k.tok, k.out_cot
    layer_out, tokens_grad, up_grad, down_grad = k.layer_out, k.tokens_grad, k.up_grad, k.down_grad
    rows, width = tok.shape
    length = rows * views
    own = width // views
    hidden = up_hbm.shape[0]
    mlp_rows = k.up.shape[0]
    half = mlp_rows // 2
    block = length // (SLOTS * SCENE_BLOCKS)
    scene = length // SLOTS
    scale = HEAD_DIM ** (-0.5)
    bf, f3 = jnp.bfloat16, jnp.float32

    s = lax.axis_index("seq")
    v = lax.axis_index("view")
    x, c, z, y = s // 2, s % 2, v // 2, v % 2
    x_s, c_s, xc_s = (1 - x) * 2 + c, x * 2 + (1 - c), (1 - x) * 2 + (1 - c)
    y_v = z * 2 + (1 - y)
    z_pair, z_two, z_flip = z + 1 - 2 * (z % 2), lax.rem(z + 2, LEVELS), LEVELS - 1 - z
    inner = (z == 1) | (z == 2)
    others_z = [z_pair, z_two, z_flip]
    low, high = z % 2, z // 2
    pair_v = z_pair * 2 + y
    own_slot, x_slot = x * 2 + low, (1 - x) * 2 + low
    pair_slot, far_slot = x * 2 + (1 - low), (1 - x) * 2 + (1 - low)
    view_peers = [lax.rem(v + d, views) for d in range(1, views)]
    seq_peers = [x_s, xc_s, c_s]

    def level(zt):
        return (s, zt * 2 + y)

    wires = Wires(k.send_sem, k.recv_sem, (c_s, v))
    in_normed = wires.inbox(2 * views)
    in_ids = wires.inbox(views)
    in_up = wires.inbox(LEVELS + 1)
    in_down = wires.inbox(LEVELS + 1)
    in_mcot = wires.inbox(4)
    in_att = wires.inbox(views)
    in_two = wires.inbox(4)
    in_part = [wires.inbox(5), wires.inbox(5)]
    in_core = [wires.inbox(1), wires.inbox(1)]
    in_grad = [wires.inbox(3), wires.inbox(3)]
    in_acot, in_pc = in_ids, in_att
    in_dw = wires.inbox(3)
    in_do = wires.inbox(3)
    in_do_z = wires.inbox(LEVELS)
    in_plane = wires.inbox(views)
    in_query = wires.inbox(views)
    in_cross = wires.inbox(views)
    in_mate = [wires.inbox(1) for unused in range(3)]
    in_out = [wires.inbox(views), wires.inbox(views)]
    in_out_mate = wires.inbox(1)
    in_gain = wires.inbox(seqs)
    in_gains = in_normed
    to_view = [wires.bulk() for unused in range(5)]
    to_mate_w = [wires.bulk() for unused in range(3)]
    to_mate_o = wires.bulk()

    def z_cast(src, dst, slot):
        wires.send(src, dst, slot, level(z_pair))
        wires.send(src, dst, slot, level(z_two))
        wires.send(src, dst, slot, level(z_flip), when=inner)

    def z_relay(ref, slot):
        wires.send(ref, ref, slot, level(z_pair), when=inner)

    barrier = pltpu.get_barrier_semaphore()
    greeted = [(s, p) for p in view_peers] + [(p, v) for p in seq_peers]
    for device in greeted:
        pl.semaphore_signal(barrier, inc=1, device_id=device, device_id_type=MESH)

    loads, kept = [], []

    def load(src, dst):
        copy = pltpu.make_async_copy(src, dst, k.local_sem.at[len(loads)])
        copy.start()
        loads.append(copy)
        return copy

    up_slot = at((c * 4 + y * 2 + high) * hidden, hidden)
    load_tok = load(tok_hbm, tok)
    load_cot = load(cot_hbm, out_cot)
    load_up = load(up_hbm, k.up.at[up_slot])
    load_down = load(down_hbm, k.down.at[up_slot])
    load_own = [
        load(w_hbm.at[:, at(t * width + v * own, own)], k.w_own.at[:, pl.ds(t * own, own)])
        for t in range(3)
    ]
    load_wo = load(wo_hbm, k.wo)
    load_w = load(w_hbm, k.w_full)

    gain_one = gain_one_ref[...].astype(f3).reshape(1, width)
    gain_two = gain_two_ref[...].astype(f3).reshape(1, width)
    load_tok.wait()
    unit, _ = norm_stats(tok[...].astype(f3))
    k.normed[at(v * rows, rows), :] = (unit * gain_one).astype(bf)
    per = rows // block
    lane = lax.broadcasted_iota(jnp.int32, (1, 128), 1)
    scenes = jnp.zeros((1, 128), jnp.int32)
    for m in range(per):
        mine = jnp.broadcast_to(ids[:, m * block : m * block + 1], (1, 128))
        scenes = jnp.where(lane == v * per + m, mine, scenes)
    k.ids_all[v] = jnp.broadcast_to(scenes, (8, 128))
    live = jnp.transpose(jnp.broadcast_to(alive[...].astype(f3), (rows, rows)))[:, :1]
    pl.semaphore_wait(barrier, len(greeted))

    def view_rows(ref, j):
        return ref.at[at(j * rows, rows)]

    for p in view_peers:
        wires.send(k.ids_all.at[v], k.ids_all.at[v], in_ids + v, (s, p), bulk=to_view[0])

    def normed_half(j, i):
        return k.normed.at[at(j * rows + i * (rows // 2), rows // 2)], in_normed + 2 * j + i

    for i in range(2):
        mine, slot = normed_half(v, i)
        wires.send(mine, mine, slot, (s, y_v))
    for zt in (z_pair, z_two):
        for i in range(2):
            mine, slot = normed_half(v, i)
            wires.send(mine, mine, slot, level(zt))
    for i in range(2):
        mine, slot = normed_half(v, i)
        wires.send(mine, mine, slot, level(z_flip), when=inner)
    load_cot.wait()
    mcot_own = at(own_slot * rows, rows)
    k.mixed_cot[mcot_own, :] = (live * out_cot[...].astype(f3)).astype(bf)

    def slot_rows(ref, slot):
        return ref.at[at(slot * rows, rows)]

    def square_send(ref, base, slot, device):
        wires.send(slot_rows(ref, slot), slot_rows(ref, slot), base + slot, device)

    def square_relay(ref, base):
        wires.wait(slot_rows(ref, pair_slot), base + pair_slot)
        square_send(ref, base, pair_slot, (x_s, v))

    square_send(k.mixed_cot, in_mcot, own_slot, (x_s, v))

    for p in view_peers:
        wires.wait(k.ids_all.at[p], in_ids + p)
    count = SLOTS * SCENE_BLOCKS
    scene_row = k.ids_all[0][:1]
    for j in range(1, views):
        scene_row = scene_row + k.ids_all[j][:1]
    big = lax.broadcasted_iota(jnp.int32, (128, 128), 0)
    wide = lax.broadcasted_iota(jnp.int32, (128, 128), 1)
    scene_mat = jnp.broadcast_to(scene_row, (128, 128))
    scene_col = jnp.transpose(scene_mat)
    ahead = (scene_col < scene_mat) | ((scene_col == scene_mat) & (big < wide))
    place = jnp.sum(jnp.where(ahead & (big < count), 1, 0), axis=0, keepdims=True)
    place_col = jnp.transpose(jnp.broadcast_to(place, (128, 128)))
    hit = jnp.where((place_col == wide) & (big < count), big, 0)
    source = jnp.sum(hit, axis=0, keepdims=True)
    k.order_vm[0:8, :] = jnp.broadcast_to(source, (8, 128))
    k.order_vm[8:16, :] = jnp.broadcast_to(place, (8, 128))
    to_scalar = load(k.order_vm, k.order_sm)

    for copy in load_own:
        copy.wait()

    def mlp_slot(ref, yt, ht):
        return ref.at[at((c * 4 + yt * 2 + ht) * hidden, hidden)]

    def send_mlp(ref, base, device):
        mine = mlp_slot(ref, y, high)
        wires.send(mine, mine, base + y * 2 + high, device)

    def mlp_relay(ref, base):
        there = mlp_slot(ref, y, 1 - high)
        wires.wait(there, base + y * 2 + 1 - high)
        wires.send(there, there, base + y * 2 + 1 - high, (s, y_v))

    def core_exchange(ref, base):
        for ht in (high, 1 - high):
            wires.wait(mlp_slot(ref, 1 - y, ht), base + (1 - y) * 2 + ht)
        mine = ref.at[at(c * half, half)]
        wires.send(mine, mine, base + LEVELS, (c_s, v))

    def project(j):
        k.qkv[at(j * rows, rows), :] = dot_nn(k.normed[at(j * rows, rows), :], k.w_own[...]).astype(bf)

    project(v)
    for zt in others_z:
        j = zt * 2 + y
        for i in range(2):
            there, slot = normed_half(j, i)
            wires.wait(there, slot)
            if zt is z_two:
                z_relay(there, slot)
            wires.send(there, there, slot, (s, y_v))
        if zt is z_two:
            load_up.wait()
            send_mlp(k.up, in_up, level(z_two))
            square_send(k.mixed_cot, in_mcot, own_slot, (s, pair_v))
        project(j)
    send_mlp(k.up, in_up, (s, y_v))
    for zt in [z] + others_z:
        j = zt * 2 + 1 - y
        for i in range(2):
            wires.wait(*normed_half(j, i))
        project(j)
    to_scalar.wait()

    def reorder(dst, src, row):
        blocks = src.reshape(count, block, src.shape[1])

        def step(i, unused):
            from_block = k.order_sm[row, i]
            dst[at(i * block, block), :] = blocks[from_block].astype(dst.dtype)
            return unused

        lax.fori_loop(0, count, step, 0, unroll=8)

    reorder(k.qkv_s, k.qkv, 0)

    head_lane = lax.broadcasted_iota(jnp.int32, (scene, own), 1) // HEAD_DIM

    def attend(g, unused):
        here = at(g * scene, scene)
        queries, keys, values = (k.qkv_s[here, pl.ds(t * own, own)] for t in range(3))
        result = jnp.zeros((scene, own), f3)
        for e in range(2):
            chosen = jnp.where(head_lane == e, queries, jnp.zeros_like(queries))
            weights = jnp.exp(dot_inner(chosen, keys) * scale)
            total = jnp.sum(weights, axis=-1, keepdims=True)
            k.weights[g * 2 + e] = weights
            k.totals[g * 2 + e] = total
            mixed = dot_nn(weights.astype(bf), values) / total
            result = jnp.where(head_lane == e, mixed, result)
        k.att_s[here, :] = result
        return unused

    lax.fori_loop(0, SLOTS, attend, 0, unroll=True)
    reorder(k.att, k.att_s, 8)
    own_cols = at(v * own, own)
    for p in view_peers:
        wires.send(view_rows(k.att, p), k.att_tok.at[:, own_cols], in_att + v, (s, p), bulk=to_view[1])
    square_relay(k.mixed_cot, in_mcot)
    mlp_relay(k.up, in_up)
    load_down.wait()
    send_mlp(k.down, in_down, level(z_two))
    send_mlp(k.down, in_down, (s, y_v))
    k.att_tok[:, own_cols] = k.att[at(v * rows, rows), :]


    load_wo.wait()
    for p in view_peers:
        wires.wait(k.att_tok.at[:, at(p * own, own)], in_att + p)
    tile = 256
    for n in range(width // tile):
        cols = pl.ds(n * tile, tile)
        k.middle[:, cols] = tok[:, cols].astype(f3) + live * dot_nn(k.att_tok[...], k.wo[:, cols])
    unit_two, _ = norm_stats(k.middle[...])
    k.normed_two[mcot_own, :] = (unit_two * gain_two).astype(bf)
    until_two = wires.total
    for device in ((s, pair_v), (x_s, v)):
        square_send(k.normed_two, in_two, own_slot, device)

    core_exchange(k.up, in_up)
    square_relay(k.normed_two, in_two)
    mlp_relay(k.down, in_down)
    wires.wait(k.up.at[at((1 - c) * half, half)], in_up + LEVELS)

    def hidden_tiles(slot):
        here = at(slot * rows, rows)

        def step(n, unused):
            cols = at(n * tile, tile)
            pre = dot_inner(k.normed_two[here, :], k.up[cols, :])
            below = 0.5 + 0.5 * lax.erf(pre * (0.5**0.5))
            k.act[here, cols] = (pre * below).astype(bf)
            k.slope[here, cols] = below + pre * (jnp.exp(-0.5 * pre * pre) * (0.5 / math.pi) ** 0.5)
            return unused

        lax.fori_loop(0, mlp_rows // tile, step, 0)

    hidden_tiles(own_slot)
    hidden_tiles(pair_slot)
    for slot in (x_slot, far_slot):
        wires.wait(slot_rows(k.normed_two, slot), in_two + slot)
        hidden_tiles(slot)

    def grad_tiles(left, right, start, dst):
        def step(n, unused):
            there = at(n * tile, tile)
            dst[there, :] = dot_outer(left[:, at(start + n * tile, tile)], right[...]).astype(dst.dtype)
            return unused

        lax.fori_loop(0, half // tile, step, 0)

    passed = []

    def grad_halves(which, left, right):
        grad_tiles(left, right, (1 - c) * half, k.grad_pass.at[which])
        passed.append(wires.send(k.grad_pass.at[which], k.grad_core.at[which], in_core[which], (c_s, v)))
        grad_tiles(left, right, c * half, k.grad_keep.at[which])

    for slot in (x_slot, far_slot):
        wires.wait(slot_rows(k.mixed_cot, slot), in_mcot + slot)
    core_exchange(k.down, in_down)
    grad_halves(0, k.act, k.mixed_cot)

    def grad_sum(which, start, size):
        there = at(start, size)
        return k.grad_keep[which, there, :].astype(f3) + k.grad_core[which, there, :].astype(f3)

    def grads_to_y(which):
        wires.wait(k.grad_core.at[which], in_core[which])
        wires.sent(passed[which])
        for i, ht in enumerate((1 - high, high)):
            start = ((1 - y) * 2 + ht) * hidden
            there = at(start, hidden)
            k.grad_pass[which, there, :] = grad_sum(which, start, hidden).astype(bf)
            wires.send(k.grad_pass.at[which, there], k.grad_y.at[which, i], in_grad[which] + i, (s, y_v))

    def grad_block(which, i, ht):
        wires.wait(k.grad_y.at[which, i], in_grad[which] + i)
        return grad_sum(which, (y * 2 + ht) * hidden, hidden) + k.grad_y[which, i].astype(f3)

    def grads_to_z(which):
        there = at((y * 2 + 1 - high) * hidden, hidden)
        k.grad_pass[which, there, :] = grad_block(which, 0, 1 - high).astype(bf)
        wires.send(k.grad_pass.at[which, there], k.grad_z.at[which], in_grad[which] + 2, level(z_two))

    def collect(which, dst):
        total = grad_block(which, 1, high)
        wires.wait(k.grad_z.at[which], in_grad[which] + 2)
        dst[...] = total + k.grad_z[which].astype(f3)


    wires.wait(k.down.at[at((1 - c) * half, half)], in_down + LEVELS)

    def cot_tile(n, unused):
        cols = at(n * tile, tile)
        up_to = dot_inner(k.mixed_cot[...], k.down[cols, :])
        k.hid_cot[:, cols] = (up_to * k.slope[:, cols]).astype(bf)
        return unused

    lax.fori_loop(0, mlp_rows // tile, cot_tile, 0)

    strip = width // 2

    def strip_cols(i):
        return pl.ds(i * strip, strip)

    def part_tiles(which, left, right):
        for i in range(2):

            def step(n, unused):
                cols = at(i * strip + n * tile, tile)
                k.part_all[:, cols] = dot_nn(left[...], right[:, cols])
                return unused

            lax.fori_loop(0, strip // tile, step, 0)
            cols = strip_cols(i)
            k.part_out[which, 0, :, cols] = k.part_all[at(far_slot * rows, rows), cols].astype(bf)
            there = k.part_out.at[which, 0, :, cols], k.part_in.at[which, 0, :, cols]
            wires.send(*there, in_part[which] + i, (x_s, v))
        k.part_out[which, 1] = k.part_all[at(x_slot * rows, rows), :].astype(bf)
        wires.send(k.part_out.at[which, 1], k.part_in.at[which, 1], in_part[which] + 2, (x_s, v))
        for i, slot in enumerate((own_slot, pair_slot)):
            k.part_own[which, i] = k.part_all[at(slot * rows, rows), :]

    def part_join(which):
        for i in range(2):
            cols = strip_cols(i)
            wires.wait(k.part_in.at[which, 0, :, cols], in_part[which] + i)
            joined = k.part_own[which, 1, :, cols] + k.part_in[which, 0, :, cols].astype(f3)
            k.part_out[which, 2, :, cols] = joined.astype(bf)
            there = k.part_out.at[which, 2, :, cols], k.part_in.at[which, 2, :, cols]
            wires.send(*there, in_part[which] + 3 + i, (s, pair_v))

    grads_to_y(0)
    part_tiles(0, k.hid_cot, k.up)
    grad_halves(1, k.hid_cot, k.normed_two)
    part_tiles(1, k.act, k.down)
    part_join(0)

    def part_sum(which):
        total = k.part_own[which, 0]
        wires.wait(k.part_in.at[which, 1], in_part[which] + 2)
        for i in range(2):
            wires.wait(k.part_in.at[which, 2, :, strip_cols(i)], in_part[which] + 3 + i)
        for i in (1, 2):
            total = total + k.part_in[which, i].astype(f3)
        return total

    unit_two, inverse_two = norm_stats(k.middle[...])
    wires.settle(until_two)
    cot_two = part_sum(0)
    until_acot = wires.total
    k.gain_own[1:2, :] = jnp.sum(cot_two * unit_two, axis=0, keepdims=True)
    middle_cot = out_cot[...].astype(f3) + norm_back(cot_two, unit_two, inverse_two, gain_two)
    tokens_grad[...] = middle_cot
    k.branch[...] = (live * middle_cot).astype(bf)
    for n in range(width // tile):
        k.acot_tok[:, pl.ds(n * tile, tile)] = dot_inner(
            k.branch[...], k.wo[pl.ds(n * tile, tile), :]
        ).astype(bf)
    for p in view_peers:
        wires.send(k.acot_tok.at[:, at(p * own, own)], view_rows(k.acot, v), in_acot + v, (s, p), bulk=to_view[2])
    k.acot[at(v * rows, rows), :] = k.acot_tok[:, own_cols]

    o_half, o_quarter, o_eighth = width // 2, width // 4, width // 8
    o_piece = o_eighth // LEVELS

    def outer_rows(start, dst, dtype):
        def step(n, unused):
            there = at(n * tile, tile)
            left = k.att_tok[:, at(start + n * tile, tile)]
            dst[there, :] = dot_outer(left, k.branch[...]).astype(dtype)
            return unused

        lax.fori_loop(0, o_half // tile, step, 0)

    outer_rows((1 - c) * o_half, k.do_core, bf)
    wires.send(k.do_core, k.do_core_in, in_do, (c_s, v))
    outer_rows(c * o_half, k.do_keep, f3)
    wires.wait(k.do_core_in, in_do)
    k.do_keep[...] = k.do_keep[...] + k.do_core_in[...].astype(f3)
    k.do_first[...] = k.do_keep[at((1 - x) * o_quarter, o_quarter), :].astype(bf)
    wires.send(k.do_first, k.do_first_in, in_do + 1, (x_s, v))

    for p in view_peers:
        wires.wait(view_rows(k.acot, p), in_acot + p)
    grads_to_y(1)
    part_join(1)
    reorder(k.acot_s, k.acot, 0)

    def attend_back(g, unused):
        here = at(g * scene, scene)
        queries, keys, values = (k.qkv_s[here, pl.ds(t * own, own)] for t in range(3))
        cots = k.acot_s[here, :]
        agree = cots.astype(f3) * k.att_s[here, :]
        outs = [jnp.zeros((scene, own), f3) for t in range(3)]
        for e in range(2):
            mine = head_lane == e
            delta = jnp.sum(jnp.where(mine, agree, 0.0), axis=-1, keepdims=True)
            chosen = jnp.where(mine, cots, jnp.zeros_like(cots))
            weights = k.weights[g * 2 + e]
            inverse = 1.0 / k.totals[g * 2 + e]
            weights_cot = dot_inner(chosen, values)
            score_cot = (weights * inverse * (weights_cot - delta)).astype(bf)
            shared = (cots.astype(f3) * inverse).astype(bf)
            new = (
                dot_nn(score_cot, keys) * scale,
                dot_outer(score_cot, queries) * scale,
                dot_outer(weights.astype(bf), shared),
            )
            outs = [jnp.where(mine, fresh, old) for fresh, old in zip(new, outs)]
        for t in range(3):
            k.pc_s[here, pl.ds(t * own, own)] = outs[t].astype(bf)
        return unused

    lax.fori_loop(0, SLOTS, attend_back, 0, unroll=True)
    pc_blocks = k.pc_s.reshape(count, block, 3 * own)

    def unsort(i, unused):
        found = pc_blocks[k.order_sm[8, i]]
        k.pc_flat[at(i * block, block), :] = found
        for t in range(3):
            k.pc[t, at(i * block, block), :] = found[:, t * own : (t + 1) * own]
        return unused

    lax.fori_loop(0, count, unsort, 0, unroll=8)
    for p in view_peers:
        wires.send(k.pc.at[:, at(p * rows, rows)], k.pc_tok.at[:, :, own_cols], in_pc + v, (s, p), bulk=to_view[3])
    for t in range(3):
        k.pc_tok[t, :, own_cols] = k.pc[t, at(v * rows, rows), :]

    part = width // seqs

    def own_dw(row_block):
        whole = dot_outer(k.normed[:, at(row_block * part, part)], k.pc_flat[...])
        return [whole[:, t * own : (t + 1) * own] for t in range(3)]

    for i, xt in enumerate((1 - x, x)):
        for t, value in enumerate(own_dw(xt * 2 + 1 - c)):
            k.dw_out[i, t] = value.astype(bf)
        wires.send(k.dw_out.at[i], k.dw_in.at[i], in_dw + i, (c_s, v))
    cross_dw = own_dw(x_s)
    wires.wait(k.dw_in.at[0], in_dw)
    for t in range(3):
        k.dw_x[t] = (cross_dw[t] + k.dw_in[0, t].astype(f3)).astype(bf)
    wires.send(k.dw_x, k.dw_in.at[2], in_dw + 2, (x_s, v))
    mine_dw = own_dw(s)
    wires.wait(k.dw_in.at[1], in_dw + 1)
    wires.settle(until_acot)
    wires.wait(k.dw_in.at[2], in_dw + 2)
    for t in range(3):
        total = mine_dw[t] + k.dw_in[1, t].astype(f3) + k.dw_in[2, t].astype(f3)
        k.dw_own[t] = total.astype(bf)

    def w_at(q, j, first, last):
        return w_grad.at[pl.ds(first, last - first), at(q * part, part), at(j * own, own)]

    def w_plane(j):
        return w_at(s, j, 0, 3)

    def w_query(j):
        return w_at(x_s, j, 0, 1)

    def w_cross(q, j):
        return w_at(q, j, 1, 3)

    wires.send(k.dw_own.at[pl.ds(0, 1)], w_at(s, v, 0, 1), in_query + v, (x_s, v))
    wires.send(k.dw_own, w_plane(v), in_plane + v, (s, y_v))
    z_cast(k.dw_own, w_plane(v), in_plane + v)
    wires.send(k.dw_own.at[pl.ds(1, 2)], w_cross(s, v), in_cross + v, (x_s, v))
    wires.send(k.dw_own, w_plane(v), in_mate[0], (c_s, v), bulk=to_mate_w[0])
    kept.append(load(k.dw_own, w_plane(v)))

    wires.wait(w_query(v), in_query + v)
    wires.send(w_query(v), w_query(v), in_query + v, (s, y_v))
    z_cast(w_query(v), w_query(v), in_query + v)
    wires.send(w_query(v), w_query(v), in_mate[1], (c_s, v), bulk=to_mate_w[1])

    wires.wait(k.do_first_in, in_do + 1)
    o_mine = at(x * o_quarter, o_quarter)
    k.do_keep[o_mine, :] = k.do_keep[o_mine, :] + k.do_first_in[...].astype(f3)
    k.do_second[...] = k.do_keep[at(x * o_quarter + (1 - y) * o_eighth, o_eighth), :].astype(bf)
    wires.send(k.do_second, k.do_second_in, in_do + 2, (s, y_v))
    def o_at(q, j):
        at_c, at_x, at_y, at_z = q % 2, q // 2, j % 2, j // 2
        return o_grad.at[at(at_c * o_half + at_x * o_quarter + at_y * o_eighth + at_z * o_piece, o_piece)]

    def to_mate(which, ref):
        wires.send(ref, ref, in_mate[which], (c_s, v), bulk=to_mate_w[which])

    def pass_plane(zt, row_y):
        j = zt * 2 + row_y
        wires.wait(w_plane(j), in_plane + j)
        if row_y is y:
            if zt is z_two:
                z_relay(w_plane(j), in_plane + j)
            wires.send(w_plane(j), w_plane(j), in_plane + j, (s, y_v))
        wires.send(w_cross(s, j), w_cross(s, j), in_cross + j, (x_s, v))
        to_mate(0, w_plane(j))

    def pass_query(zt, row_y):
        j = zt * 2 + row_y
        wires.wait(w_query(j), in_query + j)
        if row_y is y:
            if zt is z_two:
                z_relay(w_query(j), in_query + j)
            wires.send(w_query(j), w_query(j), in_query + j, (s, y_v))
        to_mate(1, w_query(j))

    across = 1 - y
    pass_plane(z, across)

    load_w.wait()
    for p in view_peers:
        wires.wait(k.pc_tok.at[:, :, at(p * own, own)], in_pc + p)

    def back_tile(n, unused):
        cols = at(n * tile, tile)
        total = dot_inner(k.pc_tok[0], k.w_full[cols, pl.ds(0, width)])
        for t in range(1, 3):
            total = total + dot_inner(k.pc_tok[t], k.w_full[cols, pl.ds(t * width, width)])
        k.part_own[0, 0, :, cols] = total
        return unused

    lax.fori_loop(0, width // tile, back_tile, 0)
    unit_one, inverse_one = norm_stats(tok[...].astype(f3))
    cot_one = k.part_own[0, 0]
    k.gain_own[0:1, :] = jnp.sum(cot_one * unit_one, axis=0, keepdims=True)
    k.gain_own[2:8, :] = jnp.zeros((6, width), f3)
    tokens_grad[...] = tokens_grad[...] + norm_back(cot_one, unit_one, inverse_one, gain_one)
    for p in seq_peers:
        wires.send(k.gain_own, k.gain_in.at[s], in_gain + s, (p, v))
    kept.append(load(tokens_grad, tokens_hbm))

    wires.wait(k.do_second_in, in_do + 2)
    total = k.do_keep[at(x * o_quarter + y * o_eighth, o_eighth), :] + k.do_second_in[...].astype(f3)
    k.do_z[...] = total.astype(bf)

    def o_level(zt):
        return at(zt * o_piece, o_piece)

    for zt in others_z:
        wires.send(k.do_z.at[o_level(zt)], k.do_z_in.at[z], in_do_z + z, level(zt))

    pass_plane(z_pair, y)
    pass_plane(z_two, y)
    pass_query(z, across)
    pass_plane(z_pair, across)
    pass_query(z_pair, y)
    pass_query(z_two, y)
    pass_plane(z_flip, y)
    pass_plane(z_two, across)
    there = at((y * 2 + 1 - high) * hidden, hidden)
    k.grad_pass[1, there, :] = grad_block(1, 0, 1 - high).astype(bf)
    kept.append(load(k.grad_pass.at[1, there], up_away))
    up_grad[...] = grad_block(1, 1, high)
    kept.append(load(up_grad, up_part))
    total = k.do_keep[at(x * o_quarter + y * o_eighth + z * o_piece, o_piece), :]
    total = total + k.do_second_in[o_level(z), :].astype(f3)
    for zt in others_z:
        wires.wait(k.do_z_in.at[zt], in_do_z + zt)
        total = total + k.do_z_in[zt].astype(f3)
    k.do_own[...] = total.astype(bf)
    wires.send(k.do_own, o_at(s, v), in_out[0] + v, (s, y_v))
    z_cast(k.do_own, o_at(s, v), in_out[0] + v)
    wires.send(k.do_own, o_at(s, v), in_out[1] + v, (x_s, v))
    wires.send(k.do_own, o_at(s, v), in_out_mate, (c_s, v), bulk=to_mate_o)
    kept.append(load(k.do_own, o_at(s, v)))
    pass_query(z_flip, y)
    pass_plane(z_flip, across)
    for zt in others_z:
        pass_query(zt, across)

    total = k.gain_own[...]
    for p in seq_peers:
        wires.wait(k.gain_in.at[p], in_gain + p)
        total = total + k.gain_in[p]
    k.gain_sum[...] = total
    for p in view_peers:
        wires.send(k.gain_sum, k.gain_all.at[v], in_gains + v, (s, p), bulk=to_view[4])

    def out_mate(q, j):
        wires.send(o_at(q, j), o_at(q, j), in_out_mate, (c_s, v), bulk=to_mate_o)

    def pass_out(zt, row_y):
        j = zt * 2 + row_y
        slot = in_out[0] + j
        wires.wait(o_at(s, j), slot)
        if row_y is y:
            if zt is z_two:
                z_relay(o_at(s, j), slot)
            wires.send(o_at(s, j), o_at(s, j), slot, (s, y_v))
        wires.send(o_at(s, j), o_at(s, j), in_out[1] + j, (x_s, v))
        out_mate(s, j)

    for zt in others_z:
        pass_out(zt, y)
    grads_to_z(0)
    for zt in [z] + others_z:
        pass_out(zt, across)

    layer_out[...] = (k.middle[...] + live * part_sum(1)).astype(bf)
    kept.append(load(layer_out, layer_hbm))
    by_arrival = [v] + [zt * 2 + y for zt in others_z] + [zt * 2 + across for zt in [z] + others_z]
    for j in by_arrival:
        wires.wait(w_cross(x_s, j), in_cross + j)
        to_mate(2, w_cross(x_s, j))
    for j in by_arrival:
        wires.wait(o_at(x_s, j), in_out[1] + j)
        out_mate(x_s, j)

    total = k.gain_sum[...]
    for p in view_peers:
        wires.wait(k.gain_all.at[p], in_gains + p)
        total = total + k.gain_all[p]
    gains[...] = total

    collect(0, down_grad)
    kept.append(load(down_grad, down_hbm_out))
    def w_rows(q, first, last):
        return w_grad.at[pl.ds(first, last - first), at(q * part, part)]

    def o_core(core):
        return o_grad.at[at(core * o_half, o_half)]

    wires.settle(wires.total)
    for whole, lane in (
        (k.ids_all.at[pl.ds(0, views - 1)], to_view[0]),
        (k.att.at[pl.ds(0, length - rows)], to_view[1]),
        (k.acot.at[pl.ds(0, length - rows)], to_view[2]),
        (k.pc.at[:, pl.ds(0, length - rows)], to_view[3]),
        (k.gain_all.at[pl.ds(0, views - 1)], to_view[4]),
        (w_rows(s, 0, 3), to_mate_w[0]),
        (w_rows(x_s, 0, 1), to_mate_w[1]),
        (w_rows(x_s, 1, 3), to_mate_w[2]),
        (o_core(c), to_mate_o),
    ):
        wires.settle_bulk(whole, lane)
    wires.wait(w_rows(c_s, 0, 3), in_mate[0])
    wires.wait(w_rows(xc_s, 0, 1), in_mate[1])
    wires.wait(w_rows(xc_s, 1, 3), in_mate[2])
    wires.wait(o_core(1 - c), in_out_mate)
    for copy in kept:
        copy.wait()


FINISH_STEPS = 8


def finish_kernel(*refs):
    (layer_in, tokens_in, gains, w_in, o_in, down_in) = refs[:6]
    (layer_out, tokens_grad, gain_one, w_out, o_out, gain_two, down_out) = refs[6:13]
    (layer, tokens, down, w_narrow, o_narrow, w_wide, o_wide, in_sem, out_sem) = refs[13:]
    width = o_in.shape[0]
    tall = width // FINISH_STEPS
    asis = ((layer_in, layer, layer_out), (tokens_in, tokens, tokens_grad), (down_in, down, down_out))

    def rows(i):
        return pl.ds(i * tall, tall)

    def start(src, dst, sem):
        copy = pltpu.make_async_copy(src, dst, sem)
        copy.start()
        return copy

    reads, writes = [], []
    for i in range(FINISH_STEPS):
        reads.append(start(w_in.at[:, rows(i)], w_narrow.at[:, rows(i)], in_sem.at[2 * i]))
        reads.append(start(o_in.at[rows(i)], o_narrow.at[rows(i)], in_sem.at[2 * i + 1]))
    late = [start(src, mid, in_sem.at[2 * FINISH_STEPS + i]) for i, (src, mid, dst) in enumerate(asis)]
    gain_one[...] = gains[0:1, :].reshape(width)
    gain_two[...] = gains[1:2, :].reshape(width)
    for i in range(FINISH_STEPS):
        reads[2 * i].wait()
        for t in range(3):
            w_wide[rows(i), t * width : (t + 1) * width] = w_narrow[t, rows(i), :].astype(jnp.float32)
        writes.append(start(w_wide.at[rows(i)], w_out.at[rows(i)], out_sem.at[2 * i]))
        reads[2 * i + 1].wait()
        o_wide[rows(i), :] = o_narrow[rows(i), :].astype(jnp.float32)
        writes.append(start(o_wide.at[rows(i)], o_out.at[rows(i)], out_sem.at[2 * i + 1]))
    for i, (src, mid, dst) in enumerate(asis):
        late[i].wait()
        writes.append(start(mid, dst, out_sem.at[2 * FINISH_STEPS + i]))
    for copy in writes:
        copy.wait()


def fused(
    seqs,
    views,
    tokens,
    scene_ids,
    live_mask,
    out_grad,
    attention_gain,
    input_weight,
    output_weight,
    feedforward_gain,
    up_weight,
    down_weight,
):
    rows, width = tokens.shape[1:]
    hidden = up_weight.shape[0]
    spec = scratch_of(rows, width, seqs, views, hidden)
    vmem = pl.BlockSpec(memory_space=pltpu.VMEM)
    anywhere = pl.BlockSpec(memory_space=pl.ANY)
    shape = jax.ShapeDtypeStruct
    bf, f3 = jnp.bfloat16, jnp.float32
    layer_raw, tokens_raw, gains, w_raw, o_raw, up_part, up_away, down_raw = pl.pallas_call(
        functools.partial(layer_kernel, tuple(spec), seqs, views),
        out_shape=(
            shape((rows, width), bf),
            shape((rows, width), f3),
            shape((8, width), f3),
            shape((3, width, width), bf),
            shape((width, width), bf),
            shape((hidden, width), f3),
            shape((hidden, width), bf),
            shape((hidden, width), f3),
        ),
        in_specs=[anywhere, vmem, vmem, anywhere, vmem, vmem] + [anywhere] * 4,
        out_specs=(anywhere, anywhere, vmem) + (anywhere,) * 5,
        scratch_shapes=list(spec.values()),
        compiler_params=pltpu.CompilerParams(
            collective_id=0, has_side_effects=True, vmem_limit_bytes=67043328
        ),
        name="layer",
    )(
        tokens[0],
        scene_ids,
        live_mask,
        out_grad[0],
        attention_gain,
        feedforward_gain,
        input_weight,
        output_weight,
        up_weight,
        down_weight,
    )
    shift = [(j, (j + views // 2) % views) for j in range(views)]
    up_grad = up_part + lax.ppermute(up_away, "view", shift).astype(f3)
    layer_out, tokens_grad, gain_one, w_grad, o_grad, gain_two, down_grad = pl.pallas_call(
        finish_kernel,
        out_shape=(
            shape((rows, width), bf),
            shape((rows, width), f3),
            shape((width,), f3),
            shape((width, 3 * width), f3),
            shape((width, width), f3),
            shape((width,), f3),
            shape((hidden, width), f3),
        ),
        in_specs=[anywhere] * 2 + [vmem] + [anywhere] * 3,
        out_specs=(anywhere, anywhere, vmem, anywhere, anywhere, vmem, anywhere),
        scratch_shapes=[
            pltpu.VMEM((rows, width), bf),
            pltpu.VMEM((rows, width), f3),
            pltpu.VMEM((hidden, width), f3),
            pltpu.VMEM((3, width, width), bf),
            pltpu.VMEM((width, width), bf),
            pltpu.VMEM((width, 3 * width), f3),
            pltpu.VMEM((width, width), f3),
            pltpu.SemaphoreType.DMA((2 * FINISH_STEPS + 4,)),
            pltpu.SemaphoreType.DMA((2 * FINISH_STEPS + 4,)),
        ],
        cost_estimate=pl.CostEstimate(
            flops=4 * width * width, transcendentals=0, bytes_accessed=28 * width * width
        ),
        name="finish",
    )(layer_raw, tokens_raw, gains, w_raw, o_raw, down_raw)
    return (
        layer_out[None],
        tokens_grad[None],
        gain_one,
        w_grad,
        o_grad,
        gain_two,
        up_grad,
        down_grad,
    )


def solution(mesh):
    seqs, views = mesh.shape["seq"], mesh.shape["view"]
    small = seqs == 4 and views == 2 * LEVELS and HEADS == 2 * views
    body = functools.partial(fused, seqs, views) if small else shards
    return jax.shard_map(
        body,
        mesh=mesh,
        in_specs=(
            P("seq", "view", None),
            P("seq", "view"),
            P("seq", "view"),
            P("seq", "view", None),
            P(),
            P(),
            P(),
            P(),
            P(("seq", "view"), None),
            P(("seq", "view"), None),
        ),
        out_specs=(
            P("seq", "view", None),
            P("seq", "view", None),
            P(),
            P(),
            P(),
            P(),
            P(("seq", "view"), None),
            P(("seq", "view"), None),
        ),
        check_vma=False,
    )
```

```python
import functools
import math
import types

import jax
import jax.numpy as jnp
from jax import lax
from jax.experimental import pallas as pl
from jax.experimental.pallas import tpu as pltpu
from jax.sharding import PartitionSpec as P

HEADS = 16
HEAD_DIM = 64


EPS = 1e-05
NEGATIVE = -1e30
MESH = pl.DeviceIdType.MESH
SLOTS = 4
SCENE_BLOCKS = 16


def layer_norm(values, gain):
    center = values - jnp.mean(values, axis=-1, keepdims=True)
    spread = jnp.mean(center * center, axis=-1, keepdims=True)
    return center * lax.rsqrt(spread + EPS) * gain


def gelu_exact(values):
    return jax.nn.gelu(values, approximate=False)


def plain_dot(left, right):
    return jnp.dot(left, right, preferred_element_type=jnp.float32)


def dot_inner(left, right):
    return lax.dot_general(
        left, right, (((1,), (1,)), ((), ())), preferred_element_type=jnp.float32
    )


def dot_outer(left, right):
    return lax.dot_general(
        left, right, (((0,), (0,)), ((), ())), preferred_element_type=jnp.float32
    )


def split_heads(values):
    return values.reshape(values.shape[0], HEADS, HEAD_DIM)


def masked_scores(queries, keys, query_tags, key_tags, scale):
    raw = jnp.einsum("qhe,khe->hqk", queries, keys, preferred_element_type=jnp.float32) * scale
    allowed = (query_tags[:, None] == key_tags[None, :])[None]
    return (raw, allowed)


def probabilities(queries, keys, query_tags, key_tags, log_total, scale):
    raw, allowed = masked_scores(queries, keys, query_tags, key_tags, scale)
    return jnp.where(
        allowed, jnp.exp(jnp.where(allowed, raw - log_total[:, :, None], NEGATIVE)), 0.0
    )


def in_blocks(step, carry, piece):
    count = piece[0].shape[0]
    size = math.gcd(count, 512)
    number = count // size
    stacked = tuple((member.reshape((number, size) + member.shape[1:]) for member in piece))

    def inner(state, item):
        members, offset = item
        return (step(state, members, offset * size), None)

    result, unused = lax.scan(inner, carry, (stacked, jnp.arange(number, dtype=jnp.int32)))
    return result


def shards(
    tokens,
    scene_ids,
    live_mask,
    out_grad,
    attention_gain,
    input_weight,
    output_weight,
    feedforward_gain,
    up_weight,
    down_weight,
):
    scale = HEAD_DIM ** (-0.5)
    inputs = tokens[0].astype(jnp.float32)
    rows = inputs.shape[0]
    width = inputs.shape[1]
    tags = scene_ids[0] * 2 + live_mask[0]
    live = live_mask[0].astype(jnp.float32)[:, None]
    every_tag = lax.all_gather(tags, "view", axis=0, tiled=True)
    up_full, down_full = (
        lax.all_gather(up_weight, ("seq", "view"), axis=0, tiled=True),
        lax.all_gather(down_weight, ("seq", "view"), axis=0, tiled=True),
    )
    gain_one = attention_gain.astype(jnp.float32)
    gain_two = feedforward_gain.astype(jnp.float32)
    normed = layer_norm(inputs, gain_one).astype(jnp.bfloat16)
    projected = plain_dot(normed, input_weight).astype(jnp.bfloat16)
    query_flat = projected[:, :width]
    queries = split_heads(query_flat)
    keys_own = projected[:, width : 2 * width]
    values_own = projected[:, 2 * width :]

    def attend_step(carry, piece, start):
        peak, total, accum = carry
        key_piece, value_piece = piece
        count = key_piece.shape[0]
        key_tags = lax.dynamic_slice_in_dim(every_tag, start, count)
        raw, allowed = masked_scores(queries, split_heads(key_piece), tags, key_tags, scale)
        masked = jnp.where(allowed, raw, NEGATIVE)
        new_peak = jnp.maximum(peak, jnp.max(masked, axis=-1))
        weights = jnp.where(allowed, jnp.exp(masked - new_peak[:, :, None]), 0.0)
        factor = jnp.exp(peak - new_peak)
        total = total * factor + jnp.sum(weights, axis=-1)
        update = jnp.einsum(
            "hqk,khe->qhe",
            weights.astype(jnp.bfloat16),
            split_heads(value_piece),
            preferred_element_type=jnp.float32,
        )
        accum = accum * jnp.transpose(factor)[:, :, None] + update
        return (new_peak, total, accum)

    start_state = (
        jnp.full((HEADS, rows), NEGATIVE, jnp.float32),
        jnp.zeros((HEADS, rows), jnp.float32),
        jnp.zeros((rows, HEADS, HEAD_DIM), jnp.float32),
    )
    peak, total, accum = in_blocks(
        attend_step,
        start_state,
        (
            lax.all_gather(keys_own, "view", axis=0, tiled=True),
            lax.all_gather(values_own, "view", axis=0, tiled=True),
        ),
    )
    attended_heads = accum / jnp.transpose(total)[:, :, None]
    log_total = peak + jnp.log(total)
    attended_low = attended_heads.reshape(rows, width).astype(jnp.bfloat16)
    branch = plain_dot(attended_low, output_weight)
    middle = inputs + live * branch
    normed_two = layer_norm(middle, gain_two).astype(jnp.bfloat16)
    hidden = dot_inner(normed_two, up_full)
    activated = gelu_exact(hidden).astype(jnp.bfloat16)
    mixed = plain_dot(activated, down_full)
    layer_out = (middle + live * mixed).astype(jnp.bfloat16)[None]
    out_cot = out_grad[0].astype(jnp.float32)
    mixed_cot = (live * out_cot).astype(jnp.bfloat16)
    down_grad = dot_outer(activated, mixed_cot)
    activated_cot = dot_inner(mixed_cot, down_full)
    hidden_cot = jax.vjp(gelu_exact, hidden)[1](activated_cot)[0].astype(jnp.bfloat16)
    up_grad = dot_outer(hidden_cot, normed_two)
    normed_two_cot = plain_dot(hidden_cot, up_full)
    second_pull = jax.vjp(layer_norm, middle, gain_two)[1]
    middle_part, gain_two_grad = second_pull(normed_two_cot)
    middle_cot = out_cot + middle_part
    branch_cot = (live * middle_cot).astype(jnp.bfloat16)
    output_weight_grad = dot_outer(attended_low, branch_cot)
    attended_cot = dot_inner(branch_cot, output_weight).astype(jnp.bfloat16)
    cot_heads = split_heads(attended_cot)
    delta = jnp.transpose(jnp.sum(cot_heads.astype(jnp.float32) * attended_heads, axis=-1))
    seq_len = every_tag.shape[0]

    def back_step(carry, piece, start):
        query_cot, key_value_cot = carry
        key_piece, value_piece = piece
        count = key_piece.shape[0]
        key_tags = lax.dynamic_slice_in_dim(every_tag, start, count)
        key_heads = split_heads(key_piece)
        value_heads = split_heads(value_piece)
        probs = probabilities(queries, key_heads, tags, key_tags, log_total, scale)
        prob_cot = jnp.einsum(
            "qhe,khe->hqk", cot_heads, value_heads, preferred_element_type=jnp.float32
        )
        score_cot = (probs * (prob_cot - delta[:, :, None])).astype(jnp.bfloat16)
        query_cot = (
            query_cot
            + jnp.einsum("hqk,khe->qhe", score_cot, key_heads, preferred_element_type=jnp.float32)
            * scale
        )
        key_cot = (
            jnp.einsum("hqk,qhe->khe", score_cot, queries, preferred_element_type=jnp.float32)
            * scale
        )
        value_cot = jnp.einsum(
            "hqk,qhe->khe",
            probs.astype(jnp.bfloat16),
            cot_heads,
            preferred_element_type=jnp.float32,
        )
        stacked = jnp.concatenate(
            [key_cot.reshape(count, width), value_cot.reshape(count, width)], axis=1
        )
        earlier = lax.dynamic_slice_in_dim(key_value_cot, start, count)
        key_value_cot = lax.dynamic_update_slice_in_dim(key_value_cot, earlier + stacked, start, 0)
        return (query_cot, key_value_cot)

    back_state = (
        jnp.zeros((rows, HEADS, HEAD_DIM), jnp.float32),
        jnp.zeros((seq_len, 2 * width), jnp.float32),
    )
    query_cot, key_value_cot = in_blocks(
        back_step,
        back_state,
        (
            lax.all_gather(keys_own, "view", axis=0, tiled=True),
            lax.all_gather(values_own, "view", axis=0, tiled=True),
        ),
    )
    own_cot = lax.psum_scatter(key_value_cot, "view", scatter_dimension=0, tiled=True)
    key_cot_own = own_cot[:, :width]
    value_cot_own = own_cot[:, width:]
    projected_cot = jnp.concatenate(
        [query_cot.reshape(rows, width), key_cot_own, value_cot_own], axis=1
    ).astype(jnp.bfloat16)
    input_weight_grad = dot_outer(normed, projected_cot)
    normed_cot = dot_inner(projected_cot, input_weight)
    first_pull = jax.vjp(layer_norm, inputs, gain_one)[1]
    input_part, gain_one_grad = first_pull(normed_cot)
    tokens_grad = (middle_cot + input_part)[None]
    up_part, down_part = (
        lax.psum_scatter(up_grad, ("seq", "view"), scatter_dimension=0, tiled=True),
        lax.psum_scatter(down_grad, ("seq", "view"), scatter_dimension=0, tiled=True),
    )
    summed = lax.psum(
        (gain_one_grad, input_weight_grad, output_weight_grad, gain_two_grad), ("seq", "view")
    )
    return (layer_out, tokens_grad, summed[0], summed[1], summed[2], summed[3], up_part, down_part)


def dot_nn(left, right):
    return lax.dot_general(left, right, (((1,), (0,)), ((), ())), preferred_element_type=jnp.float32)


def at(start, size):
    return pl.ds(pl.multiple_of(start, size), size)


def norm_stats(values):
    mean = jnp.mean(values, axis=-1, keepdims=True)
    center = values - mean
    spread = jnp.mean(center * center, axis=-1, keepdims=True)
    inverse = lax.rsqrt(spread + EPS)
    return center * inverse, inverse


def norm_back(cot, unit, inverse, gain):
    scaled = cot * gain
    first = jnp.mean(scaled, axis=-1, keepdims=True)
    second = jnp.mean(scaled * unit, axis=-1, keepdims=True)
    return inverse * (scaled - first - unit * second)


class Wires:
    def __init__(self, send_sem, recv_sem, peer):
        self.send_sem, self.recv_sem, self.peer = send_sem, recv_sem, peer
        self.free, self.recvs, self.total, self.pending = list(range(SENDS)), 0, 0, []

    def inbox(self, count):
        base = self.recvs
        self.recvs += count
        assert self.recvs <= RECVS
        return base

    def bulk(self):
        return self.free.pop(0)

    def copy(self, src, dst, lane, slot, device):
        return pltpu.make_async_remote_copy(
            src_ref=src,
            dst_ref=dst,
            send_sem=self.send_sem.at[lane],
            recv_sem=self.recv_sem.at[slot],
            device_id=device,
            device_id_type=MESH,
        )

    def send(self, src, dst, slot, device, when=None, bulk=None):
        lane = self.free.pop(0) if bulk is None else bulk
        copy = self.copy(src, dst, lane, slot, device)
        if when is None:
            copy.start()
        else:
            pl.when(when)(copy.start)
        if bulk is None:
            self.pending.append((self.total, copy, when, lane))
            self.total += 1
        return copy

    def finish(self, entry):
        unused, copy, when, lane = entry
        if when is None:
            copy.wait_send()
        else:
            pl.when(when)(copy.wait_send)
        self.free.append(lane)

    def sent(self, copy):
        for entry in [entry for entry in self.pending if entry[1] is copy]:
            self.finish(entry)
        self.pending = [entry for entry in self.pending if entry[1] is not copy]

    def settle(self, until):
        for entry in [entry for entry in self.pending if entry[0] < until]:
            self.finish(entry)
        self.pending = [entry for entry in self.pending if entry[0] >= until]

    def settle_bulk(self, whole, lane):
        self.copy(whole, whole, lane, 0, self.peer).wait_send()

    def wait(self, dst, slot):
        self.copy(dst, dst, 0, slot, self.peer).wait_recv()


SENDS, RECVS, LOCALS = 67, 126, 17
LEVELS = 4


def scratch_of(rows, width, seqs, views, hidden):
    length = rows * views
    own = width // views
    bf, f3 = jnp.bfloat16, jnp.float32
    vm = pltpu.VMEM
    mlp_rows = hidden * seqs * views // 4
    half, quarter, eighth = width // 2, width // 4, width // 8
    return dict(
        tok=vm((rows, width), bf),
        out_cot=vm((rows, width), bf),
        layer_out=vm((rows, width), bf),
        tokens_grad=vm((rows, width), f3),
        up_grad=vm((hidden, width), f3),
        down_grad=vm((hidden, width), f3),
        w_full=vm((width, 3 * width), bf),
        w_own=vm((width, 3 * own), bf),
        wo=vm((width, width), bf),
        up=vm((mlp_rows, width), bf),
        down=vm((mlp_rows, width), bf),
        ids_all=vm((views, 8, 128), jnp.int32),
        order_vm=vm((16, 128), jnp.int32),
        order_sm=pltpu.SMEM((16, 128), jnp.int32),
        normed=vm((length, width), bf),
        qkv=vm((length, 3 * own), bf),
        qkv_s=vm((length, 3 * own), bf),
        weights=vm((2 * SLOTS, length // SLOTS, length // SLOTS), f3),
        totals=vm((2 * SLOTS, length // SLOTS, 1), f3),
        att_s=vm((length, own), f3),
        att=vm((length, own), bf),
        att_tok=vm((rows, width), bf),
        middle=vm((rows, width), f3),
        normed_two=vm((4 * rows, width), bf),
        mixed_cot=vm((4 * rows, width), bf),
        wide=vm((4 * rows, mlp_rows), f3),
        act=vm((4 * rows, mlp_rows), bf),
        hid_cot=vm((4 * rows, mlp_rows), bf),
        part_own=vm((2, 2, rows, width), f3),
        part_out=vm((2, 3, rows, width), bf),
        part_in=vm((2, 3, rows, width), bf),
        grad_keep=vm((2, mlp_rows // 2, width), bf),
        grad_pass=vm((2, mlp_rows // 2, width), bf),
        grad_core=vm((2, mlp_rows // 2, width), bf),
        grad_y=vm((2, 2, hidden, width), bf),
        grad_z=vm((2, hidden, width), bf),
        branch=vm((rows, width), bf),
        acot_tok=vm((rows, width), bf),
        acot=vm((length, own), bf),
        acot_s=vm((length, own), bf),
        pc_s=vm((length, 3 * own), bf),
        pc=vm((3, length, own), bf),
        pc_flat=vm((length, 3 * own), bf),
        pc_tok=vm((3, rows, width), bf),
        dw_out=vm((2, 3, width // seqs, own), bf),
        dw_x=vm((3, width // seqs, own), bf),
        dw_in=vm((3, 3, width // seqs, own), bf),
        dw_own=vm((3, width // seqs, own), bf),
        do_core=vm((half, width), bf),
        do_core_in=vm((half, width), bf),
        do_first=vm((quarter, width), bf),
        do_first_in=vm((quarter, width), bf),
        do_second=vm((eighth, width), bf),
        do_second_in=vm((eighth, width), bf),
        do_z=vm((eighth, width), bf),
        do_z_in=vm((LEVELS, eighth // LEVELS, width), bf),
        do_own=vm((eighth // LEVELS, width), bf),
        gain_own=vm((8, width), f3),
        gain_in=vm((seqs, 8, width), f3),
        gain_sum=vm((8, width), f3),
        gain_all=vm((views, 8, width), f3),
        send_sem=pltpu.SemaphoreType.DMA((SENDS,)),
        recv_sem=pltpu.SemaphoreType.DMA((RECVS,)),
        local_sem=pltpu.SemaphoreType.DMA((LOCALS,)),
    )


def layer_kernel(names, seqs, views, *refs):
    (tok_hbm, ids, alive, cot_hbm, gain_one_ref, gain_two_ref, w_hbm, wo_hbm, up_hbm, down_hbm) = refs[:10]
    (layer_hbm, tokens_hbm, gains, w_grad, o_grad, up_part, up_away, down_hbm_out) = refs[10:18]
    k = types.SimpleNamespace(**dict(zip(names, refs[18:])))
    k.slope = k.part_all = k.do_keep = k.wide
    tok, out_cot = k.tok, k.out_cot
    layer_out, tokens_grad, up_grad, down_grad = k.layer_out, k.tokens_grad, k.up_grad, k.down_grad
    rows, width = tok.shape
    length = rows * views
    own = width // views
    hidden = up_hbm.shape[0]
    mlp_rows = k.up.shape[0]
    half = mlp_rows // 2
    block = length // (SLOTS * SCENE_BLOCKS)
    scene = length // SLOTS
    scale = HEAD_DIM ** (-0.5)
    bf, f3 = jnp.bfloat16, jnp.float32

    s = lax.axis_index("seq")
    v = lax.axis_index("view")
    x, c, z, y = s // 2, s % 2, v // 2, v % 2
    x_s, c_s, xc_s = (1 - x) * 2 + c, x * 2 + (1 - c), (1 - x) * 2 + (1 - c)
    y_v = z * 2 + (1 - y)
    z_pair, z_two, z_flip = z + 1 - 2 * (z % 2), lax.rem(z + 2, LEVELS), LEVELS - 1 - z
    inner = (z == 1) | (z == 2)
    others_z = [z_pair, z_two, z_flip]
    low, high = z % 2, z // 2
    pair_v = z_pair * 2 + y
    own_slot, x_slot = x * 2 + low, (1 - x) * 2 + low
    pair_slot, far_slot = x * 2 + (1 - low), (1 - x) * 2 + (1 - low)
    view_peers = [lax.rem(v + d, views) for d in range(1, views)]
    seq_peers = [x_s, xc_s, c_s]

    def level(zt):
        return (s, zt * 2 + y)

    wires = Wires(k.send_sem, k.recv_sem, (c_s, v))
    in_normed = wires.inbox(2 * views)
    in_ids = wires.inbox(views)
    in_up = wires.inbox(LEVELS + 1)
    in_down = wires.inbox(LEVELS + 1)
    in_mcot = wires.inbox(4)
    in_att = wires.inbox(views)
    in_two = wires.inbox(4)
    in_part = [wires.inbox(5), wires.inbox(5)]
    in_core = [wires.inbox(1), wires.inbox(1)]
    in_grad = [wires.inbox(3), wires.inbox(3)]
    in_acot, in_pc = in_ids, in_att
    in_dw = wires.inbox(3)
    in_do = wires.inbox(3)
    in_do_z = wires.inbox(LEVELS)
    in_plane = wires.inbox(views)
    in_query = wires.inbox(views)
    in_cross = wires.inbox(views)
    in_mate = [wires.inbox(1) for unused in range(3)]
    in_out = [wires.inbox(views), wires.inbox(views)]
    in_out_mate = wires.inbox(1)
    in_gain = wires.inbox(seqs)
    in_gains = in_normed
    to_view = [wires.bulk() for unused in range(5)]
    to_mate_w = [wires.bulk() for unused in range(3)]
    to_mate_o = wires.bulk()

    def z_cast(src, dst, slot):
        wires.send(src, dst, slot, level(z_pair))
        wires.send(src, dst, slot, level(z_two))
        wires.send(src, dst, slot, level(z_flip), when=inner)

    def z_relay(ref, slot):
        wires.send(ref, ref, slot, level(z_pair), when=inner)

    barrier = pltpu.get_barrier_semaphore()
    greeted = [(s, p) for p in view_peers] + [(p, v) for p in seq_peers]
    for device in greeted:
        pl.semaphore_signal(barrier, inc=1, device_id=device, device_id_type=MESH)

    loads, kept = [], []

    def load(src, dst):
        copy = pltpu.make_async_copy(src, dst, k.local_sem.at[len(loads)])
        copy.start()
        loads.append(copy)
        return copy

    up_slot = at((c * 4 + y * 2 + high) * hidden, hidden)
    load_tok = load(tok_hbm, tok)
    load_cot = load(cot_hbm, out_cot)
    load_up = load(up_hbm, k.up.at[up_slot])
    load_down = load(down_hbm, k.down.at[up_slot])
    load_own = [
        load(w_hbm.at[:, at(t * width + v * own, own)], k.w_own.at[:, pl.ds(t * own, own)])
        for t in range(3)
    ]
    load_wo = load(wo_hbm, k.wo)
    load_w = load(w_hbm, k.w_full)

    gain_one = gain_one_ref[...].astype(f3).reshape(1, width)
    gain_two = gain_two_ref[...].astype(f3).reshape(1, width)
    load_tok.wait()
    unit, _ = norm_stats(tok[...].astype(f3))
    k.normed[at(v * rows, rows), :] = (unit * gain_one).astype(bf)
    per = rows // block
    lane = lax.broadcasted_iota(jnp.int32, (1, 128), 1)
    scenes = jnp.zeros((1, 128), jnp.int32)
    for m in range(per):
        mine = jnp.broadcast_to(ids[:, m * block : m * block + 1], (1, 128))
        scenes = jnp.where(lane == v * per + m, mine, scenes)
    k.ids_all[v] = jnp.broadcast_to(scenes, (8, 128))
    live = jnp.transpose(jnp.broadcast_to(alive[...].astype(f3), (rows, rows)))[:, :1]
    pl.semaphore_wait(barrier, len(greeted))

    def view_rows(ref, j):
        return ref.at[at(j * rows, rows)]

    for p in view_peers:
        wires.send(k.ids_all.at[v], k.ids_all.at[v], in_ids + v, (s, p), bulk=to_view[0])

    def normed_half(j, i):
        return k.normed.at[at(j * rows + i * (rows // 2), rows // 2)], in_normed + 2 * j + i

    for i in range(2):
        mine, slot = normed_half(v, i)
        wires.send(mine, mine, slot, (s, y_v))
    for zt in (z_pair, z_two):
        for i in range(2):
            mine, slot = normed_half(v, i)
            wires.send(mine, mine, slot, level(zt))
    for i in range(2):
        mine, slot = normed_half(v, i)
        wires.send(mine, mine, slot, level(z_flip), when=inner)
    load_cot.wait()
    mcot_own = at(own_slot * rows, rows)
    k.mixed_cot[mcot_own, :] = (live * out_cot[...].astype(f3)).astype(bf)

    def slot_rows(ref, slot):
        return ref.at[at(slot * rows, rows)]

    def square_send(ref, base, slot, device):
        wires.send(slot_rows(ref, slot), slot_rows(ref, slot), base + slot, device)

    def square_relay(ref, base):
        wires.wait(slot_rows(ref, pair_slot), base + pair_slot)
        square_send(ref, base, pair_slot, (x_s, v))

    square_send(k.mixed_cot, in_mcot, own_slot, (x_s, v))

    for p in view_peers:
        wires.wait(k.ids_all.at[p], in_ids + p)
    count = SLOTS * SCENE_BLOCKS
    scene_row = k.ids_all[0][:1]
    for j in range(1, views):
        scene_row = scene_row + k.ids_all[j][:1]
    big = lax.broadcasted_iota(jnp.int32, (128, 128), 0)
    wide = lax.broadcasted_iota(jnp.int32, (128, 128), 1)
    scene_mat = jnp.broadcast_to(scene_row, (128, 128))
    scene_col = jnp.transpose(scene_mat)
    ahead = (scene_col < scene_mat) | ((scene_col == scene_mat) & (big < wide))
    place = jnp.sum(jnp.where(ahead & (big < count), 1, 0), axis=0, keepdims=True)
    place_col = jnp.transpose(jnp.broadcast_to(place, (128, 128)))
    hit = jnp.where((place_col == wide) & (big < count), big, 0)
    source = jnp.sum(hit, axis=0, keepdims=True)
    k.order_vm[0:8, :] = jnp.broadcast_to(source, (8, 128))
    k.order_vm[8:16, :] = jnp.broadcast_to(place, (8, 128))
    to_scalar = load(k.order_vm, k.order_sm)

    for copy in load_own:
        copy.wait()

    def mlp_slot(ref, yt, ht):
        return ref.at[at((c * 4 + yt * 2 + ht) * hidden, hidden)]

    def send_mlp(ref, base, device):
        mine = mlp_slot(ref, y, high)
        wires.send(mine, mine, base + y * 2 + high, device)

    def mlp_relay(ref, base):
        there = mlp_slot(ref, y, 1 - high)
        wires.wait(there, base + y * 2 + 1 - high)
        wires.send(there, there, base + y * 2 + 1 - high, (s, y_v))

    def core_exchange(ref, base):
        for ht in (high, 1 - high):
            wires.wait(mlp_slot(ref, 1 - y, ht), base + (1 - y) * 2 + ht)
        mine = ref.at[at(c * half, half)]
        wires.send(mine, mine, base + LEVELS, (c_s, v))

    def project(j):
        k.qkv[at(j * rows, rows), :] = dot_nn(k.normed[at(j * rows, rows), :], k.w_own[...]).astype(bf)

    project(v)
    for zt in others_z:
        j = zt * 2 + y
        for i in range(2):
            there, slot = normed_half(j, i)
            wires.wait(there, slot)
            if zt is z_two:
                z_relay(there, slot)
            wires.send(there, there, slot, (s, y_v))
        if zt is z_two:
            load_up.wait()
            send_mlp(k.up, in_up, level(z_two))
            square_send(k.mixed_cot, in_mcot, own_slot, (s, pair_v))
        project(j)
    send_mlp(k.up, in_up, (s, y_v))
    for zt in [z] + others_z:
        j = zt * 2 + 1 - y
        for i in range(2):
            wires.wait(*normed_half(j, i))
        project(j)
    to_scalar.wait()

    def reorder(dst, src, row):
        blocks = src.reshape(count, block, src.shape[1])

        def step(i, unused):
            from_block = k.order_sm[row, i]
            dst[at(i * block, block), :] = blocks[from_block].astype(dst.dtype)
            return unused

        lax.fori_loop(0, count, step, 0, unroll=8)

    reorder(k.qkv_s, k.qkv, 0)

    head_lane = lax.broadcasted_iota(jnp.int32, (scene, own), 1) // HEAD_DIM

    def attend(g, unused):
        here = at(g * scene, scene)
        queries, keys, values = (k.qkv_s[here, pl.ds(t * own, own)] for t in range(3))
        result = jnp.zeros((scene, own), f3)
        for e in range(2):
            chosen = jnp.where(head_lane == e, queries, jnp.zeros_like(queries))
            weights = jnp.exp(dot_inner(chosen, keys) * scale)
            total = jnp.sum(weights, axis=-1, keepdims=True)
            k.weights[g * 2 + e] = weights
            k.totals[g * 2 + e] = total
            mixed = dot_nn(weights.astype(bf), values) / total
            result = jnp.where(head_lane == e, mixed, result)
        k.att_s[here, :] = result
        return unused

    lax.fori_loop(0, SLOTS, attend, 0, unroll=True)
    reorder(k.att, k.att_s, 8)
    own_cols = at(v * own, own)
    for p in view_peers:
        wires.send(view_rows(k.att, p), k.att_tok.at[:, own_cols], in_att + v, (s, p), bulk=to_view[1])
    square_relay(k.mixed_cot, in_mcot)
    mlp_relay(k.up, in_up)
    load_down.wait()
    send_mlp(k.down, in_down, level(z_two))
    send_mlp(k.down, in_down, (s, y_v))
    k.att_tok[:, own_cols] = k.att[at(v * rows, rows), :]


    load_wo.wait()
    for p in view_peers:
        wires.wait(k.att_tok.at[:, at(p * own, own)], in_att + p)
    tile = 256
    for n in range(width // tile):
        cols = pl.ds(n * tile, tile)
        k.middle[:, cols] = tok[:, cols].astype(f3) + live * dot_nn(k.att_tok[...], k.wo[:, cols])
    unit_two, _ = norm_stats(k.middle[...])
    k.normed_two[mcot_own, :] = (unit_two * gain_two).astype(bf)
    until_two = wires.total
    for device in ((s, pair_v), (x_s, v)):
        square_send(k.normed_two, in_two, own_slot, device)

    core_exchange(k.up, in_up)
    square_relay(k.normed_two, in_two)
    mlp_relay(k.down, in_down)
    wires.wait(k.up.at[at((1 - c) * half, half)], in_up + LEVELS)

    def hidden_tiles(slot):
        here = at(slot * rows, rows)

        def step(n, unused):
            cols = at(n * tile, tile)
            pre = dot_inner(k.normed_two[here, :], k.up[cols, :])
            below = 0.5 + 0.5 * lax.erf(pre * (0.5**0.5))
            k.act[here, cols] = (pre * below).astype(bf)
            k.slope[here, cols] = below + pre * (jnp.exp(-0.5 * pre * pre) * (0.5 / math.pi) ** 0.5)
            return unused

        lax.fori_loop(0, mlp_rows // tile, step, 0)

    hidden_tiles(own_slot)
    hidden_tiles(pair_slot)
    for slot in (x_slot, far_slot):
        wires.wait(slot_rows(k.normed_two, slot), in_two + slot)
        hidden_tiles(slot)

    def grad_tiles(left, right, start, dst):
        def step(n, unused):
            there = at(n * tile, tile)
            dst[there, :] = dot_outer(left[:, at(start + n * tile, tile)], right[...]).astype(dst.dtype)
            return unused

        lax.fori_loop(0, half // tile, step, 0)

    passed = []

    def grad_halves(which, left, right):
        grad_tiles(left, right, (1 - c) * half, k.grad_pass.at[which])
        passed.append(wires.send(k.grad_pass.at[which], k.grad_core.at[which], in_core[which], (c_s, v)))
        grad_tiles(left, right, c * half, k.grad_keep.at[which])

    for slot in (x_slot, far_slot):
        wires.wait(slot_rows(k.mixed_cot, slot), in_mcot + slot)
    core_exchange(k.down, in_down)
    grad_halves(0, k.act, k.mixed_cot)

    def grad_sum(which, start, size):
        there = at(start, size)
        return k.grad_keep[which, there, :].astype(f3) + k.grad_core[which, there, :].astype(f3)

    def grads_to_y(which):
        wires.wait(k.grad_core.at[which], in_core[which])
        wires.sent(passed[which])
        for i, ht in enumerate((1 - high, high)):
            start = ((1 - y) * 2 + ht) * hidden
            there = at(start, hidden)
            k.grad_pass[which, there, :] = grad_sum(which, start, hidden).astype(bf)
            wires.send(k.grad_pass.at[which, there], k.grad_y.at[which, i], in_grad[which] + i, (s, y_v))

    def grad_block(which, i, ht):
        wires.wait(k.grad_y.at[which, i], in_grad[which] + i)
        return grad_sum(which, (y * 2 + ht) * hidden, hidden) + k.grad_y[which, i].astype(f3)

    def grads_to_z(which):
        there = at((y * 2 + 1 - high) * hidden, hidden)
        k.grad_pass[which, there, :] = grad_block(which, 0, 1 - high).astype(bf)
        wires.send(k.grad_pass.at[which, there], k.grad_z.at[which], in_grad[which] + 2, level(z_two))

    def collect(which, dst):
        total = grad_block(which, 1, high)
        wires.wait(k.grad_z.at[which], in_grad[which] + 2)
        dst[...] = total + k.grad_z[which].astype(f3)


    wires.wait(k.down.at[at((1 - c) * half, half)], in_down + LEVELS)

    def cot_tile(n, unused):
        cols = at(n * tile, tile)
        up_to = dot_inner(k.mixed_cot[...], k.down[cols, :])
        k.hid_cot[:, cols] = (up_to * k.slope[:, cols]).astype(bf)
        return unused

    lax.fori_loop(0, mlp_rows // tile, cot_tile, 0)

    strip = width // 2

    def strip_cols(i):
        return pl.ds(i * strip, strip)

    def part_tiles(which, left, right):
        for i in range(2):

            def step(n, unused):
                cols = at(i * strip + n * tile, tile)
                k.part_all[:, cols] = dot_nn(left[...], right[:, cols])
                return unused

            lax.fori_loop(0, strip // tile, step, 0)
            cols = strip_cols(i)
            k.part_out[which, 0, :, cols] = k.part_all[at(far_slot * rows, rows), cols].astype(bf)
            there = k.part_out.at[which, 0, :, cols], k.part_in.at[which, 0, :, cols]
            wires.send(*there, in_part[which] + i, (x_s, v))
        k.part_out[which, 1] = k.part_all[at(x_slot * rows, rows), :].astype(bf)
        wires.send(k.part_out.at[which, 1], k.part_in.at[which, 1], in_part[which] + 2, (x_s, v))
        for i, slot in enumerate((own_slot, pair_slot)):
            k.part_own[which, i] = k.part_all[at(slot * rows, rows), :]

    def part_join(which):
        for i in range(2):
            cols = strip_cols(i)
            wires.wait(k.part_in.at[which, 0, :, cols], in_part[which] + i)
            joined = k.part_own[which, 1, :, cols] + k.part_in[which, 0, :, cols].astype(f3)
            k.part_out[which, 2, :, cols] = joined.astype(bf)
            there = k.part_out.at[which, 2, :, cols], k.part_in.at[which, 2, :, cols]
            wires.send(*there, in_part[which] + 3 + i, (s, pair_v))

    grads_to_y(0)
    part_tiles(0, k.hid_cot, k.up)
    grad_halves(1, k.hid_cot, k.normed_two)
    part_tiles(1, k.act, k.down)
    part_join(0)

    def part_sum(which):
        total = k.part_own[which, 0]
        wires.wait(k.part_in.at[which, 1], in_part[which] + 2)
        for i in range(2):
            wires.wait(k.part_in.at[which, 2, :, strip_cols(i)], in_part[which] + 3 + i)
        for i in (1, 2):
            total = total + k.part_in[which, i].astype(f3)
        return total

    unit_two, inverse_two = norm_stats(k.middle[...])
    wires.settle(until_two)
    cot_two = part_sum(0)
    until_acot = wires.total
    k.gain_own[1:2, :] = jnp.sum(cot_two * unit_two, axis=0, keepdims=True)
    middle_cot = out_cot[...].astype(f3) + norm_back(cot_two, unit_two, inverse_two, gain_two)
    tokens_grad[...] = middle_cot
    k.branch[...] = (live * middle_cot).astype(bf)
    for n in range(width // tile):
        k.acot_tok[:, pl.ds(n * tile, tile)] = dot_inner(
            k.branch[...], k.wo[pl.ds(n * tile, tile), :]
        ).astype(bf)
    for p in view_peers:
        wires.send(k.acot_tok.at[:, at(p * own, own)], view_rows(k.acot, v), in_acot + v, (s, p), bulk=to_view[2])
    k.acot[at(v * rows, rows), :] = k.acot_tok[:, own_cols]

    o_half, o_quarter, o_eighth = width // 2, width // 4, width // 8
    o_piece = o_eighth // LEVELS

    def outer_rows(start, dst, dtype):
        def step(n, unused):
            there = at(n * tile, tile)
            left = k.att_tok[:, at(start + n * tile, tile)]
            dst[there, :] = dot_outer(left, k.branch[...]).astype(dtype)
            return unused

        lax.fori_loop(0, o_half // tile, step, 0)

    outer_rows((1 - c) * o_half, k.do_core, bf)
    wires.send(k.do_core, k.do_core_in, in_do, (c_s, v))
    outer_rows(c * o_half, k.do_keep, f3)
    wires.wait(k.do_core_in, in_do)
    k.do_keep[...] = k.do_keep[...] + k.do_core_in[...].astype(f3)
    k.do_first[...] = k.do_keep[at((1 - x) * o_quarter, o_quarter), :].astype(bf)

    for p in view_peers:
        wires.wait(view_rows(k.acot, p), in_acot + p)
    grads_to_y(1)
    part_join(1)
    reorder(k.acot_s, k.acot, 0)

    def attend_back(g, unused):
        here = at(g * scene, scene)
        queries, keys, values = (k.qkv_s[here, pl.ds(t * own, own)] for t in range(3))
        cots = k.acot_s[here, :]
        agree = cots.astype(f3) * k.att_s[here, :]
        outs = [jnp.zeros((scene, own), f3) for t in range(3)]
        for e in range(2):
            mine = head_lane == e
            delta = jnp.sum(jnp.where(mine, agree, 0.0), axis=-1, keepdims=True)
            chosen = jnp.where(mine, cots, jnp.zeros_like(cots))
            weights = k.weights[g * 2 + e]
            inverse = 1.0 / k.totals[g * 2 + e]
            weights_cot = dot_inner(chosen, values)
            score_cot = (weights * inverse * (weights_cot - delta)).astype(bf)
            shared = (cots.astype(f3) * inverse).astype(bf)
            new = (
                dot_nn(score_cot, keys) * scale,
                dot_outer(score_cot, queries) * scale,
                dot_outer(weights.astype(bf), shared),
            )
            outs = [jnp.where(mine, fresh, old) for fresh, old in zip(new, outs)]
        for t in range(3):
            k.pc_s[here, pl.ds(t * own, own)] = outs[t].astype(bf)
        return unused

    lax.fori_loop(0, SLOTS, attend_back, 0, unroll=True)
    pc_blocks = k.pc_s.reshape(count, block, 3 * own)

    def unsort(i, unused):
        found = pc_blocks[k.order_sm[8, i]]
        k.pc_flat[at(i * block, block), :] = found
        for t in range(3):
            k.pc[t, at(i * block, block), :] = found[:, t * own : (t + 1) * own]
        return unused

    lax.fori_loop(0, count, unsort, 0, unroll=8)
    for p in view_peers:
        wires.send(k.pc.at[:, at(p * rows, rows)], k.pc_tok.at[:, :, own_cols], in_pc + v, (s, p), bulk=to_view[3])
    for t in range(3):
        k.pc_tok[t, :, own_cols] = k.pc[t, at(v * rows, rows), :]

    part = width // seqs

    def own_dw(row_block):
        whole = dot_outer(k.normed[:, at(row_block * part, part)], k.pc_flat[...])
        return [whole[:, t * own : (t + 1) * own] for t in range(3)]

    for i, xt in enumerate((1 - x, x)):
        for t, value in enumerate(own_dw(xt * 2 + 1 - c)):
            k.dw_out[i, t] = value.astype(bf)
        wires.send(k.dw_out.at[i], k.dw_in.at[i], in_dw + i, (c_s, v))
    cross_dw = own_dw(x_s)
    wires.wait(k.dw_in.at[0], in_dw)
    for t in range(3):
        k.dw_x[t] = (cross_dw[t] + k.dw_in[0, t].astype(f3)).astype(bf)
    wires.send(k.dw_x, k.dw_in.at[2], in_dw + 2, (x_s, v))
    mine_dw = own_dw(s)
    wires.wait(k.dw_in.at[1], in_dw + 1)
    wires.settle(until_acot)
    wires.wait(k.dw_in.at[2], in_dw + 2)
    for t in range(3):
        total = mine_dw[t] + k.dw_in[1, t].astype(f3) + k.dw_in[2, t].astype(f3)
        k.dw_own[t] = total.astype(bf)

    def w_at(q, j, first, last):
        return w_grad.at[pl.ds(first, last - first), at(q * part, part), at(j * own, own)]

    def w_plane(j):
        return w_at(s, j, 0, 3)

    def w_query(j):
        return w_at(x_s, j, 0, 1)

    def w_cross(q, j):
        return w_at(q, j, 1, 3)

    wires.send(k.dw_own.at[pl.ds(0, 1)], w_at(s, v, 0, 1), in_query + v, (x_s, v))
    wires.send(k.do_first, k.do_first_in, in_do + 1, (x_s, v))
    wires.send(k.dw_own, w_plane(v), in_plane + v, (s, y_v))
    z_cast(k.dw_own, w_plane(v), in_plane + v)
    wires.send(k.dw_own.at[pl.ds(1, 2)], w_cross(s, v), in_cross + v, (x_s, v))
    wires.send(k.dw_own, w_plane(v), in_mate[0], (c_s, v), bulk=to_mate_w[0])
    kept.append(load(k.dw_own, w_plane(v)))

    wires.wait(w_query(v), in_query + v)
    wires.send(w_query(v), w_query(v), in_query + v, (s, y_v))
    z_cast(w_query(v), w_query(v), in_query + v)
    wires.send(w_query(v), w_query(v), in_mate[1], (c_s, v), bulk=to_mate_w[1])

    wires.wait(k.do_first_in, in_do + 1)
    o_mine = at(x * o_quarter, o_quarter)
    k.do_keep[o_mine, :] = k.do_keep[o_mine, :] + k.do_first_in[...].astype(f3)
    k.do_second[...] = k.do_keep[at(x * o_quarter + (1 - y) * o_eighth, o_eighth), :].astype(bf)
    wires.send(k.do_second, k.do_second_in, in_do + 2, (s, y_v))
    def o_at(q, j):
        at_c, at_x, at_y, at_z = q % 2, q // 2, j % 2, j // 2
        return o_grad.at[at(at_c * o_half + at_x * o_quarter + at_y * o_eighth + at_z * o_piece, o_piece)]

    def to_mate(which, ref):
        wires.send(ref, ref, in_mate[which], (c_s, v), bulk=to_mate_w[which])

    def pass_plane(zt, row_y):
        j = zt * 2 + row_y
        wires.wait(w_plane(j), in_plane + j)
        if row_y is y:
            if zt is z_two:
                z_relay(w_plane(j), in_plane + j)
            wires.send(w_plane(j), w_plane(j), in_plane + j, (s, y_v))
        wires.send(w_cross(s, j), w_cross(s, j), in_cross + j, (x_s, v))
        to_mate(0, w_plane(j))

    def pass_query(zt, row_y):
        j = zt * 2 + row_y
        wires.wait(w_query(j), in_query + j)
        if row_y is y:
            if zt is z_two:
                z_relay(w_query(j), in_query + j)
            wires.send(w_query(j), w_query(j), in_query + j, (s, y_v))
        to_mate(1, w_query(j))

    across = 1 - y
    pass_plane(z, across)

    load_w.wait()
    for p in view_peers:
        wires.wait(k.pc_tok.at[:, :, at(p * own, own)], in_pc + p)

    def back_tile(n, unused):
        cols = at(n * tile, tile)
        total = dot_inner(k.pc_tok[0], k.w_full[cols, pl.ds(0, width)])
        for t in range(1, 3):
            total = total + dot_inner(k.pc_tok[t], k.w_full[cols, pl.ds(t * width, width)])
        k.part_own[0, 0, :, cols] = total
        return unused

    lax.fori_loop(0, width // tile, back_tile, 0)
    unit_one, inverse_one = norm_stats(tok[...].astype(f3))
    cot_one = k.part_own[0, 0]
    k.gain_own[0:1, :] = jnp.sum(cot_one * unit_one, axis=0, keepdims=True)
    k.gain_own[2:8, :] = jnp.zeros((6, width), f3)
    tokens_grad[...] = tokens_grad[...] + norm_back(cot_one, unit_one, inverse_one, gain_one)
    for p in seq_peers:
        wires.send(k.gain_own, k.gain_in.at[s], in_gain + s, (p, v))
    kept.append(load(tokens_grad, tokens_hbm))

    wires.wait(k.do_second_in, in_do + 2)
    total = k.do_keep[at(x * o_quarter + y * o_eighth, o_eighth), :] + k.do_second_in[...].astype(f3)
    k.do_z[...] = total.astype(bf)

    def o_level(zt):
        return at(zt * o_piece, o_piece)

    for zt in others_z:
        wires.send(k.do_z.at[o_level(zt)], k.do_z_in.at[z], in_do_z + z, level(zt))

    pass_plane(z_pair, y)
    pass_plane(z_two, y)
    pass_query(z, across)
    pass_plane(z_pair, across)
    pass_query(z_pair, y)
    pass_query(z_two, y)
    pass_plane(z_flip, y)
    pass_plane(z_two, across)
    there = at((y * 2 + 1 - high) * hidden, hidden)
    k.grad_pass[1, there, :] = grad_block(1, 0, 1 - high).astype(bf)
    kept.append(load(k.grad_pass.at[1, there], up_away))
    up_grad[...] = grad_block(1, 1, high)
    kept.append(load(up_grad, up_part))
    total = k.do_keep[at(x * o_quarter + y * o_eighth + z * o_piece, o_piece), :]
    total = total + k.do_second_in[o_level(z), :].astype(f3)
    for zt in others_z:
        wires.wait(k.do_z_in.at[zt], in_do_z + zt)
        total = total + k.do_z_in[zt].astype(f3)
    k.do_own[...] = total.astype(bf)
    wires.send(k.do_own, o_at(s, v), in_out[0] + v, (s, y_v))
    z_cast(k.do_own, o_at(s, v), in_out[0] + v)
    wires.send(k.do_own, o_at(s, v), in_out[1] + v, (x_s, v))
    wires.send(k.do_own, o_at(s, v), in_out_mate, (c_s, v), bulk=to_mate_o)
    kept.append(load(k.do_own, o_at(s, v)))
    pass_query(z_flip, y)
    pass_plane(z_flip, across)
    for zt in others_z:
        pass_query(zt, across)

    total = k.gain_own[...]
    for p in seq_peers:
        wires.wait(k.gain_in.at[p], in_gain + p)
        total = total + k.gain_in[p]
    k.gain_sum[...] = total
    for p in view_peers:
        wires.send(k.gain_sum, k.gain_all.at[v], in_gains + v, (s, p), bulk=to_view[4])

    def out_mate(q, j):
        wires.send(o_at(q, j), o_at(q, j), in_out_mate, (c_s, v), bulk=to_mate_o)

    def pass_out(zt, row_y):
        j = zt * 2 + row_y
        slot = in_out[0] + j
        wires.wait(o_at(s, j), slot)
        if row_y is y:
            if zt is z_two:
                z_relay(o_at(s, j), slot)
            wires.send(o_at(s, j), o_at(s, j), slot, (s, y_v))
        wires.send(o_at(s, j), o_at(s, j), in_out[1] + j, (x_s, v))
        out_mate(s, j)

    for zt in others_z:
        pass_out(zt, y)
    grads_to_z(0)
    for zt in [z] + others_z:
        pass_out(zt, across)

    layer_out[...] = (k.middle[...] + live * part_sum(1)).astype(bf)
    kept.append(load(layer_out, layer_hbm))
    by_arrival = [v] + [zt * 2 + y for zt in others_z] + [zt * 2 + across for zt in [z] + others_z]
    for j in by_arrival:
        wires.wait(w_cross(x_s, j), in_cross + j)
        to_mate(2, w_cross(x_s, j))
    for j in by_arrival:
        wires.wait(o_at(x_s, j), in_out[1] + j)
        out_mate(x_s, j)

    total = k.gain_sum[...]
    for p in view_peers:
        wires.wait(k.gain_all.at[p], in_gains + p)
        total = total + k.gain_all[p]
    gains[...] = total

    collect(0, down_grad)
    kept.append(load(down_grad, down_hbm_out))
    def w_rows(q, first, last):
        return w_grad.at[pl.ds(first, last - first), at(q * part, part)]

    def o_core(core):
        return o_grad.at[at(core * o_half, o_half)]

    wires.settle(wires.total)
    for whole, lane in (
        (k.ids_all.at[pl.ds(0, views - 1)], to_view[0]),
        (k.att.at[pl.ds(0, length - rows)], to_view[1]),
        (k.acot.at[pl.ds(0, length - rows)], to_view[2]),
        (k.pc.at[:, pl.ds(0, length - rows)], to_view[3]),
        (k.gain_all.at[pl.ds(0, views - 1)], to_view[4]),
        (w_rows(s, 0, 3), to_mate_w[0]),
        (w_rows(x_s, 0, 1), to_mate_w[1]),
        (w_rows(x_s, 1, 3), to_mate_w[2]),
        (o_core(c), to_mate_o),
    ):
        wires.settle_bulk(whole, lane)
    wires.wait(w_rows(c_s, 0, 3), in_mate[0])
    wires.wait(w_rows(xc_s, 0, 1), in_mate[1])
    wires.wait(w_rows(xc_s, 1, 3), in_mate[2])
    wires.wait(o_core(1 - c), in_out_mate)
    for copy in kept:
        copy.wait()


FINISH_STEPS = 8


def finish_kernel(*refs):
    (layer_in, tokens_in, gains, w_in, o_in, down_in) = refs[:6]
    (layer_out, tokens_grad, gain_one, w_out, o_out, gain_two, down_out) = refs[6:13]
    (layer, tokens, down, w_narrow, o_narrow, w_wide, o_wide, in_sem, out_sem) = refs[13:]
    width = o_in.shape[0]
    tall = width // FINISH_STEPS
    asis = ((layer_in, layer, layer_out), (tokens_in, tokens, tokens_grad), (down_in, down, down_out))

    def rows(i):
        return pl.ds(i * tall, tall)

    def start(src, dst, sem):
        copy = pltpu.make_async_copy(src, dst, sem)
        copy.start()
        return copy

    reads, writes = [], []
    for i in range(FINISH_STEPS):
        reads.append(start(w_in.at[:, rows(i)], w_narrow.at[:, rows(i)], in_sem.at[2 * i]))
        reads.append(start(o_in.at[rows(i)], o_narrow.at[rows(i)], in_sem.at[2 * i + 1]))
    late = [start(src, mid, in_sem.at[2 * FINISH_STEPS + i]) for i, (src, mid, dst) in enumerate(asis)]
    gain_one[...] = gains[0:1, :].reshape(width)
    gain_two[...] = gains[1:2, :].reshape(width)
    for i in range(FINISH_STEPS):
        reads[2 * i].wait()
        for t in range(3):
            w_wide[rows(i), t * width : (t + 1) * width] = w_narrow[t, rows(i), :].astype(jnp.float32)
        writes.append(start(w_wide.at[rows(i)], w_out.at[rows(i)], out_sem.at[2 * i]))
        reads[2 * i + 1].wait()
        o_wide[rows(i), :] = o_narrow[rows(i), :].astype(jnp.float32)
        writes.append(start(o_wide.at[rows(i)], o_out.at[rows(i)], out_sem.at[2 * i + 1]))
    for i, (src, mid, dst) in enumerate(asis):
        late[i].wait()
        writes.append(start(mid, dst, out_sem.at[2 * FINISH_STEPS + i]))
    for copy in writes:
        copy.wait()


def fused(
    seqs,
    views,
    tokens,
    scene_ids,
    live_mask,
    out_grad,
    attention_gain,
    input_weight,
    output_weight,
    feedforward_gain,
    up_weight,
    down_weight,
):
    rows, width = tokens.shape[1:]
    hidden = up_weight.shape[0]
    spec = scratch_of(rows, width, seqs, views, hidden)
    vmem = pl.BlockSpec(memory_space=pltpu.VMEM)
    anywhere = pl.BlockSpec(memory_space=pl.ANY)
    shape = jax.ShapeDtypeStruct
    bf, f3 = jnp.bfloat16, jnp.float32
    layer_raw, tokens_raw, gains, w_raw, o_raw, up_part, up_away, down_raw = pl.pallas_call(
        functools.partial(layer_kernel, tuple(spec), seqs, views),
        out_shape=(
            shape((rows, width), bf),
            shape((rows, width), f3),
            shape((8, width), f3),
            shape((3, width, width), bf),
            shape((width, width), bf),
            shape((hidden, width), f3),
            shape((hidden, width), bf),
            shape((hidden, width), f3),
        ),
        in_specs=[anywhere, vmem, vmem, anywhere, vmem, vmem] + [anywhere] * 4,
        out_specs=(anywhere, anywhere, vmem) + (anywhere,) * 5,
        scratch_shapes=list(spec.values()),
        compiler_params=pltpu.CompilerParams(
            collective_id=0, has_side_effects=True, vmem_limit_bytes=67043328
        ),
        name="layer",
    )(
        tokens[0],
        scene_ids,
        live_mask,
        out_grad[0],
        attention_gain,
        feedforward_gain,
        input_weight,
        output_weight,
        up_weight,
        down_weight,
    )
    shift = [(j, (j + views // 2) % views) for j in range(views)]
    up_grad = up_part + lax.ppermute(up_away, "view", shift).astype(f3)
    layer_out, tokens_grad, gain_one, w_grad, o_grad, gain_two, down_grad = pl.pallas_call(
        finish_kernel,
        out_shape=(
            shape((rows, width), bf),
            shape((rows, width), f3),
            shape((width,), f3),
            shape((width, 3 * width), f3),
            shape((width, width), f3),
            shape((width,), f3),
            shape((hidden, width), f3),
        ),
        in_specs=[anywhere] * 2 + [vmem] + [anywhere] * 3,
        out_specs=(anywhere, anywhere, vmem, anywhere, anywhere, vmem, anywhere),
        scratch_shapes=[
            pltpu.VMEM((rows, width), bf),
            pltpu.VMEM((rows, width), f3),
            pltpu.VMEM((hidden, width), f3),
            pltpu.VMEM((3, width, width), bf),
            pltpu.VMEM((width, width), bf),
            pltpu.VMEM((width, 3 * width), f3),
            pltpu.VMEM((width, width), f3),
            pltpu.SemaphoreType.DMA((2 * FINISH_STEPS + 4,)),
            pltpu.SemaphoreType.DMA((2 * FINISH_STEPS + 4,)),
        ],
        cost_estimate=pl.CostEstimate(
            flops=4 * width * width, transcendentals=0, bytes_accessed=28 * width * width
        ),
        name="finish",
    )(layer_raw, tokens_raw, gains, w_raw, o_raw, down_raw)
    return (
        layer_out[None],
        tokens_grad[None],
        gain_one,
        w_grad,
        o_grad,
        gain_two,
        up_grad,
        down_grad,
    )


def solution(mesh):
    seqs, views = mesh.shape["seq"], mesh.shape["view"]
    small = seqs == 4 and views == 2 * LEVELS and HEADS == 2 * views
    body = functools.partial(fused, seqs, views) if small else shards
    return jax.shard_map(
        body,
        mesh=mesh,
        in_specs=(
            P("seq", "view", None),
            P("seq", "view"),
            P("seq", "view"),
            P("seq", "view", None),
            P(),
            P(),
            P(),
            P(),
            P(("seq", "view"), None),
            P(("seq", "view"), None),
        ),
        out_specs=(
            P("seq", "view", None),
            P("seq", "view", None),
            P(),
            P(),
            P(),
            P(),
            P(("seq", "view"), None),
            P(("seq", "view"), None),
        ),
        check_vma=False,
    )
```

```python
import functools
import math
import types

import jax
import jax.numpy as jnp
from jax import lax
from jax.experimental import pallas as pl
from jax.experimental.pallas import tpu as pltpu
from jax.sharding import PartitionSpec as P

HEADS = 16
HEAD_DIM = 64


EPS = 1e-05
NEGATIVE = -1e30
MESH = pl.DeviceIdType.MESH
SLOTS = 4
SCENE_BLOCKS = 16


def layer_norm(values, gain):
    center = values - jnp.mean(values, axis=-1, keepdims=True)
    spread = jnp.mean(center * center, axis=-1, keepdims=True)
    return center * lax.rsqrt(spread + EPS) * gain


def gelu_exact(values):
    return jax.nn.gelu(values, approximate=False)


def plain_dot(left, right):
    return jnp.dot(left, right, preferred_element_type=jnp.float32)


def dot_inner(left, right):
    return lax.dot_general(
        left, right, (((1,), (1,)), ((), ())), preferred_element_type=jnp.float32
    )


def dot_outer(left, right):
    return lax.dot_general(
        left, right, (((0,), (0,)), ((), ())), preferred_element_type=jnp.float32
    )


def split_heads(values):
    return values.reshape(values.shape[0], HEADS, HEAD_DIM)


def masked_scores(queries, keys, query_tags, key_tags, scale):
    raw = jnp.einsum("qhe,khe->hqk", queries, keys, preferred_element_type=jnp.float32) * scale
    allowed = (query_tags[:, None] == key_tags[None, :])[None]
    return (raw, allowed)


def probabilities(queries, keys, query_tags, key_tags, log_total, scale):
    raw, allowed = masked_scores(queries, keys, query_tags, key_tags, scale)
    return jnp.where(
        allowed, jnp.exp(jnp.where(allowed, raw - log_total[:, :, None], NEGATIVE)), 0.0
    )


def in_blocks(step, carry, piece):
    count = piece[0].shape[0]
    size = math.gcd(count, 512)
    number = count // size
    stacked = tuple((member.reshape((number, size) + member.shape[1:]) for member in piece))

    def inner(state, item):
        members, offset = item
        return (step(state, members, offset * size), None)

    result, unused = lax.scan(inner, carry, (stacked, jnp.arange(number, dtype=jnp.int32)))
    return result


def shards(
    tokens,
    scene_ids,
    live_mask,
    out_grad,
    attention_gain,
    input_weight,
    output_weight,
    feedforward_gain,
    up_weight,
    down_weight,
):
    scale = HEAD_DIM ** (-0.5)
    inputs = tokens[0].astype(jnp.float32)
    rows = inputs.shape[0]
    width = inputs.shape[1]
    tags = scene_ids[0] * 2 + live_mask[0]
    live = live_mask[0].astype(jnp.float32)[:, None]
    every_tag = lax.all_gather(tags, "view", axis=0, tiled=True)
    up_full, down_full = (
        lax.all_gather(up_weight, ("seq", "view"), axis=0, tiled=True),
        lax.all_gather(down_weight, ("seq", "view"), axis=0, tiled=True),
    )
    gain_one = attention_gain.astype(jnp.float32)
    gain_two = feedforward_gain.astype(jnp.float32)
    normed = layer_norm(inputs, gain_one).astype(jnp.bfloat16)
    projected = plain_dot(normed, input_weight).astype(jnp.bfloat16)
    query_flat = projected[:, :width]
    queries = split_heads(query_flat)
    keys_own = projected[:, width : 2 * width]
    values_own = projected[:, 2 * width :]

    def attend_step(carry, piece, start):
        peak, total, accum = carry
        key_piece, value_piece = piece
        count = key_piece.shape[0]
        key_tags = lax.dynamic_slice_in_dim(every_tag, start, count)
        raw, allowed = masked_scores(queries, split_heads(key_piece), tags, key_tags, scale)
        masked = jnp.where(allowed, raw, NEGATIVE)
        new_peak = jnp.maximum(peak, jnp.max(masked, axis=-1))
        weights = jnp.where(allowed, jnp.exp(masked - new_peak[:, :, None]), 0.0)
        factor = jnp.exp(peak - new_peak)
        total = total * factor + jnp.sum(weights, axis=-1)
        update = jnp.einsum(
            "hqk,khe->qhe",
            weights.astype(jnp.bfloat16),
            split_heads(value_piece),
            preferred_element_type=jnp.float32,
        )
        accum = accum * jnp.transpose(factor)[:, :, None] + update
        return (new_peak, total, accum)

    start_state = (
        jnp.full((HEADS, rows), NEGATIVE, jnp.float32),
        jnp.zeros((HEADS, rows), jnp.float32),
        jnp.zeros((rows, HEADS, HEAD_DIM), jnp.float32),
    )
    peak, total, accum = in_blocks(
        attend_step,
        start_state,
        (
            lax.all_gather(keys_own, "view", axis=0, tiled=True),
            lax.all_gather(values_own, "view", axis=0, tiled=True),
        ),
    )
    attended_heads = accum / jnp.transpose(total)[:, :, None]
    log_total = peak + jnp.log(total)
    attended_low = attended_heads.reshape(rows, width).astype(jnp.bfloat16)
    branch = plain_dot(attended_low, output_weight)
    middle = inputs + live * branch
    normed_two = layer_norm(middle, gain_two).astype(jnp.bfloat16)
    hidden = dot_inner(normed_two, up_full)
    activated = gelu_exact(hidden).astype(jnp.bfloat16)
    mixed = plain_dot(activated, down_full)
    layer_out = (middle + live * mixed).astype(jnp.bfloat16)[None]
    out_cot = out_grad[0].astype(jnp.float32)
    mixed_cot = (live * out_cot).astype(jnp.bfloat16)
    down_grad = dot_outer(activated, mixed_cot)
    activated_cot = dot_inner(mixed_cot, down_full)
    hidden_cot = jax.vjp(gelu_exact, hidden)[1](activated_cot)[0].astype(jnp.bfloat16)
    up_grad = dot_outer(hidden_cot, normed_two)
    normed_two_cot = plain_dot(hidden_cot, up_full)
    second_pull = jax.vjp(layer_norm, middle, gain_two)[1]
    middle_part, gain_two_grad = second_pull(normed_two_cot)
    middle_cot = out_cot + middle_part
    branch_cot = (live * middle_cot).astype(jnp.bfloat16)
    output_weight_grad = dot_outer(attended_low, branch_cot)
    attended_cot = dot_inner(branch_cot, output_weight).astype(jnp.bfloat16)
    cot_heads = split_heads(attended_cot)
    delta = jnp.transpose(jnp.sum(cot_heads.astype(jnp.float32) * attended_heads, axis=-1))
    seq_len = every_tag.shape[0]

    def back_step(carry, piece, start):
        query_cot, key_value_cot = carry
        key_piece, value_piece = piece
        count = key_piece.shape[0]
        key_tags = lax.dynamic_slice_in_dim(every_tag, start, count)
        key_heads = split_heads(key_piece)
        value_heads = split_heads(value_piece)
        probs = probabilities(queries, key_heads, tags, key_tags, log_total, scale)
        prob_cot = jnp.einsum(
            "qhe,khe->hqk", cot_heads, value_heads, preferred_element_type=jnp.float32
        )
        score_cot = (probs * (prob_cot - delta[:, :, None])).astype(jnp.bfloat16)
        query_cot = (
            query_cot
            + jnp.einsum("hqk,khe->qhe", score_cot, key_heads, preferred_element_type=jnp.float32)
            * scale
        )
        key_cot = (
            jnp.einsum("hqk,qhe->khe", score_cot, queries, preferred_element_type=jnp.float32)
            * scale
        )
        value_cot = jnp.einsum(
            "hqk,qhe->khe",
            probs.astype(jnp.bfloat16),
            cot_heads,
            preferred_element_type=jnp.float32,
        )
        stacked = jnp.concatenate(
            [key_cot.reshape(count, width), value_cot.reshape(count, width)], axis=1
        )
        earlier = lax.dynamic_slice_in_dim(key_value_cot, start, count)
        key_value_cot = lax.dynamic_update_slice_in_dim(key_value_cot, earlier + stacked, start, 0)
        return (query_cot, key_value_cot)

    back_state = (
        jnp.zeros((rows, HEADS, HEAD_DIM), jnp.float32),
        jnp.zeros((seq_len, 2 * width), jnp.float32),
    )
    query_cot, key_value_cot = in_blocks(
        back_step,
        back_state,
        (
            lax.all_gather(keys_own, "view", axis=0, tiled=True),
            lax.all_gather(values_own, "view", axis=0, tiled=True),
        ),
    )
    own_cot = lax.psum_scatter(key_value_cot, "view", scatter_dimension=0, tiled=True)
    key_cot_own = own_cot[:, :width]
    value_cot_own = own_cot[:, width:]
    projected_cot = jnp.concatenate(
        [query_cot.reshape(rows, width), key_cot_own, value_cot_own], axis=1
    ).astype(jnp.bfloat16)
    input_weight_grad = dot_outer(normed, projected_cot)
    normed_cot = dot_inner(projected_cot, input_weight)
    first_pull = jax.vjp(layer_norm, inputs, gain_one)[1]
    input_part, gain_one_grad = first_pull(normed_cot)
    tokens_grad = (middle_cot + input_part)[None]
    up_part, down_part = (
        lax.psum_scatter(up_grad, ("seq", "view"), scatter_dimension=0, tiled=True),
        lax.psum_scatter(down_grad, ("seq", "view"), scatter_dimension=0, tiled=True),
    )
    summed = lax.psum(
        (gain_one_grad, input_weight_grad, output_weight_grad, gain_two_grad), ("seq", "view")
    )
    return (layer_out, tokens_grad, summed[0], summed[1], summed[2], summed[3], up_part, down_part)


def dot_nn(left, right):
    return lax.dot_general(left, right, (((1,), (0,)), ((), ())), preferred_element_type=jnp.float32)


def at(start, size):
    return pl.ds(pl.multiple_of(start, size), size)


def norm_stats(values):
    mean = jnp.mean(values, axis=-1, keepdims=True)
    center = values - mean
    spread = jnp.mean(center * center, axis=-1, keepdims=True)
    inverse = lax.rsqrt(spread + EPS)
    return center * inverse, inverse


def norm_back(cot, unit, inverse, gain):
    scaled = cot * gain
    first = jnp.mean(scaled, axis=-1, keepdims=True)
    second = jnp.mean(scaled * unit, axis=-1, keepdims=True)
    return inverse * (scaled - first - unit * second)


class Wires:
    def __init__(self, send_sem, recv_sem, peer):
        self.send_sem, self.recv_sem, self.peer = send_sem, recv_sem, peer
        self.free, self.recvs, self.total, self.pending = list(range(SENDS)), 0, 0, []

    def inbox(self, count):
        base = self.recvs
        self.recvs += count
        assert self.recvs <= RECVS
        return base

    def bulk(self):
        return self.free.pop(0)

    def copy(self, src, dst, lane, slot, device):
        return pltpu.make_async_remote_copy(
            src_ref=src,
            dst_ref=dst,
            send_sem=self.send_sem.at[lane],
            recv_sem=self.recv_sem.at[slot],
            device_id=device,
            device_id_type=MESH,
        )

    def send(self, src, dst, slot, device, when=None, bulk=None):
        lane = self.free.pop(0) if bulk is None else bulk
        copy = self.copy(src, dst, lane, slot, device)
        if when is None:
            copy.start()
        else:
            pl.when(when)(copy.start)
        if bulk is None:
            self.pending.append((self.total, copy, when, lane))
            self.total += 1
        return copy

    def finish(self, entry):
        unused, copy, when, lane = entry
        if when is None:
            copy.wait_send()
        else:
            pl.when(when)(copy.wait_send)
        self.free.append(lane)

    def sent(self, copy):
        for entry in [entry for entry in self.pending if entry[1] is copy]:
            self.finish(entry)
        self.pending = [entry for entry in self.pending if entry[1] is not copy]

    def settle(self, until):
        for entry in [entry for entry in self.pending if entry[0] < until]:
            self.finish(entry)
        self.pending = [entry for entry in self.pending if entry[0] >= until]

    def settle_bulk(self, whole, lane):
        self.copy(whole, whole, lane, 0, self.peer).wait_send()

    def wait(self, dst, slot):
        self.copy(dst, dst, 0, slot, self.peer).wait_recv()


SENDS, RECVS, LOCALS = 67, 126, 17
LEVELS = 4


def scratch_of(rows, width, seqs, views, hidden):
    length = rows * views
    own = width // views
    bf, f3 = jnp.bfloat16, jnp.float32
    vm = pltpu.VMEM
    mlp_rows = hidden * seqs * views // 4
    half, quarter, eighth = width // 2, width // 4, width // 8
    return dict(
        tok=vm((rows, width), bf),
        out_cot=vm((rows, width), bf),
        layer_out=vm((rows, width), bf),
        tokens_grad=vm((rows, width), f3),
        up_grad=vm((hidden, width), f3),
        down_grad=vm((hidden, width), f3),
        w_full=vm((width, 3 * width), bf),
        w_own=vm((width, 3 * own), bf),
        wo=vm((width, width), bf),
        up=vm((mlp_rows, width), bf),
        down=vm((mlp_rows, width), bf),
        ids_all=vm((views, 8, 128), jnp.int32),
        order_vm=vm((16, 128), jnp.int32),
        order_sm=pltpu.SMEM((16, 128), jnp.int32),
        normed=vm((length, width), bf),
        qkv=vm((length, 3 * own), bf),
        qkv_s=vm((length, 3 * own), bf),
        weights=vm((2 * SLOTS, length // SLOTS, length // SLOTS), f3),
        totals=vm((2 * SLOTS, length // SLOTS, 1), f3),
        att_s=vm((length, own), f3),
        att=vm((length, own), bf),
        att_tok=vm((rows, width), bf),
        middle=vm((rows, width), f3),
        normed_two=vm((4 * rows, width), bf),
        mixed_cot=vm((4 * rows, width), bf),
        wide=vm((4 * rows, mlp_rows), f3),
        act=vm((4 * rows, mlp_rows), bf),
        hid_cot=vm((4 * rows, mlp_rows), bf),
        part_own=vm((2, 2, rows, width), f3),
        part_out=vm((2, 3, rows, width), bf),
        part_in=vm((2, 3, rows, width), bf),
        grad_keep=vm((2, mlp_rows // 2, width), bf),
        grad_pass=vm((2, mlp_rows // 2, width), bf),
        grad_core=vm((2, mlp_rows // 2, width), bf),
        grad_y=vm((2, 2, hidden, width), bf),
        grad_z=vm((2, hidden, width), bf),
        branch=vm((rows, width), bf),
        acot_tok=vm((rows, width), bf),
        acot=vm((length, own), bf),
        acot_s=vm((length, own), bf),
        pc_s=vm((length, 3 * own), bf),
        pc=vm((3, length, own), bf),
        pc_flat=vm((length, 3 * own), bf),
        pc_tok=vm((3, rows, width), bf),
        dw_out=vm((2, 3, width // seqs, own), bf),
        dw_x=vm((3, width // seqs, own), bf),
        dw_in=vm((3, 3, width // seqs, own), bf),
        dw_own=vm((3, width // seqs, own), bf),
        do_core=vm((half, width), bf),
        do_core_in=vm((half, width), bf),
        do_first=vm((quarter, width), bf),
        do_first_in=vm((quarter, width), bf),
        do_second=vm((eighth, width), bf),
        do_second_in=vm((eighth, width), bf),
        do_z=vm((eighth, width), bf),
        do_z_in=vm((LEVELS, eighth // LEVELS, width), bf),
        do_own=vm((eighth // LEVELS, width), bf),
        gain_own=vm((8, width), f3),
        gain_in=vm((seqs, 8, width), f3),
        gain_sum=vm((8, width), f3),
        gain_all=vm((views, 8, width), f3),
        send_sem=pltpu.SemaphoreType.DMA((SENDS,)),
        recv_sem=pltpu.SemaphoreType.DMA((RECVS,)),
        local_sem=pltpu.SemaphoreType.DMA((LOCALS,)),
    )


def layer_kernel(names, seqs, views, *refs):
    (tok_hbm, ids, alive, cot_hbm, gain_one_ref, gain_two_ref, w_hbm, wo_hbm, up_hbm, down_hbm) = refs[:10]
    (layer_hbm, tokens_hbm, gains, w_grad, o_grad, up_part, up_away, down_hbm_out) = refs[10:18]
    k = types.SimpleNamespace(**dict(zip(names, refs[18:])))
    k.slope = k.part_all = k.do_keep = k.wide
    tok, out_cot = k.tok, k.out_cot
    layer_out, tokens_grad, up_grad, down_grad = k.layer_out, k.tokens_grad, k.up_grad, k.down_grad
    rows, width = tok.shape
    length = rows * views
    own = width // views
    hidden = up_hbm.shape[0]
    mlp_rows = k.up.shape[0]
    half = mlp_rows // 2
    block = length // (SLOTS * SCENE_BLOCKS)
    scene = length // SLOTS
    scale = HEAD_DIM ** (-0.5)
    bf, f3 = jnp.bfloat16, jnp.float32

    s = lax.axis_index("seq")
    v = lax.axis_index("view")
    x, c, z, y = s // 2, s % 2, v // 2, v % 2
    x_s, c_s, xc_s = (1 - x) * 2 + c, x * 2 + (1 - c), (1 - x) * 2 + (1 - c)
    y_v = z * 2 + (1 - y)
    z_pair, z_two, z_flip = z + 1 - 2 * (z % 2), lax.rem(z + 2, LEVELS), LEVELS - 1 - z
    inner = (z == 1) | (z == 2)
    others_z = [z_pair, z_two, z_flip]
    low, high = z % 2, z // 2
    pair_v = z_pair * 2 + y
    own_slot, x_slot = x * 2 + low, (1 - x) * 2 + low
    pair_slot, far_slot = x * 2 + (1 - low), (1 - x) * 2 + (1 - low)
    view_peers = [lax.rem(v + d, views) for d in range(1, views)]
    seq_peers = [x_s, xc_s, c_s]

    def level(zt):
        return (s, zt * 2 + y)

    wires = Wires(k.send_sem, k.recv_sem, (c_s, v))
    in_normed = wires.inbox(2 * views)
    in_ids = wires.inbox(views)
    in_up = wires.inbox(LEVELS + 1)
    in_down = wires.inbox(LEVELS + 1)
    in_mcot = wires.inbox(4)
    in_att = wires.inbox(views)
    in_two = wires.inbox(4)
    in_part = [wires.inbox(5), wires.inbox(5)]
    in_core = [wires.inbox(1), wires.inbox(1)]
    in_grad = [wires.inbox(3), wires.inbox(3)]
    in_acot, in_pc = in_ids, in_att
    in_dw = wires.inbox(3)
    in_do = wires.inbox(3)
    in_do_z = wires.inbox(LEVELS)
    in_plane = wires.inbox(views)
    in_query = wires.inbox(views)
    in_cross = wires.inbox(views)
    in_mate = [wires.inbox(1) for unused in range(3)]
    in_out = [wires.inbox(views), wires.inbox(views)]
    in_out_mate = wires.inbox(1)
    in_gain = wires.inbox(seqs)
    in_gains = in_normed
    to_view = [wires.bulk() for unused in range(5)]
    to_mate_w = [wires.bulk() for unused in range(3)]
    to_mate_o = wires.bulk()

    def z_cast(src, dst, slot):
        wires.send(src, dst, slot, level(z_pair))
        wires.send(src, dst, slot, level(z_two))
        wires.send(src, dst, slot, level(z_flip), when=inner)

    def z_relay(ref, slot):
        wires.send(ref, ref, slot, level(z_pair), when=inner)

    barrier = pltpu.get_barrier_semaphore()
    greeted = [(s, p) for p in view_peers] + [(p, v) for p in seq_peers]
    for device in greeted:
        pl.semaphore_signal(barrier, inc=1, device_id=device, device_id_type=MESH)

    loads, kept = [], []

    def load(src, dst):
        copy = pltpu.make_async_copy(src, dst, k.local_sem.at[len(loads)])
        copy.start()
        loads.append(copy)
        return copy

    up_slot = at((c * 4 + y * 2 + high) * hidden, hidden)
    load_tok = load(tok_hbm, tok)
    load_cot = load(cot_hbm, out_cot)
    load_up = load(up_hbm, k.up.at[up_slot])
    load_down = load(down_hbm, k.down.at[up_slot])
    load_own = [
        load(w_hbm.at[:, at(t * width + v * own, own)], k.w_own.at[:, pl.ds(t * own, own)])
        for t in range(3)
    ]
    load_wo = load(wo_hbm, k.wo)
    load_w = load(w_hbm, k.w_full)

    gain_one = gain_one_ref[...].astype(f3).reshape(1, width)
    gain_two = gain_two_ref[...].astype(f3).reshape(1, width)
    load_tok.wait()
    unit, _ = norm_stats(tok[...].astype(f3))
    k.normed[at(v * rows, rows), :] = (unit * gain_one).astype(bf)
    per = rows // block
    lane = lax.broadcasted_iota(jnp.int32, (1, 128), 1)
    scenes = jnp.zeros((1, 128), jnp.int32)
    for m in range(per):
        mine = jnp.broadcast_to(ids[:, m * block : m * block + 1], (1, 128))
        scenes = jnp.where(lane == v * per + m, mine, scenes)
    k.ids_all[v] = jnp.broadcast_to(scenes, (8, 128))
    live = jnp.transpose(jnp.broadcast_to(alive[...].astype(f3), (rows, rows)))[:, :1]
    pl.semaphore_wait(barrier, len(greeted))

    def view_rows(ref, j):
        return ref.at[at(j * rows, rows)]

    for p in view_peers:
        wires.send(k.ids_all.at[v], k.ids_all.at[v], in_ids + v, (s, p), bulk=to_view[0])

    def normed_half(j, i):
        return k.normed.at[at(j * rows + i * (rows // 2), rows // 2)], in_normed + 2 * j + i

    for i in range(2):
        mine, slot = normed_half(v, i)
        wires.send(mine, mine, slot, (s, y_v))
    for zt in (z_pair, z_two):
        for i in range(2):
            mine, slot = normed_half(v, i)
            wires.send(mine, mine, slot, level(zt))
    for i in range(2):
        mine, slot = normed_half(v, i)
        wires.send(mine, mine, slot, level(z_flip), when=inner)
    load_cot.wait()
    mcot_own = at(own_slot * rows, rows)
    k.mixed_cot[mcot_own, :] = (live * out_cot[...].astype(f3)).astype(bf)

    def slot_rows(ref, slot):
        return ref.at[at(slot * rows, rows)]

    def square_send(ref, base, slot, device):
        wires.send(slot_rows(ref, slot), slot_rows(ref, slot), base + slot, device)

    def square_relay(ref, base):
        wires.wait(slot_rows(ref, pair_slot), base + pair_slot)
        square_send(ref, base, pair_slot, (x_s, v))

    square_send(k.mixed_cot, in_mcot, own_slot, (x_s, v))

    for p in view_peers:
        wires.wait(k.ids_all.at[p], in_ids + p)
    count = SLOTS * SCENE_BLOCKS
    scene_row = k.ids_all[0][:1]
    for j in range(1, views):
        scene_row = scene_row + k.ids_all[j][:1]
    big = lax.broadcasted_iota(jnp.int32, (128, 128), 0)
    wide = lax.broadcasted_iota(jnp.int32, (128, 128), 1)
    scene_mat = jnp.broadcast_to(scene_row, (128, 128))
    scene_col = jnp.transpose(scene_mat)
    ahead = (scene_col < scene_mat) | ((scene_col == scene_mat) & (big < wide))
    place = jnp.sum(jnp.where(ahead & (big < count), 1, 0), axis=0, keepdims=True)
    place_col = jnp.transpose(jnp.broadcast_to(place, (128, 128)))
    hit = jnp.where((place_col == wide) & (big < count), big, 0)
    source = jnp.sum(hit, axis=0, keepdims=True)
    k.order_vm[0:8, :] = jnp.broadcast_to(source, (8, 128))
    k.order_vm[8:16, :] = jnp.broadcast_to(place, (8, 128))
    to_scalar = load(k.order_vm, k.order_sm)

    for copy in load_own:
        copy.wait()

    def mlp_slot(ref, yt, ht):
        return ref.at[at((c * 4 + yt * 2 + ht) * hidden, hidden)]

    def send_mlp(ref, base, device):
        mine = mlp_slot(ref, y, high)
        wires.send(mine, mine, base + y * 2 + high, device)

    def mlp_relay(ref, base):
        there = mlp_slot(ref, y, 1 - high)
        wires.wait(there, base + y * 2 + 1 - high)
        wires.send(there, there, base + y * 2 + 1 - high, (s, y_v))

    def core_exchange(ref, base):
        for ht in (high, 1 - high):
            wires.wait(mlp_slot(ref, 1 - y, ht), base + (1 - y) * 2 + ht)
        mine = ref.at[at(c * half, half)]
        wires.send(mine, mine, base + LEVELS, (c_s, v))

    def project(j):
        k.qkv[at(j * rows, rows), :] = dot_nn(k.normed[at(j * rows, rows), :], k.w_own[...]).astype(bf)

    project(v)
    for zt in others_z:
        j = zt * 2 + y
        for i in range(2):
            there, slot = normed_half(j, i)
            wires.wait(there, slot)
            if zt is z_two:
                z_relay(there, slot)
            wires.send(there, there, slot, (s, y_v))
        if zt is z_two:
            load_up.wait()
            send_mlp(k.up, in_up, level(z_two))
            square_send(k.mixed_cot, in_mcot, own_slot, (s, pair_v))
        project(j)
    send_mlp(k.up, in_up, (s, y_v))
    for zt in [z] + others_z:
        j = zt * 2 + 1 - y
        for i in range(2):
            wires.wait(*normed_half(j, i))
        project(j)
    to_scalar.wait()

    def reorder(dst, src, row):
        blocks = src.reshape(count, block, src.shape[1])

        def step(i, unused):
            from_block = k.order_sm[row, i]
            dst[at(i * block, block), :] = blocks[from_block].astype(dst.dtype)
            return unused

        lax.fori_loop(0, count, step, 0, unroll=16)

    reorder(k.qkv_s, k.qkv, 0)

    head_lane = lax.broadcasted_iota(jnp.int32, (scene, own), 1) // HEAD_DIM

    def attend(g, unused):
        here = at(g * scene, scene)
        queries, keys, values = (k.qkv_s[here, pl.ds(t * own, own)] for t in range(3))
        result = jnp.zeros((scene, own), f3)
        for e in range(2):
            chosen = jnp.where(head_lane == e, queries, jnp.zeros_like(queries))
            weights = jnp.exp(dot_inner(chosen, keys) * scale)
            total = jnp.sum(weights, axis=-1, keepdims=True)
            k.weights[g * 2 + e] = weights
            k.totals[g * 2 + e] = total
            mixed = dot_nn(weights.astype(bf), values) / total
            result = jnp.where(head_lane == e, mixed, result)
        k.att_s[here, :] = result
        return unused

    lax.fori_loop(0, SLOTS, attend, 0, unroll=True)
    reorder(k.att, k.att_s, 8)
    own_cols = at(v * own, own)
    for p in view_peers:
        wires.send(view_rows(k.att, p), k.att_tok.at[:, own_cols], in_att + v, (s, p), bulk=to_view[1])
    square_relay(k.mixed_cot, in_mcot)
    mlp_relay(k.up, in_up)
    load_down.wait()
    send_mlp(k.down, in_down, level(z_two))
    send_mlp(k.down, in_down, (s, y_v))
    k.att_tok[:, own_cols] = k.att[at(v * rows, rows), :]


    load_wo.wait()
    for p in view_peers:
        wires.wait(k.att_tok.at[:, at(p * own, own)], in_att + p)
    tile = 256
    for n in range(width // tile):
        cols = pl.ds(n * tile, tile)
        k.middle[:, cols] = tok[:, cols].astype(f3) + live * dot_nn(k.att_tok[...], k.wo[:, cols])
    unit_two, _ = norm_stats(k.middle[...])
    k.normed_two[mcot_own, :] = (unit_two * gain_two).astype(bf)
    until_two = wires.total
    for device in ((s, pair_v), (x_s, v)):
        square_send(k.normed_two, in_two, own_slot, device)

    core_exchange(k.up, in_up)
    square_relay(k.normed_two, in_two)
    mlp_relay(k.down, in_down)
    wires.wait(k.up.at[at((1 - c) * half, half)], in_up + LEVELS)

    def hidden_tiles(slot):
        here = at(slot * rows, rows)

        def step(n, unused):
            cols = at(n * tile, tile)
            pre = dot_inner(k.normed_two[here, :], k.up[cols, :])
            below = 0.5 + 0.5 * lax.erf(pre * (0.5**0.5))
            k.act[here, cols] = (pre * below).astype(bf)
            k.slope[here, cols] = below + pre * (jnp.exp(-0.5 * pre * pre) * (0.5 / math.pi) ** 0.5)
            return unused

        lax.fori_loop(0, mlp_rows // tile, step, 0)

    hidden_tiles(own_slot)
    hidden_tiles(pair_slot)
    for slot in (x_slot, far_slot):
        wires.wait(slot_rows(k.normed_two, slot), in_two + slot)
        hidden_tiles(slot)

    def grad_tiles(left, right, start, dst):
        def step(n, unused):
            there = at(n * tile, tile)
            dst[there, :] = dot_outer(left[:, at(start + n * tile, tile)], right[...]).astype(dst.dtype)
            return unused

        lax.fori_loop(0, half // tile, step, 0)

    passed = []

    def grad_halves(which, left, right):
        grad_tiles(left, right, (1 - c) * half, k.grad_pass.at[which])
        passed.append(wires.send(k.grad_pass.at[which], k.grad_core.at[which], in_core[which], (c_s, v)))
        grad_tiles(left, right, c * half, k.grad_keep.at[which])

    for slot in (x_slot, far_slot):
        wires.wait(slot_rows(k.mixed_cot, slot), in_mcot + slot)
    core_exchange(k.down, in_down)
    grad_halves(0, k.act, k.mixed_cot)

    def grad_sum(which, start, size):
        there = at(start, size)
        return k.grad_keep[which, there, :].astype(f3) + k.grad_core[which, there, :].astype(f3)

    def grads_to_y(which):
        wires.wait(k.grad_core.at[which], in_core[which])
        wires.sent(passed[which])
        for i, ht in enumerate((1 - high, high)):
            start = ((1 - y) * 2 + ht) * hidden
            there = at(start, hidden)
            k.grad_pass[which, there, :] = grad_sum(which, start, hidden).astype(bf)
            wires.send(k.grad_pass.at[which, there], k.grad_y.at[which, i], in_grad[which] + i, (s, y_v))

    def grad_block(which, i, ht):
        wires.wait(k.grad_y.at[which, i], in_grad[which] + i)
        return grad_sum(which, (y * 2 + ht) * hidden, hidden) + k.grad_y[which, i].astype(f3)

    def grads_to_z(which):
        there = at((y * 2 + 1 - high) * hidden, hidden)
        k.grad_pass[which, there, :] = grad_block(which, 0, 1 - high).astype(bf)
        wires.send(k.grad_pass.at[which, there], k.grad_z.at[which], in_grad[which] + 2, level(z_two))

    def collect(which, dst):
        total = grad_block(which, 1, high)
        wires.wait(k.grad_z.at[which], in_grad[which] + 2)
        dst[...] = total + k.grad_z[which].astype(f3)


    wires.wait(k.down.at[at((1 - c) * half, half)], in_down + LEVELS)

    def cot_tile(n, unused):
        cols = at(n * tile, tile)
        up_to = dot_inner(k.mixed_cot[...], k.down[cols, :])
        k.hid_cot[:, cols] = (up_to * k.slope[:, cols]).astype(bf)
        return unused

    lax.fori_loop(0, mlp_rows // tile, cot_tile, 0)

    strip = width // 2

    def strip_cols(i):
        return pl.ds(i * strip, strip)

    def part_tiles(which, left, right):
        for i in range(2):

            def step(n, unused):
                cols = at(i * strip + n * tile, tile)
                k.part_all[:, cols] = dot_nn(left[...], right[:, cols])
                return unused

            lax.fori_loop(0, strip // tile, step, 0)
            cols = strip_cols(i)
            k.part_out[which, 0, :, cols] = k.part_all[at(far_slot * rows, rows), cols].astype(bf)
            there = k.part_out.at[which, 0, :, cols], k.part_in.at[which, 0, :, cols]
            wires.send(*there, in_part[which] + i, (x_s, v))
        k.part_out[which, 1] = k.part_all[at(x_slot * rows, rows), :].astype(bf)
        wires.send(k.part_out.at[which, 1], k.part_in.at[which, 1], in_part[which] + 2, (x_s, v))
        for i, slot in enumerate((own_slot, pair_slot)):
            k.part_own[which, i] = k.part_all[at(slot * rows, rows), :]

    def part_join(which):
        for i in range(2):
            cols = strip_cols(i)
            wires.wait(k.part_in.at[which, 0, :, cols], in_part[which] + i)
            joined = k.part_own[which, 1, :, cols] + k.part_in[which, 0, :, cols].astype(f3)
            k.part_out[which, 2, :, cols] = joined.astype(bf)
            there = k.part_out.at[which, 2, :, cols], k.part_in.at[which, 2, :, cols]
            wires.send(*there, in_part[which] + 3 + i, (s, pair_v))

    grads_to_y(0)
    part_tiles(0, k.hid_cot, k.up)
    grad_halves(1, k.hid_cot, k.normed_two)
    part_tiles(1, k.act, k.down)
    part_join(0)

    def part_sum(which):
        total = k.part_own[which, 0]
        wires.wait(k.part_in.at[which, 1], in_part[which] + 2)
        for i in range(2):
            wires.wait(k.part_in.at[which, 2, :, strip_cols(i)], in_part[which] + 3 + i)
        for i in (1, 2):
            total = total + k.part_in[which, i].astype(f3)
        return total

    unit_two, inverse_two = norm_stats(k.middle[...])
    wires.settle(until_two)
    cot_two = part_sum(0)
    until_acot = wires.total
    k.gain_own[1:2, :] = jnp.sum(cot_two * unit_two, axis=0, keepdims=True)
    middle_cot = out_cot[...].astype(f3) + norm_back(cot_two, unit_two, inverse_two, gain_two)
    tokens_grad[...] = middle_cot
    k.branch[...] = (live * middle_cot).astype(bf)
    for n in range(width // tile):
        k.acot_tok[:, pl.ds(n * tile, tile)] = dot_inner(
            k.branch[...], k.wo[pl.ds(n * tile, tile), :]
        ).astype(bf)
    for p in view_peers:
        wires.send(k.acot_tok.at[:, at(p * own, own)], view_rows(k.acot, v), in_acot + v, (s, p), bulk=to_view[2])
    k.acot[at(v * rows, rows), :] = k.acot_tok[:, own_cols]

    o_half, o_quarter, o_eighth = width // 2, width // 4, width // 8
    o_piece = o_eighth // LEVELS

    def outer_rows(start, dst, dtype):
        def step(n, unused):
            there = at(n * tile, tile)
            left = k.att_tok[:, at(start + n * tile, tile)]
            dst[there, :] = dot_outer(left, k.branch[...]).astype(dtype)
            return unused

        lax.fori_loop(0, o_half // tile, step, 0)

    outer_rows((1 - c) * o_half, k.do_core, bf)
    wires.send(k.do_core, k.do_core_in, in_do, (c_s, v))
    outer_rows(c * o_half, k.do_keep, f3)
    wires.wait(k.do_core_in, in_do)
    k.do_keep[...] = k.do_keep[...] + k.do_core_in[...].astype(f3)
    k.do_first[...] = k.do_keep[at((1 - x) * o_quarter, o_quarter), :].astype(bf)

    grads_to_y(1)
    part_join(1)
    for p in view_peers:
        wires.wait(view_rows(k.acot, p), in_acot + p)
    reorder(k.acot_s, k.acot, 0)

    def attend_back(g, unused):
        here = at(g * scene, scene)
        queries, keys, values = (k.qkv_s[here, pl.ds(t * own, own)] for t in range(3))
        cots = k.acot_s[here, :]
        agree = cots.astype(f3) * k.att_s[here, :]
        outs = [jnp.zeros((scene, own), f3) for t in range(3)]
        for e in range(2):
            mine = head_lane == e
            delta = jnp.sum(jnp.where(mine, agree, 0.0), axis=-1, keepdims=True)
            chosen = jnp.where(mine, cots, jnp.zeros_like(cots))
            weights = k.weights[g * 2 + e]
            inverse = 1.0 / k.totals[g * 2 + e]
            weights_cot = dot_inner(chosen, values)
            score_cot = (weights * inverse * (weights_cot - delta)).astype(bf)
            shared = (cots.astype(f3) * inverse).astype(bf)
            new = (
                dot_nn(score_cot, keys) * scale,
                dot_outer(score_cot, queries) * scale,
                dot_outer(weights.astype(bf), shared),
            )
            outs = [jnp.where(mine, fresh, old) for fresh, old in zip(new, outs)]
        for t in range(3):
            k.pc_s[here, pl.ds(t * own, own)] = outs[t].astype(bf)
        return unused

    lax.fori_loop(0, SLOTS, attend_back, 0, unroll=True)
    pc_blocks = k.pc_s.reshape(count, block, 3 * own)

    def unsort(i, unused):
        found = pc_blocks[k.order_sm[8, i]]
        k.pc_flat[at(i * block, block), :] = found
        for t in range(3):
            k.pc[t, at(i * block, block), :] = found[:, t * own : (t + 1) * own]
        return unused

    lax.fori_loop(0, count, unsort, 0, unroll=16)
    for p in view_peers:
        wires.send(k.pc.at[:, at(p * rows, rows)], k.pc_tok.at[:, :, own_cols], in_pc + v, (s, p), bulk=to_view[3])
    for t in range(3):
        k.pc_tok[t, :, own_cols] = k.pc[t, at(v * rows, rows), :]

    part = width // seqs

    def own_dw(row_block):
        whole = dot_outer(k.normed[:, at(row_block * part, part)], k.pc_flat[...])
        return [whole[:, t * own : (t + 1) * own] for t in range(3)]

    for i, xt in enumerate((1 - x, x)):
        for t, value in enumerate(own_dw(xt * 2 + 1 - c)):
            k.dw_out[i, t] = value.astype(bf)
        wires.send(k.dw_out.at[i], k.dw_in.at[i], in_dw + i, (c_s, v))
    cross_dw = own_dw(x_s)
    wires.wait(k.dw_in.at[0], in_dw)
    for t in range(3):
        k.dw_x[t] = (cross_dw[t] + k.dw_in[0, t].astype(f3)).astype(bf)
    wires.send(k.dw_x, k.dw_in.at[2], in_dw + 2, (x_s, v))
    mine_dw = own_dw(s)
    wires.wait(k.dw_in.at[1], in_dw + 1)
    wires.settle(until_acot)
    wires.wait(k.dw_in.at[2], in_dw + 2)
    for t in range(3):
        total = mine_dw[t] + k.dw_in[1, t].astype(f3) + k.dw_in[2, t].astype(f3)
        k.dw_own[t] = total.astype(bf)

    def w_at(q, j, first, last):
        return w_grad.at[pl.ds(first, last - first), at(q * part, part), at(j * own, own)]

    def w_plane(j):
        return w_at(s, j, 0, 3)

    def w_query(j):
        return w_at(x_s, j, 0, 1)

    def w_cross(q, j):
        return w_at(q, j, 1, 3)

    wires.send(k.dw_own.at[pl.ds(0, 1)], w_at(s, v, 0, 1), in_query + v, (x_s, v))
    wires.send(k.do_first, k.do_first_in, in_do + 1, (x_s, v))
    wires.send(k.dw_own, w_plane(v), in_plane + v, (s, y_v))
    z_cast(k.dw_own, w_plane(v), in_plane + v)
    wires.send(k.dw_own.at[pl.ds(1, 2)], w_cross(s, v), in_cross + v, (x_s, v))
    wires.send(k.dw_own, w_plane(v), in_mate[0], (c_s, v), bulk=to_mate_w[0])
    kept.append(load(k.dw_own, w_plane(v)))

    wires.wait(w_query(v), in_query + v)
    wires.send(w_query(v), w_query(v), in_query + v, (s, y_v))
    z_cast(w_query(v), w_query(v), in_query + v)
    wires.send(w_query(v), w_query(v), in_mate[1], (c_s, v), bulk=to_mate_w[1])

    wires.wait(k.do_first_in, in_do + 1)
    o_mine = at(x * o_quarter, o_quarter)
    k.do_keep[o_mine, :] = k.do_keep[o_mine, :] + k.do_first_in[...].astype(f3)
    k.do_second[...] = k.do_keep[at(x * o_quarter + (1 - y) * o_eighth, o_eighth), :].astype(bf)
    wires.send(k.do_second, k.do_second_in, in_do + 2, (s, y_v))
    def o_at(q, j):
        at_c, at_x, at_y, at_z = q % 2, q // 2, j % 2, j // 2
        return o_grad.at[at(at_c * o_half + at_x * o_quarter + at_y * o_eighth + at_z * o_piece, o_piece)]

    def to_mate(which, ref):
        wires.send(ref, ref, in_mate[which], (c_s, v), bulk=to_mate_w[which])

    def pass_plane(zt, row_y):
        j = zt * 2 + row_y
        wires.wait(w_plane(j), in_plane + j)
        if row_y is y:
            if zt is z_two:
                z_relay(w_plane(j), in_plane + j)
            wires.send(w_plane(j), w_plane(j), in_plane + j, (s, y_v))
        wires.send(w_cross(s, j), w_cross(s, j), in_cross + j, (x_s, v))
        to_mate(0, w_plane(j))

    def pass_query(zt, row_y):
        j = zt * 2 + row_y
        wires.wait(w_query(j), in_query + j)
        if row_y is y:
            if zt is z_two:
                z_relay(w_query(j), in_query + j)
            wires.send(w_query(j), w_query(j), in_query + j, (s, y_v))
        to_mate(1, w_query(j))

    across = 1 - y
    pass_plane(z, across)

    load_w.wait()
    for p in view_peers:
        wires.wait(k.pc_tok.at[:, :, at(p * own, own)], in_pc + p)

    def back_tile(n, unused):
        cols = at(n * tile, tile)
        total = dot_inner(k.pc_tok[0], k.w_full[cols, pl.ds(0, width)])
        for t in range(1, 3):
            total = total + dot_inner(k.pc_tok[t], k.w_full[cols, pl.ds(t * width, width)])
        k.part_own[0, 0, :, cols] = total
        return unused

    lax.fori_loop(0, width // tile, back_tile, 0)
    unit_one, inverse_one = norm_stats(tok[...].astype(f3))
    cot_one = k.part_own[0, 0]
    k.gain_own[0:1, :] = jnp.sum(cot_one * unit_one, axis=0, keepdims=True)
    k.gain_own[2:8, :] = jnp.zeros((6, width), f3)
    tokens_grad[...] = tokens_grad[...] + norm_back(cot_one, unit_one, inverse_one, gain_one)
    for p in seq_peers:
        wires.send(k.gain_own, k.gain_in.at[s], in_gain + s, (p, v))
    kept.append(load(tokens_grad, tokens_hbm))

    wires.wait(k.do_second_in, in_do + 2)
    total = k.do_keep[at(x * o_quarter + y * o_eighth, o_eighth), :] + k.do_second_in[...].astype(f3)
    k.do_z[...] = total.astype(bf)

    def o_level(zt):
        return at(zt * o_piece, o_piece)

    for zt in others_z:
        wires.send(k.do_z.at[o_level(zt)], k.do_z_in.at[z], in_do_z + z, level(zt))

    pass_plane(z_pair, y)
    pass_plane(z_two, y)
    pass_query(z, across)
    pass_plane(z_pair, across)
    pass_query(z_pair, y)
    pass_query(z_two, y)
    pass_plane(z_flip, y)
    pass_plane(z_two, across)
    there = at((y * 2 + 1 - high) * hidden, hidden)
    k.grad_pass[1, there, :] = grad_block(1, 0, 1 - high).astype(bf)
    kept.append(load(k.grad_pass.at[1, there], up_away))
    up_grad[...] = grad_block(1, 1, high)
    kept.append(load(up_grad, up_part))
    total = k.do_keep[at(x * o_quarter + y * o_eighth + z * o_piece, o_piece), :]
    total = total + k.do_second_in[o_level(z), :].astype(f3)
    for zt in others_z:
        wires.wait(k.do_z_in.at[zt], in_do_z + zt)
        total = total + k.do_z_in[zt].astype(f3)
    k.do_own[...] = total.astype(bf)
    wires.send(k.do_own, o_at(s, v), in_out[0] + v, (s, y_v))
    z_cast(k.do_own, o_at(s, v), in_out[0] + v)
    wires.send(k.do_own, o_at(s, v), in_out[1] + v, (x_s, v))
    wires.send(k.do_own, o_at(s, v), in_out_mate, (c_s, v), bulk=to_mate_o)
    kept.append(load(k.do_own, o_at(s, v)))
    pass_query(z_flip, y)
    pass_plane(z_flip, across)
    for zt in others_z:
        pass_query(zt, across)

    total = k.gain_own[...]
    for p in seq_peers:
        wires.wait(k.gain_in.at[p], in_gain + p)
        total = total + k.gain_in[p]
    k.gain_sum[...] = total
    for p in view_peers:
        wires.send(k.gain_sum, k.gain_all.at[v], in_gains + v, (s, p), bulk=to_view[4])

    def out_mate(q, j):
        wires.send(o_at(q, j), o_at(q, j), in_out_mate, (c_s, v), bulk=to_mate_o)

    def pass_out(zt, row_y):
        j = zt * 2 + row_y
        slot = in_out[0] + j
        wires.wait(o_at(s, j), slot)
        if row_y is y:
            if zt is z_two:
                z_relay(o_at(s, j), slot)
            wires.send(o_at(s, j), o_at(s, j), slot, (s, y_v))
        wires.send(o_at(s, j), o_at(s, j), in_out[1] + j, (x_s, v))
        out_mate(s, j)

    for zt in others_z:
        pass_out(zt, y)
    grads_to_z(0)
    for zt in [z] + others_z:
        pass_out(zt, across)

    layer_out[...] = (k.middle[...] + live * part_sum(1)).astype(bf)
    kept.append(load(layer_out, layer_hbm))
    by_arrival = [v] + [zt * 2 + y for zt in others_z] + [zt * 2 + across for zt in [z] + others_z]
    for j in by_arrival:
        wires.wait(w_cross(x_s, j), in_cross + j)
        to_mate(2, w_cross(x_s, j))
    for j in by_arrival:
        wires.wait(o_at(x_s, j), in_out[1] + j)
        out_mate(x_s, j)

    total = k.gain_sum[...]
    for p in view_peers:
        wires.wait(k.gain_all.at[p], in_gains + p)
        total = total + k.gain_all[p]
    gains[...] = total

    collect(0, down_grad)
    kept.append(load(down_grad, down_hbm_out))
    def w_rows(q, first, last):
        return w_grad.at[pl.ds(first, last - first), at(q * part, part)]

    def o_core(core):
        return o_grad.at[at(core * o_half, o_half)]

    wires.settle(wires.total)
    for whole, lane in (
        (k.ids_all.at[pl.ds(0, views - 1)], to_view[0]),
        (k.att.at[pl.ds(0, length - rows)], to_view[1]),
        (k.acot.at[pl.ds(0, length - rows)], to_view[2]),
        (k.pc.at[:, pl.ds(0, length - rows)], to_view[3]),
        (k.gain_all.at[pl.ds(0, views - 1)], to_view[4]),
        (w_rows(s, 0, 3), to_mate_w[0]),
        (w_rows(x_s, 0, 1), to_mate_w[1]),
        (w_rows(x_s, 1, 3), to_mate_w[2]),
        (o_core(c), to_mate_o),
    ):
        wires.settle_bulk(whole, lane)
    wires.wait(w_rows(c_s, 0, 3), in_mate[0])
    wires.wait(w_rows(xc_s, 0, 1), in_mate[1])
    wires.wait(w_rows(xc_s, 1, 3), in_mate[2])
    wires.wait(o_core(1 - c), in_out_mate)
    for copy in kept:
        copy.wait()


FINISH_STEPS = 8


def finish_kernel(*refs):
    (layer_in, tokens_in, gains, w_in, o_in, down_in) = refs[:6]
    (layer_out, tokens_grad, gain_one, w_out, o_out, gain_two, down_out) = refs[6:13]
    (layer, tokens, down, w_narrow, o_narrow, w_wide, o_wide, in_sem, out_sem) = refs[13:]
    width = o_in.shape[0]
    tall = width // FINISH_STEPS
    asis = ((layer_in, layer, layer_out), (tokens_in, tokens, tokens_grad), (down_in, down, down_out))

    def rows(i):
        return pl.ds(i * tall, tall)

    def start(src, dst, sem):
        copy = pltpu.make_async_copy(src, dst, sem)
        copy.start()
        return copy

    reads, writes = [], []
    for i in range(FINISH_STEPS):
        reads.append(start(w_in.at[:, rows(i)], w_narrow.at[:, rows(i)], in_sem.at[2 * i]))
        reads.append(start(o_in.at[rows(i)], o_narrow.at[rows(i)], in_sem.at[2 * i + 1]))
    late = [start(src, mid, in_sem.at[2 * FINISH_STEPS + i]) for i, (src, mid, dst) in enumerate(asis)]
    gain_one[...] = gains[0:1, :].reshape(width)
    gain_two[...] = gains[1:2, :].reshape(width)
    for i in range(FINISH_STEPS):
        reads[2 * i].wait()
        for t in range(3):
            w_wide[rows(i), t * width : (t + 1) * width] = w_narrow[t, rows(i), :].astype(jnp.float32)
        writes.append(start(w_wide.at[rows(i)], w_out.at[rows(i)], out_sem.at[2 * i]))
        reads[2 * i + 1].wait()
        o_wide[rows(i), :] = o_narrow[rows(i), :].astype(jnp.float32)
        writes.append(start(o_wide.at[rows(i)], o_out.at[rows(i)], out_sem.at[2 * i + 1]))
    for i, (src, mid, dst) in enumerate(asis):
        late[i].wait()
        writes.append(start(mid, dst, out_sem.at[2 * FINISH_STEPS + i]))
    for copy in writes:
        copy.wait()


def fused(
    seqs,
    views,
    tokens,
    scene_ids,
    live_mask,
    out_grad,
    attention_gain,
    input_weight,
    output_weight,
    feedforward_gain,
    up_weight,
    down_weight,
):
    rows, width = tokens.shape[1:]
    hidden = up_weight.shape[0]
    spec = scratch_of(rows, width, seqs, views, hidden)
    vmem = pl.BlockSpec(memory_space=pltpu.VMEM)
    anywhere = pl.BlockSpec(memory_space=pl.ANY)
    shape = jax.ShapeDtypeStruct
    bf, f3 = jnp.bfloat16, jnp.float32
    layer_raw, tokens_raw, gains, w_raw, o_raw, up_part, up_away, down_raw = pl.pallas_call(
        functools.partial(layer_kernel, tuple(spec), seqs, views),
        out_shape=(
            shape((rows, width), bf),
            shape((rows, width), f3),
            shape((8, width), f3),
            shape((3, width, width), bf),
            shape((width, width), bf),
            shape((hidden, width), f3),
            shape((hidden, width), bf),
            shape((hidden, width), f3),
        ),
        in_specs=[anywhere, vmem, vmem, anywhere, vmem, vmem] + [anywhere] * 4,
        out_specs=(anywhere, anywhere, vmem) + (anywhere,) * 5,
        scratch_shapes=list(spec.values()),
        compiler_params=pltpu.CompilerParams(
            collective_id=0, has_side_effects=True, vmem_limit_bytes=67043328
        ),
        name="layer",
    )(
        tokens[0],
        scene_ids,
        live_mask,
        out_grad[0],
        attention_gain,
        feedforward_gain,
        input_weight,
        output_weight,
        up_weight,
        down_weight,
    )
    shift = [(j, (j + views // 2) % views) for j in range(views)]
    up_grad = up_part + lax.ppermute(up_away, "view", shift).astype(f3)
    layer_out, tokens_grad, gain_one, w_grad, o_grad, gain_two, down_grad = pl.pallas_call(
        finish_kernel,
        out_shape=(
            shape((rows, width), bf),
            shape((rows, width), f3),
            shape((width,), f3),
            shape((width, 3 * width), f3),
            shape((width, width), f3),
            shape((width,), f3),
            shape((hidden, width), f3),
        ),
        in_specs=[anywhere] * 2 + [vmem] + [anywhere] * 3,
        out_specs=(anywhere, anywhere, vmem, anywhere, anywhere, vmem, anywhere),
        scratch_shapes=[
            pltpu.VMEM((rows, width), bf),
            pltpu.VMEM((rows, width), f3),
            pltpu.VMEM((hidden, width), f3),
            pltpu.VMEM((3, width, width), bf),
            pltpu.VMEM((width, width), bf),
            pltpu.VMEM((width, 3 * width), f3),
            pltpu.VMEM((width, width), f3),
            pltpu.SemaphoreType.DMA((2 * FINISH_STEPS + 4,)),
            pltpu.SemaphoreType.DMA((2 * FINISH_STEPS + 4,)),
        ],
        cost_estimate=pl.CostEstimate(
            flops=4 * width * width, transcendentals=0, bytes_accessed=28 * width * width
        ),
        name="finish",
    )(layer_raw, tokens_raw, gains, w_raw, o_raw, down_raw)
    return (
        layer_out[None],
        tokens_grad[None],
        gain_one,
        w_grad,
        o_grad,
        gain_two,
        up_grad,
        down_grad,
    )


def solution(mesh):
    seqs, views = mesh.shape["seq"], mesh.shape["view"]
    small = seqs == 4 and views == 2 * LEVELS and HEADS == 2 * views
    body = functools.partial(fused, seqs, views) if small else shards
    return jax.shard_map(
        body,
        mesh=mesh,
        in_specs=(
            P("seq", "view", None),
            P("seq", "view"),
            P("seq", "view"),
            P("seq", "view", None),
            P(),
            P(),
            P(),
            P(),
            P(("seq", "view"), None),
            P(("seq", "view"), None),
        ),
        out_specs=(
            P("seq", "view", None),
            P("seq", "view", None),
            P(),
            P(),
            P(),
            P(),
            P(("seq", "view"), None),
            P(("seq", "view"), None),
        ),
        check_vma=False,
    )
```

```python
import functools
import math
import types

import jax
import jax.numpy as jnp
from jax import lax
from jax.experimental import pallas as pl
from jax.experimental.pallas import tpu as pltpu
from jax.sharding import PartitionSpec as P

HEADS = 16
HEAD_DIM = 64


EPS = 1e-05
NEGATIVE = -1e30
MESH = pl.DeviceIdType.MESH
SLOTS = 4
SCENE_BLOCKS = 16


def layer_norm(values, gain):
    center = values - jnp.mean(values, axis=-1, keepdims=True)
    spread = jnp.mean(center * center, axis=-1, keepdims=True)
    return center * lax.rsqrt(spread + EPS) * gain


def gelu_exact(values):
    return jax.nn.gelu(values, approximate=False)


def plain_dot(left, right):
    return jnp.dot(left, right, preferred_element_type=jnp.float32)


def dot_inner(left, right):
    return lax.dot_general(
        left, right, (((1,), (1,)), ((), ())), preferred_element_type=jnp.float32
    )


def dot_outer(left, right):
    return lax.dot_general(
        left, right, (((0,), (0,)), ((), ())), preferred_element_type=jnp.float32
    )


def split_heads(values):
    return values.reshape(values.shape[0], HEADS, HEAD_DIM)


def masked_scores(queries, keys, query_tags, key_tags, scale):
    raw = jnp.einsum("qhe,khe->hqk", queries, keys, preferred_element_type=jnp.float32) * scale
    allowed = (query_tags[:, None] == key_tags[None, :])[None]
    return (raw, allowed)


def probabilities(queries, keys, query_tags, key_tags, log_total, scale):
    raw, allowed = masked_scores(queries, keys, query_tags, key_tags, scale)
    return jnp.where(
        allowed, jnp.exp(jnp.where(allowed, raw - log_total[:, :, None], NEGATIVE)), 0.0
    )


def in_blocks(step, carry, piece):
    count = piece[0].shape[0]
    size = math.gcd(count, 512)
    number = count // size
    stacked = tuple((member.reshape((number, size) + member.shape[1:]) for member in piece))

    def inner(state, item):
        members, offset = item
        return (step(state, members, offset * size), None)

    result, unused = lax.scan(inner, carry, (stacked, jnp.arange(number, dtype=jnp.int32)))
    return result


def shards(
    tokens,
    scene_ids,
    live_mask,
    out_grad,
    attention_gain,
    input_weight,
    output_weight,
    feedforward_gain,
    up_weight,
    down_weight,
):
    scale = HEAD_DIM ** (-0.5)
    inputs = tokens[0].astype(jnp.float32)
    rows = inputs.shape[0]
    width = inputs.shape[1]
    tags = scene_ids[0] * 2 + live_mask[0]
    live = live_mask[0].astype(jnp.float32)[:, None]
    every_tag = lax.all_gather(tags, "view", axis=0, tiled=True)
    up_full, down_full = (
        lax.all_gather(up_weight, ("seq", "view"), axis=0, tiled=True),
        lax.all_gather(down_weight, ("seq", "view"), axis=0, tiled=True),
    )
    gain_one = attention_gain.astype(jnp.float32)
    gain_two = feedforward_gain.astype(jnp.float32)
    normed = layer_norm(inputs, gain_one).astype(jnp.bfloat16)
    projected = plain_dot(normed, input_weight).astype(jnp.bfloat16)
    query_flat = projected[:, :width]
    queries = split_heads(query_flat)
    keys_own = projected[:, width : 2 * width]
    values_own = projected[:, 2 * width :]

    def attend_step(carry, piece, start):
        peak, total, accum = carry
        key_piece, value_piece = piece
        count = key_piece.shape[0]
        key_tags = lax.dynamic_slice_in_dim(every_tag, start, count)
        raw, allowed = masked_scores(queries, split_heads(key_piece), tags, key_tags, scale)
        masked = jnp.where(allowed, raw, NEGATIVE)
        new_peak = jnp.maximum(peak, jnp.max(masked, axis=-1))
        weights = jnp.where(allowed, jnp.exp(masked - new_peak[:, :, None]), 0.0)
        factor = jnp.exp(peak - new_peak)
        total = total * factor + jnp.sum(weights, axis=-1)
        update = jnp.einsum(
            "hqk,khe->qhe",
            weights.astype(jnp.bfloat16),
            split_heads(value_piece),
            preferred_element_type=jnp.float32,
        )
        accum = accum * jnp.transpose(factor)[:, :, None] + update
        return (new_peak, total, accum)

    start_state = (
        jnp.full((HEADS, rows), NEGATIVE, jnp.float32),
        jnp.zeros((HEADS, rows), jnp.float32),
        jnp.zeros((rows, HEADS, HEAD_DIM), jnp.float32),
    )
    peak, total, accum = in_blocks(
        attend_step,
        start_state,
        (
            lax.all_gather(keys_own, "view", axis=0, tiled=True),
            lax.all_gather(values_own, "view", axis=0, tiled=True),
        ),
    )
    attended_heads = accum / jnp.transpose(total)[:, :, None]
    log_total = peak + jnp.log(total)
    attended_low = attended_heads.reshape(rows, width).astype(jnp.bfloat16)
    branch = plain_dot(attended_low, output_weight)
    middle = inputs + live * branch
    normed_two = layer_norm(middle, gain_two).astype(jnp.bfloat16)
    hidden = dot_inner(normed_two, up_full)
    activated = gelu_exact(hidden).astype(jnp.bfloat16)
    mixed = plain_dot(activated, down_full)
    layer_out = (middle + live * mixed).astype(jnp.bfloat16)[None]
    out_cot = out_grad[0].astype(jnp.float32)
    mixed_cot = (live * out_cot).astype(jnp.bfloat16)
    down_grad = dot_outer(activated, mixed_cot)
    activated_cot = dot_inner(mixed_cot, down_full)
    hidden_cot = jax.vjp(gelu_exact, hidden)[1](activated_cot)[0].astype(jnp.bfloat16)
    up_grad = dot_outer(hidden_cot, normed_two)
    normed_two_cot = plain_dot(hidden_cot, up_full)
    second_pull = jax.vjp(layer_norm, middle, gain_two)[1]
    middle_part, gain_two_grad = second_pull(normed_two_cot)
    middle_cot = out_cot + middle_part
    branch_cot = (live * middle_cot).astype(jnp.bfloat16)
    output_weight_grad = dot_outer(attended_low, branch_cot)
    attended_cot = dot_inner(branch_cot, output_weight).astype(jnp.bfloat16)
    cot_heads = split_heads(attended_cot)
    delta = jnp.transpose(jnp.sum(cot_heads.astype(jnp.float32) * attended_heads, axis=-1))
    seq_len = every_tag.shape[0]

    def back_step(carry, piece, start):
        query_cot, key_value_cot = carry
        key_piece, value_piece = piece
        count = key_piece.shape[0]
        key_tags = lax.dynamic_slice_in_dim(every_tag, start, count)
        key_heads = split_heads(key_piece)
        value_heads = split_heads(value_piece)
        probs = probabilities(queries, key_heads, tags, key_tags, log_total, scale)
        prob_cot = jnp.einsum(
            "qhe,khe->hqk", cot_heads, value_heads, preferred_element_type=jnp.float32
        )
        score_cot = (probs * (prob_cot - delta[:, :, None])).astype(jnp.bfloat16)
        query_cot = (
            query_cot
            + jnp.einsum("hqk,khe->qhe", score_cot, key_heads, preferred_element_type=jnp.float32)
            * scale
        )
        key_cot = (
            jnp.einsum("hqk,qhe->khe", score_cot, queries, preferred_element_type=jnp.float32)
            * scale
        )
        value_cot = jnp.einsum(
            "hqk,qhe->khe",
            probs.astype(jnp.bfloat16),
            cot_heads,
            preferred_element_type=jnp.float32,
        )
        stacked = jnp.concatenate(
            [key_cot.reshape(count, width), value_cot.reshape(count, width)], axis=1
        )
        earlier = lax.dynamic_slice_in_dim(key_value_cot, start, count)
        key_value_cot = lax.dynamic_update_slice_in_dim(key_value_cot, earlier + stacked, start, 0)
        return (query_cot, key_value_cot)

    back_state = (
        jnp.zeros((rows, HEADS, HEAD_DIM), jnp.float32),
        jnp.zeros((seq_len, 2 * width), jnp.float32),
    )
    query_cot, key_value_cot = in_blocks(
        back_step,
        back_state,
        (
            lax.all_gather(keys_own, "view", axis=0, tiled=True),
            lax.all_gather(values_own, "view", axis=0, tiled=True),
        ),
    )
    own_cot = lax.psum_scatter(key_value_cot, "view", scatter_dimension=0, tiled=True)
    key_cot_own = own_cot[:, :width]
    value_cot_own = own_cot[:, width:]
    projected_cot = jnp.concatenate(
        [query_cot.reshape(rows, width), key_cot_own, value_cot_own], axis=1
    ).astype(jnp.bfloat16)
    input_weight_grad = dot_outer(normed, projected_cot)
    normed_cot = dot_inner(projected_cot, input_weight)
    first_pull = jax.vjp(layer_norm, inputs, gain_one)[1]
    input_part, gain_one_grad = first_pull(normed_cot)
    tokens_grad = (middle_cot + input_part)[None]
    up_part, down_part = (
        lax.psum_scatter(up_grad, ("seq", "view"), scatter_dimension=0, tiled=True),
        lax.psum_scatter(down_grad, ("seq", "view"), scatter_dimension=0, tiled=True),
    )
    summed = lax.psum(
        (gain_one_grad, input_weight_grad, output_weight_grad, gain_two_grad), ("seq", "view")
    )
    return (layer_out, tokens_grad, summed[0], summed[1], summed[2], summed[3], up_part, down_part)


def dot_nn(left, right):
    return lax.dot_general(left, right, (((1,), (0,)), ((), ())), preferred_element_type=jnp.float32)


def at(start, size):
    return pl.ds(pl.multiple_of(start, size), size)


def norm_stats(values):
    mean = jnp.mean(values, axis=-1, keepdims=True)
    center = values - mean
    spread = jnp.mean(center * center, axis=-1, keepdims=True)
    inverse = lax.rsqrt(spread + EPS)
    return center * inverse, inverse


def norm_back(cot, unit, inverse, gain):
    scaled = cot * gain
    first = jnp.mean(scaled, axis=-1, keepdims=True)
    second = jnp.mean(scaled * unit, axis=-1, keepdims=True)
    return inverse * (scaled - first - unit * second)


class Wires:
    def __init__(self, send_sem, recv_sem, peer):
        self.send_sem, self.recv_sem, self.peer = send_sem, recv_sem, peer
        self.free, self.recvs, self.total, self.pending = list(range(SENDS)), 0, 0, []

    def inbox(self, count):
        base = self.recvs
        self.recvs += count
        assert self.recvs <= RECVS
        return base

    def bulk(self):
        return self.free.pop(0)

    def copy(self, src, dst, lane, slot, device):
        return pltpu.make_async_remote_copy(
            src_ref=src,
            dst_ref=dst,
            send_sem=self.send_sem.at[lane],
            recv_sem=self.recv_sem.at[slot],
            device_id=device,
            device_id_type=MESH,
        )

    def send(self, src, dst, slot, device, when=None, bulk=None):
        lane = self.free.pop(0) if bulk is None else bulk
        copy = self.copy(src, dst, lane, slot, device)
        if when is None:
            copy.start()
        else:
            pl.when(when)(copy.start)
        if bulk is None:
            self.pending.append((self.total, copy, when, lane))
            self.total += 1
        return copy

    def finish(self, entry):
        unused, copy, when, lane = entry
        if when is None:
            copy.wait_send()
        else:
            pl.when(when)(copy.wait_send)
        self.free.append(lane)

    def sent(self, copy):
        for entry in [entry for entry in self.pending if entry[1] is copy]:
            self.finish(entry)
        self.pending = [entry for entry in self.pending if entry[1] is not copy]

    def settle(self, until):
        for entry in [entry for entry in self.pending if entry[0] < until]:
            self.finish(entry)
        self.pending = [entry for entry in self.pending if entry[0] >= until]

    def settle_bulk(self, whole, lane):
        self.copy(whole, whole, lane, 0, self.peer).wait_send()

    def wait(self, dst, slot):
        self.copy(dst, dst, 0, slot, self.peer).wait_recv()


SENDS, RECVS, LOCALS = 67, 126, 17
LEVELS = 4


def scratch_of(rows, width, seqs, views, hidden):
    length = rows * views
    own = width // views
    bf, f3 = jnp.bfloat16, jnp.float32
    vm = pltpu.VMEM
    mlp_rows = hidden * seqs * views // 4
    half, quarter, eighth = width // 2, width // 4, width // 8
    return dict(
        tok=vm((rows, width), bf),
        out_cot=vm((rows, width), bf),
        layer_out=vm((rows, width), bf),
        tokens_grad=vm((rows, width), f3),
        up_grad=vm((hidden, width), f3),
        down_grad=vm((hidden, width), f3),
        w_full=vm((width, 3 * width), bf),
        w_own=vm((width, 3 * own), bf),
        wo=vm((width, width), bf),
        up=vm((mlp_rows, width), bf),
        down=vm((mlp_rows, width), bf),
        ids_all=vm((views, 8, 128), jnp.int32),
        order_vm=vm((16, 128), jnp.int32),
        order_sm=pltpu.SMEM((16, 128), jnp.int32),
        normed=vm((length, width), bf),
        qkv=vm((length, 3 * own), bf),
        qkv_s=vm((length, 3 * own), bf),
        weights=vm((2 * SLOTS, length // SLOTS, length // SLOTS), f3),
        totals=vm((2 * SLOTS, length // SLOTS, 1), f3),
        att_s=vm((length, own), f3),
        att=vm((length, own), bf),
        att_tok=vm((rows, width), bf),
        middle=vm((rows, width), f3),
        normed_two=vm((4 * rows, width), bf),
        mixed_cot=vm((4 * rows, width), bf),
        wide=vm((4 * rows, mlp_rows), f3),
        act=vm((4 * rows, mlp_rows), bf),
        hid_cot=vm((4 * rows, mlp_rows), bf),
        part_own=vm((2, 2, rows, width), f3),
        part_out=vm((2, 3, rows, width), bf),
        part_in=vm((2, 3, rows, width), bf),
        grad_keep=vm((2, mlp_rows // 2, width), bf),
        grad_pass=vm((2, mlp_rows // 2, width), bf),
        grad_core=vm((2, mlp_rows // 2, width), bf),
        grad_y=vm((2, 2, hidden, width), bf),
        grad_z=vm((2, hidden, width), bf),
        branch=vm((rows, width), bf),
        acot_tok=vm((rows, width), bf),
        acot=vm((length, own), bf),
        acot_s=vm((length, own), bf),
        pc_s=vm((length, 3 * own), bf),
        pc=vm((3, length, own), bf),
        pc_flat=vm((length, 3 * own), bf),
        pc_tok=vm((3, rows, width), bf),
        dw_out=vm((2, 3, width // seqs, own), bf),
        dw_x=vm((3, width // seqs, own), bf),
        dw_in=vm((3, 3, width // seqs, own), bf),
        dw_own=vm((3, width // seqs, own), bf),
        do_core=vm((half, width), bf),
        do_core_in=vm((half, width), bf),
        do_first=vm((quarter, width), bf),
        do_first_in=vm((quarter, width), bf),
        do_second=vm((eighth, width), bf),
        do_second_in=vm((eighth, width), bf),
        do_z=vm((eighth, width), bf),
        do_z_in=vm((LEVELS, eighth // LEVELS, width), bf),
        do_own=vm((eighth // LEVELS, width), bf),
        gain_own=vm((8, width), f3),
        gain_in=vm((seqs, 8, width), f3),
        gain_sum=vm((8, width), f3),
        gain_all=vm((views, 8, width), f3),
        send_sem=pltpu.SemaphoreType.DMA((SENDS,)),
        recv_sem=pltpu.SemaphoreType.DMA((RECVS,)),
        local_sem=pltpu.SemaphoreType.DMA((LOCALS,)),
    )


def layer_kernel(names, seqs, views, *refs):
    (tok_hbm, ids, alive, cot_hbm, gain_one_ref, gain_two_ref, w_hbm, wo_hbm, up_hbm, down_hbm) = refs[:10]
    (layer_hbm, tokens_hbm, gains, w_grad, o_grad, up_part, up_away, down_hbm_out) = refs[10:18]
    k = types.SimpleNamespace(**dict(zip(names, refs[18:])))
    k.slope = k.part_all = k.do_keep = k.wide
    tok, out_cot = k.tok, k.out_cot
    layer_out, tokens_grad, up_grad, down_grad = k.layer_out, k.tokens_grad, k.up_grad, k.down_grad
    rows, width = tok.shape
    length = rows * views
    own = width // views
    hidden = up_hbm.shape[0]
    mlp_rows = k.up.shape[0]
    half = mlp_rows // 2
    block = length // (SLOTS * SCENE_BLOCKS)
    scene = length // SLOTS
    scale = HEAD_DIM ** (-0.5)
    bf, f3 = jnp.bfloat16, jnp.float32

    s = lax.axis_index("seq")
    v = lax.axis_index("view")
    x, c, z, y = s // 2, s % 2, v // 2, v % 2
    x_s, c_s, xc_s = (1 - x) * 2 + c, x * 2 + (1 - c), (1 - x) * 2 + (1 - c)
    y_v = z * 2 + (1 - y)
    z_pair, z_two, z_flip = z + 1 - 2 * (z % 2), lax.rem(z + 2, LEVELS), LEVELS - 1 - z
    inner = (z == 1) | (z == 2)
    others_z = [z_pair, z_two, z_flip]
    low, high = z % 2, z // 2
    pair_v = z_pair * 2 + y
    own_slot, x_slot = x * 2 + low, (1 - x) * 2 + low
    pair_slot, far_slot = x * 2 + (1 - low), (1 - x) * 2 + (1 - low)
    view_peers = [lax.rem(v + d, views) for d in range(1, views)]
    seq_peers = [x_s, xc_s, c_s]

    def level(zt):
        return (s, zt * 2 + y)

    wires = Wires(k.send_sem, k.recv_sem, (c_s, v))
    in_normed = wires.inbox(2 * views)
    in_ids = wires.inbox(views)
    in_up = wires.inbox(LEVELS + 1)
    in_down = wires.inbox(LEVELS + 1)
    in_mcot = wires.inbox(4)
    in_att = wires.inbox(views)
    in_two = wires.inbox(4)
    in_part = [wires.inbox(5), wires.inbox(5)]
    in_core = [wires.inbox(1), wires.inbox(1)]
    in_grad = [wires.inbox(3), wires.inbox(3)]
    in_acot, in_pc = in_ids, in_att
    in_dw = wires.inbox(3)
    in_do = wires.inbox(3)
    in_do_z = wires.inbox(LEVELS)
    in_plane = wires.inbox(views)
    in_query = wires.inbox(views)
    in_cross = wires.inbox(views)
    in_mate = [wires.inbox(1) for unused in range(3)]
    in_out = [wires.inbox(views), wires.inbox(views)]
    in_out_mate = wires.inbox(1)
    in_gain = wires.inbox(seqs)
    in_gains = in_normed
    to_view = [wires.bulk() for unused in range(5)]
    to_mate_w = [wires.bulk() for unused in range(3)]
    to_mate_o = wires.bulk()

    def z_cast(src, dst, slot):
        wires.send(src, dst, slot, level(z_pair))
        wires.send(src, dst, slot, level(z_two))
        wires.send(src, dst, slot, level(z_flip), when=inner)

    def z_relay(ref, slot):
        wires.send(ref, ref, slot, level(z_pair), when=inner)

    barrier = pltpu.get_barrier_semaphore()
    greeted = [(s, p) for p in view_peers] + [(p, v) for p in seq_peers]
    for device in greeted:
        pl.semaphore_signal(barrier, inc=1, device_id=device, device_id_type=MESH)

    loads, kept = [], []

    def load(src, dst):
        copy = pltpu.make_async_copy(src, dst, k.local_sem.at[len(loads)])
        copy.start()
        loads.append(copy)
        return copy

    up_slot = at((c * 4 + y * 2 + high) * hidden, hidden)
    load_tok = load(tok_hbm, tok)
    load_cot = load(cot_hbm, out_cot)
    load_up = load(up_hbm, k.up.at[up_slot])
    load_down = load(down_hbm, k.down.at[up_slot])
    load_own = [
        load(w_hbm.at[:, at(t * width + v * own, own)], k.w_own.at[:, pl.ds(t * own, own)])
        for t in range(3)
    ]
    load_wo = load(wo_hbm, k.wo)
    load_w = load(w_hbm, k.w_full)

    gain_one = gain_one_ref[...].astype(f3).reshape(1, width)
    gain_two = gain_two_ref[...].astype(f3).reshape(1, width)
    load_tok.wait()
    unit, _ = norm_stats(tok[...].astype(f3))
    k.normed[at(v * rows, rows), :] = (unit * gain_one).astype(bf)
    per = rows // block
    lane = lax.broadcasted_iota(jnp.int32, (1, 128), 1)
    scenes = jnp.zeros((1, 128), jnp.int32)
    for m in range(per):
        mine = jnp.broadcast_to(ids[:, m * block : m * block + 1], (1, 128))
        scenes = jnp.where(lane == v * per + m, mine, scenes)
    k.ids_all[v] = jnp.broadcast_to(scenes, (8, 128))
    live = jnp.transpose(jnp.broadcast_to(alive[...].astype(f3), (rows, rows)))[:, :1]
    pl.semaphore_wait(barrier, len(greeted))

    def view_rows(ref, j):
        return ref.at[at(j * rows, rows)]

    for p in view_peers:
        wires.send(k.ids_all.at[v], k.ids_all.at[v], in_ids + v, (s, p), bulk=to_view[0])

    def normed_half(j, i):
        return k.normed.at[at(j * rows + i * (rows // 2), rows // 2)], in_normed + 2 * j + i

    for i in range(2):
        mine, slot = normed_half(v, i)
        wires.send(mine, mine, slot, (s, y_v))
    for zt in (z_pair, z_two):
        for i in range(2):
            mine, slot = normed_half(v, i)
            wires.send(mine, mine, slot, level(zt))
    for i in range(2):
        mine, slot = normed_half(v, i)
        wires.send(mine, mine, slot, level(z_flip), when=inner)
    load_cot.wait()
    mcot_own = at(own_slot * rows, rows)
    k.mixed_cot[mcot_own, :] = (live * out_cot[...].astype(f3)).astype(bf)

    def slot_rows(ref, slot):
        return ref.at[at(slot * rows, rows)]

    def square_send(ref, base, slot, device):
        wires.send(slot_rows(ref, slot), slot_rows(ref, slot), base + slot, device)

    def square_relay(ref, base):
        wires.wait(slot_rows(ref, pair_slot), base + pair_slot)
        square_send(ref, base, pair_slot, (x_s, v))

    square_send(k.mixed_cot, in_mcot, own_slot, (x_s, v))

    for p in view_peers:
        wires.wait(k.ids_all.at[p], in_ids + p)
    count = SLOTS * SCENE_BLOCKS
    scene_row = k.ids_all[0][:1]
    for j in range(1, views):
        scene_row = scene_row + k.ids_all[j][:1]
    big = lax.broadcasted_iota(jnp.int32, (128, 128), 0)
    wide = lax.broadcasted_iota(jnp.int32, (128, 128), 1)
    scene_mat = jnp.broadcast_to(scene_row, (128, 128))
    scene_col = jnp.transpose(scene_mat)
    ahead = (scene_col < scene_mat) | ((scene_col == scene_mat) & (big < wide))
    place = jnp.sum(jnp.where(ahead & (big < count), 1, 0), axis=0, keepdims=True)
    place_col = jnp.transpose(jnp.broadcast_to(place, (128, 128)))
    hit = jnp.where((place_col == wide) & (big < count), big, 0)
    source = jnp.sum(hit, axis=0, keepdims=True)
    k.order_vm[0:8, :] = jnp.broadcast_to(source, (8, 128))
    k.order_vm[8:16, :] = jnp.broadcast_to(place, (8, 128))
    to_scalar = load(k.order_vm, k.order_sm)

    for copy in load_own:
        copy.wait()

    def mlp_slot(ref, yt, ht):
        return ref.at[at((c * 4 + yt * 2 + ht) * hidden, hidden)]

    def send_mlp(ref, base, device):
        mine = mlp_slot(ref, y, high)
        wires.send(mine, mine, base + y * 2 + high, device)

    def mlp_relay(ref, base):
        there = mlp_slot(ref, y, 1 - high)
        wires.wait(there, base + y * 2 + 1 - high)
        wires.send(there, there, base + y * 2 + 1 - high, (s, y_v))

    def core_exchange(ref, base):
        for ht in (high, 1 - high):
            wires.wait(mlp_slot(ref, 1 - y, ht), base + (1 - y) * 2 + ht)
        mine = ref.at[at(c * half, half)]
        wires.send(mine, mine, base + LEVELS, (c_s, v))

    def project(j):
        k.qkv[at(j * rows, rows), :] = dot_nn(k.normed[at(j * rows, rows), :], k.w_own[...]).astype(bf)

    project(v)
    for zt in others_z:
        j = zt * 2 + y
        for i in range(2):
            there, slot = normed_half(j, i)
            wires.wait(there, slot)
            if zt is z_two:
                z_relay(there, slot)
            wires.send(there, there, slot, (s, y_v))
        if zt is z_two:
            load_up.wait()
            send_mlp(k.up, in_up, level(z_two))
            square_send(k.mixed_cot, in_mcot, own_slot, (s, pair_v))
        project(j)
    send_mlp(k.up, in_up, (s, y_v))
    for zt in [z] + others_z:
        j = zt * 2 + 1 - y
        for i in range(2):
            wires.wait(*normed_half(j, i))
        project(j)
    to_scalar.wait()

    def reorder(dst, src, row):
        blocks = src.reshape(count, block, src.shape[1])

        def step(i, unused):
            from_block = k.order_sm[row, i]
            dst[at(i * block, block), :] = blocks[from_block].astype(dst.dtype)
            return unused

        lax.fori_loop(0, count, step, 0, unroll=16)

    reorder(k.qkv_s, k.qkv, 0)

    head_lane = lax.broadcasted_iota(jnp.int32, (scene, own), 1) // HEAD_DIM

    def attend(g, unused):
        here = at(g * scene, scene)
        queries, keys, values = (k.qkv_s[here, pl.ds(t * own, own)] for t in range(3))
        result = jnp.zeros((scene, own), f3)
        for e in range(2):
            chosen = jnp.where(head_lane == e, queries, jnp.zeros_like(queries))
            weights = jnp.exp(dot_inner(chosen, keys) * scale)
            total = jnp.sum(weights, axis=-1, keepdims=True)
            k.weights[g * 2 + e] = weights
            k.totals[g * 2 + e] = total
            mixed = dot_nn(weights.astype(bf), values) / total
            result = jnp.where(head_lane == e, mixed, result)
        k.att_s[here, :] = result
        return unused

    lax.fori_loop(0, SLOTS, attend, 0, unroll=True)
    reorder(k.att, k.att_s, 8)
    own_cols = at(v * own, own)
    for p in view_peers:
        wires.send(view_rows(k.att, p), k.att_tok.at[:, own_cols], in_att + v, (s, p), bulk=to_view[1])
    square_relay(k.mixed_cot, in_mcot)
    mlp_relay(k.up, in_up)
    load_down.wait()
    send_mlp(k.down, in_down, level(z_two))
    send_mlp(k.down, in_down, (s, y_v))
    k.att_tok[:, own_cols] = k.att[at(v * rows, rows), :]


    load_wo.wait()
    for p in view_peers:
        wires.wait(k.att_tok.at[:, at(p * own, own)], in_att + p)
    tile = 256
    for n in range(width // tile):
        cols = pl.ds(n * tile, tile)
        k.middle[:, cols] = tok[:, cols].astype(f3) + live * dot_nn(k.att_tok[...], k.wo[:, cols])
    unit_two, _ = norm_stats(k.middle[...])
    k.normed_two[mcot_own, :] = (unit_two * gain_two).astype(bf)
    until_two = wires.total
    for device in ((s, pair_v), (x_s, v)):
        square_send(k.normed_two, in_two, own_slot, device)

    core_exchange(k.up, in_up)
    square_relay(k.normed_two, in_two)
    mlp_relay(k.down, in_down)
    wires.wait(k.up.at[at((1 - c) * half, half)], in_up + LEVELS)

    def hidden_tiles(slot):
        here = at(slot * rows, rows)

        def step(n, unused):
            cols = at(n * tile, tile)
            pre = dot_inner(k.normed_two[here, :], k.up[cols, :])
            below = 0.5 + 0.5 * lax.erf(pre * (0.5**0.5))
            k.act[here, cols] = (pre * below).astype(bf)
            k.slope[here, cols] = below + pre * (jnp.exp(-0.5 * pre * pre) * (0.5 / math.pi) ** 0.5)
            return unused

        lax.fori_loop(0, mlp_rows // tile, step, 0)

    hidden_tiles(own_slot)
    hidden_tiles(pair_slot)
    for slot in (x_slot, far_slot):
        wires.wait(slot_rows(k.normed_two, slot), in_two + slot)
        hidden_tiles(slot)

    def grad_tiles(left, right, start, dst):
        def step(n, unused):
            there = at(n * tile, tile)
            dst[there, :] = dot_outer(left[:, at(start + n * tile, tile)], right[...]).astype(dst.dtype)
            return unused

        lax.fori_loop(0, half // tile, step, 0)

    passed = []

    def grad_halves(which, left, right):
        grad_tiles(left, right, (1 - c) * half, k.grad_pass.at[which])
        passed.append(wires.send(k.grad_pass.at[which], k.grad_core.at[which], in_core[which], (c_s, v)))
        grad_tiles(left, right, c * half, k.grad_keep.at[which])

    for slot in (x_slot, far_slot):
        wires.wait(slot_rows(k.mixed_cot, slot), in_mcot + slot)
    core_exchange(k.down, in_down)
    grad_halves(0, k.act, k.mixed_cot)

    def grad_sum(which, start, size):
        there = at(start, size)
        return k.grad_keep[which, there, :].astype(f3) + k.grad_core[which, there, :].astype(f3)

    def grads_to_y(which):
        wires.wait(k.grad_core.at[which], in_core[which])
        wires.sent(passed[which])
        for i, ht in enumerate((1 - high, high)):
            start = ((1 - y) * 2 + ht) * hidden
            there = at(start, hidden)
            k.grad_pass[which, there, :] = grad_sum(which, start, hidden).astype(bf)
            wires.send(k.grad_pass.at[which, there], k.grad_y.at[which, i], in_grad[which] + i, (s, y_v))

    def grad_block(which, i, ht):
        wires.wait(k.grad_y.at[which, i], in_grad[which] + i)
        return grad_sum(which, (y * 2 + ht) * hidden, hidden) + k.grad_y[which, i].astype(f3)

    def grads_to_z(which):
        there = at((y * 2 + 1 - high) * hidden, hidden)
        k.grad_pass[which, there, :] = grad_block(which, 0, 1 - high).astype(bf)
        wires.send(k.grad_pass.at[which, there], k.grad_z.at[which], in_grad[which] + 2, level(z_two))

    def collect(which, dst):
        total = grad_block(which, 1, high)
        wires.wait(k.grad_z.at[which], in_grad[which] + 2)
        dst[...] = total + k.grad_z[which].astype(f3)


    wires.wait(k.down.at[at((1 - c) * half, half)], in_down + LEVELS)

    def cot_tile(n, unused):
        cols = at(n * tile, tile)
        up_to = dot_inner(k.mixed_cot[...], k.down[cols, :])
        k.hid_cot[:, cols] = (up_to * k.slope[:, cols]).astype(bf)
        return unused

    lax.fori_loop(0, mlp_rows // tile, cot_tile, 0, unroll=True)

    strip = width // 2

    def strip_cols(i):
        return pl.ds(i * strip, strip)

    def part_tiles(which, left, right):
        for i in range(2):

            def step(n, unused):
                cols = at(i * strip + n * tile, tile)
                k.part_all[:, cols] = dot_nn(left[...], right[:, cols])
                return unused

            lax.fori_loop(0, strip // tile, step, 0, unroll=True)
            cols = strip_cols(i)
            k.part_out[which, 0, :, cols] = k.part_all[at(far_slot * rows, rows), cols].astype(bf)
            there = k.part_out.at[which, 0, :, cols], k.part_in.at[which, 0, :, cols]
            wires.send(*there, in_part[which] + i, (x_s, v))
        k.part_out[which, 1] = k.part_all[at(x_slot * rows, rows), :].astype(bf)
        wires.send(k.part_out.at[which, 1], k.part_in.at[which, 1], in_part[which] + 2, (x_s, v))
        for i, slot in enumerate((own_slot, pair_slot)):
            k.part_own[which, i] = k.part_all[at(slot * rows, rows), :]

    def part_join(which):
        for i in range(2):
            cols = strip_cols(i)
            wires.wait(k.part_in.at[which, 0, :, cols], in_part[which] + i)
            joined = k.part_own[which, 1, :, cols] + k.part_in[which, 0, :, cols].astype(f3)
            k.part_out[which, 2, :, cols] = joined.astype(bf)
            there = k.part_out.at[which, 2, :, cols], k.part_in.at[which, 2, :, cols]
            wires.send(*there, in_part[which] + 3 + i, (s, pair_v))

    grads_to_y(0)
    part_tiles(0, k.hid_cot, k.up)
    grad_halves(1, k.hid_cot, k.normed_two)
    part_tiles(1, k.act, k.down)
    part_join(0)

    def part_sum(which):
        total = k.part_own[which, 0]
        wires.wait(k.part_in.at[which, 1], in_part[which] + 2)
        for i in range(2):
            wires.wait(k.part_in.at[which, 2, :, strip_cols(i)], in_part[which] + 3 + i)
        for i in (1, 2):
            total = total + k.part_in[which, i].astype(f3)
        return total

    unit_two, inverse_two = norm_stats(k.middle[...])
    wires.settle(until_two)
    cot_two = part_sum(0)
    until_acot = wires.total
    k.gain_own[1:2, :] = jnp.sum(cot_two * unit_two, axis=0, keepdims=True)
    middle_cot = out_cot[...].astype(f3) + norm_back(cot_two, unit_two, inverse_two, gain_two)
    tokens_grad[...] = middle_cot
    k.branch[...] = (live * middle_cot).astype(bf)
    for n in range(width // tile):
        k.acot_tok[:, pl.ds(n * tile, tile)] = dot_inner(
            k.branch[...], k.wo[pl.ds(n * tile, tile), :]
        ).astype(bf)
    for p in view_peers:
        wires.send(k.acot_tok.at[:, at(p * own, own)], view_rows(k.acot, v), in_acot + v, (s, p), bulk=to_view[2])
    k.acot[at(v * rows, rows), :] = k.acot_tok[:, own_cols]

    o_half, o_quarter, o_eighth = width // 2, width // 4, width // 8
    o_piece = o_eighth // LEVELS

    def outer_rows(start, dst, dtype):
        def step(n, unused):
            there = at(n * tile, tile)
            left = k.att_tok[:, at(start + n * tile, tile)]
            dst[there, :] = dot_outer(left, k.branch[...]).astype(dtype)
            return unused

        lax.fori_loop(0, o_half // tile, step, 0)

    outer_rows((1 - c) * o_half, k.do_core, bf)
    wires.send(k.do_core, k.do_core_in, in_do, (c_s, v))
    outer_rows(c * o_half, k.do_keep, f3)
    wires.wait(k.do_core_in, in_do)
    k.do_keep[...] = k.do_keep[...] + k.do_core_in[...].astype(f3)
    k.do_first[...] = k.do_keep[at((1 - x) * o_quarter, o_quarter), :].astype(bf)

    grads_to_y(1)
    part_join(1)
    for p in view_peers:
        wires.wait(view_rows(k.acot, p), in_acot + p)
    reorder(k.acot_s, k.acot, 0)

    def attend_back(g, unused):
        here = at(g * scene, scene)
        queries, keys, values = (k.qkv_s[here, pl.ds(t * own, own)] for t in range(3))
        cots = k.acot_s[here, :]
        agree = cots.astype(f3) * k.att_s[here, :]
        outs = [jnp.zeros((scene, own), f3) for t in range(3)]
        for e in range(2):
            mine = head_lane == e
            delta = jnp.sum(jnp.where(mine, agree, 0.0), axis=-1, keepdims=True)
            chosen = jnp.where(mine, cots, jnp.zeros_like(cots))
            weights = k.weights[g * 2 + e]
            inverse = 1.0 / k.totals[g * 2 + e]
            weights_cot = dot_inner(chosen, values)
            score_cot = (weights * inverse * (weights_cot - delta)).astype(bf)
            shared = (cots.astype(f3) * inverse).astype(bf)
            new = (
                dot_nn(score_cot, keys) * scale,
                dot_outer(score_cot, queries) * scale,
                dot_outer(weights.astype(bf), shared),
            )
            outs = [jnp.where(mine, fresh, old) for fresh, old in zip(new, outs)]
        for t in range(3):
            k.pc_s[here, pl.ds(t * own, own)] = outs[t].astype(bf)
        return unused

    lax.fori_loop(0, SLOTS, attend_back, 0, unroll=True)
    pc_blocks = k.pc_s.reshape(count, block, 3 * own)

    def unsort(i, unused):
        found = pc_blocks[k.order_sm[8, i]]
        k.pc_flat[at(i * block, block), :] = found
        for t in range(3):
            k.pc[t, at(i * block, block), :] = found[:, t * own : (t + 1) * own]
        return unused

    lax.fori_loop(0, count, unsort, 0, unroll=16)
    for p in view_peers:
        wires.send(k.pc.at[:, at(p * rows, rows)], k.pc_tok.at[:, :, own_cols], in_pc + v, (s, p), bulk=to_view[3])
    for t in range(3):
        k.pc_tok[t, :, own_cols] = k.pc[t, at(v * rows, rows), :]

    part = width // seqs

    def own_dw(row_block):
        whole = dot_outer(k.normed[:, at(row_block * part, part)], k.pc_flat[...])
        return [whole[:, t * own : (t + 1) * own] for t in range(3)]

    for i, xt in enumerate((1 - x, x)):
        for t, value in enumerate(own_dw(xt * 2 + 1 - c)):
            k.dw_out[i, t] = value.astype(bf)
        wires.send(k.dw_out.at[i], k.dw_in.at[i], in_dw + i, (c_s, v))
    cross_dw = own_dw(x_s)
    wires.wait(k.dw_in.at[0], in_dw)
    for t in range(3):
        k.dw_x[t] = (cross_dw[t] + k.dw_in[0, t].astype(f3)).astype(bf)
    wires.send(k.dw_x, k.dw_in.at[2], in_dw + 2, (x_s, v))
    mine_dw = own_dw(s)
    wires.wait(k.dw_in.at[1], in_dw + 1)
    wires.settle(until_acot)
    wires.wait(k.dw_in.at[2], in_dw + 2)
    for t in range(3):
        total = mine_dw[t] + k.dw_in[1, t].astype(f3) + k.dw_in[2, t].astype(f3)
        k.dw_own[t] = total.astype(bf)

    def w_at(q, j, first, last):
        return w_grad.at[pl.ds(first, last - first), at(q * part, part), at(j * own, own)]

    def w_plane(j):
        return w_at(s, j, 0, 3)

    def w_query(j):
        return w_at(x_s, j, 0, 1)

    def w_cross(q, j):
        return w_at(q, j, 1, 3)

    wires.send(k.dw_own.at[pl.ds(0, 1)], w_at(s, v, 0, 1), in_query + v, (x_s, v))
    wires.send(k.do_first, k.do_first_in, in_do + 1, (x_s, v))
    wires.send(k.dw_own, w_plane(v), in_plane + v, (s, y_v))
    z_cast(k.dw_own, w_plane(v), in_plane + v)
    wires.send(k.dw_own.at[pl.ds(1, 2)], w_cross(s, v), in_cross + v, (x_s, v))
    wires.send(k.dw_own, w_plane(v), in_mate[0], (c_s, v), bulk=to_mate_w[0])
    kept.append(load(k.dw_own, w_plane(v)))

    wires.wait(w_query(v), in_query + v)
    wires.send(w_query(v), w_query(v), in_query + v, (s, y_v))
    z_cast(w_query(v), w_query(v), in_query + v)
    wires.send(w_query(v), w_query(v), in_mate[1], (c_s, v), bulk=to_mate_w[1])

    wires.wait(k.do_first_in, in_do + 1)
    o_mine = at(x * o_quarter, o_quarter)
    k.do_keep[o_mine, :] = k.do_keep[o_mine, :] + k.do_first_in[...].astype(f3)
    k.do_second[...] = k.do_keep[at(x * o_quarter + (1 - y) * o_eighth, o_eighth), :].astype(bf)
    wires.send(k.do_second, k.do_second_in, in_do + 2, (s, y_v))
    def o_at(q, j):
        at_c, at_x, at_y, at_z = q % 2, q // 2, j % 2, j // 2
        return o_grad.at[at(at_c * o_half + at_x * o_quarter + at_y * o_eighth + at_z * o_piece, o_piece)]

    def to_mate(which, ref):
        wires.send(ref, ref, in_mate[which], (c_s, v), bulk=to_mate_w[which])

    def pass_plane(zt, row_y):
        j = zt * 2 + row_y
        wires.wait(w_plane(j), in_plane + j)
        if row_y is y:
            if zt is z_two:
                z_relay(w_plane(j), in_plane + j)
            wires.send(w_plane(j), w_plane(j), in_plane + j, (s, y_v))
        wires.send(w_cross(s, j), w_cross(s, j), in_cross + j, (x_s, v))
        to_mate(0, w_plane(j))

    def pass_query(zt, row_y):
        j = zt * 2 + row_y
        wires.wait(w_query(j), in_query + j)
        if row_y is y:
            if zt is z_two:
                z_relay(w_query(j), in_query + j)
            wires.send(w_query(j), w_query(j), in_query + j, (s, y_v))
        to_mate(1, w_query(j))

    across = 1 - y
    pass_plane(z, across)

    load_w.wait()
    for p in view_peers:
        wires.wait(k.pc_tok.at[:, :, at(p * own, own)], in_pc + p)

    def back_tile(n, unused):
        cols = at(n * tile, tile)
        total = dot_inner(k.pc_tok[0], k.w_full[cols, pl.ds(0, width)])
        for t in range(1, 3):
            total = total + dot_inner(k.pc_tok[t], k.w_full[cols, pl.ds(t * width, width)])
        k.part_own[0, 0, :, cols] = total
        return unused

    lax.fori_loop(0, width // tile, back_tile, 0)
    unit_one, inverse_one = norm_stats(tok[...].astype(f3))
    cot_one = k.part_own[0, 0]
    k.gain_own[0:1, :] = jnp.sum(cot_one * unit_one, axis=0, keepdims=True)
    k.gain_own[2:8, :] = jnp.zeros((6, width), f3)
    tokens_grad[...] = tokens_grad[...] + norm_back(cot_one, unit_one, inverse_one, gain_one)
    for p in seq_peers:
        wires.send(k.gain_own, k.gain_in.at[s], in_gain + s, (p, v))
    kept.append(load(tokens_grad, tokens_hbm))

    wires.wait(k.do_second_in, in_do + 2)
    total = k.do_keep[at(x * o_quarter + y * o_eighth, o_eighth), :] + k.do_second_in[...].astype(f3)
    k.do_z[...] = total.astype(bf)

    def o_level(zt):
        return at(zt * o_piece, o_piece)

    for zt in others_z:
        wires.send(k.do_z.at[o_level(zt)], k.do_z_in.at[z], in_do_z + z, level(zt))

    pass_plane(z_pair, y)
    pass_plane(z_two, y)
    pass_query(z, across)
    pass_plane(z_pair, across)
    pass_query(z_pair, y)
    pass_query(z_two, y)
    pass_plane(z_flip, y)
    pass_plane(z_two, across)
    there = at((y * 2 + 1 - high) * hidden, hidden)
    k.grad_pass[1, there, :] = grad_block(1, 0, 1 - high).astype(bf)
    kept.append(load(k.grad_pass.at[1, there], up_away))
    up_grad[...] = grad_block(1, 1, high)
    kept.append(load(up_grad, up_part))
    total = k.do_keep[at(x * o_quarter + y * o_eighth + z * o_piece, o_piece), :]
    total = total + k.do_second_in[o_level(z), :].astype(f3)
    for zt in others_z:
        wires.wait(k.do_z_in.at[zt], in_do_z + zt)
        total = total + k.do_z_in[zt].astype(f3)
    k.do_own[...] = total.astype(bf)
    wires.send(k.do_own, o_at(s, v), in_out[0] + v, (s, y_v))
    z_cast(k.do_own, o_at(s, v), in_out[0] + v)
    wires.send(k.do_own, o_at(s, v), in_out[1] + v, (x_s, v))
    wires.send(k.do_own, o_at(s, v), in_out_mate, (c_s, v), bulk=to_mate_o)
    kept.append(load(k.do_own, o_at(s, v)))
    pass_query(z_flip, y)
    pass_plane(z_flip, across)
    for zt in others_z:
        pass_query(zt, across)

    total = k.gain_own[...]
    for p in seq_peers:
        wires.wait(k.gain_in.at[p], in_gain + p)
        total = total + k.gain_in[p]
    k.gain_sum[...] = total
    for p in view_peers:
        wires.send(k.gain_sum, k.gain_all.at[v], in_gains + v, (s, p), bulk=to_view[4])

    def out_mate(q, j):
        wires.send(o_at(q, j), o_at(q, j), in_out_mate, (c_s, v), bulk=to_mate_o)

    def pass_out(zt, row_y):
        j = zt * 2 + row_y
        slot = in_out[0] + j
        wires.wait(o_at(s, j), slot)
        if row_y is y:
            if zt is z_two:
                z_relay(o_at(s, j), slot)
            wires.send(o_at(s, j), o_at(s, j), slot, (s, y_v))
        wires.send(o_at(s, j), o_at(s, j), in_out[1] + j, (x_s, v))
        out_mate(s, j)

    for zt in others_z:
        pass_out(zt, y)
    grads_to_z(0)
    for zt in [z] + others_z:
        pass_out(zt, across)

    layer_out[...] = (k.middle[...] + live * part_sum(1)).astype(bf)
    kept.append(load(layer_out, layer_hbm))
    by_arrival = [v] + [zt * 2 + y for zt in others_z] + [zt * 2 + across for zt in [z] + others_z]
    for j in by_arrival:
        wires.wait(w_cross(x_s, j), in_cross + j)
        to_mate(2, w_cross(x_s, j))
    for j in by_arrival:
        wires.wait(o_at(x_s, j), in_out[1] + j)
        out_mate(x_s, j)

    total = k.gain_sum[...]
    for p in view_peers:
        wires.wait(k.gain_all.at[p], in_gains + p)
        total = total + k.gain_all[p]
    gains[...] = total

    collect(0, down_grad)
    kept.append(load(down_grad, down_hbm_out))
    def w_rows(q, first, last):
        return w_grad.at[pl.ds(first, last - first), at(q * part, part)]

    def o_core(core):
        return o_grad.at[at(core * o_half, o_half)]

    wires.settle(wires.total)
    for whole, lane in (
        (k.ids_all.at[pl.ds(0, views - 1)], to_view[0]),
        (k.att.at[pl.ds(0, length - rows)], to_view[1]),
        (k.acot.at[pl.ds(0, length - rows)], to_view[2]),
        (k.pc.at[:, pl.ds(0, length - rows)], to_view[3]),
        (k.gain_all.at[pl.ds(0, views - 1)], to_view[4]),
        (w_rows(s, 0, 3), to_mate_w[0]),
        (w_rows(x_s, 0, 1), to_mate_w[1]),
        (w_rows(x_s, 1, 3), to_mate_w[2]),
        (o_core(c), to_mate_o),
    ):
        wires.settle_bulk(whole, lane)
    wires.wait(w_rows(c_s, 0, 3), in_mate[0])
    wires.wait(w_rows(xc_s, 0, 1), in_mate[1])
    wires.wait(w_rows(xc_s, 1, 3), in_mate[2])
    wires.wait(o_core(1 - c), in_out_mate)
    for copy in kept:
        copy.wait()


FINISH_STEPS = 8


def finish_kernel(*refs):
    (layer_in, tokens_in, gains, w_in, o_in, down_in) = refs[:6]
    (layer_out, tokens_grad, gain_one, w_out, o_out, gain_two, down_out) = refs[6:13]
    (layer, tokens, down, w_narrow, o_narrow, w_wide, o_wide, in_sem, out_sem) = refs[13:]
    width = o_in.shape[0]
    tall = width // FINISH_STEPS
    asis = ((layer_in, layer, layer_out), (tokens_in, tokens, tokens_grad), (down_in, down, down_out))

    def rows(i):
        return pl.ds(i * tall, tall)

    def start(src, dst, sem):
        copy = pltpu.make_async_copy(src, dst, sem)
        copy.start()
        return copy

    reads, writes = [], []
    for i in range(FINISH_STEPS):
        reads.append(start(w_in.at[:, rows(i)], w_narrow.at[:, rows(i)], in_sem.at[2 * i]))
        reads.append(start(o_in.at[rows(i)], o_narrow.at[rows(i)], in_sem.at[2 * i + 1]))
    late = [start(src, mid, in_sem.at[2 * FINISH_STEPS + i]) for i, (src, mid, dst) in enumerate(asis)]
    gain_one[...] = gains[0:1, :].reshape(width)
    gain_two[...] = gains[1:2, :].reshape(width)
    for i in range(FINISH_STEPS):
        reads[2 * i].wait()
        for t in range(3):
            w_wide[rows(i), t * width : (t + 1) * width] = w_narrow[t, rows(i), :].astype(jnp.float32)
        writes.append(start(w_wide.at[rows(i)], w_out.at[rows(i)], out_sem.at[2 * i]))
        reads[2 * i + 1].wait()
        o_wide[rows(i), :] = o_narrow[rows(i), :].astype(jnp.float32)
        writes.append(start(o_wide.at[rows(i)], o_out.at[rows(i)], out_sem.at[2 * i + 1]))
    for i, (src, mid, dst) in enumerate(asis):
        late[i].wait()
        writes.append(start(mid, dst, out_sem.at[2 * FINISH_STEPS + i]))
    for copy in writes:
        copy.wait()


def fused(
    seqs,
    views,
    tokens,
    scene_ids,
    live_mask,
    out_grad,
    attention_gain,
    input_weight,
    output_weight,
    feedforward_gain,
    up_weight,
    down_weight,
):
    rows, width = tokens.shape[1:]
    hidden = up_weight.shape[0]
    spec = scratch_of(rows, width, seqs, views, hidden)
    vmem = pl.BlockSpec(memory_space=pltpu.VMEM)
    anywhere = pl.BlockSpec(memory_space=pl.ANY)
    shape = jax.ShapeDtypeStruct
    bf, f3 = jnp.bfloat16, jnp.float32
    layer_raw, tokens_raw, gains, w_raw, o_raw, up_part, up_away, down_raw = pl.pallas_call(
        functools.partial(layer_kernel, tuple(spec), seqs, views),
        out_shape=(
            shape((rows, width), bf),
            shape((rows, width), f3),
            shape((8, width), f3),
            shape((3, width, width), bf),
            shape((width, width), bf),
            shape((hidden, width), f3),
            shape((hidden, width), bf),
            shape((hidden, width), f3),
        ),
        in_specs=[anywhere, vmem, vmem, anywhere, vmem, vmem] + [anywhere] * 4,
        out_specs=(anywhere, anywhere, vmem) + (anywhere,) * 5,
        scratch_shapes=list(spec.values()),
        compiler_params=pltpu.CompilerParams(
            collective_id=0, has_side_effects=True, vmem_limit_bytes=67043328
        ),
        name="layer",
    )(
        tokens[0],
        scene_ids,
        live_mask,
        out_grad[0],
        attention_gain,
        feedforward_gain,
        input_weight,
        output_weight,
        up_weight,
        down_weight,
    )
    shift = [(j, (j + views // 2) % views) for j in range(views)]
    up_grad = up_part + lax.ppermute(up_away, "view", shift).astype(f3)
    layer_out, tokens_grad, gain_one, w_grad, o_grad, gain_two, down_grad = pl.pallas_call(
        finish_kernel,
        out_shape=(
            shape((rows, width), bf),
            shape((rows, width), f3),
            shape((width,), f3),
            shape((width, 3 * width), f3),
            shape((width, width), f3),
            shape((width,), f3),
            shape((hidden, width), f3),
        ),
        in_specs=[anywhere] * 2 + [vmem] + [anywhere] * 3,
        out_specs=(anywhere, anywhere, vmem, anywhere, anywhere, vmem, anywhere),
        scratch_shapes=[
            pltpu.VMEM((rows, width), bf),
            pltpu.VMEM((rows, width), f3),
            pltpu.VMEM((hidden, width), f3),
            pltpu.VMEM((3, width, width), bf),
            pltpu.VMEM((width, width), bf),
            pltpu.VMEM((width, 3 * width), f3),
            pltpu.VMEM((width, width), f3),
            pltpu.SemaphoreType.DMA((2 * FINISH_STEPS + 4,)),
            pltpu.SemaphoreType.DMA((2 * FINISH_STEPS + 4,)),
        ],
        cost_estimate=pl.CostEstimate(
            flops=4 * width * width, transcendentals=0, bytes_accessed=28 * width * width
        ),
        name="finish",
    )(layer_raw, tokens_raw, gains, w_raw, o_raw, down_raw)
    return (
        layer_out[None],
        tokens_grad[None],
        gain_one,
        w_grad,
        o_grad,
        gain_two,
        up_grad,
        down_grad,
    )


def solution(mesh):
    seqs, views = mesh.shape["seq"], mesh.shape["view"]
    small = seqs == 4 and views == 2 * LEVELS and HEADS == 2 * views
    body = functools.partial(fused, seqs, views) if small else shards
    return jax.shard_map(
        body,
        mesh=mesh,
        in_specs=(
            P("seq", "view", None),
            P("seq", "view"),
            P("seq", "view"),
            P("seq", "view", None),
            P(),
            P(),
            P(),
            P(),
            P(("seq", "view"), None),
            P(("seq", "view"), None),
        ),
        out_specs=(
            P("seq", "view", None),
            P("seq", "view", None),
            P(),
            P(),
            P(),
            P(),
            P(("seq", "view"), None),
            P(("seq", "view"), None),
        ),
        check_vma=False,
    )
```
